32 devices in a mesh: fsdp: 8 (over z, y), seq: 4 (over x, core).
Axes of the slice: x: 2, y: 2, z: 4, core: 2. Of those that a mesh axis runs over, the one named last changes fastest.
Arguments:
- tokens: bfloat16 [4096, 2048], P(('fsdp', 'seq')), may hold values from -6 to 6
- doc_starts: int32 [8, 8], P('fsdp'), may hold values from 0 to 511, as said below
- attn_gain: bfloat16 [2048], P(('fsdp', 'seq')), may hold values from 0.5 to 1.5
- query_gain: bfloat16 [128], P(('fsdp', 'seq')), may hold values from 0.5 to 1.5
- key_gain: bfloat16 [128], P(('fsdp', 'seq')), may hold values from 0.5 to 1.5
- w_query: bfloat16 [2048, 2048], P(('fsdp', 'seq')), may hold values from -0.125 to 0.125
- key_weight: bfloat16 [2048, 1024], P(('fsdp', 'seq')), may hold values from -0.125 to 0.125
- value_weight: bfloat16 [2048, 1024], P(('fsdp', 'seq')), may hold values from -0.125 to 0.125
- w_headgate: bfloat16 [2048, 16], P(('fsdp', 'seq')), may hold values from -0.125 to 0.125
- w_out: bfloat16 [2048, 2048], P(('fsdp', 'seq')), may hold values from -1 to 1
- ffn_gain: bfloat16 [2048], P(('fsdp', 'seq')), may hold values from 0.5 to 1.5
- w_gate: bfloat16 [2048, 6144], P(('fsdp', 'seq')), may hold values from -0.125 to 0.125
- w_up: bfloat16 [2048, 6144], P(('fsdp', 'seq')), may hold values from -0.125 to 0.125
- w_down: bfloat16 [6144, 2048], P(('fsdp', 'seq')), may hold values from -0.078125 to 0.078125
- cotangent: bfloat16 [4096, 2048], P(('fsdp', 'seq')), may hold values from -6 to 6
Outputs:
- layer_out: bfloat16 [4096, 2048], P(('fsdp', 'seq'))
- tokens_grad: bfloat16 [4096, 2048], P(('fsdp', 'seq'))
- attn_gain_grad: float32 [2048], P(('fsdp', 'seq'))
- query_gain_grad: float32 [128], P(('fsdp', 'seq'))
- key_gain_grad: float32 [128], P(('fsdp', 'seq'))
- query_grad: float32 [2048, 2048], P(('fsdp', 'seq'))
- key_grad: float32 [2048, 1024], P(('fsdp', 'seq'))
- value_grad: float32 [2048, 1024], P(('fsdp', 'seq'))
- headgate_grad: float32 [2048, 16], P(('fsdp', 'seq'))
- out_grad: float32 [2048, 2048], P(('fsdp', 'seq'))
- ffn_gain_grad: float32 [2048], P(('fsdp', 'seq'))
- gate_grad: float32 [2048, 6144], P(('fsdp', 'seq'))
- up_grad: float32 [2048, 6144], P(('fsdp', 'seq'))
- down_grad: float32 [6144, 2048], P(('fsdp', 'seq'))
The draws below stay inside these ranges and needn't reach their ends.
Inputs may be any that keep to these rules, and one draw needn't show every extreme that they name: `doc_starts`: each row begins with 0 and rises strictly.
All inputs are finite; a program needn't handle non-finite values.
Results may differ from the reference program's by a relative error of at most 0.015.
Values may be sent and summed in bfloat16 or wider, within the bound.
A program may use at most 384 MiB of HBM per device.

```python
import jax
import jax.numpy as jnp
from jax import lax

MODEL_WIDTH = 2048
QUERY_HEADS = 16
KEY_VALUE_HEADS = 8
HEAD_SIZE = 128
FF = 6144
DOCS = 8
LENGTH = 512
TOKENS = 4096
N_FSDP = 8


def draw_doc_starts(key, part):
    stream_keys = jax.random.split(jax.random.fold_in(key, 17), N_FSDP)
    row_ids = jnp.arange(N_FSDP, dtype=jnp.int32)

    def one_row(row_key, row_id):
        chosen = jax.random.permutation(row_key, LENGTH - 1)[:DOCS - 1] + 1
        ordered = jnp.sort(chosen.astype(jnp.int32))
        last_entry = jnp.where(row_id == 0, jnp.int32(LENGTH - 1), ordered[DOCS - 2]).astype(jnp.int32)
        ordered = ordered.at[DOCS - 2].set(last_entry)
        return jnp.concatenate([jnp.zeros((1,), jnp.int32), ordered]).astype(jnp.int32)
    return jax.vmap(one_row)(stream_keys, row_ids)


def levels(rng, extent, shards, smallest, largest):
    level, own = 1.0, jax.random.fold_in(rng, 6)
    for axis_at, shards_of in shards:
        draws = jnp.exp(jax.random.uniform(jax.random.fold_in(own, axis_at), (shards_of,), jnp.float32, smallest / len(shards), largest / len(shards)))
        level = level * jnp.repeat(draws, extent[axis_at] // shards_of).reshape([-1 if axis == axis_at else 1 for axis in range(len(extent))])
    return level


def normal_values(stream_key, extent, scale, reach, pieces=(), kind=jnp.bfloat16):
    gain = levels(stream_key, extent, pieces, -0.22, 0.18) if pieces else 1.0
    result = jax.random.normal(stream_key, extent, jnp.float32) * scale * gain
    return jnp.minimum(jnp.maximum(result, -reach), reach).astype(kind)


def setup_inputs(seed: int = 0) -> dict:
    splits = jax.random.split(jax.random.key(seed), 16)
    tokens = normal_values(splits[0], (TOKENS, MODEL_WIDTH), 1.0, 6.0, ((0, 32),))
    doc_starts = draw_doc_starts(jax.random.fold_in(splits[15], 71), 0)
    attn_gain = jnp.clip(1.0 + 0.1 * jax.random.normal(splits[2], (MODEL_WIDTH,), jnp.float32), 0.5, 1.5).astype(jnp.bfloat16)
    query_gain = jnp.clip(1.0 + 0.1 * jax.random.normal(splits[3], (HEAD_SIZE,), jnp.float32), 0.5, 1.5).astype(jnp.bfloat16)
    key_gain = jnp.clip(1.0 + 0.1 * jax.random.normal(splits[4], (HEAD_SIZE,), jnp.float32), 0.5, 1.5).astype(jnp.bfloat16)
    w_query = normal_values(splits[5], (MODEL_WIDTH, QUERY_HEADS * HEAD_SIZE), MODEL_WIDTH ** -0.5, 0.125, ((0, 32),))
    key_weight = normal_values(splits[6], (MODEL_WIDTH, KEY_VALUE_HEADS * HEAD_SIZE), MODEL_WIDTH ** -0.5, 0.125, ((0, 32),))
    value_weight = normal_values(splits[7], (MODEL_WIDTH, KEY_VALUE_HEADS * HEAD_SIZE), MODEL_WIDTH ** -0.5, 0.125, ((0, 32),))
    w_headgate = normal_values(splits[8], (MODEL_WIDTH, QUERY_HEADS), MODEL_WIDTH ** -0.5, 0.125, ((0, 32),))
    w_out = normal_values(splits[9], (QUERY_HEADS * HEAD_SIZE, MODEL_WIDTH), (QUERY_HEADS * HEAD_SIZE // 64) ** -0.5, 1.0, ((0, 32),))
    ffn_gain = jnp.clip(1.0 + 0.1 * jax.random.normal(splits[10], (MODEL_WIDTH,), jnp.float32), 0.5, 1.5).astype(jnp.bfloat16)
    w_gate = normal_values(splits[11], (MODEL_WIDTH, FF), MODEL_WIDTH ** -0.5, 0.125, ((0, 32),))
    w_up = normal_values(splits[12], (MODEL_WIDTH, FF), MODEL_WIDTH ** -0.5, 0.125, ((0, 32),))
    w_down = normal_values(splits[13], (FF, MODEL_WIDTH), FF ** -0.5, 0.078125, ((0, 32),))
    cotangent = normal_values(splits[14], (TOKENS, MODEL_WIDTH), 1.0, 6.0, ((0, 32),))
    return dict(tokens=tokens, doc_starts=doc_starts, attn_gain=attn_gain, query_gain=query_gain, key_gain=key_gain, w_query=w_query, key_weight=key_weight, value_weight=value_weight, w_headgate=w_headgate, w_out=w_out, ffn_gain=ffn_gain, w_gate=w_gate, w_up=w_up, w_down=w_down, cotangent=cotangent)


@jax.custom_vjp
def reduced_precision(v):
    return lax.optimization_barrier(v.astype(jnp.bfloat16)).astype(jnp.float32)

@jax.custom_vjp
def reduced_backward(v):
    return v

def low_keep(v):
    return (reduced_precision(v), None)

def low_pass(kept, grad):
    return (grad,)

def back_keep(v):
    return (v, None)

def back_low(kept, grad):
    return (reduced_precision(grad),)
reduced_precision.defvjp(low_keep, low_pass)
reduced_backward.defvjp(back_keep, back_low)
NORM_EPS = 1e-06
ROPE_BASE = 1000000.0
MASK_FILL = -1e+30
TOP_PRECISION = lax.Precision.HIGHEST

def rms_scale(vector):
    return lax.rsqrt(lax.optimization_barrier(jnp.mean(vector * vector, axis=-1, keepdims=True)) + NORM_EPS)

def rotary_tables(positions):
    half_width = HEAD_SIZE // 2
    exponent = jnp.arange(half_width, dtype=jnp.int32).astype(jnp.float32) * (2.0 / HEAD_SIZE)
    inverse = jnp.power(ROPE_BASE, -exponent)
    angles = positions.astype(jnp.float32)[:, None] * inverse[None, :]
    return (jnp.cos(angles)[:, None, :], jnp.sin(angles)[:, None, :])

def rotate(vector, cosine, sine_table):
    half_width = vector.shape[-1] // 2
    first_half = vector[..., :half_width]
    second = vector[..., half_width:]
    return jnp.concatenate([first_half * cosine - second * sine_table, second * cosine + first_half * sine_table], axis=-1)

def attend(query, keys, values, segment):
    sequence_length = query.shape[0]
    block_rows = min(512, sequence_length)
    block_count = sequence_length // block_rows
    query_group_width = QUERY_HEADS // KEY_VALUE_HEADS
    keys_full = jnp.repeat(keys, query_group_width, axis=1)
    values_full = jnp.repeat(values, query_group_width, axis=1)
    positions = jnp.arange(sequence_length, dtype=jnp.int32)
    score_scale = HEAD_SIZE ** (-0.5)

    def one_block(block_index):
        row_start = (block_index * block_rows).astype(jnp.int32)
        rows_query = lax.dynamic_slice_in_dim(query, row_start, block_rows, 0)
        row_pos = lax.dynamic_slice_in_dim(positions, row_start, block_rows, 0)
        row_seg = lax.dynamic_slice_in_dim(segment, row_start, block_rows, 0)
        scores = jnp.einsum('qhd,khd->hqk', rows_query, keys_full, precision=TOP_PRECISION) * score_scale
        scores = reduced_backward(scores)
        allowed = (row_pos[:, None] >= positions[None, :]) & (row_seg[:, None] == segment[None, :])
        scores = jnp.where(allowed[None], scores, MASK_FILL)
        row_max = lax.optimization_barrier(jnp.max(scores, axis=-1, keepdims=True))
        weights = jnp.exp(scores - row_max)
        probs = reduced_precision(weights / lax.optimization_barrier(jnp.sum(weights, axis=-1, keepdims=True)))
        return jnp.einsum('hqk,khd->qhd', probs, values_full, precision=TOP_PRECISION)
    blocks = lax.map(jax.checkpoint(one_block), jnp.arange(block_count, dtype=jnp.int32))
    return blocks.reshape(sequence_length, QUERY_HEADS, HEAD_SIZE)

def stream_forward(params, stream, starts):
    attn_gain, query_gain, key_gain, w_query, key_weight, value_weight, w_headgate, w_out, ffn_gain, w_gate, w_up, w_down = params
    sequence_length = stream.shape[0]
    positions = jnp.arange(sequence_length, dtype=jnp.int32)
    segment = (lax.optimization_barrier(jnp.sum((positions[:, None] >= starts[None, :]).astype(jnp.int32), axis=1)) - 1).astype(jnp.int32)
    hidden_state = reduced_precision(stream * rms_scale(stream) * attn_gain)
    query_raw = reduced_backward(jnp.dot(hidden_state, w_query, precision=TOP_PRECISION)).reshape(sequence_length, QUERY_HEADS, HEAD_SIZE)
    unnormed_key = reduced_backward(jnp.dot(hidden_state, key_weight, precision=TOP_PRECISION)).reshape(sequence_length, KEY_VALUE_HEADS, HEAD_SIZE)
    value_matrix_rows = reduced_backward(reduced_precision(jnp.dot(hidden_state, value_weight, precision=TOP_PRECISION))).reshape(sequence_length, KEY_VALUE_HEADS, HEAD_SIZE)
    gate_logit = reduced_backward(jnp.dot(hidden_state, w_headgate, precision=TOP_PRECISION))
    cosine, sine_table = rotary_tables(positions)
    query_rows = reduced_backward(reduced_precision(rotate(query_raw * rms_scale(query_raw) * query_gain, cosine, sine_table)))
    key_rows = reduced_backward(reduced_precision(rotate(unnormed_key * rms_scale(unnormed_key) * key_gain, cosine, sine_table)))
    mixed = reduced_backward(reduced_precision(attend(query_rows, key_rows, value_matrix_rows, segment)))
    gated = reduced_precision(mixed * jax.nn.sigmoid(gate_logit)[:, :, None]).reshape(sequence_length, QUERY_HEADS * HEAD_SIZE)
    branch = reduced_backward(jnp.dot(gated, w_out, precision=TOP_PRECISION))
    middle = stream + branch
    hidden_two = reduced_precision(middle * rms_scale(middle) * ffn_gain)
    gate_pre = reduced_backward(jnp.dot(hidden_two, w_gate, precision=TOP_PRECISION))
    up_proj = reduced_backward(jnp.dot(hidden_two, w_up, precision=TOP_PRECISION))
    inner_act = reduced_precision(jax.nn.silu(gate_pre) * up_proj)
    return middle + jnp.dot(inner_act, w_down, precision=TOP_PRECISION)

def reference(tokens, doc_starts, attn_gain, query_gain, key_gain, w_query, key_weight, value_weight, w_headgate, w_out, ffn_gain, w_gate, w_up, w_down, cotangent):
    params = tuple((weight.astype(jnp.float32) for weight in (attn_gain, query_gain, key_gain, w_query, key_weight, value_weight, w_headgate, w_out, ffn_gain, w_gate, w_up, w_down)))
    streams = tokens.astype(jnp.float32).reshape(N_FSDP, LENGTH, MODEL_WIDTH)

    def forward(weight_set, inputs):

        def one_stream(stream_pair):
            return stream_forward(weight_set, stream_pair[0], stream_pair[1])
        return lax.map(one_stream, (inputs, doc_starts))
    output, pullback = jax.vjp(forward, params, streams)
    grads, stream_grad = pullback(cotangent.astype(jnp.float32).reshape(N_FSDP, LENGTH, MODEL_WIDTH))
    return (output.reshape(TOKENS, MODEL_WIDTH).astype(jnp.bfloat16), stream_grad.reshape(TOKENS, MODEL_WIDTH).astype(jnp.bfloat16), grads[0].astype(jnp.float32), grads[1].astype(jnp.float32), grads[2].astype(jnp.float32), grads[3].astype(jnp.float32), grads[4].astype(jnp.float32), grads[5].astype(jnp.float32), grads[6].astype(jnp.float32), grads[7].astype(jnp.float32), grads[8].astype(jnp.float32), grads[9].astype(jnp.float32), grads[10].astype(jnp.float32), grads[11].astype(jnp.float32))
```

```python
import jax
import jax.numpy as jnp
import numpy as np
from jax import lax
from jax.sharding import Mesh, PartitionSpec as P

QUERY_HEADS = 16
KEY_VALUE_HEADS = 8
HEAD_SIZE = 128
GROUP = 8
NORM_EPS = 1e-06
ROPE_BASE = 1000000.0
MASK_FILL = -1e30

DP = "dp"
TP = ("st", "seq")
ALL = ("dp", "st", "seq")
f32 = jnp.float32
bf16 = jnp.bfloat16


def rms_scale(vector):
    return lax.rsqrt(jnp.mean(vector * vector, axis=-1, keepdims=True) + NORM_EPS)


def rotary_tables(positions):
    half_width = HEAD_SIZE // 2
    exponent = jnp.arange(half_width, dtype=jnp.int32).astype(f32) * (2.0 / HEAD_SIZE)
    inverse = jnp.power(ROPE_BASE, -exponent)
    angles = positions.astype(f32)[:, None] * inverse[None, :]
    return (jnp.cos(angles)[:, None, :], jnp.sin(angles)[:, None, :])


def rotate(vector, cosine, sine):
    a, b = jnp.split(vector, 2, axis=-1)
    return jnp.concatenate([a * cosine - b * sine, b * cosine + a * sine], axis=-1)


def rotate_back(vector, cosine, sine):
    a, b = jnp.split(vector, 2, axis=-1)
    return jnp.concatenate([a * cosine + b * sine, b * cosine - a * sine], axis=-1)


def norm_back(grad, normed, scale):
    return scale * (grad - normed * jnp.mean(grad * normed, axis=-1, keepdims=True))


def mm(left, right):
    return jnp.dot(left, right, preferred_element_type=f32)


def mm_t(left, right):
    return lax.dot_general(left, right, (((0,), (0,)), ((), ())), preferred_element_type=f32)


def mm_b(left, right):
    return lax.dot_general(left, right, (((1,), (1,)), ((), ())), preferred_element_type=f32)


def gather_tp(x):
    return lax.all_gather(x, TP, axis=0, tiled=True)


def scatter_tp(x):
    return lax.psum_scatter(x.astype(bf16), TP, scatter_dimension=0, tiled=True).astype(f32)


def gather_dp(x):
    return lax.all_gather(x, DP, axis=0, tiled=True)


def scatter_dp(x):
    return lax.psum_scatter(x.astype(bf16), DP, scatter_dimension=0, tiled=True)


def exchange_tp(x):
    return lax.all_to_all(x, TP, split_axis=0, concat_axis=0, tiled=True)


def local(
    tokens, doc_starts, attn_gain, query_gain, key_gain, w_query, key_weight, value_weight,
    w_headgate, w_out, ffn_gain, w_gate, w_up, w_down, cotangent,
):
    planes = lax.axis_size(DP)
    streams = lax.axis_size("st")
    shards = lax.axis_size("seq")
    devices = planes * GROUP
    rows, width = tokens.shape
    length = rows * shards
    group_rows = rows * GROUP
    wrows = w_query.shape[0]
    brows = w_down.shape[0]
    hidden = brows * planes
    qcols = w_query.shape[1] // GROUP
    kcols = key_weight.shape[1] // GROUP
    group_heads = qcols // HEAD_SIZE
    all_heads = w_headgate.shape[1]
    score_scale = HEAD_SIZE ** (-0.5)
    dp = lax.axis_index(DP)
    tp = lax.axis_index(TP)

    small = jnp.concatenate(
        [w_headgate.reshape(-1), attn_gain, ffn_gain, query_gain, key_gain]
    )[None, :]
    small = lax.all_gather(small, ALL, axis=0, tiled=True)
    hg = wrows * all_heads
    headgate_all = small[:, :hg].reshape(width, all_heads)
    attn_gain_f = small[:, hg : hg + wrows].reshape(-1).astype(f32)
    ffn_gain_f = small[:, hg + wrows : hg + 2 * wrows].reshape(-1).astype(f32)
    gcols = query_gain.shape[0]
    at = hg + 2 * wrows
    query_gain_f = small[:, at : at + gcols].reshape(-1).astype(f32)
    key_gain_f = small[:, at + gcols : at + 2 * gcols].reshape(-1).astype(f32)
    headgate_own = lax.dynamic_slice_in_dim(headgate_all, tp * group_heads, group_heads, 1)

    attn_pack = jnp.concatenate(
        [
            w_query.reshape(wrows, GROUP, qcols),
            key_weight.reshape(wrows, GROUP, kcols),
            value_weight.reshape(wrows, GROUP, kcols),
        ],
        axis=2,
    ).transpose(1, 0, 2)
    ffn_pack = (
        jnp.stack([w_gate, w_up], axis=1)
        .reshape(wrows, 2, planes, GROUP, brows)
        .transpose(3, 0, 1, 2, 4)
        .reshape(GROUP, wrows, 2 * hidden)
    )
    qkv_w = gather_dp(exchange_tp(attn_pack).reshape(GROUP * wrows, qcols + 2 * kcols))
    pieces = []
    for step in range(planes):
        perm = []
        for src in range(devices):
            perm.append((src, (src % planes + step) % planes * GROUP + src // planes))
        pieces.append(lax.ppermute(w_out, ALL, perm))
    pieces = jnp.stack(pieces)
    order = (dp - jnp.arange(planes)) % planes
    out_w = jnp.take(pieces, order, axis=0).reshape(planes * wrows, width)
    down_w = gather_dp(w_down)
    ffn_w = gather_dp(exchange_tp(ffn_pack).reshape(GROUP * wrows, 2 * hidden))

    starts = lax.all_gather(doc_starts, "st", axis=0, tiled=True)
    tokens_all = gather_tp(tokens)
    cot_all = gather_tp(cotangent)

    residual_all = tokens_all.astype(f32)
    hidden_all = (residual_all * rms_scale(residual_all) * attn_gain_f).astype(bf16)
    qkv = mm(hidden_all, qkv_w)
    gate_logit = mm(hidden_all, headgate_own)
    query_raw = qkv[:, :qcols].reshape(group_rows, group_heads, HEAD_SIZE)
    key_raw = qkv[:, qcols : qcols + kcols].reshape(group_rows, 1, HEAD_SIZE)
    value = qkv[:, qcols + kcols :].astype(bf16).reshape(streams, length, HEAD_SIZE)
    positions = jnp.tile(jnp.arange(length, dtype=jnp.int32), streams)
    cosine, sine = rotary_tables(positions)
    query_scale = rms_scale(query_raw)
    query_normed = query_raw * query_scale
    query = rotate(query_normed * query_gain_f, cosine, sine).astype(bf16)
    query = query.reshape(streams, length, group_heads, HEAD_SIZE)
    key_scale = rms_scale(key_raw)
    key_normed = key_raw * key_scale
    key = rotate(key_normed * key_gain_f, cosine, sine).astype(bf16)
    key = key.reshape(streams, length, HEAD_SIZE)
    stream_pos = jnp.arange(length, dtype=jnp.int32)
    segment = jnp.sum((stream_pos[None, :, None] >= starts[:, None, :]).astype(jnp.int32), axis=2)
    allowed = (stream_pos[:, None] >= stream_pos[None, :])[None] & (
        segment[:, :, None] == segment[:, None, :]
    )
    scores = jnp.einsum("bqgd,bkd->bgqk", query, key, preferred_element_type=f32) * score_scale
    scores = jnp.where(allowed[:, None], scores, MASK_FILL)
    row_max = jnp.max(scores, axis=-1, keepdims=True)
    weights = jnp.exp(scores - row_max)
    probs = weights / jnp.sum(weights, axis=-1, keepdims=True)
    probs_low = probs.astype(bf16)
    mixed = jnp.einsum("bgqk,bkd->bqgd", probs_low, value, preferred_element_type=f32).astype(bf16)
    mixed_f = mixed.astype(f32).reshape(group_rows, group_heads, HEAD_SIZE)
    head_gate = jax.nn.sigmoid(gate_logit)[:, :, None]
    gated = (mixed_f * head_gate).astype(bf16).reshape(group_rows, qcols)

    residual = tokens.astype(f32)
    middle = residual + scatter_tp(mm(gated, out_w))
    scale_two = rms_scale(middle)
    normed_two = middle * scale_two
    hidden_two = gather_tp((normed_two * ffn_gain_f).astype(bf16))

    grad_inner = mm_b(cot_all, down_w)
    gate_up = mm(hidden_two, ffn_w)
    gate_pre, up_proj = gate_up[:, :hidden], gate_up[:, hidden:]
    gate_sig = jax.nn.sigmoid(gate_pre)
    inner_act = (gate_pre * gate_sig * up_proj).astype(bf16)
    down_grad = scatter_dp(mm_t(inner_act, cot_all))
    grad_gate = (grad_inner * up_proj * gate_sig * (1.0 + gate_pre * (1.0 - gate_sig))).astype(bf16)
    grad_up = (grad_inner * gate_pre * gate_sig).astype(bf16)
    grad_gu = jnp.concatenate([grad_gate, grad_up], axis=1)
    ffn_grad = scatter_dp(mm_t(hidden_two, grad_gu))
    layer_out = (middle + scatter_tp(mm(inner_act, down_w))).astype(bf16)
    grad_hidden_two = scatter_tp(mm_b(grad_gu, ffn_w))
    ffn_gain_part = jnp.sum(grad_hidden_two * normed_two, axis=0)
    grad_middle = cotangent.astype(f32) + norm_back(
        grad_hidden_two * ffn_gain_f, normed_two, scale_two
    )
    grad_branch = gather_tp(grad_middle.astype(bf16))

    out_grad = scatter_dp(mm_t(gated, grad_branch))
    grad_gated = mm_b(grad_branch, out_w).reshape(group_rows, group_heads, HEAD_SIZE)
    grad_mixed = (grad_gated * head_gate).astype(bf16).reshape(
        streams, length, group_heads, HEAD_SIZE
    )
    gate_flat = head_gate[:, :, 0]
    grad_logit = (
        jnp.sum(grad_gated * mixed_f, axis=-1) * gate_flat * (1.0 - gate_flat)
    ).astype(bf16)
    grad_probs = jnp.einsum("bqgd,bkd->bgqk", grad_mixed, value, preferred_element_type=f32)
    row_delta = jnp.sum(probs * grad_probs, axis=-1, keepdims=True)
    grad_scores = (probs * (grad_probs - row_delta)).astype(bf16)
    grad_query = (
        jnp.einsum("bgqk,bkd->bqgd", grad_scores, key, preferred_element_type=f32) * score_scale
    ).astype(bf16)
    grad_key = (
        jnp.einsum("bgqk,bqgd->bkd", grad_scores, query, preferred_element_type=f32) * score_scale
    ).astype(bf16)
    grad_value = jnp.einsum(
        "bgqk,bqgd->bkd", probs_low, grad_mixed, preferred_element_type=f32
    ).astype(bf16)
    gqn = rotate_back(
        grad_query.astype(f32).reshape(group_rows, group_heads, HEAD_SIZE), cosine, sine
    )
    query_gain_part = jnp.sum(gqn * query_normed, axis=(0, 1))
    grad_query_raw = norm_back(gqn * query_gain_f, query_normed, query_scale).astype(bf16)
    gkn = rotate_back(grad_key.astype(f32).reshape(group_rows, 1, HEAD_SIZE), cosine, sine)
    key_gain_part = jnp.sum(gkn * key_normed, axis=(0, 1))
    grad_key_raw = norm_back(gkn * key_gain_f, key_normed, key_scale).astype(bf16)
    grad_qkv = jnp.concatenate(
        [
            grad_query_raw.reshape(group_rows, qcols),
            grad_key_raw.reshape(group_rows, kcols),
            grad_value.reshape(group_rows, kcols),
        ],
        axis=1,
    )
    grad_hidden = scatter_tp(mm_b(grad_qkv, qkv_w) + mm_b(grad_logit, headgate_own))
    qkv_grad = scatter_dp(mm_t(hidden_all, grad_qkv))
    headgate_part = mm_t(hidden_all, grad_logit)
    headgate_part = lax.dynamic_update_slice(
        jnp.zeros((width, all_heads), f32), headgate_part, (0, tp * group_heads)
    )
    scale_one = rms_scale(residual)
    normed_one = residual * scale_one
    attn_gain_part = jnp.sum(grad_hidden * normed_one, axis=0)
    tokens_grad = (
        grad_middle + norm_back(grad_hidden * attn_gain_f, normed_one, scale_one)
    ).astype(bf16)

    small_sum = jnp.concatenate(
        [
            headgate_part.reshape(devices, hg),
            attn_gain_part.reshape(devices, wrows),
            ffn_gain_part.reshape(devices, wrows),
            query_gain_part.reshape(devices, gcols),
            key_gain_part.reshape(devices, gcols),
        ],
        axis=1,
    )
    small_sum = lax.psum_scatter(small_sum, ALL, scatter_dimension=0, tiled=True)[0]

    ffn_grad = (
        exchange_tp(ffn_grad.reshape(GROUP, wrows, 2 * hidden))
        .reshape(GROUP, wrows, 2, planes, brows)
        .transpose(2, 1, 3, 0, 4)
        .reshape(2, wrows, hidden * GROUP)
        .astype(f32)
    )
    qkv_grad = (
        exchange_tp(qkv_grad.reshape(GROUP, wrows, qcols + 2 * kcols))
        .transpose(1, 0, 2)
        .astype(f32)
    )
    perm = [(src, src % GROUP * planes + src // GROUP) for src in range(devices)]
    out_grad = lax.ppermute(out_grad, ALL, perm).astype(f32)
    return (
        layer_out,
        tokens_grad,
        small_sum[hg : hg + wrows],
        small_sum[at : at + gcols],
        small_sum[at + gcols : at + 2 * gcols],
        qkv_grad[:, :, :qcols].reshape(wrows, GROUP * qcols),
        qkv_grad[:, :, qcols : qcols + kcols].reshape(wrows, GROUP * kcols),
        qkv_grad[:, :, qcols + kcols :].reshape(wrows, GROUP * kcols),
        small_sum[:hg].reshape(wrows, all_heads),
        out_grad,
        small_sum[hg + wrows : hg + 2 * wrows],
        ffn_grad[0],
        ffn_grad[1],
        down_grad.astype(f32),
    )


def solution(mesh):
    shards = mesh.shape["seq"]
    grouped = Mesh(mesh.devices.reshape(-1, GROUP // shards, shards), ("dp", "st", "seq"))
    two = P(ALL, None)
    one = P(ALL)
    return jax.shard_map(
        local,
        mesh=grouped,
        in_specs=(
            two, P(("dp", "st"), None), one, one, one, two, two, two, two, two, one, two, two,
            two, two,
        ),
        out_specs=(two, two, one, one, one, two, two, two, two, two, one, two, two, two),
        check_vma=False,
    )
```

```python
import jax
import jax.numpy as jnp
from jax import lax
from jax.experimental import pallas as pl
from jax.experimental.pallas import tpu as pltpu
from jax.sharding import Mesh, PartitionSpec as P

QUERY_HEADS = 16
KEY_VALUE_HEADS = 8
HEAD_SIZE = 128
GROUP = 8
NORM_EPS = 1e-06
ROPE_BASE = 1000000.0
MASK_FILL = -1e30

DP = "dp"
TP = ("st", "seq")
ALL = ("dp", "st", "seq")
f32 = jnp.float32
bf16 = jnp.bfloat16


def rms_scale(vector):
    return lax.rsqrt(jnp.mean(vector * vector, axis=-1, keepdims=True) + NORM_EPS)


def rotary_tables(positions):
    half_width = HEAD_SIZE // 2
    exponent = jnp.arange(half_width, dtype=jnp.int32).astype(f32) * (2.0 / HEAD_SIZE)
    inverse = jnp.power(ROPE_BASE, -exponent)
    angles = positions.astype(f32)[:, None] * inverse[None, :]
    return (jnp.cos(angles)[:, None, :], jnp.sin(angles)[:, None, :])


def rotate(vector, cosine, sine):
    a, b = jnp.split(vector, 2, axis=-1)
    return jnp.concatenate([a * cosine - b * sine, b * cosine + a * sine], axis=-1)


def rotate_back(vector, cosine, sine):
    a, b = jnp.split(vector, 2, axis=-1)
    return jnp.concatenate([a * cosine + b * sine, b * cosine - a * sine], axis=-1)


def norm_back(grad, normed, scale):
    return scale * (grad - normed * jnp.mean(grad * normed, axis=-1, keepdims=True))


def mm(left, right):
    return jnp.dot(left, right, preferred_element_type=f32)


def mm_t(left, right):
    return lax.dot_general(left, right, (((0,), (0,)), ((), ())), preferred_element_type=f32)


def mm_b(left, right):
    return lax.dot_general(left, right, (((1,), (1,)), ((), ())), preferred_element_type=f32)


def gather_dp(x):
    return lax.all_gather(x, DP, axis=0, tiled=True)


def scatter_dp(x):
    return lax.psum_scatter(x.astype(bf16), DP, scatter_dimension=0, tiled=True)


def pallas(body, out_shape, in_specs, out_specs, scratch, cid, micros):
    return pl.pallas_call(
        body,
        out_shape=out_shape,
        in_specs=in_specs,
        out_specs=out_specs,
        scratch_shapes=scratch,
        compiler_params=pltpu.CompilerParams(
            collective_id=cid, has_side_effects=True, vmem_limit_bytes=40 * 1024 * 1024
        ),
        cost_estimate=pl.CostEstimate(
            flops=0, bytes_accessed=int(micros * 3.6e6), transcendentals=0
        ),
    )


ANY = pl.BlockSpec(memory_space=pl.ANY)
VMEM = pl.BlockSpec(memory_space=pltpu.VMEM)
DMA = pltpu.SemaphoreType.DMA


def remote(src, dst, send, recv, device):
    return pltpu.make_async_remote_copy(
        src_ref=src,
        dst_ref=dst,
        send_sem=send,
        recv_sem=recv,
        device_id=device,
        device_id_type=pl.DeviceIdType.MESH,
    )


class Place:
    def __init__(self, shards):
        self.shards = shards
        self.tp = lax.axis_index("st") * shards + lax.axis_index("seq")
        self.core = self.tp % 2
        self.ring = self.turn(self.tp // 2)

    def turn(self, place):
        if self.shards == GROUP:
            return place
        return place + (place // 2) * (1 - 2 * (place % 2))

    def block(self, ahead, other=False):
        core = 1 - self.core if other else self.core
        return self.turn((self.ring + ahead) % 4) * 2 + core

    def device(self, index):
        return {"st": index // self.shards, "seq": index % self.shards}

    def right(self):
        return self.device(self.block(1))

    def left(self):
        return self.device(self.block(3))

    def partner(self):
        return self.device(self.block(0, True))


def greet(devices):
    barrier = pltpu.get_barrier_semaphore()
    for device in devices:
        pl.semaphore_signal(
            barrier, inc=1, device_id=device, device_id_type=pl.DeviceIdType.MESH
        )
    pl.semaphore_wait(barrier, len(devices))


class RingGather:
    SEMS = 12

    def __init__(self, place, own, out, send, recv):
        rows = out.shape[1]
        half = rows // 2
        first, second = pl.ds(0, half), pl.ds(half, half)
        me, left, right = place.block(0), place.block(3), place.block(1)
        opposite = place.block(2)
        to_left, to_right, to_partner = place.left(), place.right(), place.partner()

        def copy(index, src, block, part, device):
            return remote(src, out.at[block, part], send.at[index], recv.at[index], device)

        self.local = pltpu.make_async_copy(own, out.at[me], send.at[self.SEMS])
        self.own = [
            copy(0, own.at[first], me, first, to_right),
            copy(1, own.at[second], me, second, to_left),
            copy(2, own.at[second], me, second, to_right),
            copy(3, own.at[first], me, first, to_left),
            remote(own, out.at[me], send.at[4], recv.at[4], to_partner),
        ]
        self.on = [
            copy(5, out.at[left, first], left, first, to_right),
            copy(6, out.at[right, second], right, second, to_left),
        ]
        self.across = [
            remote(out.at[left], out.at[left], send.at[7], recv.at[7], to_partner),
            remote(out.at[right], out.at[right], send.at[8], recv.at[8], to_partner),
            copy(9, out.at[opposite, first], opposite, first, to_partner),
            copy(10, out.at[opposite, second], opposite, second, to_partner),
        ]

    def start(self):
        self.local.start()
        for c in self.own:
            c.start()

    def step_near(self):
        self.own[0].wait_recv()
        self.on[0].start()
        self.own[1].wait_recv()
        self.on[1].start()

    def step_across(self):
        self.own[2].wait_recv()
        self.across[0].start()
        self.own[3].wait_recv()
        self.across[1].start()

    def step_far(self):
        self.on[0].wait_recv()
        self.across[2].start()
        self.on[1].wait_recv()
        self.across[3].start()

    def finish(self):
        self.own[4].wait_recv()
        for c in self.across:
            c.wait_recv()
        for c in self.own + self.on + self.across:
            c.wait_send()
        self.local.wait()

    def run(self):
        self.start()
        self.step_near()
        self.step_across()
        self.step_far()
        self.finish()


def ring_scatter(place, x, pair, out, near, far, send, recv, emit):
    rows = x.shape[1]
    half = rows // 2
    step = 32
    to_left, to_right, to_partner = place.left(), place.right(), place.partner()
    swaps = {}
    for q in (2, 1, 3, 0):
        swaps[q] = remote(
            x.at[place.block(q, True)], pair.at[q], send.at[q], recv.at[q], to_partner
        )
        swaps[q].start()

    def add(q, low, high, extra=None):
        block = place.block(q)
        for at in range(low, high, step):
            part = pl.ds(at, step)
            total = x[block, part].astype(f32) + pair[q, part].astype(f32)
            if extra is not None:
                total = total + far[extra, pl.ds(at - low, step)].astype(f32)
            out[q - 1, part] = total.astype(bf16)

    first, second = pl.ds(0, half), pl.ds(half, half)

    def send_to(index, q, part, dst, device):
        c = remote(out.at[q - 1, part], dst, send.at[index], recv.at[index], device)
        c.start()
        return c

    swaps[2].wait_recv()
    add(2, 0, half)
    a = send_to(4, 2, first, far.at[0], to_right)
    add(2, half, rows)
    b = send_to(5, 2, second, far.at[1], to_left)
    swaps[1].wait_recv()
    add(1, half, rows)
    c = send_to(6, 1, second, near.at[0, second], to_right)
    swaps[3].wait_recv()
    add(3, 0, half)
    d = send_to(7, 3, first, near.at[1, first], to_left)
    a.wait_recv()
    add(1, 0, half, 0)
    e = send_to(8, 1, first, near.at[0, first], to_right)
    b.wait_recv()
    add(3, half, rows, 1)
    g = send_to(9, 3, second, near.at[1, second], to_left)
    swaps[0].wait_recv()
    own = place.block(0)
    c.wait_recv()
    d.wait_recv()
    e.wait_recv()
    g.wait_recv()
    for at in range(0, rows, step):
        part = pl.ds(at, step)
        emit(
            part,
            (x[own, part].astype(f32) + pair[0, part].astype(f32))
            + (near[0, part].astype(f32) + near[1, part].astype(f32)),
        )
    for copy in list(swaps.values()) + [a, b, c, d, e, g]:
        copy.wait_send()


def scatter_scratch(rows, width):
    return [
        pltpu.VMEM((4, rows, width), bf16),
        pltpu.VMEM((3, rows, width), bf16),
        pltpu.VMEM((2, rows, width), bf16),
        pltpu.VMEM((2, rows // 2, width), bf16),
        DMA((10,)),
        DMA((10,)),
    ]


def gather_scratch():
    return [DMA((RingGather.SEMS + 1,)), DMA((RingGather.SEMS,))]


def scatter_sum(x, base, shards, cid):
    _, rows, width = x.shape

    def body(x_ref, base_ref, out_ref, pair, out, near, far, send, recv):
        place = Place(shards)
        greet([place.right(), place.left(), place.partner()])

        def emit(part, total):
            out_ref[part] = (base_ref[part] + total).astype(bf16)

        ring_scatter(place, x_ref, pair, out, near, far, send, recv, emit)

    return pallas(
        body, jax.ShapeDtypeStruct((rows, width), bf16), [VMEM, VMEM], VMEM,
        scatter_scratch(rows, width), cid, 25,
    )(x, base)


def middle_step(x, tokens, gain, shards, cid):
    _, rows, width = x.shape

    def body(
        x_ref, tok_ref, gain_ref, mid_ref, all_ref, held, pair, out, near, far, send, recv,
        gsend, grecv,
    ):
        place = Place(shards)
        greet([place.right(), place.left(), place.partner()])

        def emit(part, total):
            middle = tok_ref[part].astype(f32) + total
            mid_ref[part] = middle
            held[part] = (middle * rms_scale(middle) * gain_ref[...]).astype(bf16)

        ring_scatter(place, x_ref, pair, out, near, far, send, recv, emit)
        RingGather(place, held, all_ref, gsend, grecv).run()

    return pallas(
        body,
        (
            jax.ShapeDtypeStruct((rows, width), f32),
            jax.ShapeDtypeStruct((GROUP, rows, width), bf16),
        ),
        [VMEM, VMEM, VMEM],
        (VMEM, ANY),
        [pltpu.VMEM((rows, width), bf16)] + scatter_scratch(rows, width) + gather_scratch(),
        cid,
        50,
    )(x, tokens, gain)


def middle_back(x, middle, cotangent, gain, shards, cid):
    _, rows, width = x.shape

    def body(
        x_ref, mid_ref, cot_ref, gain_ref, dm_ref, part_ref, all_ref, held, pair, out, near, far,
        send, recv, gsend, grecv,
    ):
        place = Place(shards)
        greet([place.right(), place.left(), place.partner()])
        part_ref[...] = jnp.zeros_like(part_ref)

        def emit(part, total):
            middle = mid_ref[part]
            scale = rms_scale(middle)
            normed = middle * scale
            part_ref[...] += jnp.sum(total * normed, axis=0, keepdims=True)
            dm = cot_ref[part].astype(f32) + norm_back(total * gain_ref[...], normed, scale)
            dm_ref[part] = dm
            held[part] = dm.astype(bf16)

        ring_scatter(place, x_ref, pair, out, near, far, send, recv, emit)
        RingGather(place, held, all_ref, gsend, grecv).run()

    return pallas(
        body,
        (
            jax.ShapeDtypeStruct((rows, width), f32),
            jax.ShapeDtypeStruct((1, width), f32),
            jax.ShapeDtypeStruct((GROUP, rows, width), bf16),
        ),
        [VMEM, VMEM, VMEM, VMEM],
        (VMEM, VMEM, ANY),
        [pltpu.VMEM((rows, width), bf16)] + scatter_scratch(rows, width) + gather_scratch(),
        cid,
        50,
    )(x, middle, cotangent, gain)


def tokens_back(x, tokens, dm, gain, shards, cid):
    _, rows, width = x.shape

    def body(
        x_ref, tok_ref, dm_ref, gain_ref, grad_ref, part_ref, pair, out, near, far, send, recv
    ):
        place = Place(shards)
        greet([place.right(), place.left(), place.partner()])
        part_ref[...] = jnp.zeros_like(part_ref)

        def emit(part, total):
            tok = tok_ref[part].astype(f32)
            scale = rms_scale(tok)
            normed = tok * scale
            part_ref[...] += jnp.sum(total * normed, axis=0, keepdims=True)
            grad_ref[part] = (
                dm_ref[part] + norm_back(total * gain_ref[...], normed, scale)
            ).astype(bf16)

        ring_scatter(place, x_ref, pair, out, near, far, send, recv, emit)

    return pallas(
        body,
        (
            jax.ShapeDtypeStruct((rows, width), bf16),
            jax.ShapeDtypeStruct((1, width), f32),
        ),
        [VMEM, VMEM, VMEM, VMEM],
        (VMEM, VMEM),
        scatter_scratch(rows, width),
        cid,
        25,
    )(x, tokens, dm, gain)


class Exchange:
    SEMS = GROUP

    def __init__(self, place, x, out, send, recv):
        self.local = pltpu.make_async_copy(x.at[place.tp], out.at[place.tp], send.at[0])
        self.copies = []
        for k in range(1, GROUP):
            peer = (place.tp + k) % GROUP
            self.copies.append(
                remote(x.at[peer], out.at[place.tp], send.at[k], recv.at[k], place.device(peer))
            )

    def start(self):
        for c in self.copies:
            c.start()
        self.local.start()

    def finish(self):
        for c in self.copies:
            c.wait_recv()
        for c in self.copies:
            c.wait_send()
        self.local.wait()


def group_peers(place):
    return [place.device((place.tp + k) % GROUP) for k in range(1, GROUP)]


def exchange(x, shards, cid, micros):
    def body(x_ref, out_ref, send, recv):
        place = Place(shards)
        greet(group_peers(place))
        run = Exchange(place, x_ref, out_ref, send, recv)
        run.start()
        run.finish()

    return pallas(
        body, jax.ShapeDtypeStruct(x.shape, x.dtype), [VMEM], VMEM,
        [DMA((GROUP,)), DMA((GROUP,))], cid, micros,
    )(x)


def spread(tokens, cotangent, small, w_out, ffn_pack, planes, shards, cid):
    rows, width = tokens.shape
    wrows = w_out.shape[0]
    srows, scols = small.shape

    def body(
        tok_ref, cot_ref, small_ref, wout_ref, ffn_ref, tok_all, cot_all, small_all, wout_all,
        ffn_all, tsend, trecv, csend, crecv, ssend, srecv, psend, precv, wsend, wrecv, fsend,
        frecv,
    ):
        place = Place(shards)
        dp = lax.axis_index(DP)
        tp = place.tp
        flat = dp * GROUP + tp
        owner = flat // planes
        slot = flat % planes
        barrier = pltpu.get_barrier_semaphore()

        def signal(device):
            pl.semaphore_signal(
                barrier, inc=1, device_id=device, device_id_type=pl.DeviceIdType.MESH
            )

        for device in group_peers(place):
            signal(device)
        for k in range(1, planes):
            signal({"dp": (dp + k) % planes})
        for j in range(planes):
            source = tp * planes + j

            @pl.when(source != flat)
            def _():
                signal({"dp": source // GROUP, **place.device(source % GROUP)})

        pl.semaphore_wait(
            barrier, GROUP - 1 + 2 * (planes - 1) + (owner != tp).astype(jnp.int32)
        )

        small_own = pltpu.make_async_copy(small_ref, small_all.at[tp, dp], ssend.at[0])
        small_own.start()
        small_dp = []
        for k in range(1, planes):
            small_dp.append(
                remote(
                    small_ref, small_all.at[tp, dp], ssend.at[k], srecv.at[k],
                    {"dp": (dp + k) % planes},
                )
            )
            small_dp[-1].start()

        tok = RingGather(place, tok_ref, tok_all, tsend, trecv)
        tok.start()
        ffn = Exchange(place, ffn_ref, ffn_all, fsend, frecv)
        ffn.start()

        def wout_copy(k):
            device = {"dp": (dp + k) % planes, **place.device(owner)}
            return remote(wout_ref, wout_all.at[slot], wsend.at[k], wrecv.at[slot], device)

        wout_own = pltpu.make_async_copy(wout_ref, wout_all.at[slot], wsend.at[0])

        @pl.when(owner == tp)
        def _():
            wout_own.start()

        @pl.when(owner != tp)
        def _():
            wout_copy(0).start()

        for k in range(1, planes):
            wout_copy(k).start()

        small_own.wait()
        for c in small_dp:
            c.wait_recv()
        small_tp = []
        for k in range(1, GROUP):
            small_tp.append(
                remote(
                    small_all.at[tp], small_all.at[tp], psend.at[k], precv.at[k],
                    place.device((tp + k) % GROUP),
                )
            )
            small_tp[-1].start()

        cot = RingGather(place, cot_ref, cot_all, csend, crecv)
        tok.step_near()
        tok.step_across()
        cot.start()
        tok.step_far()
        cot.step_near()
        cot.step_across()
        cot.step_far()
        tok.finish()
        cot.finish()
        ffn.finish()
        for c in small_tp:
            c.wait_recv()
        for c in small_dp + small_tp:
            c.wait_send()

        @pl.when(owner == tp)
        def _():
            wout_own.wait()

        @pl.when(owner != tp)
        def _():
            wout_copy(0).wait_send()

        for k in range(1, planes):
            wout_copy(k).wait_send()
        for j in range(planes):

            @pl.when(tp * planes + j != flat)
            def _():
                remote(
                    wout_ref, wout_all.at[j], wsend.at[0], wrecv.at[j], place.partner()
                ).wait_recv()

    return pallas(
        body,
        (
            jax.ShapeDtypeStruct((GROUP, rows, width), bf16),
            jax.ShapeDtypeStruct((GROUP, rows, width), bf16),
            jax.ShapeDtypeStruct((GROUP, planes, srows, scols), bf16),
            jax.ShapeDtypeStruct((planes, wrows, width), bf16),
            jax.ShapeDtypeStruct(ffn_pack.shape, bf16),
        ),
        [VMEM, VMEM, VMEM, VMEM, VMEM],
        (ANY, ANY, VMEM, VMEM, VMEM),
        gather_scratch() + gather_scratch()
        + [
            DMA((planes,)), DMA((planes,)), DMA((GROUP,)), DMA((GROUP,)),
            DMA((planes,)), DMA((planes,)), DMA((GROUP,)), DMA((GROUP,)),
        ],
        cid,
        60,
    )(tokens, cotangent, small, w_out, ffn_pack)


def settle(qkv_grad, out_grad, small, planes, shards, cid):
    srows = small.shape[1] // planes
    cols = small.shape[2]

    def body(
        q_ref, o_ref, s_ref, q_out, o_out, s_out, got, held, line, qsend, qrecv, osend, orecv,
        asend, arecv, bsend, brecv,
    ):
        place = Place(shards)
        dp = lax.axis_index(DP)
        tp = place.tp
        flat = dp * GROUP + tp
        owner = tp * planes + dp
        source = flat // planes, flat % planes
        barrier = pltpu.get_barrier_semaphore()

        def signal(device):
            pl.semaphore_signal(
                barrier, inc=1, device_id=device, device_id_type=pl.DeviceIdType.MESH
            )

        for device in group_peers(place):
            signal(device)
        for k in range(1, planes):
            signal({"dp": (dp + k) % planes})

        @pl.when(owner != flat)
        def _():
            signal({"dp": source[1], **place.device(source[0])})

        pl.semaphore_wait(barrier, GROUP + planes - 2 + (owner != flat).astype(jnp.int32))

        sums = Exchange(place, s_ref, got, asend, arecv)
        sums.start()
        qkv = Exchange(place, q_ref, q_out, qsend, qrecv)
        qkv.start()
        out_own = pltpu.make_async_copy(o_ref, o_out, osend)
        out_far = remote(
            o_ref, o_out, osend, orecv,
            {"dp": owner // GROUP, **place.device(owner % GROUP)},
        )

        @pl.when(owner == flat)
        def _():
            out_own.start()

        @pl.when(owner != flat)
        def _():
            out_far.start()

        sums.finish()
        held[...] = jnp.sum(got[...], axis=0).reshape(held.shape)
        line_own = pltpu.make_async_copy(held.at[dp], line.at[dp], bsend.at[0])
        line_own.start()
        lines = []
        for k in range(1, planes):
            to = (dp + k) % planes
            lines.append(
                remote(held.at[to], line.at[dp], bsend.at[k], brecv.at[k], {"dp": to})
            )
            lines[-1].start()
        for c in lines:
            c.wait_recv()
        line_own.wait()
        s_out[...] = jnp.sum(line[...], axis=0)
        qkv.finish()
        for c in lines:
            c.wait_send()

        @pl.when(owner == flat)
        def _():
            out_own.wait()

        @pl.when(owner != flat)
        def _():
            out_far.wait()

    return pallas(
        body,
        (
            jax.ShapeDtypeStruct(qkv_grad.shape, bf16),
            jax.ShapeDtypeStruct(out_grad.shape, bf16),
            jax.ShapeDtypeStruct((srows, cols), f32),
        ),
        [VMEM, VMEM, VMEM],
        (VMEM, VMEM, VMEM),
        [
            pltpu.VMEM(small.shape, f32),
            pltpu.VMEM((planes, srows, cols), f32),
            pltpu.VMEM((planes, srows, cols), f32),
            DMA((GROUP,)), DMA((GROUP,)), DMA, DMA,
            DMA((GROUP,)), DMA((GROUP,)), DMA((planes,)), DMA((planes,)),
        ],
        cid,
        20,
    )(qkv_grad, out_grad, small)


def local(
    tokens, doc_starts, attn_gain, query_gain, key_gain, w_query, key_weight, value_weight,
    w_headgate, w_out, ffn_gain, w_gate, w_up, w_down, cotangent,
):
    planes = lax.axis_size(DP)
    streams = lax.axis_size("st")
    shards = lax.axis_size("seq")
    devices = planes * GROUP
    rows, width = tokens.shape
    length = rows * shards
    group_rows = rows * GROUP
    wrows = w_query.shape[0]
    brows = w_down.shape[0]
    hidden = brows * planes
    qcols = w_query.shape[1] // GROUP
    kcols = key_weight.shape[1] // GROUP
    group_heads = qcols // HEAD_SIZE
    all_heads = w_headgate.shape[1]
    score_scale = HEAD_SIZE ** (-0.5)
    dp = lax.axis_index(DP)
    tp = lax.axis_index(TP)

    hg = wrows * all_heads
    gcols = query_gain.shape[0]
    at = hg + 2 * wrows
    docs = doc_starts.shape[1]
    dat = at + 2 * gcols
    count = dat + 2 * docs
    srows = -(-count // 2048) * 16
    small = jnp.concatenate(
        [
            w_headgate.reshape(-1), attn_gain, ffn_gain, query_gain, key_gain,
            (doc_starts[0] // 128).astype(bf16), (doc_starts[0] % 128).astype(bf16),
        ]
    )
    small = jnp.pad(small, (0, srows * 128 - count)).reshape(srows, 128)

    attn_pack = jnp.concatenate(
        [
            w_query.reshape(wrows, GROUP, qcols),
            key_weight.reshape(wrows, GROUP, kcols),
            value_weight.reshape(wrows, GROUP, kcols),
        ],
        axis=2,
    ).transpose(1, 0, 2)
    ffn_pack = (
        jnp.stack([w_gate, w_up], axis=1)
        .reshape(wrows, 2, planes, GROUP, brows)
        .transpose(3, 0, 1, 2, 4)
        .reshape(GROUP, wrows, 2 * hidden)
    )
    attn_pack = exchange(attn_pack, shards, 0, 12)
    qkv_w = gather_dp(attn_pack.reshape(GROUP * wrows, qcols + 2 * kcols))
    tokens_all, cot_all, small, out_w, ffn_w = spread(
        tokens, cotangent, small, w_out, ffn_pack, planes, shards, 1
    )
    tokens_all = tokens_all.reshape(group_rows, width)
    cot_all = cot_all.reshape(group_rows, width)
    out_w = out_w.reshape(planes * wrows, width)
    ffn_w = gather_dp(ffn_w.reshape(GROUP * wrows, 2 * hidden))
    down_w = gather_dp(w_down)
    small = small.transpose(1, 0, 2, 3).reshape(devices, srows * 128)
    headgate_all = small[:, :hg].reshape(width, all_heads)
    attn_gain_f = small[:, hg : hg + wrows].reshape(1, -1).astype(f32)
    ffn_gain_f = small[:, hg + wrows : at].reshape(1, -1).astype(f32)
    query_gain_f = small[:, at : at + gcols].reshape(-1).astype(f32)
    key_gain_f = small[:, at + gcols : dat].reshape(-1).astype(f32)
    headgate_own = lax.dynamic_slice_in_dim(headgate_all, tp * group_heads, group_heads, 1)

    starts = lax.dynamic_slice_in_dim(small, dp * GROUP, GROUP, 0)[::shards, dat:count]
    starts = starts.astype(jnp.int32)
    starts = starts[:, :docs] * 128 + starts[:, docs:]

    residual_all = tokens_all.astype(f32)
    hidden_all = (residual_all * rms_scale(residual_all) * attn_gain_f).astype(bf16)
    qkv = mm(hidden_all, qkv_w)
    gate_logit = mm(hidden_all, headgate_own)
    query_raw = qkv[:, :qcols].reshape(group_rows, group_heads, HEAD_SIZE)
    key_raw = qkv[:, qcols : qcols + kcols].reshape(group_rows, 1, HEAD_SIZE)
    value = qkv[:, qcols + kcols :].astype(bf16).reshape(streams, length, HEAD_SIZE)
    positions = jnp.tile(jnp.arange(length, dtype=jnp.int32), streams)
    cosine, sine = rotary_tables(positions)
    query_scale = rms_scale(query_raw)
    query_normed = query_raw * query_scale
    query = rotate(query_normed * query_gain_f, cosine, sine).astype(bf16)
    query = query.reshape(streams, length, group_heads, HEAD_SIZE)
    key_scale = rms_scale(key_raw)
    key_normed = key_raw * key_scale
    key = rotate(key_normed * key_gain_f, cosine, sine).astype(bf16)
    key = key.reshape(streams, length, HEAD_SIZE)
    stream_pos = jnp.arange(length, dtype=jnp.int32)
    segment = jnp.sum((stream_pos[None, :, None] >= starts[:, None, :]).astype(jnp.int32), axis=2)
    allowed = (stream_pos[:, None] >= stream_pos[None, :])[None] & (
        segment[:, :, None] == segment[:, None, :]
    )
    scores = jnp.einsum("bqgd,bkd->bgqk", query, key, preferred_element_type=f32) * score_scale
    scores = jnp.where(allowed[:, None], scores, MASK_FILL)
    row_max = jnp.max(scores, axis=-1, keepdims=True)
    weights = jnp.exp(scores - row_max)
    probs = weights / jnp.sum(weights, axis=-1, keepdims=True)
    probs_low = probs.astype(bf16)
    mixed = jnp.einsum("bgqk,bkd->bqgd", probs_low, value, preferred_element_type=f32).astype(bf16)
    mixed_f = mixed.astype(f32).reshape(group_rows, group_heads, HEAD_SIZE)
    head_gate = jax.nn.sigmoid(gate_logit)[:, :, None]
    gated = (mixed_f * head_gate).astype(bf16).reshape(group_rows, qcols)

    def parts(x):
        return x.astype(bf16).reshape(GROUP, rows, width)

    middle, hidden_two = middle_step(parts(mm(gated, out_w)), tokens, ffn_gain_f, shards, 2)
    hidden_two = hidden_two.reshape(group_rows, width)

    gate_up = mm(hidden_two, ffn_w)
    gate_pre, up_proj = gate_up[:, :hidden], gate_up[:, hidden:]
    gate_sig = jax.nn.sigmoid(gate_pre)
    inner_act = (gate_pre * gate_sig * up_proj).astype(bf16)
    down_grad = mm_t(inner_act, cot_all).astype(bf16)
    down_w, down_grad = lax.optimization_barrier((down_w, down_grad))
    down_grad = scatter_dp(down_grad)
    grad_inner = mm_b(cot_all, down_w)
    grad_gate = (grad_inner * up_proj * gate_sig * (1.0 + gate_pre * (1.0 - gate_sig))).astype(bf16)
    grad_up = (grad_inner * gate_pre * gate_sig).astype(bf16)
    grad_gu = jnp.concatenate([grad_gate, grad_up], axis=1)
    ffn_grad = mm_t(hidden_two, grad_gu).astype(bf16)
    grad_gu, ffn_grad = lax.optimization_barrier((grad_gu, ffn_grad))
    ffn_grad = scatter_dp(ffn_grad)
    grad_middle, ffn_gain_part, grad_branch = middle_back(
        parts(mm_b(grad_gu, ffn_w)), middle, cotangent, ffn_gain_f, shards, 3
    )
    grad_branch = grad_branch.reshape(group_rows, width)
    layer_out = scatter_sum(parts(mm(inner_act, down_w)), middle, shards, 4)

    out_grad = mm_t(gated, grad_branch).astype(bf16)
    grad_gated = mm_b(grad_branch, out_w).reshape(group_rows, group_heads, HEAD_SIZE)
    grad_mixed = (grad_gated * head_gate).astype(bf16).reshape(
        streams, length, group_heads, HEAD_SIZE
    )
    gate_flat = head_gate[:, :, 0]
    grad_logit = (
        jnp.sum(grad_gated * mixed_f, axis=-1) * gate_flat * (1.0 - gate_flat)
    ).astype(bf16)
    grad_probs = jnp.einsum("bqgd,bkd->bgqk", grad_mixed, value, preferred_element_type=f32)
    row_delta = jnp.sum(probs * grad_probs, axis=-1, keepdims=True)
    grad_scores = (probs * (grad_probs - row_delta)).astype(bf16)
    grad_query = (
        jnp.einsum("bgqk,bkd->bqgd", grad_scores, key, preferred_element_type=f32) * score_scale
    ).astype(bf16)
    grad_key = (
        jnp.einsum("bgqk,bqgd->bkd", grad_scores, query, preferred_element_type=f32) * score_scale
    ).astype(bf16)
    grad_value = jnp.einsum(
        "bgqk,bqgd->bkd", probs_low, grad_mixed, preferred_element_type=f32
    ).astype(bf16)
    gqn = rotate_back(
        grad_query.astype(f32).reshape(group_rows, group_heads, HEAD_SIZE), cosine, sine
    )
    query_gain_part = jnp.sum(gqn * query_normed, axis=(0, 1))
    grad_query_raw = norm_back(gqn * query_gain_f, query_normed, query_scale).astype(bf16)
    gkn = rotate_back(grad_key.astype(f32).reshape(group_rows, 1, HEAD_SIZE), cosine, sine)
    key_gain_part = jnp.sum(gkn * key_normed, axis=(0, 1))
    grad_key_raw = norm_back(gkn * key_gain_f, key_normed, key_scale).astype(bf16)
    grad_qkv = jnp.concatenate(
        [
            grad_query_raw.reshape(group_rows, qcols),
            grad_key_raw.reshape(group_rows, kcols),
            grad_value.reshape(group_rows, kcols),
        ],
        axis=1,
    )
    tokens_grad, attn_gain_part = tokens_back(
        parts(mm_b(grad_qkv, qkv_w) + mm_b(grad_logit, headgate_own)),
        tokens, grad_middle, attn_gain_f, shards, 5,
    )
    qkv_grad = mm_t(hidden_all, grad_qkv).astype(bf16)
    ffn_grad, down_grad, qkv_grad, out_grad = lax.optimization_barrier(
        (ffn_grad, down_grad, qkv_grad, out_grad)
    )
    out_grad = scatter_dp(out_grad)
    qkv_grad = scatter_dp(qkv_grad)
    headgate_part = mm_t(hidden_all, grad_logit)
    headgate_part = lax.dynamic_update_slice(
        jnp.zeros((width, all_heads), f32), headgate_part, (0, tp * group_heads)
    )

    small_sum = jnp.concatenate(
        [
            headgate_part.reshape(devices, hg),
            attn_gain_part.reshape(devices, wrows),
            ffn_gain_part.reshape(devices, wrows),
            query_gain_part.reshape(devices, gcols),
            key_gain_part.reshape(devices, gcols),
        ],
        axis=1,
    )
    small_sum = jnp.pad(small_sum, ((0, 0), (0, srows * 128 - dat)))
    small_sum = small_sum.reshape(planes, GROUP, srows, 128).transpose(1, 0, 2, 3)
    small_sum = small_sum.reshape(GROUP, planes * srows, 128)

    ffn_grad = (
        exchange(ffn_grad.reshape(GROUP, wrows, 2 * hidden), shards, 6, 25)
        .reshape(GROUP, wrows, 2, planes, brows)
        .transpose(2, 1, 3, 0, 4)
        .reshape(2, wrows, hidden * GROUP)
        .astype(f32)
    )
    qkv_grad, out_grad, small_sum = settle(
        qkv_grad.reshape(GROUP, wrows, qcols + 2 * kcols), out_grad, small_sum, planes, shards, 7
    )
    qkv_grad = qkv_grad.transpose(1, 0, 2).astype(f32)
    out_grad = out_grad.astype(f32)
    small_sum = small_sum.reshape(-1)
    return (
        layer_out,
        tokens_grad,
        small_sum[hg : hg + wrows],
        small_sum[at : at + gcols],
        small_sum[at + gcols : at + 2 * gcols],
        qkv_grad[:, :, :qcols].reshape(wrows, GROUP * qcols),
        qkv_grad[:, :, qcols : qcols + kcols].reshape(wrows, GROUP * kcols),
        qkv_grad[:, :, qcols + kcols :].reshape(wrows, GROUP * kcols),
        small_sum[:hg].reshape(wrows, all_heads),
        out_grad,
        small_sum[hg + wrows : hg + 2 * wrows],
        ffn_grad[0],
        ffn_grad[1],
        down_grad.astype(f32),
    )


def solution(mesh):
    shards = mesh.shape["seq"]
    grouped = Mesh(mesh.devices.reshape(-1, GROUP // shards, shards), ("dp", "st", "seq"))
    two = P(ALL, None)
    one = P(ALL)
    return jax.shard_map(
        local,
        mesh=grouped,
        in_specs=(
            two, P(("dp", "st"), None), one, one, one, two, two, two, two, two, one, two, two,
            two, two,
        ),
        out_specs=(two, two, one, one, one, two, two, two, two, two, one, two, two, two),
        check_vma=False,
    )
```

```python
import jax
import jax.numpy as jnp
from jax import lax
from jax.experimental import pallas as pl
from jax.experimental.pallas import tpu as pltpu
from jax.sharding import Mesh, PartitionSpec as P

QUERY_HEADS = 16
KEY_VALUE_HEADS = 8
HEAD_SIZE = 128
GROUP = 8
NORM_EPS = 1e-06
ROPE_BASE = 1000000.0
MASK_FILL = -1e30

DP = ("zh", "y")
TP = ("st", "seq")
ALL = ("zh", "st", "y", "seq")
f32 = jnp.float32
bf16 = jnp.bfloat16


def rms_scale(vector):
    return lax.rsqrt(jnp.mean(vector * vector, axis=-1, keepdims=True) + NORM_EPS)


def rotary_tables(positions):
    half_width = HEAD_SIZE // 2
    exponent = jnp.arange(half_width, dtype=jnp.int32).astype(f32) * (2.0 / HEAD_SIZE)
    inverse = jnp.power(ROPE_BASE, -exponent)
    angles = positions.astype(f32)[:, None] * inverse[None, :]
    return (jnp.cos(angles)[:, None, :], jnp.sin(angles)[:, None, :])


def rotate(vector, cosine, sine):
    a, b = jnp.split(vector, 2, axis=-1)
    return jnp.concatenate([a * cosine - b * sine, b * cosine + a * sine], axis=-1)


def rotate_back(vector, cosine, sine):
    a, b = jnp.split(vector, 2, axis=-1)
    return jnp.concatenate([a * cosine + b * sine, b * cosine - a * sine], axis=-1)


def norm_back(grad, normed, scale):
    return scale * (grad - normed * jnp.mean(grad * normed, axis=-1, keepdims=True))


def mm(left, right):
    return jnp.dot(left, right, preferred_element_type=f32)


def mm_t(left, right):
    return lax.dot_general(left, right, (((0,), (0,)), ((), ())), preferred_element_type=f32)


def mm_b(left, right):
    return lax.dot_general(left, right, (((1,), (1,)), ((), ())), preferred_element_type=f32)


SWAP = [(0, 1), (1, 0)]


def over_dp(x):
    streams, shards = lax.axis_size("st"), lax.axis_size("seq")
    zs, ys = lax.axis_size("zh"), lax.axis_size("y")
    rows, columns = x.shape[1] * shards, x.shape[2]
    x = x.reshape(streams, rows, columns)
    if zs == 2 and ys == 2:
        z, y = lax.axis_index("zh"), lax.axis_index("y")
        z_piece = lax.ppermute(x, "zh", SWAP)
        y_piece = lax.ppermute(x, "y", SWAP)
        zy_piece = lax.ppermute(z_piece, "y", SWAP)
        whole = jnp.zeros((zs, streams, ys, rows, columns), x.dtype)
        for piece, zp, yp in (
            (x, z, y), (y_piece, z, 1 - y), (z_piece, 1 - z, y), (zy_piece, 1 - z, 1 - y)
        ):
            whole = lax.dynamic_update_slice(whole, piece[None, :, None], (zp, 0, yp, 0, 0))
    else:
        whole = lax.all_gather(x, DP, axis=0, tiled=False)
        whole = whole.reshape(zs, ys, streams, rows, columns).transpose(0, 2, 1, 3, 4)
    return whole.reshape(-1, columns)


def pick(x, axis, index):
    return lax.dynamic_index_in_dim(x, index, axis, keepdims=False)


def sum_dp(x):
    zs, ys = x.shape[:2]
    if zs == 2 and ys == 2:
        z, y = lax.axis_index("zh"), lax.axis_index("y")

        def piece(zp, yp):
            return pick(pick(x, 0, zp), 0, yp)

        first = lax.ppermute(piece(1 - z, 1 - y), "y", SWAP)
        second = lax.ppermute(piece(z, 1 - y), "y", SWAP)
        far = (piece(1 - z, y).astype(f32) + first.astype(f32)).astype(bf16)
        third = lax.ppermute(far, "zh", SWAP)
        near = piece(z, y).astype(f32) + second.astype(f32)
        return (near + third.astype(f32)).astype(bf16)
    return lax.psum_scatter(
        x.reshape((zs * ys,) + x.shape[2:]), DP, scatter_dimension=0, tiled=False
    )


def sum_dp_rows(x):
    streams, shards = lax.axis_size("st"), lax.axis_size("seq")
    zs, ys = lax.axis_size("zh"), lax.axis_size("y")
    columns = x.shape[1]
    x = x.reshape(zs, streams, ys, -1, columns).transpose(0, 2, 1, 3, 4)
    return sum_dp(x).reshape(GROUP, -1, columns)


def pallas(body, out_shape, in_specs, out_specs, scratch, cid, micros):
    return pl.pallas_call(
        body,
        out_shape=out_shape,
        in_specs=in_specs,
        out_specs=out_specs,
        scratch_shapes=scratch,
        compiler_params=pltpu.CompilerParams(
            collective_id=cid, has_side_effects=True, vmem_limit_bytes=40 * 1024 * 1024
        ),
        cost_estimate=pl.CostEstimate(
            flops=0, bytes_accessed=int(micros * 3.6e6), transcendentals=0
        ),
    )


ANY = pl.BlockSpec(memory_space=pl.ANY)
VMEM = pl.BlockSpec(memory_space=pltpu.VMEM)
DMA = pltpu.SemaphoreType.DMA


def remote(src, dst, send, recv, device):
    return pltpu.make_async_remote_copy(
        src_ref=src,
        dst_ref=dst,
        send_sem=send,
        recv_sem=recv,
        device_id=device,
        device_id_type=pl.DeviceIdType.MESH,
    )


class Place:
    def __init__(self, shards):
        self.shards = shards
        self.tp = lax.axis_index("st") * shards + lax.axis_index("seq")
        self.core = self.tp % 2
        self.ring = self.turn(self.tp // 2)

    def turn(self, place):
        if self.shards == GROUP:
            return place
        return place + (place // 2) * (1 - 2 * (place % 2))

    def block(self, ahead, other=False):
        core = 1 - self.core if other else self.core
        return self.turn((self.ring + ahead) % 4) * 2 + core

    def device(self, index):
        return {"st": index // self.shards, "seq": index % self.shards}

    def dp_device(self, dp):
        ys = lax.axis_size("y")
        return {"zh": dp // ys, "y": dp % ys}

    def any_device(self, flat):
        ys, streams = lax.axis_size("y"), lax.axis_size("st")
        return {
            "zh": flat // (streams * ys * self.shards),
            "st": flat // (ys * self.shards) % streams,
            "y": flat // self.shards % ys,
            "seq": flat % self.shards,
        }

    def flat(self):
        ys, streams = lax.axis_size("y"), lax.axis_size("st")
        z, y = lax.axis_index("zh"), lax.axis_index("y")
        st, seq = lax.axis_index("st"), lax.axis_index("seq")
        return ((z * streams + st) * ys + y) * self.shards + seq

    def dp(self):
        return lax.axis_index("zh") * lax.axis_size("y") + lax.axis_index("y")

    def right(self):
        return self.device(self.block(1))

    def left(self):
        return self.device(self.block(3))

    def partner(self):
        return self.device(self.block(0, True))


def greet(devices):
    barrier = pltpu.get_barrier_semaphore()
    for device in devices:
        pl.semaphore_signal(
            barrier, inc=1, device_id=device, device_id_type=pl.DeviceIdType.MESH
        )
    pl.semaphore_wait(barrier, len(devices))


class RingGather:
    SEMS = 12

    def __init__(self, place, own, out, send, recv):
        rows = out.shape[1]
        half = rows // 2
        first, second = pl.ds(0, half), pl.ds(half, half)
        me, left, right = place.block(0), place.block(3), place.block(1)
        opposite = place.block(2)
        to_left, to_right, to_partner = place.left(), place.right(), place.partner()

        def copy(index, src, block, part, device):
            return remote(src, out.at[block, part], send.at[index], recv.at[index], device)

        self.local = pltpu.make_async_copy(own, out.at[me], send.at[self.SEMS])
        self.own = [
            copy(0, own.at[first], me, first, to_right),
            copy(1, own.at[second], me, second, to_left),
            copy(2, own.at[second], me, second, to_right),
            copy(3, own.at[first], me, first, to_left),
            remote(own, out.at[me], send.at[4], recv.at[4], to_partner),
        ]
        self.on = [
            copy(5, out.at[left, first], left, first, to_right),
            copy(6, out.at[right, second], right, second, to_left),
        ]
        self.across = [
            remote(out.at[left], out.at[left], send.at[7], recv.at[7], to_partner),
            remote(out.at[right], out.at[right], send.at[8], recv.at[8], to_partner),
            copy(9, out.at[opposite, first], opposite, first, to_partner),
            copy(10, out.at[opposite, second], opposite, second, to_partner),
        ]

    def start(self):
        self.local.start()
        for c in self.own:
            c.start()

    def step_near(self):
        self.own[0].wait_recv()
        self.on[0].start()
        self.own[1].wait_recv()
        self.on[1].start()

    def step_across(self):
        self.own[2].wait_recv()
        self.across[0].start()
        self.own[3].wait_recv()
        self.across[1].start()

    def step_far(self):
        self.on[0].wait_recv()
        self.across[2].start()
        self.on[1].wait_recv()
        self.across[3].start()

    def finish(self):
        self.own[4].wait_recv()
        for c in self.across:
            c.wait_recv()
        for c in self.own + self.on + self.across:
            c.wait_send()
        self.local.wait()

    def run(self):
        self.start()
        self.step_near()
        self.step_across()
        self.step_far()
        self.finish()


def ring_scatter(place, x, pair, out, near, far, send, recv, emit):
    rows = x.shape[1]
    half = rows // 2
    step = 32
    to_left, to_right, to_partner = place.left(), place.right(), place.partner()
    swaps = {}
    for q in (2, 1, 3, 0):
        swaps[q] = remote(
            x.at[place.block(q, True)], pair.at[q], send.at[q], recv.at[q], to_partner
        )
        swaps[q].start()

    def add(q, low, high, extra=None):
        block = place.block(q)
        for at in range(low, high, step):
            part = pl.ds(at, step)
            total = x[block, part].astype(f32) + pair[q, part].astype(f32)
            if extra is not None:
                total = total + far[extra, pl.ds(at - low, step)].astype(f32)
            out[q - 1, part] = total.astype(bf16)

    first, second = pl.ds(0, half), pl.ds(half, half)

    def send_to(index, q, part, dst, device):
        c = remote(out.at[q - 1, part], dst, send.at[index], recv.at[index], device)
        c.start()
        return c

    swaps[2].wait_recv()
    add(2, 0, half)
    a = send_to(4, 2, first, far.at[0], to_right)
    add(2, half, rows)
    b = send_to(5, 2, second, far.at[1], to_left)
    swaps[1].wait_recv()
    add(1, half, rows)
    c = send_to(6, 1, second, near.at[0, second], to_right)
    swaps[3].wait_recv()
    add(3, 0, half)
    d = send_to(7, 3, first, near.at[1, first], to_left)
    a.wait_recv()
    add(1, 0, half, 0)
    e = send_to(8, 1, first, near.at[0, first], to_right)
    b.wait_recv()
    add(3, half, rows, 1)
    g = send_to(9, 3, second, near.at[1, second], to_left)
    swaps[0].wait_recv()
    own = place.block(0)
    c.wait_recv()
    d.wait_recv()
    e.wait_recv()
    g.wait_recv()
    for at in range(0, rows, step):
        part = pl.ds(at, step)
        emit(
            part,
            (x[own, part].astype(f32) + pair[0, part].astype(f32))
            + (near[0, part].astype(f32) + near[1, part].astype(f32)),
        )
    for copy in list(swaps.values()) + [a, b, c, d, e, g]:
        copy.wait_send()


def scatter_scratch(rows, width):
    return [
        pltpu.VMEM((4, rows, width), bf16),
        pltpu.VMEM((3, rows, width), bf16),
        pltpu.VMEM((2, rows, width), bf16),
        pltpu.VMEM((2, rows // 2, width), bf16),
        DMA((10,)),
        DMA((10,)),
    ]


def gather_scratch():
    return [DMA((RingGather.SEMS + 1,)), DMA((RingGather.SEMS,))]


def scatter_sum(x, base, shards, cid):
    _, rows, width = x.shape

    def body(x_ref, base_ref, out_ref, pair, out, near, far, send, recv):
        place = Place(shards)
        greet([place.right(), place.left(), place.partner()])

        def emit(part, total):
            out_ref[part] = (base_ref[part] + total).astype(bf16)

        ring_scatter(place, x_ref, pair, out, near, far, send, recv, emit)

    return pallas(
        body, jax.ShapeDtypeStruct((rows, width), bf16), [VMEM, VMEM], VMEM,
        scatter_scratch(rows, width), cid, 25,
    )(x, base)


def middle_step(x, tokens, gain, shards, cid):
    _, rows, width = x.shape

    def body(
        x_ref, tok_ref, gain_ref, mid_ref, all_ref, held, pair, out, near, far, send, recv,
        gsend, grecv,
    ):
        place = Place(shards)
        greet([place.right(), place.left(), place.partner()])

        def emit(part, total):
            middle = tok_ref[part].astype(f32) + total
            mid_ref[part] = middle
            held[part] = (middle * rms_scale(middle) * gain_ref[...]).astype(bf16)

        ring_scatter(place, x_ref, pair, out, near, far, send, recv, emit)
        RingGather(place, held, all_ref, gsend, grecv).run()

    return pallas(
        body,
        (
            jax.ShapeDtypeStruct((rows, width), f32),
            jax.ShapeDtypeStruct((GROUP, rows, width), bf16),
        ),
        [VMEM, VMEM, VMEM],
        (VMEM, ANY),
        [pltpu.VMEM((rows, width), bf16)] + scatter_scratch(rows, width) + gather_scratch(),
        cid,
        50,
    )(x, tokens, gain)


def middle_back(x, middle, cotangent, gain, shards, cid):
    _, rows, width = x.shape

    def body(
        x_ref, mid_ref, cot_ref, gain_ref, dm_ref, part_ref, all_ref, held, pair, out, near, far,
        send, recv, gsend, grecv,
    ):
        place = Place(shards)
        greet([place.right(), place.left(), place.partner()])
        part_ref[...] = jnp.zeros_like(part_ref)

        def emit(part, total):
            middle = mid_ref[part]
            scale = rms_scale(middle)
            normed = middle * scale
            part_ref[...] += jnp.sum(total * normed, axis=0, keepdims=True)
            dm = cot_ref[part].astype(f32) + norm_back(total * gain_ref[...], normed, scale)
            dm_ref[part] = dm
            held[part] = dm.astype(bf16)

        ring_scatter(place, x_ref, pair, out, near, far, send, recv, emit)
        RingGather(place, held, all_ref, gsend, grecv).run()

    return pallas(
        body,
        (
            jax.ShapeDtypeStruct((rows, width), f32),
            jax.ShapeDtypeStruct((1, width), f32),
            jax.ShapeDtypeStruct((GROUP, rows, width), bf16),
        ),
        [VMEM, VMEM, VMEM, VMEM],
        (VMEM, VMEM, ANY),
        [pltpu.VMEM((rows, width), bf16)] + scatter_scratch(rows, width) + gather_scratch(),
        cid,
        50,
    )(x, middle, cotangent, gain)


def tokens_back(x, tokens, dm, gain, shards, cid):
    _, rows, width = x.shape

    def body(
        x_ref, tok_ref, dm_ref, gain_ref, grad_ref, part_ref, pair, out, near, far, send, recv
    ):
        place = Place(shards)
        greet([place.right(), place.left(), place.partner()])
        part_ref[...] = jnp.zeros_like(part_ref)

        def emit(part, total):
            tok = tok_ref[part].astype(f32)
            scale = rms_scale(tok)
            normed = tok * scale
            part_ref[...] += jnp.sum(total * normed, axis=0, keepdims=True)
            grad_ref[part] = (
                dm_ref[part] + norm_back(total * gain_ref[...], normed, scale)
            ).astype(bf16)

        ring_scatter(place, x_ref, pair, out, near, far, send, recv, emit)

    return pallas(
        body,
        (
            jax.ShapeDtypeStruct((rows, width), bf16),
            jax.ShapeDtypeStruct((1, width), f32),
        ),
        [VMEM, VMEM, VMEM, VMEM],
        (VMEM, VMEM),
        scatter_scratch(rows, width),
        cid,
        25,
    )(x, tokens, dm, gain)


class Exchange:
    SEMS = GROUP

    def __init__(self, place, x, out, send, recv):
        self.local = pltpu.make_async_copy(x.at[place.tp], out.at[place.tp], send.at[0])
        self.copies = []
        for k in range(1, GROUP):
            peer = (place.tp + k) % GROUP
            self.copies.append(
                remote(x.at[peer], out.at[place.tp], send.at[k], recv.at[k], place.device(peer))
            )

    def start(self):
        for c in self.copies:
            c.start()
        self.local.start()

    def finish(self):
        for c in self.copies:
            c.wait_recv()
        for c in self.copies:
            c.wait_send()
        self.local.wait()


def group_peers(place):
    return [place.device((place.tp + k) % GROUP) for k in range(1, GROUP)]


def columns_of(dp, t, shards):
    ys, streams = lax.axis_size("y"), lax.axis_size("st")
    z, y = dp // ys, dp % ys
    return ((z * streams + t // shards) * ys + y) * shards + t % shards


def exchange_back(x, planes, shards, cid):
    _, wrows, both = x.shape
    hidden = both // 2
    brows = hidden // planes
    step = min(wrows, 32)

    def body(x_ref, gate_ref, up_ref, got, send, recv):
        place = Place(shards)
        greet(group_peers(place))
        run = Exchange(place, x_ref, got, send, recv)
        run.start()
        run.finish()
        for t in range(GROUP):
            for dp in range(planes):
                flat = columns_of(dp, t, shards)
                for m, out in enumerate((gate_ref, up_ref)):
                    for at in range(0, wrows, step):
                        part = pl.ds(at, step)
                        out[part, flat * brows : (flat + 1) * brows] = got[
                            t, part, m * hidden + dp * brows : m * hidden + (dp + 1) * brows
                        ].astype(f32)

    shape = jax.ShapeDtypeStruct((wrows, hidden * GROUP), f32)
    return pallas(
        body, (shape, shape), [VMEM], (VMEM, VMEM),
        [pltpu.VMEM(x.shape, bf16), DMA((GROUP,)), DMA((GROUP,))], cid, 25,
    )(x)


class PlaceGather:
    SEMS = 5

    def __init__(self, place, out, send, recv, halves):
        z, y = lax.axis_index("zh"), lax.axis_index("y")
        dp, across = z * 2 + y, (1 - z) * 2 + y
        to_z, to_y = {"zh": 1 - z}, {"y": 1 - y}

        def copy(index, slot, part, device):
            return remote(
                out.at[slot, part], out.at[slot, part], send.at[index], recv.at[index], device
            )

        first, second = halves
        self.z = [copy(0, dp, first, to_z), copy(1, dp, second, to_z)]
        self.y = [
            remote(out.at[dp], out.at[dp], send.at[2], recv.at[2], to_y),
            copy(3, across, first, to_y),
            copy(4, across, second, to_y),
        ]

    def start(self):
        self.z[0].start()
        self.y[0].start()
        self.z[1].start()

    def forward(self, half):
        self.z[half].wait_recv()
        self.y[1 + half].start()

    def finish(self):
        for c in self.y:
            c.wait_recv()
        for c in self.z + self.y:
            c.wait_send()


def front(tokens, cotangent, small, w_out, w_query, key_weight, value_weight, w_gate, w_up,
          w_down, planes, direct, shards, cid):
    rows, width = tokens.shape
    wrows = w_out.shape[0]
    srows, scols = small.shape
    brows = w_down.shape[0]
    hidden = brows * planes
    parts = [w_query.shape[1] // GROUP, key_weight.shape[1] // GROUP, value_weight.shape[1] // GROUP]
    qkv = sum(parts)
    slots = planes if direct else 1

    def body(
        tok_ref, cot_ref, small_ref, wout_ref, wq_ref, wk_ref, wv_ref, wg_ref, wu_ref, wd_ref,
        tok_all, cot_all, small_all, wout_all, attn_all, ffn_all, down_all,
        pack, tsend, trecv, csend, crecv, ssend, srecv, psend, precv, wsend, wrecv, fsend, frecv,
        asend, arecv, aasend, aarecv, dsend, drecv,
    ):
        place = Place(shards)
        tp, dp, flat = place.tp, place.dp(), place.flat()
        owner, slot = flat // planes, flat % planes
        barrier = pltpu.get_barrier_semaphore()

        def signal(device):
            pl.semaphore_signal(
                barrier, inc=1, device_id=device, device_id_type=pl.DeviceIdType.MESH
            )

        for device in group_peers(place):
            signal(device)
        for k in range(1, planes):
            signal(place.dp_device((dp + k) % planes))
        for j in range(planes):
            source = tp * planes + j

            @pl.when(source != flat)
            def _():
                signal(place.any_device(source))

        pl.semaphore_wait(
            barrier, GROUP - 1 + 2 * (planes - 1) + (owner != tp).astype(jnp.int32)
        )

        here = dp if direct else 0
        attn = []
        at = 0
        for i, (ref, cols) in enumerate(zip((wq_ref, wk_ref, wv_ref), parts)):
            for k in range(GROUP):
                peer = (tp + k) % GROUP
                src = ref.at[:, pl.ds(pl.multiple_of(peer * cols, cols), cols)]
                dst = attn_all.at[here, tp, :, pl.ds(at, cols)]
                sem = i * GROUP + k
                if k == 0:
                    attn.append(pltpu.make_async_copy(src, dst, asend.at[sem]))
                else:
                    attn.append(
                        remote(src, dst, asend.at[sem], arecv.at[sem], place.device(peer))
                    )
            at += cols
        for c in attn:
            c.start()

        small_own = pltpu.make_async_copy(small_ref, small_all.at[tp, dp], ssend.at[0])
        small_own.start()
        small_dp = []
        for k in range(1, planes):
            small_dp.append(
                remote(
                    small_ref, small_all.at[tp, dp], ssend.at[k], srecv.at[k],
                    place.dp_device((dp + k) % planes),
                )
            )
            small_dp[-1].start()

        tok = RingGather(place, tok_ref, tok_all, tsend, trecv)
        tok.start()
        down_own = pltpu.make_async_copy(wd_ref, down_all.at[here], dsend.at[PlaceGather.SEMS])
        down_own.start()

        def wout_copy(k):
            device = {**place.dp_device((dp + k) % planes), **place.device(owner)}
            return remote(wout_ref, wout_all.at[slot], wsend.at[k], wrecv.at[slot], device)

        wout_own = pltpu.make_async_copy(wout_ref, wout_all.at[slot], wsend.at[0])

        @pl.when(owner == tp)
        def _():
            wout_own.start()

        @pl.when(owner != tp)
        def _():
            wout_copy(0).start()

        for k in range(1, planes):
            wout_copy(k).start()

        for t in range(GROUP):
            for d in range(planes):
                column = columns_of(d, t, shards)
                for m, ref in enumerate((wg_ref, wu_ref)):
                    low = m * hidden + d * brows
                    pack[t, :, low : low + brows] = ref[:, column * brows : (column + 1) * brows]

        for i in range(len(parts)):
            for k in range(GROUP):
                c = attn[i * GROUP + k]
                if k == 0:
                    c.wait()
                else:
                    c.wait_recv()
        down_own.wait()
        if direct:
            half = GROUP // 2
            attn_dp = PlaceGather(
                place, attn_all, aasend, aarecv, (pl.ds(0, half), pl.ds(half, half))
            )
            attn_dp.start()
            half = brows // 2
            down_dp = PlaceGather(
                place, down_all, dsend, drecv, (pl.ds(0, half), pl.ds(half, half))
            )
            down_dp.start()
        ffn = Exchange(place, pack, ffn_all, fsend, frecv)
        ffn.start()

        small_own.wait()
        for c in small_dp:
            c.wait_recv()
        small_tp = []
        for k in range(1, GROUP):
            small_tp.append(
                remote(
                    small_all.at[tp], small_all.at[tp], psend.at[k], precv.at[k],
                    place.device((tp + k) % GROUP),
                )
            )
            small_tp[-1].start()

        cot = RingGather(place, cot_ref, cot_all, csend, crecv)
        tok.step_near()
        tok.step_across()
        if direct:
            attn_dp.forward(0)
        cot.start()
        tok.step_far()
        if direct:
            attn_dp.forward(1)
        cot.step_near()
        if direct:
            down_dp.forward(0)
        cot.step_across()
        cot.step_far()
        if direct:
            down_dp.forward(1)
        tok.finish()
        cot.finish()
        ffn.finish()
        for i in range(len(parts)):
            for k in range(1, GROUP):
                attn[i * GROUP + k].wait_send()
        for c in small_tp:
            c.wait_recv()
        for c in small_dp + small_tp:
            c.wait_send()
        if direct:
            attn_dp.finish()
            down_dp.finish()

        @pl.when(owner == tp)
        def _():
            wout_own.wait()

        @pl.when(owner != tp)
        def _():
            wout_copy(0).wait_send()

        for k in range(1, planes):
            wout_copy(k).wait_send()
        for j in range(planes):

            @pl.when(tp * planes + j != flat)
            def _():
                remote(
                    wout_ref, wout_all.at[j], wsend.at[0], wrecv.at[j], place.partner()
                ).wait_recv()

    return pallas(
        body,
        (
            jax.ShapeDtypeStruct((GROUP, rows, width), bf16),
            jax.ShapeDtypeStruct((GROUP, rows, width), bf16),
            jax.ShapeDtypeStruct((GROUP, planes, srows, scols), bf16),
            jax.ShapeDtypeStruct((planes, wrows, width), bf16),
            jax.ShapeDtypeStruct((slots, GROUP, wrows, qkv), bf16),
            jax.ShapeDtypeStruct((GROUP, wrows, 2 * hidden), bf16),
            jax.ShapeDtypeStruct((slots, brows, width), bf16),
        ),
        [VMEM] * 10,
        (ANY, ANY, VMEM, ANY, ANY, ANY, ANY),
        [pltpu.VMEM((GROUP, wrows, 2 * hidden), bf16)]
        + gather_scratch() + gather_scratch()
        + [
            DMA((planes,)), DMA((planes,)), DMA((GROUP,)), DMA((GROUP,)),
            DMA((planes,)), DMA((planes,)), DMA((GROUP,)), DMA((GROUP,)),
            DMA((3 * GROUP,)), DMA((3 * GROUP,)), DMA((PlaceGather.SEMS,)),
            DMA((PlaceGather.SEMS,)), DMA((PlaceGather.SEMS + 1,)), DMA((PlaceGather.SEMS,)),
        ],
        cid,
        60,
    )(tokens, cotangent, small, w_out, w_query, key_weight, value_weight, w_gate, w_up, w_down)


def settle(qkv_grad, out_grad, small, planes, shards, cid):
    srows = small.shape[1] // planes
    cols = small.shape[2]

    def body(
        q_ref, o_ref, s_ref, q_out, o_out, s_out, got, held, line, qsend, qrecv, osend, orecv,
        asend, arecv, bsend, brecv,
    ):
        place = Place(shards)
        tp, dp, flat = place.tp, place.dp(), place.flat()
        owner = tp * planes + dp
        source = flat // planes, flat % planes
        barrier = pltpu.get_barrier_semaphore()

        def signal(device):
            pl.semaphore_signal(
                barrier, inc=1, device_id=device, device_id_type=pl.DeviceIdType.MESH
            )

        for device in group_peers(place):
            signal(device)
        for k in range(1, planes):
            signal(place.dp_device((dp + k) % planes))

        @pl.when(owner != flat)
        def _():
            signal({**place.dp_device(source[1]), **place.device(source[0])})

        pl.semaphore_wait(barrier, GROUP + planes - 2 + (owner != flat).astype(jnp.int32))

        sums = Exchange(place, s_ref, got, asend, arecv)
        sums.start()
        qkv = Exchange(place, q_ref, q_out, qsend, qrecv)
        qkv.start()
        out_own = pltpu.make_async_copy(o_ref, o_out, osend)
        out_far = remote(
            o_ref, o_out, osend, orecv, place.any_device(owner)
        )

        @pl.when(owner == flat)
        def _():
            out_own.start()

        @pl.when(owner != flat)
        def _():
            out_far.start()

        sums.finish()
        held[...] = jnp.sum(got[...], axis=0).reshape(held.shape)
        line_own = pltpu.make_async_copy(held.at[dp], line.at[dp], bsend.at[0])
        line_own.start()
        lines = []
        for k in range(1, planes):
            to = (dp + k) % planes
            lines.append(
                remote(
                    held.at[to], line.at[dp], bsend.at[k], brecv.at[k], place.dp_device(to)
                )
            )
            lines[-1].start()
        for c in lines:
            c.wait_recv()
        line_own.wait()
        s_out[...] = jnp.sum(line[...], axis=0)
        qkv.finish()
        for c in lines:
            c.wait_send()

        @pl.when(owner == flat)
        def _():
            out_own.wait()

        @pl.when(owner != flat)
        def _():
            out_far.wait()

    return pallas(
        body,
        (
            jax.ShapeDtypeStruct(qkv_grad.shape, bf16),
            jax.ShapeDtypeStruct(out_grad.shape, bf16),
            jax.ShapeDtypeStruct((srows, cols), f32),
        ),
        [VMEM, VMEM, VMEM],
        (VMEM, VMEM, VMEM),
        [
            pltpu.VMEM(small.shape, f32),
            pltpu.VMEM((planes, srows, cols), f32),
            pltpu.VMEM((planes, srows, cols), f32),
            DMA((GROUP,)), DMA((GROUP,)), DMA, DMA,
            DMA((GROUP,)), DMA((GROUP,)), DMA((planes,)), DMA((planes,)),
        ],
        cid,
        20,
    )(qkv_grad, out_grad, small)


def local(
    tokens, doc_starts, attn_gain, query_gain, key_gain, w_query, key_weight, value_weight,
    w_headgate, w_out, ffn_gain, w_gate, w_up, w_down, cotangent,
):
    zs, ys = lax.axis_size("zh"), lax.axis_size("y")
    planes = zs * ys
    direct = zs == 2 and ys == 2
    streams = lax.axis_size("st")
    shards = lax.axis_size("seq")
    devices = planes * GROUP
    rows, width = tokens.shape
    length = rows * shards
    group_rows = rows * GROUP
    wrows = w_query.shape[0]
    brows = w_down.shape[0]
    hidden = brows * planes
    qcols = w_query.shape[1] // GROUP
    kcols = key_weight.shape[1] // GROUP
    group_heads = qcols // HEAD_SIZE
    all_heads = w_headgate.shape[1]
    score_scale = HEAD_SIZE ** (-0.5)
    dp = lax.axis_index(DP)
    tp = lax.axis_index(TP)

    hg = wrows * all_heads
    gcols = query_gain.shape[0]
    at = hg + 2 * wrows
    docs = doc_starts.shape[1]
    dat = at + 2 * gcols
    count = dat + 2 * docs
    srows = -(-count // 2048) * 16
    small = jnp.concatenate(
        [
            w_headgate.reshape(-1), attn_gain, ffn_gain, query_gain, key_gain,
            (doc_starts[0] // 128).astype(bf16), (doc_starts[0] % 128).astype(bf16),
        ]
    )
    small = jnp.pad(small, (0, srows * 128 - count)).reshape(srows, 128)

    tokens_all, cot_all, small, out_w, qkv_w, ffn_w, down_w = front(
        tokens, cotangent, small, w_out, w_query, key_weight, value_weight, w_gate, w_up, w_down,
        planes, direct, shards, 0,
    )
    tokens_all = tokens_all.reshape(group_rows, width)
    cot_all = cot_all.reshape(group_rows, width)
    out_w = out_w.reshape(planes * wrows, width)
    ffn_w = over_dp(ffn_w)
    if direct:
        qkv_w = qkv_w.reshape(zs, ys, streams, shards * wrows, qcols + 2 * kcols)
        qkv_w = qkv_w.transpose(0, 2, 1, 3, 4).reshape(width, qcols + 2 * kcols)
        down_w = down_w.reshape(hidden, width)
    else:
        qkv_w = over_dp(qkv_w[0])
        down_w = lax.all_gather(down_w[0], DP, axis=0, tiled=True)
    starts = pick(small[::shards], 1, dp).reshape(streams, -1)[:, dat:count].astype(jnp.int32)
    starts = starts[:, :docs] * 128 + starts[:, docs:]
    small = small.reshape(streams, shards, zs, ys, srows * 128).transpose(2, 0, 3, 1, 4)
    small = small.reshape(devices, srows * 128)
    headgate_all = small[:, :hg].reshape(width, all_heads)
    attn_gain_f = small[:, hg : hg + wrows].reshape(1, -1).astype(f32)
    ffn_gain_f = small[:, hg + wrows : at].reshape(1, -1).astype(f32)
    query_gain_f = small[:, at : at + gcols].reshape(-1).astype(f32)
    key_gain_f = small[:, at + gcols : dat].reshape(-1).astype(f32)
    headgate_own = lax.dynamic_slice_in_dim(headgate_all, tp * group_heads, group_heads, 1)


    residual_all = tokens_all.astype(f32)
    hidden_all = (residual_all * rms_scale(residual_all) * attn_gain_f).astype(bf16)
    qkv = mm(hidden_all, qkv_w)
    gate_logit = mm(hidden_all, headgate_own)
    query_raw = qkv[:, :qcols].reshape(group_rows, group_heads, HEAD_SIZE)
    key_raw = qkv[:, qcols : qcols + kcols].reshape(group_rows, 1, HEAD_SIZE)
    value = qkv[:, qcols + kcols :].astype(bf16).reshape(streams, length, HEAD_SIZE)
    positions = jnp.tile(jnp.arange(length, dtype=jnp.int32), streams)
    cosine, sine = rotary_tables(positions)
    query_scale = rms_scale(query_raw)
    query_normed = query_raw * query_scale
    query = rotate(query_normed * query_gain_f, cosine, sine).astype(bf16)
    query = query.reshape(streams, length, group_heads, HEAD_SIZE)
    key_scale = rms_scale(key_raw)
    key_normed = key_raw * key_scale
    key = rotate(key_normed * key_gain_f, cosine, sine).astype(bf16)
    key = key.reshape(streams, length, HEAD_SIZE)
    stream_pos = jnp.arange(length, dtype=jnp.int32)
    segment = jnp.sum((stream_pos[None, :, None] >= starts[:, None, :]).astype(jnp.int32), axis=2)
    allowed = (stream_pos[:, None] >= stream_pos[None, :])[None] & (
        segment[:, :, None] == segment[:, None, :]
    )
    scores = jnp.einsum("bqgd,bkd->bgqk", query, key, preferred_element_type=f32) * score_scale
    scores = jnp.where(allowed[:, None], scores, MASK_FILL)
    row_max = jnp.max(scores, axis=-1, keepdims=True)
    weights = jnp.exp(scores - row_max)
    probs = weights / jnp.sum(weights, axis=-1, keepdims=True)
    probs_low = probs.astype(bf16)
    mixed = jnp.einsum("bgqk,bkd->bqgd", probs_low, value, preferred_element_type=f32).astype(bf16)
    mixed_f = mixed.astype(f32).reshape(group_rows, group_heads, HEAD_SIZE)
    head_gate = jax.nn.sigmoid(gate_logit)[:, :, None]
    gated = (mixed_f * head_gate).astype(bf16).reshape(group_rows, qcols)

    def parts(x):
        return x.astype(bf16).reshape(GROUP, rows, width)

    middle, hidden_two = middle_step(parts(mm(gated, out_w)), tokens, ffn_gain_f, shards, 2)
    hidden_two = hidden_two.reshape(group_rows, width)

    gate_up = mm(hidden_two, ffn_w)
    gate_pre, up_proj = gate_up[:, :hidden], gate_up[:, hidden:]
    gate_sig = jax.nn.sigmoid(gate_pre)
    inner_act = (gate_pre * gate_sig * up_proj).astype(bf16)
    down_grad = mm_t(inner_act, cot_all).astype(bf16)
    down_w, down_grad = lax.optimization_barrier((down_w, down_grad))
    down_grad = sum_dp(down_grad.reshape(zs, ys, brows, width))
    grad_inner = mm_b(cot_all, down_w)
    grad_gate = (grad_inner * up_proj * gate_sig * (1.0 + gate_pre * (1.0 - gate_sig))).astype(bf16)
    grad_up = (grad_inner * gate_pre * gate_sig).astype(bf16)
    grad_gu = jnp.concatenate([grad_gate, grad_up], axis=1)
    ffn_grad = mm_t(hidden_two, grad_gu).astype(bf16)
    grad_gu, ffn_grad = lax.optimization_barrier((grad_gu, ffn_grad))
    ffn_grad = sum_dp_rows(ffn_grad)
    grad_middle, ffn_gain_part, grad_branch = middle_back(
        parts(mm_b(grad_gu, ffn_w)), middle, cotangent, ffn_gain_f, shards, 3
    )
    grad_branch = grad_branch.reshape(group_rows, width)
    layer_out = scatter_sum(parts(mm(inner_act, down_w)), middle, shards, 4)

    out_grad = mm_t(gated, grad_branch).astype(bf16)
    grad_gated = mm_b(grad_branch, out_w).reshape(group_rows, group_heads, HEAD_SIZE)
    grad_mixed = (grad_gated * head_gate).astype(bf16).reshape(
        streams, length, group_heads, HEAD_SIZE
    )
    gate_flat = head_gate[:, :, 0]
    grad_logit = (
        jnp.sum(grad_gated * mixed_f, axis=-1) * gate_flat * (1.0 - gate_flat)
    ).astype(bf16)
    grad_probs = jnp.einsum("bqgd,bkd->bgqk", grad_mixed, value, preferred_element_type=f32)
    row_delta = jnp.sum(probs * grad_probs, axis=-1, keepdims=True)
    grad_scores = (probs * (grad_probs - row_delta)).astype(bf16)
    grad_query = (
        jnp.einsum("bgqk,bkd->bqgd", grad_scores, key, preferred_element_type=f32) * score_scale
    ).astype(bf16)
    grad_key = (
        jnp.einsum("bgqk,bqgd->bkd", grad_scores, query, preferred_element_type=f32) * score_scale
    ).astype(bf16)
    grad_value = jnp.einsum(
        "bgqk,bqgd->bkd", probs_low, grad_mixed, preferred_element_type=f32
    ).astype(bf16)
    gqn = rotate_back(
        grad_query.astype(f32).reshape(group_rows, group_heads, HEAD_SIZE), cosine, sine
    )
    query_gain_part = jnp.sum(gqn * query_normed, axis=(0, 1))
    grad_query_raw = norm_back(gqn * query_gain_f, query_normed, query_scale).astype(bf16)
    gkn = rotate_back(grad_key.astype(f32).reshape(group_rows, 1, HEAD_SIZE), cosine, sine)
    key_gain_part = jnp.sum(gkn * key_normed, axis=(0, 1))
    grad_key_raw = norm_back(gkn * key_gain_f, key_normed, key_scale).astype(bf16)
    grad_qkv = jnp.concatenate(
        [
            grad_query_raw.reshape(group_rows, qcols),
            grad_key_raw.reshape(group_rows, kcols),
            grad_value.reshape(group_rows, kcols),
        ],
        axis=1,
    )
    tokens_grad, attn_gain_part = tokens_back(
        parts(mm_b(grad_qkv, qkv_w) + mm_b(grad_logit, headgate_own)),
        tokens, grad_middle, attn_gain_f, shards, 5,
    )
    qkv_grad = mm_t(hidden_all, grad_qkv).astype(bf16)
    ffn_grad, down_grad, qkv_grad, out_grad = lax.optimization_barrier(
        (ffn_grad, down_grad, qkv_grad, out_grad)
    )
    out_grad = sum_dp(out_grad.reshape(zs, ys, wrows, width))
    qkv_grad = sum_dp_rows(qkv_grad)
    headgate_part = mm_t(hidden_all, grad_logit)
    headgate_part = lax.dynamic_update_slice(
        jnp.zeros((width, all_heads), f32), headgate_part, (0, tp * group_heads)
    )

    small_sum = jnp.concatenate(
        [
            headgate_part.reshape(devices, hg),
            attn_gain_part.reshape(devices, wrows),
            ffn_gain_part.reshape(devices, wrows),
            query_gain_part.reshape(devices, gcols),
            key_gain_part.reshape(devices, gcols),
        ],
        axis=1,
    )
    small_sum = jnp.pad(small_sum, ((0, 0), (0, srows * 128 - dat)))
    small_sum = small_sum.reshape(zs, streams, ys, shards, srows, 128)
    small_sum = small_sum.transpose(1, 3, 0, 2, 4, 5)
    small_sum = small_sum.reshape(GROUP, planes * srows, 128)

    gate_grad, up_grad = exchange_back(ffn_grad, planes, shards, 6)
    qkv_grad, out_grad, small_sum = settle(
        qkv_grad, out_grad, small_sum, planes, shards, 7
    )
    qkv_grad = qkv_grad.transpose(1, 0, 2).astype(f32)
    out_grad = out_grad.astype(f32)
    small_sum = small_sum.reshape(-1)
    return (
        layer_out,
        tokens_grad,
        small_sum[hg : hg + wrows],
        small_sum[at : at + gcols],
        small_sum[at + gcols : at + 2 * gcols],
        qkv_grad[:, :, :qcols].reshape(wrows, GROUP * qcols),
        qkv_grad[:, :, qcols : qcols + kcols].reshape(wrows, GROUP * kcols),
        qkv_grad[:, :, qcols + kcols :].reshape(wrows, GROUP * kcols),
        small_sum[:hg].reshape(wrows, all_heads),
        out_grad,
        small_sum[hg + wrows : hg + 2 * wrows],
        gate_grad,
        up_grad,
        down_grad.astype(f32),
    )


def solution(mesh):
    shards = mesh.shape["seq"]
    planes = (2, 2, 2) if shards == 4 and mesh.size == 32 else (1, GROUP // shards, -1)
    grouped = Mesh(mesh.devices.reshape(planes + (shards,)), ALL)
    two = P(ALL, None)
    one = P(ALL)
    return jax.shard_map(
        local,
        mesh=grouped,
        in_specs=(
            two, P(("zh", "st", "y"), None), one, one, one, two, two, two, two, two, one, two, two,
            two, two,
        ),
        out_specs=(two, two, one, one, one, two, two, two, two, two, one, two, two, two),
        check_vma=False,
    )
```

```python
import jax
import jax.numpy as jnp
import numpy as np
from jax import lax
from jax.experimental import pallas as pl
from jax.experimental.pallas import tpu as pltpu
from jax.sharding import Mesh, PartitionSpec as P

QUERY_HEADS = 16
KEY_VALUE_HEADS = 8
HEAD_SIZE = 128
GROUP = 8
NORM_EPS = 1e-06
ROPE_BASE = 1000000.0
MASK_FILL = -1e30

DP = ("zh", "y")
TP = ("st", "seq")
ALL = ("zh", "st", "y", "seq")
f32 = jnp.float32
bf16 = jnp.bfloat16


def rms_scale(vector):
    return lax.rsqrt(jnp.mean(vector * vector, axis=-1, keepdims=True) + NORM_EPS)


def rotary_tables(positions):
    half_width = HEAD_SIZE // 2
    exponent = jnp.arange(half_width, dtype=jnp.int32).astype(f32) * (2.0 / HEAD_SIZE)
    inverse = jnp.power(ROPE_BASE, -exponent)
    angles = positions.astype(f32)[:, None] * inverse[None, :]
    return (jnp.cos(angles)[:, None, :], jnp.sin(angles)[:, None, :])


def rotate(vector, cosine, sine):
    a, b = jnp.split(vector, 2, axis=-1)
    return jnp.concatenate([a * cosine - b * sine, b * cosine + a * sine], axis=-1)


def rotate_back(vector, cosine, sine):
    a, b = jnp.split(vector, 2, axis=-1)
    return jnp.concatenate([a * cosine + b * sine, b * cosine - a * sine], axis=-1)


def norm_back(grad, normed, scale):
    return scale * (grad - normed * jnp.mean(grad * normed, axis=-1, keepdims=True))


def mm(left, right):
    return jnp.dot(left, right, preferred_element_type=f32)


def mm_t(left, right):
    return lax.dot_general(left, right, (((0,), (0,)), ((), ())), preferred_element_type=f32)


def mm_b(left, right):
    return lax.dot_general(left, right, (((1,), (1,)), ((), ())), preferred_element_type=f32)


SWAP = [(0, 1), (1, 0)]


def over_dp(x):
    streams, shards = lax.axis_size("st"), lax.axis_size("seq")
    zs, ys = lax.axis_size("zh"), lax.axis_size("y")
    rows, columns = x.shape[1] * shards, x.shape[2]
    whole = lax.all_gather(x, DP, axis=0, tiled=False)
    whole = whole.reshape(zs, ys, streams, rows, columns).transpose(0, 2, 1, 3, 4)
    return whole.reshape(-1, columns)


def pick(x, axis, index):
    return lax.dynamic_index_in_dim(x, index, axis, keepdims=False)


def plus(left, right):
    return left.astype(f32) + right.astype(f32)


class PlaceSum:
    def __init__(self, x):
        self.x = x
        self.z, self.y = lax.axis_index("zh"), lax.axis_index("y")

    def piece(self, zp, yp):
        return pick(pick(self.x, 0, zp), 0, yp)

    def over_y(self):
        got = lax.ppermute(pick(self.x, 1, 1 - self.y), "y", SWAP)
        self.take(pick(got, 0, 1 - self.z), pick(got, 0, self.z))

    def over_y_near(self):
        return lax.ppermute(self.piece(self.z, 1 - self.y), "y", SWAP)

    def take(self, far, near):
        self.far, self.near = far, near

    def over_z(self):
        far = plus(self.piece(1 - self.z, self.y), self.far).astype(bf16)
        return lax.ppermute(far, "zh", SWAP)

    def total(self, got):
        return (plus(self.piece(self.z, self.y), self.near) + got.astype(f32)).astype(bf16)


def scatter_dp(x):
    zs, ys = x.shape[:2]
    return lax.psum_scatter(
        x.reshape((zs * ys,) + x.shape[2:]), DP, scatter_dimension=0, tiled=False
    )


def by_place(x):
    streams = lax.axis_size("st")
    zs, ys = lax.axis_size("zh"), lax.axis_size("y")
    columns = x.shape[1]
    x = x.reshape(zs, streams, ys, -1, columns).transpose(0, 2, 1, 3, 4)
    return x.reshape(zs, ys, -1, columns)


def pallas(body, out_shape, in_specs, out_specs, scratch, cid, micros, mib=40):
    return pl.pallas_call(
        body,
        out_shape=out_shape,
        in_specs=in_specs,
        out_specs=out_specs,
        scratch_shapes=scratch,
        compiler_params=pltpu.CompilerParams(
            collective_id=cid, has_side_effects=True, vmem_limit_bytes=mib * 1024 * 1024
        ),
        cost_estimate=pl.CostEstimate(
            flops=0, bytes_accessed=int(micros * 3.6e5), transcendentals=0
        ),
    )


ANY = pl.BlockSpec(memory_space=pl.ANY)
VMEM = pl.BlockSpec(memory_space=pltpu.VMEM)
DMA = pltpu.SemaphoreType.DMA


def remote(src, dst, send, recv, device):
    return pltpu.make_async_remote_copy(
        src_ref=src,
        dst_ref=dst,
        send_sem=send,
        recv_sem=recv,
        device_id=device,
        device_id_type=pl.DeviceIdType.MESH,
    )


class Place:
    def __init__(self, shards):
        self.shards = shards
        self.tp = lax.axis_index("st") * shards + lax.axis_index("seq")
        self.core = self.tp % 2
        self.ring = self.turn(self.tp // 2)

    def turn(self, place):
        if self.shards == GROUP:
            return place
        return place + (place // 2) * (1 - 2 * (place % 2))

    def head(self, index):
        if self.shards == GROUP:
            return index
        return index // 4 * 2 + index % 4 // 2 * 4 + index % 2

    def block(self, ahead, other=False):
        ring = self.ring
        if ahead == 1:
            ring = ring + 1 - 2 * (ring % 2)
        elif ahead == 3:
            ring = 3 - ring
        elif ahead == 2:
            ring = (ring + 2) % 4
        core = 1 - self.core if other else self.core
        return self.turn(ring) * 2 + core

    def device(self, index):
        return {"st": index // self.shards, "seq": index % self.shards}

    def dp_device(self, dp):
        ys = lax.axis_size("y")
        return {"zh": dp // ys, "y": dp % ys}

    def any_device(self, flat):
        ys, streams = lax.axis_size("y"), lax.axis_size("st")
        return {
            "zh": flat // (streams * ys * self.shards),
            "st": flat // (ys * self.shards) % streams,
            "y": flat // self.shards % ys,
            "seq": flat % self.shards,
        }

    def flat(self):
        ys, streams = lax.axis_size("y"), lax.axis_size("st")
        z, y = lax.axis_index("zh"), lax.axis_index("y")
        st, seq = lax.axis_index("st"), lax.axis_index("seq")
        return ((z * streams + st) * ys + y) * self.shards + seq

    def dp(self):
        return lax.axis_index("zh") * lax.axis_size("y") + lax.axis_index("y")

    def right(self):
        return self.device(self.block(1))

    def left(self):
        return self.device(self.block(3))

    def across(self):
        return {"y": 1 - lax.axis_index("y")}

    def partner(self):
        return self.device(self.block(0, True))


def greet(devices):
    barrier = pltpu.get_barrier_semaphore()
    for device in devices:
        pl.semaphore_signal(
            barrier, inc=1, device_id=device, device_id_type=pl.DeviceIdType.MESH
        )
    pl.semaphore_wait(barrier, len(devices))


class RingGather:
    SEMS = 11

    def __init__(self, place, own, out, send, recv, one_way=False):
        rows = out.shape[1]
        half = rows // 2
        first, second = pl.ds(0, half), pl.ds(half, half)
        me, near, next_, opposite = (place.block(i) for i in (0, 1, 3, 2))
        to_near, to_next, to_partner = place.device(near), place.device(next_), place.partner()

        def copy(index, src, block, part, device):
            return remote(src, out.at[block, part], send.at[index], recv.at[index], device)

        self.local = pltpu.make_async_copy(own, out.at[me], send.at[self.SEMS])
        self.next = [
            copy(0, own.at[first], me, first, to_next),
            copy(1, own.at[second], me, second, to_next),
        ]
        self.near = [
            copy(2, own.at[first], me, first, to_near),
            copy(3, own.at[second], me, second, to_near),
        ]
        self.mate = remote(own, out.at[me], send.at[4], recv.at[4], to_partner)
        self.on = [copy(5, out.at[next_, first], next_, first, to_near)]
        if one_way:
            self.on.append(copy(6, out.at[next_, second], next_, second, to_near))
        else:
            self.on.append(copy(6, out.at[near, second], near, second, to_next))
        self.one_way = one_way
        self.across = [
            remote(out.at[next_], out.at[next_], send.at[7], recv.at[7], to_partner),
            remote(out.at[near], out.at[near], send.at[8], recv.at[8], to_partner),
            copy(9, out.at[opposite, first], opposite, first, to_partner),
            copy(10, out.at[opposite, second], opposite, second, to_partner),
        ]

    def start(self):
        self.next[0].start()
        self.near[0 if self.one_way else 1].start()
        self.next[1].start()
        self.near[1 if self.one_way else 0].start()
        self.mate.start()
        self.local.start()

    def pass_on(self):
        self.next[0].wait_recv()
        self.on[0].start()
        if self.one_way:
            self.next[1].wait_recv()
        else:
            self.near[1].wait_recv()
        self.on[1].start()

    def step_across(self):
        if not self.one_way:
            self.next[1].wait_recv()
        self.across[0].start()
        self.near[0].wait_recv()
        if self.one_way:
            self.near[1].wait_recv()
        self.across[1].start()

    def step_far(self):
        self.on[0].wait_recv()
        self.across[2].start()
        self.on[1].wait_recv()
        self.across[3].start()

    def finish(self):
        self.mate.wait_recv()
        for c in self.across:
            c.wait_recv()
        for c in self.next + self.near + [self.mate] + self.on + self.across:
            c.wait_send()
        self.local.wait()

    def run(self):
        self.start()
        self.pass_on()
        self.step_across()
        self.step_far()
        self.finish()


def ring_scatter(place, x, pair, out, near, far, send, recv, emit):
    rows = x.shape[1]
    half = rows // 2
    step = 32
    to_left, to_right, to_partner = place.left(), place.right(), place.partner()
    swaps = {}
    for q in (2, 1, 3, 0):
        swaps[q] = remote(
            x.at[place.block(q, True)], pair.at[q], send.at[q], recv.at[q], to_partner
        )
        swaps[q].start()

    def add(q, low, high, extra=None):
        block = place.block(q)
        for at in range(low, high, step):
            part = pl.ds(at, step)
            total = x[block, part].astype(f32) + pair[q, part].astype(f32)
            if extra is not None:
                total = total + far[extra, pl.ds(at - low, step)].astype(f32)
            out[q - 1, part] = total.astype(bf16)

    first, second = pl.ds(0, half), pl.ds(half, half)

    def send_to(index, q, part, dst, device):
        c = remote(out.at[q - 1, part], dst, send.at[index], recv.at[index], device)
        c.start()
        return c

    swaps[2].wait_recv()
    add(2, 0, half)
    a = send_to(4, 2, first, far.at[0], to_right)
    add(2, half, rows)
    b = send_to(5, 2, second, far.at[1], to_left)
    swaps[1].wait_recv()
    add(1, 0, half)
    c = send_to(6, 1, first, near.at[0, first], to_right)
    swaps[3].wait_recv()
    add(3, half, rows)
    d = send_to(7, 3, second, near.at[1, second], to_left)
    a.wait_recv()
    add(3, 0, half, 0)
    e = send_to(8, 3, first, near.at[1, first], to_left)
    b.wait_recv()
    add(1, half, rows, 1)
    g = send_to(9, 1, second, near.at[0, second], to_right)
    swaps[0].wait_recv()
    own = place.block(0)
    c.wait_recv()
    d.wait_recv()
    e.wait_recv()
    g.wait_recv()
    for at in range(0, rows, step):
        part = pl.ds(at, step)
        emit(
            part,
            (x[own, part].astype(f32) + pair[0, part].astype(f32))
            + (near[0, part].astype(f32) + near[1, part].astype(f32)),
        )
    for copy in list(swaps.values()) + [a, b, c, d, e, g]:
        copy.wait_send()


def scatter_scratch(rows, width):
    return [
        pltpu.VMEM((4, rows, width), bf16),
        pltpu.VMEM((3, rows, width), bf16),
        pltpu.VMEM((2, rows, width), bf16),
        pltpu.VMEM((2, rows // 2, width), bf16),
        DMA((10,)),
        DMA((10,)),
    ]


def gather_scratch():
    return [DMA((RingGather.SEMS + 1,)), DMA((RingGather.SEMS,))]


def scatter_sum(x, base, shards, cid):
    _, rows, width = x.shape

    def body(x_ref, base_ref, out_ref, pair, out, near, far, send, recv):
        place = Place(shards)
        greet([place.right(), place.left(), place.partner()])

        def emit(part, total):
            out_ref[part] = (base_ref[part] + total).astype(bf16)

        ring_scatter(place, x_ref, pair, out, near, far, send, recv, emit)

    return pallas(
        body, jax.ShapeDtypeStruct((rows, width), bf16), [VMEM, VMEM], VMEM,
        scatter_scratch(rows, width), cid, 25,
    )(x, base)


def middle_step(x, tokens, gain, carry, shards, cid):
    _, rows, width = x.shape
    carries = [] if carry is None else [carry]

    def body(x_ref, tok_ref, gain_ref, *refs):
        refs = list(refs)
        carry_ref = refs.pop(0) if carries else None
        mid_ref, all_ref = refs.pop(0), refs.pop(0)
        carry_out = refs.pop(0) if carries else None
        held, pair, out, near, far, send, recv, gsend, grecv, ysend, yrecv = refs
        place = Place(shards)
        greet(
            [place.right(), place.left(), place.partner()]
            + ([place.across()] if carries else [])
        )
        if carries:
            over = remote(carry_ref, carry_out, ysend, yrecv, place.across())
            over.start()

        def emit(part, total):
            middle = tok_ref[part].astype(f32) + total
            mid_ref[part] = middle
            held[part] = (middle * rms_scale(middle) * gain_ref[...]).astype(bf16)

        ring_scatter(place, x_ref, pair, out, near, far, send, recv, emit)
        RingGather(place, held, all_ref, gsend, grecv).run()
        if carries:
            over.wait()

    return pallas(
        body,
        [
            jax.ShapeDtypeStruct((rows, width), f32),
            jax.ShapeDtypeStruct((GROUP, rows, width), bf16),
        ]
        + [jax.ShapeDtypeStruct(c.shape, c.dtype) for c in carries],
        [VMEM, VMEM, VMEM] + [ANY] * len(carries),
        [VMEM, ANY] + [ANY] * len(carries),
        [pltpu.VMEM((rows, width), bf16)] + scatter_scratch(rows, width) + gather_scratch()
        + [DMA, DMA],
        cid,
        50,
    )(x, tokens, gain, *carries)


def middle_back(x, middle, cotangent, gain, grads, shards, cid):
    _, rows, width = x.shape
    carries = [] if grads is None else [grads]

    def body(x_ref, mid_ref, cot_ref, gain_ref, *refs):
        refs = list(refs)
        grads_ref = refs.pop(0) if carries else None
        dm_ref, part_ref, all_ref = refs.pop(0), refs.pop(0), refs.pop(0)
        grads_out = refs.pop(0) if carries else None
        held, pair, out, near, far, send, recv, gsend, grecv, ysend, yrecv = refs
        place = Place(shards)
        greet(
            [place.right(), place.left(), place.partner()]
            + ([place.across()] if carries else [])
        )
        if carries:
            z, y = lax.axis_index("zh"), lax.axis_index("y")
            over = [
                remote(
                    grads_ref.at[1 - z, st, 1 - y], grads_out.at[st], ysend.at[st],
                    yrecv.at[st], place.across(),
                )
                for st in range(grads.shape[1])
            ]
            for c in over:
                c.start()
        part_ref[...] = jnp.zeros_like(part_ref)

        def emit(part, total):
            middle = mid_ref[part]
            scale = rms_scale(middle)
            normed = middle * scale
            part_ref[...] += jnp.sum(total * normed, axis=0, keepdims=True)
            dm = cot_ref[part].astype(f32) + norm_back(total * gain_ref[...], normed, scale)
            dm_ref[part] = dm
            held[part] = dm.astype(bf16)

        ring_scatter(place, x_ref, pair, out, near, far, send, recv, emit)
        RingGather(place, held, all_ref, gsend, grecv).run()
        if carries:
            for c in over:
                c.wait()

    return pallas(
        body,
        [
            jax.ShapeDtypeStruct((rows, width), f32),
            jax.ShapeDtypeStruct((1, width), f32),
            jax.ShapeDtypeStruct((GROUP, rows, width), bf16),
        ]
        + [jax.ShapeDtypeStruct((c.shape[1],) + c.shape[3:], c.dtype) for c in carries],
        [VMEM, VMEM, VMEM, VMEM] + [ANY] * len(carries),
        [VMEM, VMEM, ANY] + [ANY] * len(carries),
        [pltpu.VMEM((rows, width), bf16)] + scatter_scratch(rows, width) + gather_scratch()
        + [DMA((2,)), DMA((2,))],
        cid,
        50,
    )(x, middle, cotangent, gain, *carries)


def tokens_back(x, tokens, dm, gain, shards, cid):
    _, rows, width = x.shape

    def body(
        x_ref, tok_ref, dm_ref, gain_ref, grad_ref, part_ref, pair, out, near, far, send, recv
    ):
        place = Place(shards)
        greet([place.right(), place.left(), place.partner()])
        part_ref[...] = jnp.zeros_like(part_ref)

        def emit(part, total):
            tok = tok_ref[part].astype(f32)
            scale = rms_scale(tok)
            normed = tok * scale
            part_ref[...] += jnp.sum(total * normed, axis=0, keepdims=True)
            grad_ref[part] = (
                dm_ref[part] + norm_back(total * gain_ref[...], normed, scale)
            ).astype(bf16)

        ring_scatter(place, x_ref, pair, out, near, far, send, recv, emit)

    return pallas(
        body,
        (
            jax.ShapeDtypeStruct((rows, width), bf16),
            jax.ShapeDtypeStruct((1, width), f32),
        ),
        [VMEM, VMEM, VMEM, VMEM],
        (VMEM, VMEM),
        scatter_scratch(rows, width),
        cid,
        25,
    )(x, tokens, dm, gain)


class Exchange:
    SEMS = GROUP

    def __init__(self, place, x, out, send, recv):
        self.local = pltpu.make_async_copy(x.at[place.tp], out.at[place.tp], send.at[0])
        self.copies = []
        for k in range(1, GROUP):
            peer = (place.tp + k) % GROUP
            self.copies.append(
                remote(x.at[peer], out.at[place.tp], send.at[k], recv.at[k], place.device(peer))
            )

    def start(self):
        for c in self.copies:
            c.start()
        self.local.start()

    def finish(self):
        for c in self.copies:
            c.wait_recv()
        for c in self.copies:
            c.wait_send()
        self.local.wait()


def group_peers(place):
    return [place.device((place.tp + k) % GROUP) for k in range(1, GROUP)]


def columns_of(dp, t, shards):
    ys, streams = lax.axis_size("y"), lax.axis_size("st")
    z, y = dp // ys, dp % ys
    return ((z * streams + t // shards) * ys + y) * shards + t % shards


def exchange_back(x, planes, shards, cid):
    _, wrows, both = x.shape
    hidden = both // 2
    brows = hidden // planes
    step = min(wrows, 32)

    def body(x_ref, gate_ref, up_ref, got, send, recv):
        place = Place(shards)
        greet(group_peers(place))
        run = Exchange(place, x_ref, got, send, recv)
        run.start()
        run.finish()
        for t in range(GROUP):
            for dp in range(planes):
                flat = columns_of(dp, t, shards)
                for m, out in enumerate((gate_ref, up_ref)):
                    for at in range(0, wrows, step):
                        part = pl.ds(at, step)
                        out[part, flat * brows : (flat + 1) * brows] = got[
                            t, part, m * hidden + dp * brows : m * hidden + (dp + 1) * brows
                        ].astype(f32)

    shape = jax.ShapeDtypeStruct((wrows, hidden * GROUP), f32)
    return pallas(
        body, (shape, shape), [VMEM], (VMEM, VMEM),
        [pltpu.VMEM(x.shape, bf16), DMA((GROUP,)), DMA((GROUP,))], cid, 25,
    )(x)


class PlaceGather:
    SEMS = 5

    def __init__(self, own, out, send, recv, halves):
        z, y = lax.axis_index("zh"), lax.axis_index("y")
        dp, across = z * 2 + y, (1 - z) * 2 + y
        to_z, to_y = {"zh": 1 - z}, {"y": 1 - y}

        def copy(index, src, slot, part, device):
            return remote(
                src.at[part], out.at[slot, part], send.at[index], recv.at[index], device
            )

        first, second = halves
        self.local = pltpu.make_async_copy(own, out.at[dp], send.at[send.shape[0] - 1])
        self.z = [copy(0, own, dp, first, to_z), copy(1, own, dp, second, to_z)]
        self.y = [
            remote(own, out.at[dp], send.at[2], recv.at[2], to_y),
            copy(3, out.at[across], across, first, to_y),
            copy(4, out.at[across], across, second, to_y),
        ]

    def forward(self, half):
        self.z[half].wait_recv()
        self.y[1 + half].start()

    def finish(self):
        for c in self.y:
            c.wait_recv()
        for c in self.z + self.y:
            c.wait_send()


def front(tokens, cotangent, small, w_out, w_query, key_weight, value_weight, w_gate, w_up,
          w_down, planes, direct, shards, cid):
    rows, width = tokens.shape
    wrows = w_out.shape[0]
    srows, scols = small.shape
    brows = w_down.shape[0]
    hidden = brows * planes
    parts = [w_query.shape[1] // GROUP, key_weight.shape[1] // GROUP, value_weight.shape[1] // GROUP]
    qkv = sum(parts)
    slots = planes if direct else 1
    inputs = [tokens, cotangent, w_query, key_weight, value_weight, w_gate, w_up]
    if direct:
        inputs += [w_down, w_out]

    def body(*refs):
        refs = list(refs)

        def take(count):
            taken = refs[:count]
            del refs[:count]
            return taken

        small_ref, = take(1)
        sources = take(len(inputs))
        tok_all, cot_all, small_all, attn_all, ffn_all = take(5)
        down_all, wout_all = take(2) if direct else (None, None)
        held = take(len(inputs))
        (pack, isem, tsend, trecv, csend, crecv, ssend, srecv, psend, precv, fsend, frecv, asend,
         arecv, aasend, aarecv, dsend, drecv, wsend, wrecv) = refs
        place = Place(shards)
        tp, dp, flat = place.tp, place.dp(), place.flat()

        loads = [
            pltpu.make_async_copy(s, h, isem.at[i]) for i, (s, h) in enumerate(zip(sources, held))
        ]
        for i in (2, 3, 4, 0, 5, 6) + ((7, 8) if direct else ()) + (1,):
            loads[i].start()
        tok_ref, cot_ref, wq_ref, wk_ref, wv_ref, wg_ref, wu_ref = held[:7]

        barrier = pltpu.get_barrier_semaphore()

        def signal(device):
            pl.semaphore_signal(
                barrier, inc=1, device_id=device, device_id_type=pl.DeviceIdType.MESH
            )

        for device in group_peers(place):
            signal(device)
        for k in range(1, planes):
            signal(place.dp_device((dp + k) % planes))
        if direct:
            high, low = lax.axis_index("zh"), lax.axis_index("st")
            y, seq = lax.axis_index("y"), lax.axis_index("seq")
            to_seq = high * 2 + y
            from_high, from_y = seq // 2, seq % 2
            selfish = seq == to_seq
            mine = y == from_y
            for j in range(4):

                @pl.when(jnp.logical_and(mine, (from_high * 4 + j) != (high * 4 + seq)))
                def _():
                    signal({"zh": from_high, "seq": jnp.int32(j)})

            pl.semaphore_wait(
                barrier, GROUP - 1 + planes - 1 + 2 - selfish.astype(jnp.int32)
            )
        else:
            pl.semaphore_wait(barrier, GROUP - 1 + planes - 1)

        here = dp if direct else 0
        attn = []
        at = 0
        for i, (ref, cols) in enumerate(zip((wq_ref, wk_ref, wv_ref), parts)):
            loads[2 + i].wait()
            for k in range(GROUP):
                peer = (tp + k) % GROUP
                column = place.head(peer) * cols
                src = ref.at[:, pl.ds(pl.multiple_of(column, cols), cols)]
                dst = attn_all.at[here, tp, :, pl.ds(at, cols)]
                sem = i * GROUP + k
                if k == 0:
                    attn.append(pltpu.make_async_copy(src, dst, asend.at[sem]))
                else:
                    attn.append(
                        remote(src, dst, asend.at[sem], arecv.at[sem], place.device(peer))
                    )
                attn[-1].start()
            at += cols

        small_own = pltpu.make_async_copy(small_ref, small_all.at[tp, dp], ssend.at[0])
        small_own.start()
        small_dp = []
        for k in range(1, planes):
            small_dp.append(
                remote(
                    small_ref, small_all.at[tp, dp], ssend.at[k], srecv.at[k],
                    place.dp_device((dp + k) % planes),
                )
            )
            small_dp[-1].start()

        if direct:
            down_ref, wout_ref = held[7:]
            loads[7].wait()
            half = brows // 2
            down_dp = PlaceGather(
                down_ref, down_all, dsend, drecv, (pl.ds(0, half), pl.ds(half, half))
            )
            down_dp.z[0].start()
        loads[0].wait()
        tok = RingGather(place, tok_ref, tok_all, tsend, trecv, direct)
        tok.start()

        loads[5].wait()
        loads[6].wait()
        for t in range(GROUP):
            for d in range(planes):
                column = columns_of(d, t, shards)
                for m, ref in enumerate((wg_ref, wu_ref)):
                    lane = m * hidden + d * brows
                    pack[t, :, lane : lane + brows] = ref[:, column * brows : (column + 1) * brows]
        ffn = Exchange(place, pack, ffn_all, fsend, frecv)
        ffn.start()

        if direct:
            down_dp.y[0].start()
            down_dp.local.start()
            loads[8].wait()
            wout_copies = [
                remote(
                    wout_ref, wout_all.at[seq], wsend.at[k], wrecv.at[seq],
                    {"zh": z, "seq": to_seq},
                )
                for k, z in enumerate((high, 1 - high))
            ]
            wout_own = pltpu.make_async_copy(wout_ref, wout_all.at[seq], wsend.at[0])
            wout_over = remote(
                wout_all, wout_all, wsend.at[2], wrecv.at[4], place.across()
            )

            @pl.when(selfish)
            def _():
                wout_own.start()

            @pl.when(jnp.logical_not(selfish))
            def _():
                wout_copies[0].start()

            wout_copies[1].start()

        for i in range(3 * GROUP):
            if i % GROUP == 0:
                attn[i].wait()
            else:
                attn[i].wait_recv()
        if direct:
            half = GROUP // 2
            attn_dp = PlaceGather(
                attn_all.at[dp], attn_all, aasend, aarecv, (pl.ds(0, half), pl.ds(half, half))
            )
            attn_dp.z[0].start()
            attn_dp.y[0].start()
            attn_dp.z[1].start()
            down_dp.z[1].start()

        small_own.wait()
        for c in small_dp:
            c.wait_recv()
        small_tp = []
        for k in range(1, GROUP):
            small_tp.append(
                remote(
                    small_all.at[tp], small_all.at[tp], psend.at[k], precv.at[k],
                    place.device((tp + k) % GROUP),
                )
            )
            small_tp[-1].start()

        loads[1].wait()
        cot = RingGather(place, cot_ref, cot_all, csend, crecv, direct)
        tok.pass_on()
        cot.start()
        tok.step_across()
        if direct:
            down_dp.forward(0)

            @pl.when(mine)
            def _():
                for j in range(4):

                    @pl.when((from_high * 4 + j) != (high * 4 + seq))
                    def _():
                        remote(
                            wout_ref, wout_all.at[j], wsend.at[0], wrecv.at[j], place.across()
                        ).wait_recv()

                @pl.when(selfish)
                def _():
                    wout_own.wait()

                wout_over.start()

            attn_dp.forward(0)
        tok.step_far()
        cot.pass_on()
        if direct:
            attn_dp.forward(1)
        cot.step_across()
        if direct:
            down_dp.forward(1)
        cot.step_far()
        tok.finish()
        cot.finish()
        ffn.finish()
        for i in range(3 * GROUP):
            if i % GROUP:
                attn[i].wait_send()
        for c in small_tp:
            c.wait_recv()
        for c in small_dp + small_tp:
            c.wait_send()
        if direct:
            attn_dp.finish()
            down_dp.finish()
            down_dp.local.wait()

            @pl.when(jnp.logical_not(selfish))
            def _():
                wout_copies[0].wait_send()

            wout_copies[1].wait_send()

            @pl.when(mine)
            def _():
                wout_over.wait_send()

            @pl.when(jnp.logical_not(mine))
            def _():
                wout_over.wait_recv()

    shapes = [
        jax.ShapeDtypeStruct((GROUP, rows, width), bf16),
        jax.ShapeDtypeStruct((GROUP, rows, width), bf16),
        jax.ShapeDtypeStruct((GROUP, planes, srows, scols), bf16),
        jax.ShapeDtypeStruct((slots, GROUP, wrows, qkv), bf16),
        jax.ShapeDtypeStruct((GROUP, wrows, 2 * hidden), bf16),
    ]
    if direct:
        shapes += [
            jax.ShapeDtypeStruct((planes, brows, width), bf16),
            jax.ShapeDtypeStruct((planes, wrows, width), bf16),
        ]
    return pallas(
        body,
        shapes,
        [VMEM] + [ANY] * len(inputs),
        [ANY, ANY, VMEM] + [ANY] * (len(shapes) - 3),
        [pltpu.VMEM(x.shape, x.dtype) for x in inputs]
        + [pltpu.VMEM((GROUP, wrows, 2 * hidden), bf16), DMA((len(inputs),))]
        + gather_scratch() + gather_scratch()
        + [
            DMA((planes,)), DMA((planes,)), DMA((GROUP,)), DMA((GROUP,)),
            DMA((GROUP,)), DMA((GROUP,)), DMA((3 * GROUP,)), DMA((3 * GROUP,)),
            DMA((PlaceGather.SEMS,)), DMA((PlaceGather.SEMS,)),
            DMA((PlaceGather.SEMS + 1,)), DMA((PlaceGather.SEMS,)), DMA((3,)), DMA((5,)),
        ],
        cid,
        60,
    )(small, *inputs)


class Spread:
    SEMS = 6

    def __init__(self, out, send, recv):
        z, y = lax.axis_index("zh"), lax.axis_index("y")
        to_z, to_y = {"zh": 1 - z}, {"y": 1 - y}

        def copy(index, zp, st, device):
            part = out.at[zp, st, y]
            return remote(part, part, send.at[index], recv.at[index], device)

        self.z = [copy(st, z, st, to_z) for st in range(2)]
        self.y = [copy(2 + st, z, st, to_y) for st in range(2)]
        self.on = [copy(4 + st, 1 - z, st, to_y) for st in range(2)]

    def start_z(self):
        for c in self.z:
            c.start()

    def start_y(self):
        for c in self.y:
            c.start()

    def forward(self, half):
        self.z[half].wait_recv()
        self.on[half].start()

    def finish(self):
        for c in self.y + self.on:
            c.wait_recv()
        for c in self.z + self.y + self.on:
            c.wait_send()


def rope_constants(length):
    exponent = np.arange(HEAD_SIZE // 2, dtype=np.float32) * np.float32(2.0 / HEAD_SIZE)
    inverse = np.power(np.float32(ROPE_BASE), -exponent).astype(np.float32)
    angles = np.arange(length, dtype=np.float32)[:, None] * inverse[None, :]
    cosine, sine = np.cos(angles.astype(np.float64)), np.sin(angles.astype(np.float64))
    return (
        jnp.asarray(np.concatenate([cosine, cosine], axis=1).astype(np.float32)),
        jnp.asarray(np.concatenate([-sine, sine], axis=1).astype(np.float32)),
    )


def document_mask(row, docs, low, count, keys):
    at_row = low + lax.broadcasted_iota(jnp.int32, (count, 1), 0)
    at_col = lax.broadcasted_iota(jnp.int32, (1, keys), 1)
    seg_row = jnp.zeros((count, 1), jnp.int32)
    seg_col = jnp.zeros((1, keys), jnp.int32)
    for d in range(docs):
        start = (row[:, d : d + 1] * 128.0 + row[:, docs + d : docs + d + 1]).astype(jnp.int32)
        seg_row = seg_row + jnp.where(at_row >= start, 1, 0)
        seg_col = seg_col + jnp.where(at_col >= start, 1, 0)
    return jnp.logical_and(at_row >= at_col, seg_row == seg_col)


def forward_pass(tokens, cotangent, small, w_out, w_query, key_weight, value_weight, w_gate,
                 w_up, w_down, docs, shards, cid):
    rows, width = tokens.shape
    wrows = w_out.shape[0]
    srows = small.shape[0]
    brows = w_down.shape[0]
    planes = 4
    hidden = brows * planes
    parts = [w_query.shape[1] // GROUP, key_weight.shape[1] // GROUP, value_weight.shape[1] // GROUP]
    qkv = sum(parts)
    qcols = parts[0]
    heads = qcols // HEAD_SIZE
    group_rows = rows * GROUP
    length = rows * shards
    streams = GROUP // shards
    gain_rows = width // 128
    grows = srows - wrows
    cosine, sine = rope_constants(length)
    inputs = [tokens, cotangent, w_query, key_weight, value_weight, w_gate, w_up, w_down, w_out]
    score_scale = HEAD_SIZE ** (-0.5)

    def body(
        small_ref, cos_ref, sin_ref, s0, s1, s2, s3, s4, s5, s6, s7, s8,
        cot_all, ffn_all, down_all, h1_out, h2_all, small_all, gains_ref, attn_all, wout_all,
        qkv_ref, low_ref, gate_ref, mixed_ref, gated_ref, mid_ref, hg, starts_ref,
        h0, h1, h2, h3, h4, h5, h6, h7, h8, pack, tok_all, hid, partial, held_two, isem, osem,
        tsend, trecv, csend, crecv, gsend, grecv, ssend, srecv, psend, precv, fsend, frecv, asend,
        arecv, aasend, aarecv, ffsend, ffrecv, dsend, drecv, wsend, wrecv, pair, out, near, far,
        rsend, rrecv,
    ):
        sources = [s0, s1, s2, s3, s4, s5, s6, s7, s8]
        held = [h0, h1, h2, h3, h4, h5, h6, h7, h8]
        place = Place(shards)
        tp, dp = place.tp, place.dp()
        high, low = lax.axis_index("zh"), lax.axis_index("st")
        y, seq = lax.axis_index("y"), lax.axis_index("seq")
        loads = [
            pltpu.make_async_copy(s, h, isem.at[i]) for i, (s, h) in enumerate(zip(sources, held))
        ]
        for i in (2, 3, 4, 8, 0, 5, 6, 7, 1):
            loads[i].start()
        tok_ref, cot_ref, wq_ref, wk_ref, wv_ref, wg_ref, wu_ref, down_ref, wout_ref = held

        barrier = pltpu.get_barrier_semaphore()

        def signal(device):
            pl.semaphore_signal(
                barrier, inc=1, device_id=device, device_id_type=pl.DeviceIdType.MESH
            )

        for device in group_peers(place):
            signal(device)
        for k in range(1, planes):
            signal(place.dp_device((dp + k) % planes))
        to_seq = high * 2 + y
        from_high, from_y = seq // 2, seq % 2
        selfish = seq == to_seq
        mine = y == from_y
        for j in range(4):

            @pl.when(jnp.logical_and(mine, (from_high * 4 + j) != (high * 4 + seq)))
            def _():
                signal({"zh": from_high, "seq": jnp.int32(j)})

        pl.semaphore_wait(barrier, GROUP - 1 + planes - 1 + 2 - selfish.astype(jnp.int32))

        attn = []
        at = 0
        for i, (ref, cols) in enumerate(zip((wq_ref, wk_ref, wv_ref), parts)):
            loads[2 + i].wait()
            for k in range(GROUP):
                peer = (tp + k) % GROUP
                column = place.head(peer) * cols
                src = ref.at[:, pl.ds(pl.multiple_of(column, cols), cols)]
                dst = attn_all.at[high, low, y, pl.ds(seq * wrows, wrows), pl.ds(at, cols)]
                sem = i * GROUP + k
                if k == 0:
                    attn.append(pltpu.make_async_copy(src, dst, asend.at[sem]))
                else:
                    attn.append(
                        remote(src, dst, asend.at[sem], arecv.at[sem], place.device(peer))
                    )
                attn[-1].start()
            at += cols

        small_own = pltpu.make_async_copy(small_ref, small_all.at[tp, dp], ssend.at[0])
        small_own.start()
        small_dp = []
        for k in range(1, planes):
            small_dp.append(
                remote(
                    small_ref, small_all.at[tp, dp], ssend.at[k], srecv.at[k],
                    place.dp_device((dp + k) % planes),
                )
            )
            small_dp[-1].start()

        loads[8].wait()
        wout_copies = [
            remote(
                wout_ref, wout_all.at[seq], wsend.at[k], wrecv.at[seq], {"zh": z, "seq": to_seq}
            )
            for k, z in enumerate((high, 1 - high))
        ]
        wout_own = pltpu.make_async_copy(wout_ref, wout_all.at[seq], wsend.at[0])
        wout_over = remote(wout_all, wout_all, wsend.at[2], wrecv.at[4], place.across())
        wout_copies[1].start()

        @pl.when(selfish)
        def _():
            wout_own.start()

        @pl.when(jnp.logical_not(selfish))
        def _():
            wout_copies[0].start()

        loads[0].wait()
        tok = RingGather(place, tok_ref, tok_all, tsend, trecv, True)
        tok.start()

        loads[5].wait()
        loads[6].wait()
        for t in range(GROUP):
            for d in range(planes):
                column = columns_of(d, t, shards)
                for m, ref in enumerate((wg_ref, wu_ref)):
                    lane = m * hidden + d * brows
                    pack[t, :, lane : lane + brows] = ref[:, column * brows : (column + 1) * brows]
        ffn = []
        for k in range(GROUP):
            peer = (tp + k) % GROUP
            src = pack.at[peer]
            dst = ffn_all.at[high, low, y, pl.ds(seq * wrows, wrows)]
            if k == 0:
                ffn.append(pltpu.make_async_copy(src, dst, fsend.at[k]))
            else:
                ffn.append(remote(src, dst, fsend.at[k], frecv.at[k], place.device(peer)))
            ffn[-1].start()

        def arrived(copies):
            for i, c in enumerate(copies):
                if i % GROUP == 0:
                    c.wait()
                else:
                    c.wait_recv()

        arrived(attn)
        attn_dp = Spread(attn_all, aasend, aarecv)
        attn_dp.start_z()
        attn_dp.start_y()

        small_own.wait()
        for c in small_dp:
            c.wait_recv()
        small_tp = []
        for k in range(1, GROUP):
            small_tp.append(
                remote(
                    small_all.at[tp], small_all.at[tp], psend.at[k], precv.at[k],
                    place.device((tp + k) % GROUP),
                )
            )
            small_tp[-1].start()

        @pl.when(mine)
        def _():
            for j in range(4):

                @pl.when((from_high * 4 + j) != (high * 4 + seq))
                def _():
                    remote(
                        wout_ref, wout_all.at[j], wsend.at[0], wrecv.at[j], place.across()
                    ).wait_recv()

            @pl.when(selfish)
            def _():
                wout_own.wait()

            wout_over.start()

        tok.pass_on()
        arrived(ffn)
        ffn_dp = Spread(ffn_all, ffsend, ffrecv)
        ffn_dp.start_z()
        ffn_dp.start_y()
        loads[7].wait()
        half = brows // 2
        down_dp = PlaceGather(
            down_ref, down_all, dsend, drecv, (pl.ds(0, half), pl.ds(half, half))
        )
        down_dp.local.start()
        down_dp.z[0].start()
        down_dp.z[1].start()
        down_dp.y[0].start()
        loads[1].wait()
        cot = RingGather(place, cot_ref, cot_all, csend, crecv, True)
        cot.start()
        tok.step_across()
        attn_dp.forward(0)
        attn_dp.forward(1)
        tok.step_far()

        for c in small_tp:
            c.wait_recv()
        gains = jnp.zeros((grows, 128), f32)
        for t in range(GROUP):
            for d in range(planes):
                gains = gains + small_all[t, d, pl.ds(wrows, grows)].astype(f32)
                flat = columns_of(d, t, shards)
                hg[flat * wrows : (flat + 1) * wrows] = small_all[t, d, pl.ds(0, wrows)]
        gains_ref[...] = gains
        gain_one = jnp.concatenate([gains[i : i + 1] for i in range(gain_rows)], axis=1)
        gain_two = jnp.concatenate(
            [gains[gain_rows + i : gain_rows + i + 1] for i in range(gain_rows)], axis=1
        )
        query_gain = gains[2 * gain_rows : 2 * gain_rows + 1]
        key_gain = gains[2 * gain_rows + 1 : 2 * gain_rows + 2]
        starts = []
        for st in range(streams):
            block = small_all[st * shards, dp, pl.ds(wrows, grows)].astype(f32)
            starts.append(block[2 * gain_rows + 2 : 2 * gain_rows + 3])
            starts_ref[st : st + 1] = starts[st]

        tok.finish()
        step = 32

        def norm(i, _):
            block = i // (rows // step)
            inner = pl.ds(pl.multiple_of(i % (rows // step) * step, step), step)
            value = tok_all[block, inner].astype(f32)
            hid[block, inner] = (value * rms_scale(value) * gain_one).astype(bf16)
            return 0

        lax.fori_loop(0, group_rows // step, norm, 0)
        save = pltpu.make_async_copy(hid, h1_out, osem)
        save.start()
        cot.pass_on()
        attn_dp.finish()
        weight = attn_all[...].reshape(width, qkv)
        head = place.head(tp)
        lanes = lax.broadcasted_iota(jnp.int32, (1, 128), 1)

        def rotary(x, gain, s):
            scaled = x * rms_scale(x) * gain
            return (
                scaled * cos_ref[...] + pltpu.roll(scaled, HEAD_SIZE // 2, 1) * sin_ref[...]
            ).astype(bf16)

        for s in range(streams):
            part = pl.ds(s * length, length)
            normed = hid[s * shards : (s + 1) * shards].reshape(length, width)
            raw = jnp.dot(normed, weight, preferred_element_type=f32)
            qkv_ref[part] = raw
            logit = jnp.dot(normed, hg[...], preferred_element_type=f32)
            for g in range(heads):
                at = g * HEAD_SIZE
                low_ref[part, at : at + HEAD_SIZE] = rotary(
                    raw[:, at : at + HEAD_SIZE], query_gain, s
                )
                own = jnp.sum(
                    jnp.where(lanes == head * heads + g, logit, 0.0), axis=1, keepdims=True
                )
                gate_ref[part, at : at + HEAD_SIZE] = jnp.broadcast_to(
                    jax.nn.sigmoid(own), (length, HEAD_SIZE)
                )
            low_ref[part, qcols : qcols + HEAD_SIZE] = rotary(
                raw[:, qcols : qcols + HEAD_SIZE], key_gain, s
            )
            low_ref[part, qcols + HEAD_SIZE :] = raw[:, qcols + HEAD_SIZE :].astype(bf16)
            if s == 0:
                cot.step_across()
        cot.step_far()
        block = 128
        for s in range(streams):
            base = s * length
            for r in range(0, length, block):
                keys = r + block
                allowed = document_mask(starts[s], docs, r, block, keys)
                key = low_ref[pl.ds(base, keys), qcols : qcols + HEAD_SIZE]
                value = low_ref[pl.ds(base, keys), qcols + HEAD_SIZE :]
                part = pl.ds(base + r, block)
                for g in range(heads):
                    at = g * HEAD_SIZE
                    scores = (
                        lax.dot_general(
                            low_ref[part, at : at + HEAD_SIZE], key, (((1,), (1,)), ((), ())),
                            preferred_element_type=f32,
                        )
                        * score_scale
                    )
                    scores = jnp.where(allowed, scores, MASK_FILL)
                    weights = jnp.exp(scores - jnp.max(scores, axis=1, keepdims=True))
                    probs = weights / jnp.sum(weights, axis=1, keepdims=True)
                    mixed = jnp.dot(
                        probs.astype(bf16), value, preferred_element_type=f32
                    ).astype(bf16)
                    mixed_ref[part, at : at + HEAD_SIZE] = mixed
                    gated_ref[part, at : at + HEAD_SIZE] = (
                        mixed.astype(f32) * gate_ref[part, at : at + HEAD_SIZE]
                    ).astype(bf16)

        @pl.when(jnp.logical_not(mine))
        def _():
            wout_over.wait_recv()

        wide = 512
        for s in range(streams):
            for c in range(0, width, wide):
                product = jnp.dot(
                    gated_ref[pl.ds(s * length, length)],
                    wout_all[:, :, c : c + wide].reshape(qcols, wide),
                    preferred_element_type=f32,
                )
                partial[s * shards : (s + 1) * shards, :, c : c + wide] = product.astype(
                    bf16
                ).reshape(shards, rows, wide)
        ffn_dp.forward(0)

        def emit(part, total):
            middle = tok_ref[part].astype(f32) + total
            mid_ref[part] = middle
            held_two[part] = (middle * rms_scale(middle) * gain_two).astype(bf16)

        ring_scatter(place, partial, pair, out, near, far, rsend, rrecv, emit)
        two = RingGather(place, held_two, h2_all, gsend, grecv)
        two.start()
        two.pass_on()
        ffn_dp.forward(1)
        two.step_across()
        two.step_far()
        down_dp.forward(0)
        two.finish()
        down_dp.forward(1)
        cot.finish()
        ffn_dp.finish()
        down_dp.finish()
        down_dp.local.wait()
        save.wait()
        for i, c in enumerate(attn):
            if i % GROUP:
                c.wait_send()
        for c in ffn[1:] + small_dp + small_tp:
            c.wait_send()

        @pl.when(jnp.logical_not(selfish))
        def _():
            wout_copies[0].wait_send()

        wout_copies[1].wait_send()

        @pl.when(mine)
        def _():
            wout_over.wait_send()

    pieces = (2, streams, 2, shards * wrows)
    shape = jax.ShapeDtypeStruct
    return pallas(
        body,
        [
            shape((GROUP, rows, width), bf16),
            shape(pieces + (2 * hidden,), bf16),
            shape((planes, brows, width), bf16),
            shape((GROUP, rows, width), bf16),
            shape((GROUP, rows, width), bf16),
            shape((GROUP, planes, srows, 128), bf16),
            shape((grows, 128), f32),
            shape(pieces + (qkv,), bf16),
            shape((planes, wrows, width), bf16),
            shape((group_rows, qkv), f32),
            shape((group_rows, qkv), bf16),
            shape((group_rows, qcols), f32),
            shape((group_rows, qcols), bf16),
            shape((group_rows, qcols), bf16),
            shape((rows, width), f32),
            shape((width, 128), bf16),
            shape((streams, 128), f32),
        ],
        [VMEM] * 3 + [ANY] * len(inputs),
        [ANY] * 5 + [VMEM] * 12,
        [pltpu.VMEM(x.shape, x.dtype) for x in inputs]
        + [
            pltpu.VMEM((GROUP, wrows, 2 * hidden), bf16),
            pltpu.VMEM((GROUP, rows, width), bf16),
            pltpu.VMEM((GROUP, rows, width), bf16),
            pltpu.VMEM((GROUP, rows, width), bf16),
            pltpu.VMEM((rows, width), bf16),
            DMA((len(inputs),)),
            DMA,
        ]
        + gather_scratch() + gather_scratch() + gather_scratch()
        + [
            DMA((planes,)), DMA((planes,)), DMA((GROUP,)), DMA((GROUP,)),
            DMA((GROUP,)), DMA((GROUP,)), DMA((3 * GROUP,)), DMA((3 * GROUP,)),
            DMA((Spread.SEMS,)), DMA((Spread.SEMS,)), DMA((Spread.SEMS,)), DMA((Spread.SEMS,)),
            DMA((PlaceGather.SEMS + 1,)), DMA((PlaceGather.SEMS,)), DMA((3,)), DMA((5,)),
        ]
        + scatter_scratch(rows, width),
        cid,
        100,
        56,
    )(small, cosine, sine, *inputs)


class PlaceSums:
    def __init__(self, piece, got, far, near, send, recv):
        z, y = lax.axis_index("zh"), lax.axis_index("y")
        to_z, to_y = {"zh": 1 - z}, {"y": 1 - y}
        self.got, self.far, self.near = got, far, near
        self.y_far = remote(piece(1 - z, 1 - y), got.at[0], send.at[0], recv.at[0], to_y)
        self.y_near = remote(piece(z, 1 - y), got.at[1], send.at[1], recv.at[1], to_y)
        self.z = remote(far, got.at[2], send.at[2], recv.at[2], to_z)
        self.loads = [
            pltpu.make_async_copy(piece(1 - z, y), far, send.at[3]),
            pltpu.make_async_copy(piece(z, y), near, send.at[4]),
        ]

    def load(self):
        for c in self.loads:
            c.start()

    def over_z(self):
        self.loads[0].wait()
        self.y_far.wait_recv()
        self.each(lambda at: self.put(at))
        self.z.start()

    def put(self, at):
        self.far[at] = (self.far[at].astype(f32) + self.got[(0,) + at].astype(f32)).astype(bf16)

    def each(self, visit):
        lead, rows = self.far.shape[:-2], self.far.shape[-2]

        def inner(i, _):
            part = pl.ds(pl.multiple_of(i * 32, 32), 32)
            if lead:
                for k in range(lead[0]):
                    visit((k, part))
            else:
                visit((part,))
            return 0

        lax.fori_loop(0, rows // 32, inner, 0)

    def total(self, at):
        return (self.near[at].astype(f32) + self.got[(1,) + at].astype(f32)) + self.got[
            (2,) + at
        ].astype(f32)

    def arrive(self):
        self.loads[1].wait()
        self.y_near.wait_recv()
        self.z.wait_recv()

    def drain(self):
        for c in (self.y_far, self.y_near, self.z):
            c.wait_send()


def backward_pass(x, final, middle, tokens, cotangent, gains, headgate, qkv_w, out_w, hidden_one,
                  qkv, low, gate, mixed, gated, starts, down_grad, ffn_grad, docs, shards, cid):
    _, rows, width = x.shape
    planes = 4
    streams = GROUP // shards
    length = rows * shards
    group_rows = rows * GROUP
    qcols = gate.shape[1]
    qkv_cols = qkv.shape[1]
    kcols = (qkv_cols - qcols) // 2
    heads = qcols // HEAD_SIZE
    brows = down_grad.shape[2]
    both = ffn_grad.shape[4]
    hidden = both // 2
    wrows = width // (planes * GROUP)
    gain_rows = width // 128
    score_scale = HEAD_SIZE ** (-0.5)
    cosine, sine = rope_constants(length)
    srows = 24
    inputs = [
        x, middle, tokens, cotangent, headgate, qkv_w, out_w, qkv, low, gate, mixed, gated,
    ]

    def body(
        gains_ref, starts_ref, cos_ref, sin_ref, final_ref, h1_ref, down_ref, ffn_ref,
        i0, i1, i2, i3, i4, i5, i6, i7, i8, i9, i10, i11,
        layer_ref, tgrad_ref, gate_out, up_out, query_out, key_out, value_out, o_out, down_out,
        s_out,
        partial, mid_ref, tok_ref, cot_ref, hg_ref, wq_ref, wout_ref, qkv_ref, low_ref, gate_ref,
        mixed_ref, gated_ref,
        held, db_all, dmid, gq, dgl, dk_acc, dv_acc, dmix, small, stage, s_got, s_held, s_line,
        g_got, g_far, g_near, g_in, d_got, d_far, d_near, q_own, q_got, q_far, q_near, q_in,
        o_own, o_got, o_far, o_near, o_in,
        pair, out, near, far, rsend, rrecv, r2send, r2recv, r3send, r3recv, csend, crecv,
        isem, gsend, grecv, dsend, drecv, qsend, qrecv, osend, orecv, gxsend, gxrecv, qxsend,
        qxrecv, oxsend, oxrecv, asend, arecv, bsend, brecv, lsem, turn,
    ):
        sources = [i0, i1, i2, i3, i4, i5, i6, i7, i8, i9, i10, i11]
        targets = [
            partial, mid_ref, tok_ref, cot_ref, hg_ref, wq_ref, wout_ref, qkv_ref, low_ref,
            gate_ref, mixed_ref, gated_ref,
        ]
        place = Place(shards)
        tp, dp, flat = place.tp, place.dp(), place.flat()
        high, y, seq = lax.axis_index("zh"), lax.axis_index("y"), lax.axis_index("seq")
        loads = [
            pltpu.make_async_copy(s, t, isem.at[i])
            for i, (s, t) in enumerate(zip(sources, targets))
        ]
        for c in loads[:4]:
            c.start()
        barrier = pltpu.get_barrier_semaphore()

        def signal(device, semaphore=barrier):
            pl.semaphore_signal(
                semaphore, inc=1, device_id=device, device_id_type=pl.DeviceIdType.MESH
            )

        for device in group_peers(place):
            signal(device)
        for k in range(1, planes):
            signal(place.dp_device((dp + k) % planes))
        owner = place.head(tp) * planes + dp
        source = {"st": lax.axis_index("st"), "seq": high * 2 + y}
        source.update(place.dp_device(seq))

        @pl.when(owner != flat)
        def _():
            signal(source)

        pl.semaphore_wait(barrier, GROUP + planes - 2 + (owner != flat).astype(jnp.int32))

        ffn = PlaceSums(
            lambda zp, yp: ffn_ref.at[zp, :, yp], g_got, g_far, g_near, gsend, grecv
        )
        down = PlaceSums(lambda zp, yp: down_ref.at[zp, yp], d_got, d_far, d_near, dsend, drecv)
        down.y_far.start()
        ffn.y_far.start()
        ffn.y_near.start()
        down.load()
        ffn.load()
        for c in loads[4:]:
            c.start()

        small[...] = jnp.zeros_like(small)
        gain_all = gains_ref[...]
        gain_one = jnp.concatenate([gain_all[i : i + 1] for i in range(gain_rows)], axis=1)
        gain_two = jnp.concatenate(
            [gain_all[gain_rows + i : gain_rows + i + 1] for i in range(gain_rows)], axis=1
        )
        query_gain = gain_all[2 * gain_rows : 2 * gain_rows + 1]
        key_gain = gain_all[2 * gain_rows + 1 : 2 * gain_rows + 2]
        for c in loads[:4]:
            c.wait()

        def emit_dm(part, total):
            value = mid_ref[part]
            scale = rms_scale(value)
            normed = value * scale
            small[17:18] += jnp.sum(total * normed, axis=0, keepdims=True)
            dm = cot_ref[part].astype(f32) + norm_back(total * gain_two, normed, scale)
            dmid[part] = dm
            held[part] = dm.astype(bf16)

        ring_scatter(place, partial, pair, out, near, far, rsend, rrecv, emit_dm)
        grad = RingGather(place, held, db_all, csend, crecv)
        grad.start()
        h1_all = partial
        load_h1 = pltpu.make_async_copy(h1_ref, h1_all, lsem.at[0])
        load_h1.start()
        down.over_z()
        grad.pass_on()
        grad.step_across()
        grad.step_far()
        for c in loads[4:]:
            c.wait()
        grad.finish()

        lanes = lax.broadcasted_iota(jnp.int32, (1, 128), 1)
        head = place.head(tp)
        for s in range(streams):
            part = pl.ds(s * length, length)
            db = db_all[s * shards : (s + 1) * shards].reshape(length, width)
            da = lax.dot_general(
                db, wout_ref[...], (((1,), (1,)), ((), ())), preferred_element_type=f32
            )
            logits = jnp.zeros((length, 128), f32)
            for g in range(heads):
                at = g * HEAD_SIZE
                piece = da[:, at : at + HEAD_SIZE]
                opened = gate_ref[part, at : at + HEAD_SIZE]
                dmix[part, at : at + HEAD_SIZE] = (piece * opened).astype(bf16)
                own = jnp.sum(
                    piece * mixed_ref[part, at : at + HEAD_SIZE].astype(f32), axis=1,
                    keepdims=True,
                )
                logits = jnp.where(
                    lanes == head * heads + g, own * opened * (1.0 - opened), logits
                )
            dgl[part] = logits.astype(bf16)
        wide = 512
        for c in range(0, width, wide):
            product = lax.dot_general(
                gated_ref[...], db_all[:, :, c : c + wide].reshape(group_rows, wide),
                (((0,), (0,)), ((), ())), preferred_element_type=f32,
            ).astype(bf16)
            for j in range(planes):
                o_own[j // 2, j % 2, :, c : c + wide] = product[j * wrows : (j + 1) * wrows]
        outs = PlaceSums(lambda zp, yp: o_own.at[zp, yp], o_got, o_far, o_near, osend, orecv)
        outs.y_far.start()
        outs.load()
        ffn.over_z()

        block = 128
        query_part = jnp.zeros((1, HEAD_SIZE), f32)
        key_part = jnp.zeros((1, HEAD_SIZE), f32)
        for s in range(streams):
            base = s * length
            row = starts_ref[s : s + 1]
            dk_acc[...] = jnp.zeros_like(dk_acc)
            dv_acc[...] = jnp.zeros_like(dv_acc)

            def back(grad_rotated, raw, gain):
                grad_gained = grad_rotated * cos_ref[...] - pltpu.roll(
                    grad_rotated, HEAD_SIZE // 2, 1
                ) * sin_ref[...]
                scale = rms_scale(raw)
                normed = raw * scale
                return (
                    jnp.sum(grad_gained * normed, axis=0, keepdims=True),
                    norm_back(grad_gained * gain, normed, scale).astype(bf16),
                )

            for r in range(0, length, block):
                keys = r + block
                allowed = document_mask(row, docs, r, block, keys)
                key = low_ref[pl.ds(base, keys), qcols : qcols + HEAD_SIZE]
                value = low_ref[pl.ds(base, keys), qcols + HEAD_SIZE :]
                part = pl.ds(base + r, block)
                for g in range(heads):
                    at = g * HEAD_SIZE
                    query = low_ref[part, at : at + HEAD_SIZE]
                    scores = (
                        lax.dot_general(
                            query, key, (((1,), (1,)), ((), ())), preferred_element_type=f32
                        )
                        * score_scale
                    )
                    scores = jnp.where(allowed, scores, MASK_FILL)
                    weights = jnp.exp(scores - jnp.max(scores, axis=1, keepdims=True))
                    probs = weights / jnp.sum(weights, axis=1, keepdims=True)
                    dout = dmix[part, at : at + HEAD_SIZE]
                    dprobs = lax.dot_general(
                        dout, value, (((1,), (1,)), ((), ())), preferred_element_type=f32
                    )
                    delta = jnp.sum(probs * dprobs, axis=1, keepdims=True)
                    dscores = (probs * (dprobs - delta)).astype(bf16)
                    dq = jnp.dot(dscores, key, preferred_element_type=f32) * score_scale
                    gq[part, at : at + HEAD_SIZE] = dq.astype(bf16)
                    dk_acc[0:keys] += lax.dot_general(
                        dscores, query, (((0,), (0,)), ((), ())), preferred_element_type=f32
                    )
                    dv_acc[0:keys] += lax.dot_general(
                        probs.astype(bf16), dout, (((0,), (0,)), ((), ())),
                        preferred_element_type=f32,
                    )
            part = pl.ds(base, length)
            for g in range(heads):
                at = g * HEAD_SIZE
                sums, grads = back(
                    gq[part, at : at + HEAD_SIZE].astype(f32), qkv_ref[part, at : at + HEAD_SIZE],
                    query_gain,
                )
                query_part = query_part + sums
                gq[part, at : at + HEAD_SIZE] = grads
            sums, grads = back(
                (dk_acc[...] * score_scale).astype(bf16).astype(f32),
                qkv_ref[part, qcols : qcols + HEAD_SIZE], key_gain,
            )
            key_part = key_part + sums
            gq[part, qcols : qcols + HEAD_SIZE] = grads
            gq[part, qcols + HEAD_SIZE :] = dv_acc[...].astype(bf16)

        load_h1.wait()
        for n in range(width // 256):
            cols = slice(n * 256, (n + 1) * 256)
            product = lax.dot_general(
                h1_all[:, :, cols].reshape(group_rows, 256), gq[...], (((0,), (0,)), ((), ())),
                preferred_element_type=f32,
            )
            q_own[n // 4, n // 2 % 2, n % 2] = product.astype(bf16)
        qkvs = PlaceSums(lambda zp, yp: q_own.at[zp, :, yp], q_got, q_far, q_near, qsend, qrecv)
        qkvs.y_far.start()
        outs.y_near.start()
        qkvs.y_near.start()
        down.y_near.start()
        qkvs.load()
        for c in range(0, width, wide):
            small[0:16, c : c + wide] = lax.dot_general(
                dgl[...], h1_all[:, :, c : c + wide].reshape(group_rows, wide),
                (((0,), (0,)), ((), ())), preferred_element_type=f32,
            )[0:16]

        for s in range(streams):
            part = pl.ds(s * length, length)
            for c in range(0, width, wide):
                product = lax.dot_general(
                    gq[part], wq_ref[c : c + wide], (((1,), (1,)), ((), ())),
                    preferred_element_type=f32,
                ) + lax.dot_general(
                    dgl[part], hg_ref[c : c + wide], (((1,), (1,)), ((), ())),
                    preferred_element_type=f32,
                )
                partial[s * shards : (s + 1) * shards, :, c : c + wide] = product.astype(
                    bf16
                ).reshape(shards, rows, wide)

        def emit_tokens(part, total):
            tok = tok_ref[part].astype(f32)
            scale = rms_scale(tok)
            normed = tok * scale
            small[16:17] += jnp.sum(total * normed, axis=0, keepdims=True)
            tgrad_ref[part] = (
                dmid[part] + norm_back(total * gain_one, normed, scale)
            ).astype(bf16)

        load_final = pltpu.make_async_copy(final_ref, db_all, lsem.at[1])
        load_final.start()
        ring_scatter(place, partial, pair, out, near, far, r2send, r2recv, emit_tokens)
        ring_peers = [place.right(), place.left(), place.partner()]
        for device in ring_peers:
            signal(device, turn)
        outs.over_z()
        qkvs.over_z()

        small[18:19] = jnp.concatenate([query_part] * gain_rows, axis=1)
        small[19:20] = jnp.concatenate([key_part] * gain_rows, axis=1)
        for t in range(GROUP):
            for d in range(planes):
                lane = columns_of(d, t, shards) // 2 * 128
                stage[t, d * srows : (d + 1) * srows] = small[:, lane : lane + 128]
        sums = Exchange(place, stage, s_got, asend, arecv)
        sums.start()

        load_final.wait()
        pl.semaphore_wait(turn, len(ring_peers))

        def emit_layer(part, total):
            layer_ref[part] = (mid_ref[part] + total).astype(bf16)

        ring_scatter(place, db_all, pair, out, near, far, r3send, r3recv, emit_layer)
        sums.finish()
        s_held[...] = jnp.sum(s_got[...], axis=0).reshape(s_held.shape)
        line_own = pltpu.make_async_copy(s_held.at[dp], s_line.at[dp], bsend.at[0])
        line_own.start()
        lines = []
        for k in range(1, planes):
            to = (dp + k) % planes
            lines.append(
                remote(
                    s_held.at[to], s_line.at[dp], bsend.at[k], brecv.at[k], place.dp_device(to)
                )
            )
            lines[-1].start()

        def scatter_rows(total, ready, send, recv, into):
            def keep(at):
                ready[at] = total(at).astype(bf16)

            copies = []
            for k in range(GROUP):
                peer = (tp + k) % GROUP
                src = ready.at[peer // shards, pl.ds(peer % shards * wrows, wrows)]
                if k == 0:
                    copies.append(pltpu.make_async_copy(src, into.at[tp], send.at[0]))
                else:
                    copies.append(
                        remote(src, into.at[tp], send.at[k], recv.at[k], place.device(peer))
                    )
            return keep, copies

        ffn.arrive()
        keep, ffn_rows = scatter_rows(ffn.total, g_near, gxsend, gxrecv, g_in)
        ffn.each(keep)
        for c in ffn_rows:
            c.start()
        down.arrive()

        def put_down(at):
            down_out[at] = down.total(at)

        down.each(put_down)

        outs.arrive()

        def keep_out(at):
            o_near[at] = outs.total(at).astype(bf16)

        outs.each(keep_out)
        out_own = pltpu.make_async_copy(o_near, o_in, oxsend)
        out_far = remote(o_near, o_in, oxsend, oxrecv, place.any_device(owner))

        @pl.when(owner == flat)
        def _():
            out_own.start()

        @pl.when(owner != flat)
        def _():
            out_far.start()

        qkvs.arrive()
        keep, qkv_rows = scatter_rows(qkvs.total, q_near, qxsend, qxrecv, q_in)
        qkvs.each(keep)
        for c in qkv_rows:
            c.start()

        def landed(copies):
            copies[0].wait()
            for c in copies[1:]:
                c.wait_recv()

        landed(ffn_rows)
        for t in range(GROUP):
            for d in range(planes):
                column = columns_of(d, t, shards)
                for m, ref in enumerate((gate_out, up_out)):
                    lane = m * hidden + d * brows
                    for at in range(0, wrows, 32):
                        ref[at : at + 32, column * brows : (column + 1) * brows] = g_in[
                            t, at : at + 32, lane : lane + brows
                        ].astype(f32)
        landed(qkv_rows)
        for t in range(GROUP):
            home = place.head(t)
            query_out[:, home * qcols : (home + 1) * qcols] = q_in[t, :, :qcols].astype(f32)
            key_out[:, home * kcols : (home + 1) * kcols] = q_in[
                t, :, qcols : qcols + kcols
            ].astype(f32)
            value_out[:, home * kcols : (home + 1) * kcols] = q_in[
                t, :, qcols + kcols :
            ].astype(f32)

        @pl.when(owner == flat)
        def _():
            out_own.wait()

        @pl.when(owner != flat)
        def _():
            out_far.wait()

        o_out[...] = o_in[...].astype(f32)
        for c in lines:
            c.wait_recv()
        line_own.wait()
        s_out[...] = jnp.sum(s_line[...], axis=0)
        for c in lines + ffn_rows[1:] + qkv_rows[1:]:
            c.wait_send()
        for c in (ffn, down, qkvs, outs):
            c.drain()

    shape = jax.ShapeDtypeStruct
    vmem = pltpu.VMEM
    wide_rows = shards * wrows
    return pallas(
        body,
        [
            shape((rows, width), bf16),
            shape((rows, width), bf16),
            shape((wrows, hidden * GROUP), f32),
            shape((wrows, hidden * GROUP), f32),
            shape((wrows, qcols * GROUP), f32),
            shape((wrows, kcols * GROUP), f32),
            shape((wrows, kcols * GROUP), f32),
            shape((wrows, width), f32),
            shape((brows, width), f32),
            shape((srows, 128), f32),
        ],
        [VMEM] * 4 + [ANY] * (4 + len(inputs)),
        [VMEM] * 10,
        [vmem(i.shape, i.dtype) for i in inputs]
        + [
            vmem((rows, width), bf16),
            vmem((GROUP, rows, width), bf16),
            vmem((rows, width), f32),
            vmem((group_rows, qkv_cols), bf16),
            vmem((group_rows, 128), bf16),
            vmem((length, HEAD_SIZE), f32),
            vmem((length, HEAD_SIZE), f32),
            vmem((group_rows, qcols), bf16),
            vmem((srows, width), f32),
            vmem((GROUP, planes * srows, 128), f32),
            vmem((GROUP, planes * srows, 128), f32),
            vmem((planes, srows, 128), f32),
            vmem((planes, srows, 128), f32),
            vmem((3, streams, wide_rows, both), bf16),
            vmem((streams, wide_rows, both), bf16),
            vmem((streams, wide_rows, both), bf16),
            vmem((GROUP, wrows, both), bf16),
            vmem((3, brows, width), bf16),
            vmem((brows, width), bf16),
            vmem((brows, width), bf16),
            vmem((2, streams, 2, wide_rows, qkv_cols), bf16),
            vmem((3, streams, wide_rows, qkv_cols), bf16),
            vmem((streams, wide_rows, qkv_cols), bf16),
            vmem((streams, wide_rows, qkv_cols), bf16),
            vmem((GROUP, wrows, qkv_cols), bf16),
            vmem((2, 2, wrows, width), bf16),
            vmem((3, wrows, width), bf16),
            vmem((wrows, width), bf16),
            vmem((wrows, width), bf16),
            vmem((wrows, width), bf16),
        ]
        + scatter_scratch(rows, width)
        + [DMA((10,)), DMA((10,)), DMA((10,)), DMA((10,))]
        + gather_scratch()
        + [DMA((len(inputs),))]
        + [DMA((5,)), DMA((3,))] * 4
        + [DMA((GROUP,)), DMA((GROUP,)), DMA((GROUP,)), DMA((GROUP,)), DMA, DMA]
        + [DMA((GROUP,)), DMA((GROUP,)), DMA((planes,)), DMA((planes,)), DMA((2,))]
        + [pltpu.SemaphoreType.REGULAR],
        cid,
        180,
        62,
    )(gains, starts, cosine, sine, final, hidden_one, down_grad, ffn_grad, *inputs)


def settle(qkv_grad, out_grad, small, qcols, kcols, planes, direct, shards, cid):
    srows = small.shape[1] // planes
    cols = small.shape[2]
    wrows, width = out_grad.shape

    def body(
        q_ref, o_ref, s_ref, query_out, key_out, value_out, o_out, s_out, q_got, o_got, got, held,
        line, qsend, qrecv, osend, orecv, asend, arecv, bsend, brecv,
    ):
        place = Place(shards)
        tp, dp, flat = place.tp, place.dp(), place.flat()
        barrier = pltpu.get_barrier_semaphore()

        def signal(device):
            pl.semaphore_signal(
                barrier, inc=1, device_id=device, device_id_type=pl.DeviceIdType.MESH
            )

        for device in group_peers(place):
            signal(device)
        for k in range(1, planes):
            signal(place.dp_device((dp + k) % planes))
        if direct:
            owner = place.head(tp) * planes + dp
            high, y = lax.axis_index("zh"), lax.axis_index("y")
            source = {"st": lax.axis_index("st"), "seq": high * 2 + y}
            source.update(place.dp_device(lax.axis_index("seq")))

            @pl.when(owner != flat)
            def _():
                signal(source)

            pl.semaphore_wait(barrier, GROUP + planes - 2 + (owner != flat).astype(jnp.int32))
        else:
            pl.semaphore_wait(barrier, GROUP + planes - 2)

        sums = Exchange(place, s_ref, got, asend, arecv)
        sums.start()
        qkv = Exchange(place, q_ref, q_got, qsend, qrecv)
        qkv.start()
        if direct:
            out_own = pltpu.make_async_copy(o_ref, o_got, osend)
            out_far = remote(o_ref, o_got, osend, orecv, place.any_device(owner))

            @pl.when(owner == flat)
            def _():
                out_own.start()

            @pl.when(owner != flat)
            def _():
                out_far.start()

        sums.finish()
        held[...] = jnp.sum(got[...], axis=0).reshape(held.shape)
        line_own = pltpu.make_async_copy(held.at[dp], line.at[dp], bsend.at[0])
        line_own.start()
        lines = []
        for k in range(1, planes):
            to = (dp + k) % planes
            lines.append(
                remote(held.at[to], line.at[dp], bsend.at[k], brecv.at[k], place.dp_device(to))
            )
            lines[-1].start()
        qkv.finish()
        for t in range(GROUP):
            head = place.head(t)
            query_out[:, head * qcols : (head + 1) * qcols] = q_got[t, :, :qcols].astype(f32)
            key_out[:, head * kcols : (head + 1) * kcols] = q_got[
                t, :, qcols : qcols + kcols
            ].astype(f32)
            value_out[:, head * kcols : (head + 1) * kcols] = q_got[t, :, qcols + kcols :].astype(
                f32
            )
        if direct:

            @pl.when(owner == flat)
            def _():
                out_own.wait()

            @pl.when(owner != flat)
            def _():
                out_far.wait()

            o_out[...] = o_got[...].astype(f32)
        else:
            o_out[...] = o_ref[...].astype(f32)
        for c in lines:
            c.wait_recv()
        line_own.wait()
        s_out[...] = jnp.sum(line[...], axis=0)
        for c in lines:
            c.wait_send()

    return pallas(
        body,
        [
            jax.ShapeDtypeStruct((wrows, GROUP * qcols), f32),
            jax.ShapeDtypeStruct((wrows, GROUP * kcols), f32),
            jax.ShapeDtypeStruct((wrows, GROUP * kcols), f32),
            jax.ShapeDtypeStruct((wrows, width), f32),
            jax.ShapeDtypeStruct((srows, cols), f32),
        ],
        [VMEM, VMEM, VMEM],
        [VMEM] * 5,
        [
            pltpu.VMEM(qkv_grad.shape, bf16),
            pltpu.VMEM(out_grad.shape, bf16),
            pltpu.VMEM(small.shape, f32),
            pltpu.VMEM((planes, srows, cols), f32),
            pltpu.VMEM((planes, srows, cols), f32),
            DMA((GROUP,)), DMA((GROUP,)), DMA, DMA,
            DMA((GROUP,)), DMA((GROUP,)), DMA((planes,)), DMA((planes,)),
        ],
        cid,
        20,
    )(qkv_grad, out_grad, small)


def local(
    tokens, doc_starts, attn_gain, query_gain, key_gain, w_query, key_weight, value_weight,
    w_headgate, w_out, ffn_gain, w_gate, w_up, w_down, cotangent,
):
    zs, ys = lax.axis_size("zh"), lax.axis_size("y")
    planes = zs * ys
    direct = zs == 2 and ys == 2
    streams = lax.axis_size("st")
    shards = lax.axis_size("seq")
    devices = planes * GROUP
    rows, width = tokens.shape
    length = rows * shards
    group_rows = rows * GROUP
    wrows = w_query.shape[0]
    brows = w_down.shape[0]
    hidden = brows * planes
    qcols = w_query.shape[1] // GROUP
    kcols = key_weight.shape[1] // GROUP
    group_heads = qcols // HEAD_SIZE
    all_heads = w_headgate.shape[1]
    score_scale = HEAD_SIZE ** (-0.5)
    dp = lax.axis_index(DP)
    tp = lax.axis_index(TP)

    hg = wrows * all_heads
    gcols = query_gain.shape[0]
    at = hg + 2 * wrows
    count = at + 2 * gcols
    sums = -(-count // 1024) * 8
    docs = doc_starts.shape[1]
    qkv_cols = qcols + 2 * kcols
    starts_row = jnp.concatenate(
        [(doc_starts[0] // 128).astype(bf16), (doc_starts[0] % 128).astype(bf16)]
    )
    headgate_rows = jnp.pad(w_headgate, ((0, 0), (0, 128 - all_heads)))
    if direct:
        flat = lax.axis_index(ALL)
        gain_rows = width // 128
        grows = -(-(2 * gain_rows + 3) // 16) * 16
        row_of = lax.broadcasted_iota(jnp.int32, (grows, 128), 0)
        lane_of = lax.broadcasted_iota(jnp.int32, (grows, 128), 1)

        def placed(values, base):
            size = values.shape[0]
            where = (row_of - base) * 128 + lane_of - flat * size
            full = jnp.tile(values, 128 // size)[None]
            return jnp.where((where >= 0) & (where < size), full, 0)

        gain_block = (
            placed(attn_gain, 0) + placed(ffn_gain, gain_rows)
            + placed(query_gain, 2 * gain_rows) + placed(key_gain, 2 * gain_rows + 1)
            + jnp.where(
                row_of == 2 * gain_rows + 2, jnp.pad(starts_row, (0, 128 - 2 * docs))[None], 0
            )
        )
        small = jnp.concatenate([headgate_rows, gain_block])
        (
            cot_all, ffn_w, down_w, hidden_one, hidden_two, small, gains, qkv_w, out_w, qkv,
            low, gate_full, mixed, gated, middle, headgate, starts,
        ) = forward_pass(
            tokens, cotangent, small, w_out, w_query, key_weight, value_weight, w_gate, w_up,
            w_down, docs, shards, 0,
        )
        cot_all = cot_all.reshape(group_rows, width)
        hidden_two = hidden_two.reshape(group_rows, width)
        ffn_w = ffn_w.reshape(width, 2 * hidden)
        down_w = down_w.reshape(hidden, width)
        gate_up = mm(hidden_two, ffn_w)
        gate_pre, up_proj = gate_up[:, :hidden], gate_up[:, hidden:]
        gate_sig = jax.nn.sigmoid(gate_pre)
        inner_act = (gate_pre * gate_sig * up_proj).astype(bf16)
        down_grad = mm_t(inner_act, cot_all).astype(bf16)
        grad_inner = mm_b(cot_all, down_w)
        grad_gate = grad_inner * up_proj * gate_sig * (1.0 + gate_pre * (1.0 - gate_sig))
        grad_up = grad_inner * gate_pre * gate_sig
        grad_gu = jnp.concatenate([grad_gate.astype(bf16), grad_up.astype(bf16)], axis=1)
        ffn_grad = mm_t(hidden_two, grad_gu).astype(bf16)
        places = (GROUP, rows, width)
        (
            layer_out, tokens_grad, gate_grad, up_grad, query_grad, key_grad, value_grad,
            out_grad, down_grad, small_sum,
        ) = backward_pass(
            mm_b(grad_gu, ffn_w).astype(bf16).reshape(places),
            mm(inner_act, down_w).astype(bf16).reshape(places),
            middle, tokens, cotangent, gains, headgate,
            qkv_w.reshape(width, qkv_cols), out_w.reshape(qcols, width), hidden_one, qkv, low,
            gate_full, mixed, gated, starts, down_grad.reshape(zs, ys, brows, width),
            ffn_grad.reshape(zs, streams, ys, shards * wrows, 2 * hidden), docs, shards, 1,
        )
        half = lax.dynamic_slice_in_dim(small_sum, flat % 2 * wrows, wrows, 1)
        return (
            layer_out,
            tokens_grad,
            half[all_heads],
            lax.dynamic_slice_in_dim(small_sum[18], flat * gcols, gcols, 0),
            lax.dynamic_slice_in_dim(small_sum[19], flat * gcols, gcols, 0),
            query_grad,
            key_grad,
            value_grad,
            half[:all_heads].T,
            out_grad,
            half[all_heads + 1],
            gate_grad,
            up_grad,
            down_grad,
        )
    else:
        srows = -(-(wrows + 6) // 16) * 16
        others = [attn_gain, ffn_gain, query_gain, key_gain, starts_row[:docs], starts_row[docs:]]
        small = jnp.concatenate(
            [headgate_rows]
            + [jnp.pad(row, (0, 128 - row.shape[0]))[None] for row in others]
            + [jnp.zeros((srows - wrows - 6, 128), bf16)]
        )
        tokens_all, cot_all, small, qkv_w, ffn_own = front(
            tokens, cotangent, small, w_out, w_query, key_weight, value_weight, w_gate, w_up,
            w_down, planes, False, shards, 0,
        )
        tokens_all = tokens_all.reshape(group_rows, width)
        cot_all = cot_all.reshape(group_rows, width)
        qkv_w = over_dp(qkv_w[0])
        ffn_w = over_dp(ffn_own)
        down_w = lax.all_gather(w_down, DP, axis=0, tiled=True)
        out_w = lax.all_gather(w_out, ALL, axis=0, tiled=True)
        out_w = lax.dynamic_slice_in_dim(out_w, tp * qcols, qcols, 0)
        head = tp
        here = pick(small[::shards], 1, dp)
        starts = here[:, wrows + 4, :docs].astype(jnp.int32) * 128
        starts = starts + here[:, wrows + 5, :docs].astype(jnp.int32)
    small = small.reshape(streams, shards, zs, ys, srows, 128).transpose(2, 0, 3, 1, 4, 5)
    small = small.reshape(devices, srows, 128)
    headgate_all = small[:, :wrows, :all_heads].reshape(width, all_heads)
    if not direct:
        attn_gain_f = small[:, wrows, :wrows].reshape(1, -1).astype(f32)
        ffn_gain_f = small[:, wrows + 1, :wrows].reshape(1, -1).astype(f32)
        query_gain_f = small[:, wrows + 2, :gcols].reshape(-1).astype(f32)
        key_gain_f = small[:, wrows + 3, :gcols].reshape(-1).astype(f32)
    headgate_own = lax.dynamic_slice_in_dim(headgate_all, head * group_heads, group_heads, 1)

    if not direct:
        residual_all = tokens_all.astype(f32)
        hidden_all = (residual_all * rms_scale(residual_all) * attn_gain_f).astype(bf16)
        qkv = mm(hidden_all, qkv_w)
    query_raw = qkv[:, :qcols].reshape(group_rows, group_heads, HEAD_SIZE)
    key_raw = qkv[:, qcols : qcols + kcols].reshape(group_rows, 1, HEAD_SIZE)
    value = qkv[:, qcols + kcols :].astype(bf16).reshape(streams, length, HEAD_SIZE)
    positions = jnp.tile(jnp.arange(length, dtype=jnp.int32), streams)
    cosine, sine = rotary_tables(positions)
    query_scale = rms_scale(query_raw)
    query_normed = query_raw * query_scale
    query = rotate(query_normed * query_gain_f, cosine, sine).astype(bf16)
    query = query.reshape(streams, length, group_heads, HEAD_SIZE)
    key_scale = rms_scale(key_raw)
    key_normed = key_raw * key_scale
    key = rotate(key_normed * key_gain_f, cosine, sine).astype(bf16)
    key = key.reshape(streams, length, HEAD_SIZE)
    stream_pos = jnp.arange(length, dtype=jnp.int32)
    segment = jnp.sum((stream_pos[None, :, None] >= starts[:, None, :]).astype(jnp.int32), axis=2)
    allowed = (stream_pos[:, None] >= stream_pos[None, :])[None] & (
        segment[:, :, None] == segment[:, None, :]
    )
    scores = jnp.einsum("bqgd,bkd->bgqk", query, key, preferred_element_type=f32) * score_scale
    scores = jnp.where(allowed[:, None], scores, MASK_FILL)
    row_max = jnp.max(scores, axis=-1, keepdims=True)
    weights = jnp.exp(scores - row_max)
    probs = weights / jnp.sum(weights, axis=-1, keepdims=True)
    probs_low = probs.astype(bf16)
    if not direct:
        mixed = jnp.einsum(
            "bgqk,bkd->bqgd", probs_low, value, preferred_element_type=f32
        ).astype(bf16)
    mixed_f = mixed.astype(f32).reshape(group_rows, group_heads, HEAD_SIZE)
    if direct:
        head_gate = gate_full.reshape(group_rows, group_heads, HEAD_SIZE)[:, :, :1]
    else:
        head_gate = jax.nn.sigmoid(mm(hidden_all, headgate_own))[:, :, None]
        gated = (mixed_f * head_gate).astype(bf16).reshape(group_rows, qcols)

    def parts(x):
        return x.astype(bf16).reshape(GROUP, rows, width)

    if not direct:
        middle, hidden_two = middle_step(
            parts(mm(gated, out_w)), tokens, ffn_gain_f, None, shards, 2
        )
        hidden_two = hidden_two.reshape(group_rows, width)

    gate_up = mm(hidden_two, ffn_w)
    gate_pre, up_proj = gate_up[:, :hidden], gate_up[:, hidden:]
    gate_sig = jax.nn.sigmoid(gate_pre)
    inner_act = (gate_pre * gate_sig * up_proj).astype(bf16)
    down_grad = mm_t(inner_act, cot_all).astype(bf16).reshape(zs, ys, brows, width)
    if direct:
        down_sum = PlaceSum(down_grad)
        down_sum.over_y()
    else:
        down_grad = scatter_dp(down_grad)
    grad_inner = mm_b(cot_all, down_w)
    grad_gate = (grad_inner * up_proj * gate_sig * (1.0 + gate_pre * (1.0 - gate_sig))).astype(bf16)
    grad_up = (grad_inner * gate_pre * gate_sig).astype(bf16)
    grad_gu = jnp.concatenate([grad_gate, grad_up], axis=1)
    ffn_grad = mm_t(hidden_two, grad_gu).astype(bf16)
    grad_gu, ffn_grad = lax.optimization_barrier((grad_gu, ffn_grad))
    if not direct:
        ffn_grad = scatter_dp(by_place(ffn_grad))
    grad_middle, ffn_gain_part, grad_branch, *ffn_first = middle_back(
        parts(mm_b(grad_gu, ffn_w)), middle, cotangent, ffn_gain_f,
        ffn_grad.reshape(zs, streams, ys, -1, 2 * hidden) if direct else None, shards, 3,
    )
    if direct:
        grad_branch, down_sum.far, down_sum.near, ffn_first = lax.optimization_barrier(
            (grad_branch, down_sum.far, down_sum.near, ffn_first[0])
        )
        down_z = down_sum.over_z()
        ffn_sum = PlaceSum(by_place(ffn_grad))
        ffn_sum.take(ffn_first.reshape(-1, 2 * hidden), None)
        ffn_z = ffn_sum.over_z()
        ffn_sum.near = ffn_sum.over_y_near()
    grad_branch = grad_branch.reshape(group_rows, width)
    layer_out = scatter_sum(parts(mm(inner_act, down_w)), middle, shards, 4)

    out_grad = mm_t(gated, grad_branch).astype(bf16).reshape(zs, ys, wrows, width)
    grad_gated = mm_b(grad_branch, out_w).reshape(group_rows, group_heads, HEAD_SIZE)
    grad_mixed = (grad_gated * head_gate).astype(bf16).reshape(
        streams, length, group_heads, HEAD_SIZE
    )
    gate_flat = head_gate[:, :, 0]
    grad_logit = (
        jnp.sum(grad_gated * mixed_f, axis=-1) * gate_flat * (1.0 - gate_flat)
    ).astype(bf16)
    grad_probs = jnp.einsum("bqgd,bkd->bgqk", grad_mixed, value, preferred_element_type=f32)
    row_delta = jnp.sum(probs * grad_probs, axis=-1, keepdims=True)
    grad_scores = (probs * (grad_probs - row_delta)).astype(bf16)
    grad_query = (
        jnp.einsum("bgqk,bkd->bqgd", grad_scores, key, preferred_element_type=f32) * score_scale
    ).astype(bf16)
    grad_key = (
        jnp.einsum("bgqk,bqgd->bkd", grad_scores, query, preferred_element_type=f32) * score_scale
    ).astype(bf16)
    grad_value = jnp.einsum(
        "bgqk,bqgd->bkd", probs_low, grad_mixed, preferred_element_type=f32
    ).astype(bf16)
    gqn = rotate_back(
        grad_query.astype(f32).reshape(group_rows, group_heads, HEAD_SIZE), cosine, sine
    )
    query_gain_part = jnp.sum(gqn * query_normed, axis=(0, 1))
    grad_query_raw = norm_back(gqn * query_gain_f, query_normed, query_scale).astype(bf16)
    gkn = rotate_back(grad_key.astype(f32).reshape(group_rows, 1, HEAD_SIZE), cosine, sine)
    key_gain_part = jnp.sum(gkn * key_normed, axis=(0, 1))
    grad_key_raw = norm_back(gkn * key_gain_f, key_normed, key_scale).astype(bf16)
    grad_qkv = jnp.concatenate(
        [
            grad_query_raw.reshape(group_rows, qcols),
            grad_key_raw.reshape(group_rows, kcols),
            grad_value.reshape(group_rows, kcols),
        ],
        axis=1,
    )
    qkv_grad = mm_t(hidden_all, grad_qkv).astype(bf16)
    if direct:
        qkv_grad, out_grad, grad_qkv, down_z = lax.optimization_barrier(
            (qkv_grad, out_grad, grad_qkv, down_z)
        )
        down_grad = down_sum.total(down_z)
        qkv_sum, out_sum = PlaceSum(by_place(qkv_grad)), PlaceSum(out_grad)
        qkv_sum.over_y()
        out_sum.over_y()
        qkv_z, out_z = qkv_sum.over_z(), out_sum.over_z()
        ffn_grad = ffn_sum.total(ffn_z)
        qkv_grad, out_grad = qkv_sum.total(qkv_z), out_sum.total(out_z)
    else:
        qkv_grad = scatter_dp(by_place(qkv_grad))
        out_grad = lax.dynamic_update_slice(
            jnp.zeros((width, width), bf16), out_grad.reshape(qcols, width), (tp * qcols, 0)
        )
        out_grad = lax.psum_scatter(out_grad, ALL, scatter_dimension=0, tiled=True)
    tokens_grad, attn_gain_part = tokens_back(
        parts(mm_b(grad_qkv, qkv_w) + mm_b(grad_logit, headgate_own)),
        tokens, grad_middle, attn_gain_f, shards, 5,
    )
    headgate_part = mm_t(hidden_all, grad_logit)
    headgate_part = lax.dynamic_update_slice(
        jnp.zeros((width, all_heads), f32), headgate_part, (0, head * group_heads)
    )

    small_sum = jnp.concatenate(
        [
            headgate_part.reshape(devices, hg),
            attn_gain_part.reshape(devices, wrows),
            ffn_gain_part.reshape(devices, wrows),
            query_gain_part.reshape(devices, gcols),
            key_gain_part.reshape(devices, gcols),
        ],
        axis=1,
    )
    small_sum = jnp.pad(small_sum, ((0, 0), (0, sums * 128 - count)))
    small_sum = small_sum.reshape(zs, streams, ys, shards, sums, 128)
    small_sum = small_sum.transpose(1, 3, 0, 2, 4, 5)
    small_sum = small_sum.reshape(GROUP, planes * sums, 128)

    gate_grad, up_grad = exchange_back(
        ffn_grad.reshape(GROUP, wrows, 2 * hidden), planes, shards, 6
    )
    query_grad, key_grad, value_grad, out_grad, small_sum = settle(
        qkv_grad.reshape(GROUP, wrows, qkv_cols), out_grad, small_sum, qcols, kcols, planes,
        direct, shards, 7,
    )
    small_sum = small_sum.reshape(-1)
    return (
        layer_out,
        tokens_grad,
        small_sum[hg : hg + wrows],
        small_sum[at : at + gcols],
        small_sum[at + gcols : at + 2 * gcols],
        query_grad,
        key_grad,
        value_grad,
        small_sum[:hg].reshape(wrows, all_heads),
        out_grad,
        small_sum[hg + wrows : hg + 2 * wrows],
        gate_grad,
        up_grad,
        down_grad.astype(f32),
    )


def solution(mesh):
    shards = mesh.shape["seq"]
    planes = (2, 2, 2) if shards == 4 and mesh.size == 32 else (1, GROUP // shards, -1)
    grouped = Mesh(mesh.devices.reshape(planes + (shards,)), ALL)
    two = P(ALL, None)
    one = P(ALL)
    return jax.shard_map(
        local,
        mesh=grouped,
        in_specs=(
            two, P(("zh", "st", "y"), None), one, one, one, two, two, two, two, two, one, two, two,
            two, two,
        ),
        out_specs=(two, two, one, one, one, two, two, two, two, two, one, two, two, two),
        check_vma=False,
    )
```

```python
import jax
import jax.numpy as jnp
import numpy as np
from jax import lax
from jax.experimental import pallas as pl
from jax.experimental.pallas import tpu as pltpu
from jax.sharding import Mesh, PartitionSpec as P

QUERY_HEADS = 16
KEY_VALUE_HEADS = 8
HEAD_SIZE = 128
GROUP = 8
NORM_EPS = 1e-06
ROPE_BASE = 1000000.0
MASK_FILL = -1e30

DP = ("zh", "y")
TP = ("st", "seq")
ALL = ("zh", "st", "y", "seq")
f32 = jnp.float32
bf16 = jnp.bfloat16


def rms_scale(vector):
    return lax.rsqrt(jnp.mean(vector * vector, axis=-1, keepdims=True) + NORM_EPS)


def rotary_tables(positions):
    half_width = HEAD_SIZE // 2
    exponent = jnp.arange(half_width, dtype=jnp.int32).astype(f32) * (2.0 / HEAD_SIZE)
    inverse = jnp.power(ROPE_BASE, -exponent)
    angles = positions.astype(f32)[:, None] * inverse[None, :]
    return (jnp.cos(angles)[:, None, :], jnp.sin(angles)[:, None, :])


def rotate(vector, cosine, sine):
    a, b = jnp.split(vector, 2, axis=-1)
    return jnp.concatenate([a * cosine - b * sine, b * cosine + a * sine], axis=-1)


def rotate_back(vector, cosine, sine):
    a, b = jnp.split(vector, 2, axis=-1)
    return jnp.concatenate([a * cosine + b * sine, b * cosine - a * sine], axis=-1)


def norm_back(grad, normed, scale):
    return scale * (grad - normed * jnp.mean(grad * normed, axis=-1, keepdims=True))


def mm(left, right):
    return jnp.dot(left, right, preferred_element_type=f32)


def mm_t(left, right):
    return lax.dot_general(left, right, (((0,), (0,)), ((), ())), preferred_element_type=f32)


def mm_b(left, right):
    return lax.dot_general(left, right, (((1,), (1,)), ((), ())), preferred_element_type=f32)


SWAP = [(0, 1), (1, 0)]


def over_dp(x):
    streams, shards = lax.axis_size("st"), lax.axis_size("seq")
    zs, ys = lax.axis_size("zh"), lax.axis_size("y")
    rows, columns = x.shape[1] * shards, x.shape[2]
    whole = lax.all_gather(x, DP, axis=0, tiled=False)
    whole = whole.reshape(zs, ys, streams, rows, columns).transpose(0, 2, 1, 3, 4)
    return whole.reshape(-1, columns)


def pick(x, axis, index):
    return lax.dynamic_index_in_dim(x, index, axis, keepdims=False)


def plus(left, right):
    return left.astype(f32) + right.astype(f32)


class PlaceSum:
    def __init__(self, x):
        self.x = x
        self.z, self.y = lax.axis_index("zh"), lax.axis_index("y")

    def piece(self, zp, yp):
        return pick(pick(self.x, 0, zp), 0, yp)

    def over_y(self):
        got = lax.ppermute(pick(self.x, 1, 1 - self.y), "y", SWAP)
        self.take(pick(got, 0, 1 - self.z), pick(got, 0, self.z))

    def over_y_near(self):
        return lax.ppermute(self.piece(self.z, 1 - self.y), "y", SWAP)

    def take(self, far, near):
        self.far, self.near = far, near

    def over_z(self):
        far = plus(self.piece(1 - self.z, self.y), self.far).astype(bf16)
        return lax.ppermute(far, "zh", SWAP)

    def total(self, got):
        return (plus(self.piece(self.z, self.y), self.near) + got.astype(f32)).astype(bf16)


def scatter_dp(x):
    zs, ys = x.shape[:2]
    return lax.psum_scatter(
        x.reshape((zs * ys,) + x.shape[2:]), DP, scatter_dimension=0, tiled=False
    )


def by_place(x):
    streams = lax.axis_size("st")
    zs, ys = lax.axis_size("zh"), lax.axis_size("y")
    columns = x.shape[1]
    x = x.reshape(zs, streams, ys, -1, columns).transpose(0, 2, 1, 3, 4)
    return x.reshape(zs, ys, -1, columns)


def pallas(body, out_shape, in_specs, out_specs, scratch, cid, micros, mib=40):
    return pl.pallas_call(
        body,
        out_shape=out_shape,
        in_specs=in_specs,
        out_specs=out_specs,
        scratch_shapes=scratch,
        compiler_params=pltpu.CompilerParams(
            collective_id=cid, has_side_effects=True, vmem_limit_bytes=mib * 1024 * 1024
        ),
        cost_estimate=pl.CostEstimate(
            flops=0, bytes_accessed=int(micros * 3.6e5), transcendentals=0
        ),
    )


ANY = pl.BlockSpec(memory_space=pl.ANY)
VMEM = pl.BlockSpec(memory_space=pltpu.VMEM)
DMA = pltpu.SemaphoreType.DMA


def remote(src, dst, send, recv, device):
    return pltpu.make_async_remote_copy(
        src_ref=src,
        dst_ref=dst,
        send_sem=send,
        recv_sem=recv,
        device_id=device,
        device_id_type=pl.DeviceIdType.MESH,
    )


class Place:
    def __init__(self, shards):
        self.shards = shards
        self.tp = lax.axis_index("st") * shards + lax.axis_index("seq")
        self.core = self.tp % 2
        self.ring = self.turn(self.tp // 2)

    def turn(self, place):
        if self.shards == GROUP:
            return place
        return place + (place // 2) * (1 - 2 * (place % 2))

    def head(self, index):
        if self.shards == GROUP:
            return index
        return index // 4 * 2 + index % 4 // 2 * 4 + index % 2

    def block(self, ahead, other=False):
        ring = self.ring
        if ahead == 1:
            ring = ring + 1 - 2 * (ring % 2)
        elif ahead == 3:
            ring = 3 - ring
        elif ahead == 2:
            ring = (ring + 2) % 4
        core = 1 - self.core if other else self.core
        return self.turn(ring) * 2 + core

    def device(self, index):
        return {"st": index // self.shards, "seq": index % self.shards}

    def dp_device(self, dp):
        ys = lax.axis_size("y")
        return {"zh": dp // ys, "y": dp % ys}

    def any_device(self, flat):
        ys, streams = lax.axis_size("y"), lax.axis_size("st")
        return {
            "zh": flat // (streams * ys * self.shards),
            "st": flat // (ys * self.shards) % streams,
            "y": flat // self.shards % ys,
            "seq": flat % self.shards,
        }

    def flat(self):
        ys, streams = lax.axis_size("y"), lax.axis_size("st")
        z, y = lax.axis_index("zh"), lax.axis_index("y")
        st, seq = lax.axis_index("st"), lax.axis_index("seq")
        return ((z * streams + st) * ys + y) * self.shards + seq

    def dp(self):
        return lax.axis_index("zh") * lax.axis_size("y") + lax.axis_index("y")

    def right(self):
        return self.device(self.block(1))

    def left(self):
        return self.device(self.block(3))

    def across(self):
        return {"y": 1 - lax.axis_index("y")}

    def partner(self):
        return self.device(self.block(0, True))


def greet(devices):
    barrier = pltpu.get_barrier_semaphore()
    for device in devices:
        pl.semaphore_signal(
            barrier, inc=1, device_id=device, device_id_type=pl.DeviceIdType.MESH
        )
    pl.semaphore_wait(barrier, len(devices))


class RingGather:
    SEMS = 11

    def __init__(self, place, own, out, send, recv, one_way=False):
        rows = out.shape[1]
        half = rows // 2
        first, second = pl.ds(0, half), pl.ds(half, half)
        me, near, next_, opposite = (place.block(i) for i in (0, 1, 3, 2))
        to_near, to_next, to_partner = place.device(near), place.device(next_), place.partner()

        def copy(index, src, block, part, device):
            return remote(src, out.at[block, part], send.at[index], recv.at[index], device)

        self.local = pltpu.make_async_copy(own, out.at[me], send.at[self.SEMS])
        self.next = [
            copy(0, own.at[first], me, first, to_next),
            copy(1, own.at[second], me, second, to_next),
        ]
        self.near = [
            copy(2, own.at[first], me, first, to_near),
            copy(3, own.at[second], me, second, to_near),
        ]
        self.mate = remote(own, out.at[me], send.at[4], recv.at[4], to_partner)
        self.on = [copy(5, out.at[next_, first], next_, first, to_near)]
        if one_way:
            self.on.append(copy(6, out.at[next_, second], next_, second, to_near))
        else:
            self.on.append(copy(6, out.at[near, second], near, second, to_next))
        self.one_way = one_way
        self.across = [
            remote(out.at[next_], out.at[next_], send.at[7], recv.at[7], to_partner),
            remote(out.at[near], out.at[near], send.at[8], recv.at[8], to_partner),
            copy(9, out.at[opposite, first], opposite, first, to_partner),
            copy(10, out.at[opposite, second], opposite, second, to_partner),
        ]

    def start(self):
        self.next[0].start()
        self.near[0 if self.one_way else 1].start()
        self.next[1].start()
        self.near[1 if self.one_way else 0].start()
        self.mate.start()
        self.local.start()

    def pass_on(self):
        self.next[0].wait_recv()
        self.on[0].start()
        if self.one_way:
            self.next[1].wait_recv()
        else:
            self.near[1].wait_recv()
        self.on[1].start()

    def step_across(self):
        if not self.one_way:
            self.next[1].wait_recv()
        self.across[0].start()
        self.near[0].wait_recv()
        if self.one_way:
            self.near[1].wait_recv()
        self.across[1].start()

    def step_far(self):
        self.on[0].wait_recv()
        self.across[2].start()
        self.on[1].wait_recv()
        self.across[3].start()

    def finish(self):
        self.mate.wait_recv()
        for c in self.across:
            c.wait_recv()
        for c in self.next + self.near + [self.mate] + self.on + self.across:
            c.wait_send()
        self.local.wait()

    def run(self):
        self.start()
        self.pass_on()
        self.step_across()
        self.step_far()
        self.finish()


def ring_scatter(place, x, pair, out, near, far, send, recv, emit, between=()):
    between = list(between) + [lambda: None] * 3
    rows = x.shape[1]
    half = rows // 2
    step = 32
    to_left, to_right, to_partner = place.left(), place.right(), place.partner()
    swaps = {}
    for q in (2, 1, 3, 0):
        swaps[q] = remote(
            x.at[place.block(q, True)], pair.at[q], send.at[q], recv.at[q], to_partner
        )
        swaps[q].start()

    def add(q, low, high, extra=None):
        block = place.block(q)
        for at in range(low, high, step):
            part = pl.ds(at, step)
            total = x[block, part].astype(f32) + pair[q, part].astype(f32)
            if extra is not None:
                total = total + far[extra, pl.ds(at - low, step)].astype(f32)
            out[q - 1, part] = total.astype(bf16)

    first, second = pl.ds(0, half), pl.ds(half, half)

    def send_to(index, q, part, dst, device):
        c = remote(out.at[q - 1, part], dst, send.at[index], recv.at[index], device)
        c.start()
        return c

    swaps[2].wait_recv()
    add(2, 0, half)
    a = send_to(4, 2, first, far.at[0], to_right)
    add(2, half, rows)
    b = send_to(5, 2, second, far.at[1], to_left)
    swaps[1].wait_recv()
    add(1, 0, half)
    c = send_to(6, 1, first, near.at[0, first], to_right)
    swaps[3].wait_recv()
    add(3, half, rows)
    d = send_to(7, 3, second, near.at[1, second], to_left)
    between[0]()
    a.wait_recv()
    add(3, 0, half, 0)
    e = send_to(8, 3, first, near.at[1, first], to_left)
    b.wait_recv()
    add(1, half, rows, 1)
    g = send_to(9, 1, second, near.at[0, second], to_right)
    between[1]()
    swaps[0].wait_recv()
    own = place.block(0)
    c.wait_recv()
    d.wait_recv()
    e.wait_recv()
    g.wait_recv()
    for at in range(0, rows, step):
        part = pl.ds(at, step)
        emit(
            part,
            (x[own, part].astype(f32) + pair[0, part].astype(f32))
            + (near[0, part].astype(f32) + near[1, part].astype(f32)),
        )
    for copy in list(swaps.values()) + [a, b, c, d, e, g]:
        copy.wait_send()


def scatter_scratch(rows, width):
    return [
        pltpu.VMEM((4, rows, width), bf16),
        pltpu.VMEM((3, rows, width), bf16),
        pltpu.VMEM((2, rows, width), bf16),
        pltpu.VMEM((2, rows // 2, width), bf16),
        DMA((10,)),
        DMA((10,)),
    ]


def gather_scratch():
    return [DMA((RingGather.SEMS + 1,)), DMA((RingGather.SEMS,))]


def scatter_sum(x, base, shards, cid):
    _, rows, width = x.shape

    def body(x_ref, base_ref, out_ref, pair, out, near, far, send, recv):
        place = Place(shards)
        greet([place.right(), place.left(), place.partner()])

        def emit(part, total):
            out_ref[part] = (base_ref[part] + total).astype(bf16)

        ring_scatter(place, x_ref, pair, out, near, far, send, recv, emit)

    return pallas(
        body, jax.ShapeDtypeStruct((rows, width), bf16), [VMEM, VMEM], VMEM,
        scatter_scratch(rows, width), cid, 25,
    )(x, base)


def middle_step(x, tokens, gain, carry, shards, cid):
    _, rows, width = x.shape
    carries = [] if carry is None else [carry]

    def body(x_ref, tok_ref, gain_ref, *refs):
        refs = list(refs)
        carry_ref = refs.pop(0) if carries else None
        mid_ref, all_ref = refs.pop(0), refs.pop(0)
        carry_out = refs.pop(0) if carries else None
        held, pair, out, near, far, send, recv, gsend, grecv, ysend, yrecv = refs
        place = Place(shards)
        greet(
            [place.right(), place.left(), place.partner()]
            + ([place.across()] if carries else [])
        )
        if carries:
            over = remote(carry_ref, carry_out, ysend, yrecv, place.across())
            over.start()

        def emit(part, total):
            middle = tok_ref[part].astype(f32) + total
            mid_ref[part] = middle
            held[part] = (middle * rms_scale(middle) * gain_ref[...]).astype(bf16)

        ring_scatter(place, x_ref, pair, out, near, far, send, recv, emit)
        RingGather(place, held, all_ref, gsend, grecv).run()
        if carries:
            over.wait()

    return pallas(
        body,
        [
            jax.ShapeDtypeStruct((rows, width), f32),
            jax.ShapeDtypeStruct((GROUP, rows, width), bf16),
        ]
        + [jax.ShapeDtypeStruct(c.shape, c.dtype) for c in carries],
        [VMEM, VMEM, VMEM] + [ANY] * len(carries),
        [VMEM, ANY] + [ANY] * len(carries),
        [pltpu.VMEM((rows, width), bf16)] + scatter_scratch(rows, width) + gather_scratch()
        + [DMA, DMA],
        cid,
        50,
    )(x, tokens, gain, *carries)


def middle_back(x, middle, cotangent, gain, grads, shards, cid):
    _, rows, width = x.shape
    carries = [] if grads is None else [grads]

    def body(x_ref, mid_ref, cot_ref, gain_ref, *refs):
        refs = list(refs)
        grads_ref = refs.pop(0) if carries else None
        dm_ref, part_ref, all_ref = refs.pop(0), refs.pop(0), refs.pop(0)
        grads_out = refs.pop(0) if carries else None
        held, pair, out, near, far, send, recv, gsend, grecv, ysend, yrecv = refs
        place = Place(shards)
        greet(
            [place.right(), place.left(), place.partner()]
            + ([place.across()] if carries else [])
        )
        if carries:
            z, y = lax.axis_index("zh"), lax.axis_index("y")
            over = [
                remote(
                    grads_ref.at[1 - z, st, 1 - y], grads_out.at[st], ysend.at[st],
                    yrecv.at[st], place.across(),
                )
                for st in range(grads.shape[1])
            ]
            for c in over:
                c.start()
        part_ref[...] = jnp.zeros_like(part_ref)

        def emit(part, total):
            middle = mid_ref[part]
            scale = rms_scale(middle)
            normed = middle * scale
            part_ref[...] += jnp.sum(total * normed, axis=0, keepdims=True)
            dm = cot_ref[part].astype(f32) + norm_back(total * gain_ref[...], normed, scale)
            dm_ref[part] = dm
            held[part] = dm.astype(bf16)

        ring_scatter(place, x_ref, pair, out, near, far, send, recv, emit)
        RingGather(place, held, all_ref, gsend, grecv).run()
        if carries:
            for c in over:
                c.wait()

    return pallas(
        body,
        [
            jax.ShapeDtypeStruct((rows, width), f32),
            jax.ShapeDtypeStruct((1, width), f32),
            jax.ShapeDtypeStruct((GROUP, rows, width), bf16),
        ]
        + [jax.ShapeDtypeStruct((c.shape[1],) + c.shape[3:], c.dtype) for c in carries],
        [VMEM, VMEM, VMEM, VMEM] + [ANY] * len(carries),
        [VMEM, VMEM, ANY] + [ANY] * len(carries),
        [pltpu.VMEM((rows, width), bf16)] + scatter_scratch(rows, width) + gather_scratch()
        + [DMA((2,)), DMA((2,))],
        cid,
        50,
    )(x, middle, cotangent, gain, *carries)


def tokens_back(x, tokens, dm, gain, shards, cid):
    _, rows, width = x.shape

    def body(
        x_ref, tok_ref, dm_ref, gain_ref, grad_ref, part_ref, pair, out, near, far, send, recv
    ):
        place = Place(shards)
        greet([place.right(), place.left(), place.partner()])
        part_ref[...] = jnp.zeros_like(part_ref)

        def emit(part, total):
            tok = tok_ref[part].astype(f32)
            scale = rms_scale(tok)
            normed = tok * scale
            part_ref[...] += jnp.sum(total * normed, axis=0, keepdims=True)
            grad_ref[part] = (
                dm_ref[part] + norm_back(total * gain_ref[...], normed, scale)
            ).astype(bf16)

        ring_scatter(place, x_ref, pair, out, near, far, send, recv, emit)

    return pallas(
        body,
        (
            jax.ShapeDtypeStruct((rows, width), bf16),
            jax.ShapeDtypeStruct((1, width), f32),
        ),
        [VMEM, VMEM, VMEM, VMEM],
        (VMEM, VMEM),
        scatter_scratch(rows, width),
        cid,
        25,
    )(x, tokens, dm, gain)


class Exchange:
    SEMS = GROUP

    def __init__(self, place, x, out, send, recv):
        self.local = pltpu.make_async_copy(x.at[place.tp], out.at[place.tp], send.at[0])
        self.copies = []
        for k in range(1, GROUP):
            peer = (place.tp + k) % GROUP
            self.copies.append(
                remote(x.at[peer], out.at[place.tp], send.at[k], recv.at[k], place.device(peer))
            )

    def start(self):
        for c in self.copies:
            c.start()
        self.local.start()

    def finish(self):
        for c in self.copies:
            c.wait_recv()
        for c in self.copies:
            c.wait_send()
        self.local.wait()


def group_peers(place):
    return [place.device((place.tp + k) % GROUP) for k in range(1, GROUP)]


def columns_of(dp, t, shards):
    ys, streams = lax.axis_size("y"), lax.axis_size("st")
    z, y = dp // ys, dp % ys
    return ((z * streams + t // shards) * ys + y) * shards + t % shards


def exchange_back(x, planes, shards, cid):
    _, wrows, both = x.shape
    hidden = both // 2
    brows = hidden // planes
    step = min(wrows, 32)

    def body(x_ref, gate_ref, up_ref, got, send, recv):
        place = Place(shards)
        greet(group_peers(place))
        run = Exchange(place, x_ref, got, send, recv)
        run.start()
        run.finish()
        for t in range(GROUP):
            for dp in range(planes):
                flat = columns_of(dp, t, shards)
                for m, out in enumerate((gate_ref, up_ref)):
                    for at in range(0, wrows, step):
                        part = pl.ds(at, step)
                        out[part, flat * brows : (flat + 1) * brows] = got[
                            t, part, m * hidden + dp * brows : m * hidden + (dp + 1) * brows
                        ].astype(f32)

    shape = jax.ShapeDtypeStruct((wrows, hidden * GROUP), f32)
    return pallas(
        body, (shape, shape), [VMEM], (VMEM, VMEM),
        [pltpu.VMEM(x.shape, bf16), DMA((GROUP,)), DMA((GROUP,))], cid, 25,
    )(x)


class PlaceGather:
    SEMS = 5

    def __init__(self, own, out, send, recv, halves):
        z, y = lax.axis_index("zh"), lax.axis_index("y")
        dp, across = z * 2 + y, (1 - z) * 2 + y
        to_z, to_y = {"zh": 1 - z}, {"y": 1 - y}

        def copy(index, src, slot, part, device):
            return remote(
                src.at[part], out.at[slot, part], send.at[index], recv.at[index], device
            )

        first, second = halves
        self.local = pltpu.make_async_copy(own, out.at[dp], send.at[send.shape[0] - 1])
        self.z = [copy(0, own, dp, first, to_z), copy(1, own, dp, second, to_z)]
        self.y = [
            remote(own, out.at[dp], send.at[2], recv.at[2], to_y),
            copy(3, out.at[across], across, first, to_y),
            copy(4, out.at[across], across, second, to_y),
        ]

    def forward(self, half):
        self.z[half].wait_recv()
        self.y[1 + half].start()

    def finish(self):
        for c in self.y:
            c.wait_recv()
        for c in self.z + self.y:
            c.wait_send()


def front(tokens, cotangent, small, w_out, w_query, key_weight, value_weight, w_gate, w_up,
          w_down, planes, direct, shards, cid):
    rows, width = tokens.shape
    wrows = w_out.shape[0]
    srows, scols = small.shape
    brows = w_down.shape[0]
    hidden = brows * planes
    parts = [w_query.shape[1] // GROUP, key_weight.shape[1] // GROUP, value_weight.shape[1] // GROUP]
    qkv = sum(parts)
    slots = planes if direct else 1
    inputs = [tokens, cotangent, w_query, key_weight, value_weight, w_gate, w_up]
    if direct:
        inputs += [w_down, w_out]

    def body(*refs):
        refs = list(refs)

        def take(count):
            taken = refs[:count]
            del refs[:count]
            return taken

        small_ref, = take(1)
        sources = take(len(inputs))
        tok_all, cot_all, small_all, attn_all, ffn_all = take(5)
        down_all, wout_all = take(2) if direct else (None, None)
        held = take(len(inputs))
        (pack, isem, tsend, trecv, csend, crecv, ssend, srecv, psend, precv, fsend, frecv, asend,
         arecv, aasend, aarecv, dsend, drecv, wsend, wrecv) = refs
        place = Place(shards)
        tp, dp, flat = place.tp, place.dp(), place.flat()

        loads = [
            pltpu.make_async_copy(s, h, isem.at[i]) for i, (s, h) in enumerate(zip(sources, held))
        ]
        for i in (2, 3, 4, 0, 5, 6) + ((7, 8) if direct else ()) + (1,):
            loads[i].start()
        tok_ref, cot_ref, wq_ref, wk_ref, wv_ref, wg_ref, wu_ref = held[:7]

        barrier = pltpu.get_barrier_semaphore()

        def signal(device):
            pl.semaphore_signal(
                barrier, inc=1, device_id=device, device_id_type=pl.DeviceIdType.MESH
            )

        for device in group_peers(place):
            signal(device)
        for k in range(1, planes):
            signal(place.dp_device((dp + k) % planes))
        if direct:
            high, low = lax.axis_index("zh"), lax.axis_index("st")
            y, seq = lax.axis_index("y"), lax.axis_index("seq")
            to_seq = high * 2 + y
            from_high, from_y = seq // 2, seq % 2
            selfish = seq == to_seq
            mine = y == from_y
            for j in range(4):

                @pl.when(jnp.logical_and(mine, (from_high * 4 + j) != (high * 4 + seq)))
                def _():
                    signal({"zh": from_high, "seq": jnp.int32(j)})

            pl.semaphore_wait(
                barrier, GROUP - 1 + planes - 1 + 2 - selfish.astype(jnp.int32)
            )
        else:
            pl.semaphore_wait(barrier, GROUP - 1 + planes - 1)

        here = dp if direct else 0
        attn = []
        at = 0
        for i, (ref, cols) in enumerate(zip((wq_ref, wk_ref, wv_ref), parts)):
            loads[2 + i].wait()
            for k in range(GROUP):
                peer = (tp + k) % GROUP
                column = place.head(peer) * cols
                src = ref.at[:, pl.ds(pl.multiple_of(column, cols), cols)]
                dst = attn_all.at[here, tp, :, pl.ds(at, cols)]
                sem = i * GROUP + k
                if k == 0:
                    attn.append(pltpu.make_async_copy(src, dst, asend.at[sem]))
                else:
                    attn.append(
                        remote(src, dst, asend.at[sem], arecv.at[sem], place.device(peer))
                    )
                attn[-1].start()
            at += cols

        small_own = pltpu.make_async_copy(small_ref, small_all.at[tp, dp], ssend.at[0])
        small_own.start()
        small_dp = []
        for k in range(1, planes):
            small_dp.append(
                remote(
                    small_ref, small_all.at[tp, dp], ssend.at[k], srecv.at[k],
                    place.dp_device((dp + k) % planes),
                )
            )
            small_dp[-1].start()

        if direct:
            down_ref, wout_ref = held[7:]
            loads[7].wait()
            half = brows // 2
            down_dp = PlaceGather(
                down_ref, down_all, dsend, drecv, (pl.ds(0, half), pl.ds(half, half))
            )
            down_dp.z[0].start()
        loads[0].wait()
        tok = RingGather(place, tok_ref, tok_all, tsend, trecv, direct)
        tok.start()

        loads[5].wait()
        loads[6].wait()
        for t in range(GROUP):
            for d in range(planes):
                column = columns_of(d, t, shards)
                for m, ref in enumerate((wg_ref, wu_ref)):
                    lane = m * hidden + d * brows
                    pack[t, :, lane : lane + brows] = ref[:, column * brows : (column + 1) * brows]
        ffn = Exchange(place, pack, ffn_all, fsend, frecv)
        ffn.start()

        if direct:
            down_dp.y[0].start()
            down_dp.local.start()
            loads[8].wait()
            wout_copies = [
                remote(
                    wout_ref, wout_all.at[seq], wsend.at[k], wrecv.at[seq],
                    {"zh": z, "seq": to_seq},
                )
                for k, z in enumerate((high, 1 - high))
            ]
            wout_own = pltpu.make_async_copy(wout_ref, wout_all.at[seq], wsend.at[0])
            wout_over = remote(
                wout_all, wout_all, wsend.at[2], wrecv.at[4], place.across()
            )

            @pl.when(selfish)
            def _():
                wout_own.start()

            @pl.when(jnp.logical_not(selfish))
            def _():
                wout_copies[0].start()

            wout_copies[1].start()

        for i in range(3 * GROUP):
            if i % GROUP == 0:
                attn[i].wait()
            else:
                attn[i].wait_recv()
        if direct:
            half = GROUP // 2
            attn_dp = PlaceGather(
                attn_all.at[dp], attn_all, aasend, aarecv, (pl.ds(0, half), pl.ds(half, half))
            )
            attn_dp.z[0].start()
            attn_dp.y[0].start()
            attn_dp.z[1].start()
            down_dp.z[1].start()

        small_own.wait()
        for c in small_dp:
            c.wait_recv()
        small_tp = []
        for k in range(1, GROUP):
            small_tp.append(
                remote(
                    small_all.at[tp], small_all.at[tp], psend.at[k], precv.at[k],
                    place.device((tp + k) % GROUP),
                )
            )
            small_tp[-1].start()

        loads[1].wait()
        cot = RingGather(place, cot_ref, cot_all, csend, crecv, direct)
        tok.pass_on()
        cot.start()
        tok.step_across()
        if direct:
            down_dp.forward(0)

            @pl.when(mine)
            def _():
                for j in range(4):

                    @pl.when((from_high * 4 + j) != (high * 4 + seq))
                    def _():
                        remote(
                            wout_ref, wout_all.at[j], wsend.at[0], wrecv.at[j], place.across()
                        ).wait_recv()

                @pl.when(selfish)
                def _():
                    wout_own.wait()

                wout_over.start()

            attn_dp.forward(0)
        tok.step_far()
        cot.pass_on()
        if direct:
            attn_dp.forward(1)
        cot.step_across()
        if direct:
            down_dp.forward(1)
        cot.step_far()
        tok.finish()
        cot.finish()
        ffn.finish()
        for i in range(3 * GROUP):
            if i % GROUP:
                attn[i].wait_send()
        for c in small_tp:
            c.wait_recv()
        for c in small_dp + small_tp:
            c.wait_send()
        if direct:
            attn_dp.finish()
            down_dp.finish()
            down_dp.local.wait()

            @pl.when(jnp.logical_not(selfish))
            def _():
                wout_copies[0].wait_send()

            wout_copies[1].wait_send()

            @pl.when(mine)
            def _():
                wout_over.wait_send()

            @pl.when(jnp.logical_not(mine))
            def _():
                wout_over.wait_recv()

    shapes = [
        jax.ShapeDtypeStruct((GROUP, rows, width), bf16),
        jax.ShapeDtypeStruct((GROUP, rows, width), bf16),
        jax.ShapeDtypeStruct((GROUP, planes, srows, scols), bf16),
        jax.ShapeDtypeStruct((slots, GROUP, wrows, qkv), bf16),
        jax.ShapeDtypeStruct((GROUP, wrows, 2 * hidden), bf16),
    ]
    if direct:
        shapes += [
            jax.ShapeDtypeStruct((planes, brows, width), bf16),
            jax.ShapeDtypeStruct((planes, wrows, width), bf16),
        ]
    return pallas(
        body,
        shapes,
        [VMEM] + [ANY] * len(inputs),
        [ANY, ANY, VMEM] + [ANY] * (len(shapes) - 3),
        [pltpu.VMEM(x.shape, x.dtype) for x in inputs]
        + [pltpu.VMEM((GROUP, wrows, 2 * hidden), bf16), DMA((len(inputs),))]
        + gather_scratch() + gather_scratch()
        + [
            DMA((planes,)), DMA((planes,)), DMA((GROUP,)), DMA((GROUP,)),
            DMA((GROUP,)), DMA((GROUP,)), DMA((3 * GROUP,)), DMA((3 * GROUP,)),
            DMA((PlaceGather.SEMS,)), DMA((PlaceGather.SEMS,)),
            DMA((PlaceGather.SEMS + 1,)), DMA((PlaceGather.SEMS,)), DMA((3,)), DMA((5,)),
        ],
        cid,
        60,
    )(small, *inputs)


class Spread:
    SEMS = 8

    def __init__(self, own, piece, relay, send, recv):
        z, low, y = (lax.axis_index(a) for a in ("zh", "st", "y"))
        to_z, to_y = {"zh": 1 - z}, {"y": 1 - y}
        beside, middle = {"st": 1 - low}, {"zh": 1 - z, "st": 1 - low}
        self.outer = z == low
        self.inner = z != low
        halves = range(2)
        self.direct = [
            remote(own(h), piece(z, h, y), send.at[h], recv.at[h], to_z) for h in halves
        ]
        self.toward = [
            remote(own(h), relay.at[h], send.at[h], recv.at[6 + h], beside) for h in halves
        ]
        self.onward = [
            remote(relay.at[h], piece(z, h, y), send.at[6 + h], recv.at[h], middle)
            for h in halves
        ]
        self.y = [
            remote(own(h), piece(z, h, y), send.at[2 + h], recv.at[2 + h], to_y) for h in halves
        ]
        self.on = [
            remote(
                piece(1 - z, h, y), piece(1 - z, h, y), send.at[4 + h], recv.at[4 + h], to_y
            )
            for h in halves
        ]

    def start_z(self):
        @pl.when(self.outer)
        def _():
            for c in self.toward:
                c.start()

        @pl.when(self.inner)
        def _():
            for c in self.direct:
                c.start()

    def start_y(self):
        for c in self.y:
            c.start()

    def relay(self, half):
        @pl.when(self.inner)
        def _():
            self.toward[half].wait_recv()
            self.onward[half].start()

    def forward(self, half):
        self.direct[half].wait_recv()
        self.on[half].start()

    def finish(self):
        for c in self.y + self.on:
            c.wait_recv()
        for c in self.direct + self.y + self.on:
            c.wait_send()

        @pl.when(self.inner)
        def _():
            for c in self.onward:
                c.wait_send()


def rope_constants(length):
    exponent = np.arange(HEAD_SIZE // 2, dtype=np.float32) * np.float32(2.0 / HEAD_SIZE)
    inverse = np.power(np.float32(ROPE_BASE), -exponent).astype(np.float32)
    angles = np.arange(length, dtype=np.float32)[:, None] * inverse[None, :]
    cosine, sine = np.cos(angles.astype(np.float64)), np.sin(angles.astype(np.float64))
    return (
        jnp.asarray(np.concatenate([cosine, cosine], axis=1).astype(np.float32)),
        jnp.asarray(np.concatenate([-sine, sine], axis=1).astype(np.float32)),
    )


def document_mask(row, docs, low, count, keys):
    at_row = low + lax.broadcasted_iota(jnp.int32, (count, 1), 0)
    at_col = lax.broadcasted_iota(jnp.int32, (1, keys), 1)
    seg_row = jnp.zeros((count, 1), jnp.int32)
    seg_col = jnp.zeros((1, keys), jnp.int32)
    for d in range(docs):
        start = (row[:, d : d + 1] * 128.0 + row[:, docs + d : docs + d + 1]).astype(jnp.int32)
        seg_row = seg_row + jnp.where(at_row >= start, 1, 0)
        seg_col = seg_col + jnp.where(at_col >= start, 1, 0)
    return jnp.logical_and(at_row >= at_col, seg_row == seg_col)


def forward_pass(tokens, cotangent, small, w_out, w_query, key_weight, value_weight, w_gate,
                 w_up, w_down, docs, shards, cid):
    rows, width = tokens.shape
    wrows = w_out.shape[0]
    srows = small.shape[0]
    brows = w_down.shape[0]
    planes = 4
    hidden = brows * planes
    parts = [w_query.shape[1] // GROUP, key_weight.shape[1] // GROUP, value_weight.shape[1] // GROUP]
    qkv = sum(parts)
    qcols = parts[0]
    heads = qcols // HEAD_SIZE
    group_rows = rows * GROUP
    length = rows * shards
    streams = GROUP // shards
    gain_rows = width // 128
    grows = srows - wrows
    cosine, sine = rope_constants(length)
    inputs = [tokens, cotangent, w_query, key_weight, value_weight, w_gate, w_up, w_down, w_out]
    score_scale = HEAD_SIZE ** (-0.5)

    def body(
        small_ref, cos_ref, sin_ref, s0, s1, s2, s3, s4, s5, s6, s7, s8,
        cot_all, ffn_all, down_all, h1_out, h2_all, small_all, gains_ref, attn_all, wout_all,
        qkv_ref, low_ref, gate_ref, mixed_ref, gated_ref, mid_ref, hg, starts_ref,
        h0, h1, h2, h3, h4, h5, h6, h7, h8, pack, attn_relay, ffn_relay, down_relay, tok_all, hid, partial, held_two, isem, osem,
        tsend, trecv, csend, crecv, gsend, grecv, ssend, srecv, psend, precv, fsend, frecv, asend,
        arecv, aasend, aarecv, ffsend, ffrecv, dsend, drecv, wsend, wrecv, pair, out, near, far,
        rsend, rrecv,
    ):
        sources = [s0, s1, s2, s3, s4, s5, s6, s7, s8]
        held = [h0, h1, h2, h3, h4, h5, h6, h7, h8]
        place = Place(shards)
        tp, dp = place.tp, place.dp()
        high, low = lax.axis_index("zh"), lax.axis_index("st")
        y, seq = lax.axis_index("y"), lax.axis_index("seq")
        loads = [
            pltpu.make_async_copy(s, h, isem.at[i]) for i, (s, h) in enumerate(zip(sources, held))
        ]
        for i in (2, 3, 4, 8, 0, 5, 6, 7, 1):
            loads[i].start()
        tok_ref, cot_ref, wq_ref, wk_ref, wv_ref, wg_ref, wu_ref, down_ref, wout_ref = held

        barrier = pltpu.get_barrier_semaphore()

        def signal(device):
            pl.semaphore_signal(
                barrier, inc=1, device_id=device, device_id_type=pl.DeviceIdType.MESH
            )

        for device in group_peers(place):
            signal(device)
        for k in range(1, planes):
            signal(place.dp_device((dp + k) % planes))
        to_seq = high * 2 + y
        from_high, from_y = seq // 2, seq % 2
        selfish = seq == to_seq
        mine = y == from_y
        for j in range(4):

            @pl.when(jnp.logical_and(mine, (from_high * 4 + j) != (high * 4 + seq)))
            def _():
                signal({"zh": from_high, "seq": jnp.int32(j)})

        inner = high != low

        @pl.when(inner)
        def _():
            signal({"zh": 1 - high, "st": 1 - low})

        pl.semaphore_wait(
            barrier,
            GROUP - 1 + planes - 1 + 2 - selfish.astype(jnp.int32) + inner.astype(jnp.int32),
        )

        attn = []
        at = 0
        for i, (ref, cols) in enumerate(zip((wq_ref, wk_ref, wv_ref), parts)):
            loads[2 + i].wait()
            for k in range(GROUP):
                peer = (tp + k) % GROUP
                column = place.head(peer) * cols
                src = ref.at[:, pl.ds(pl.multiple_of(column, cols), cols)]
                dst = attn_all.at[high, low, y, pl.ds(seq * wrows, wrows), pl.ds(at, cols)]
                sem = i * GROUP + k
                if k == 0:
                    attn.append(pltpu.make_async_copy(src, dst, asend.at[sem]))
                else:
                    attn.append(
                        remote(src, dst, asend.at[sem], arecv.at[sem], place.device(peer))
                    )
                attn[-1].start()
            at += cols

        small_own = pltpu.make_async_copy(small_ref, small_all.at[tp, dp], ssend.at[0])
        small_own.start()
        small_dp = []
        for k in range(1, planes):
            small_dp.append(
                remote(
                    small_ref, small_all.at[tp, dp], ssend.at[k], srecv.at[k],
                    place.dp_device((dp + k) % planes),
                )
            )
            small_dp[-1].start()

        loads[5].wait()
        loads[6].wait()
        for t in range(GROUP):
            for d in range(planes):
                column = columns_of(d, t, shards)
                for m, ref in enumerate((wg_ref, wu_ref)):
                    lane = m * hidden + d * brows
                    pack[t, :, lane : lane + brows] = ref[:, column * brows : (column + 1) * brows]

        def arrived(copies):
            for i, c in enumerate(copies):
                if i % GROUP == 0:
                    c.wait()
                else:
                    c.wait_recv()

        arrived(attn)

        def attn_piece(zp, half, yp):
            return attn_all.at[zp, half, yp]

        attn_dp = Spread(
            lambda half: attn_piece(high, half, y), attn_piece, attn_relay, aasend, aarecv
        )
        attn_dp.start_z()
        attn_dp.start_y()
        loads[0].wait()
        tok = RingGather(place, tok_ref, tok_all, tsend, trecv, True)
        tok.start()
        small_own.wait()
        for c in small_dp:
            c.wait_recv()
        small_tp = []
        for k in range(1, GROUP):
            small_tp.append(
                remote(
                    small_all.at[tp], small_all.at[tp], psend.at[k], precv.at[k],
                    place.device((tp + k) % GROUP),
                )
            )
            small_tp[-1].start()
        attn_dp.relay(0)
        attn_dp.relay(1)

        loads[7].wait()
        half_rows = brows // 2

        def down_piece(zp, half, yp):
            return down_all.at[zp * 2 + yp, pl.ds(half * half_rows, half_rows)]

        down_dp = Spread(
            lambda half: down_ref.at[pl.ds(half * half_rows, half_rows)], down_piece, down_relay,
            dsend, drecv,
        )
        down_own = pltpu.make_async_copy(down_ref, down_all.at[dp], dsend.at[Spread.SEMS])
        down_own.start()
        down_dp.start_z()
        tok.pass_on()
        ffn_dst = ffn_all.at[high, low, y, pl.ds(seq * wrows, wrows)]
        ffn = [pltpu.make_async_copy(pack.at[tp], ffn_dst, fsend.at[0])]
        for k, (ahead, other) in enumerate(
            ((3, False), (3, True), (0, True), (1, False), (1, True), (2, False), (2, True))
        ):
            peer = place.block(ahead, other)
            ffn.append(
                remote(
                    pack.at[peer], ffn_dst, fsend.at[k + 1], frecv.at[k + 1], place.device(peer)
                )
            )
        for c in ffn[:4]:
            c.start()
        loads[8].wait()
        wout_copies = [
            remote(
                wout_ref, wout_all.at[seq], wsend.at[k], wrecv.at[seq], {"zh": z, "seq": to_seq}
            )
            for k, z in enumerate((high, 1 - high))
        ]
        wout_own = pltpu.make_async_copy(wout_ref, wout_all.at[seq], wsend.at[0])
        wout_over = remote(wout_all, wout_all, wsend.at[2], wrecv.at[4], place.across())
        wout_copies[1].start()

        @pl.when(selfish)
        def _():
            wout_own.start()

        @pl.when(jnp.logical_not(selfish))
        def _():
            wout_copies[0].start()

        attn_dp.forward(0)
        attn_dp.forward(1)
        down_dp.start_y()
        tok.step_across()
        down_dp.relay(0)
        tok.step_far()
        for c in ffn[4:]:
            c.start()

        @pl.when(mine)
        def _():
            for j in range(4):

                @pl.when((from_high * 4 + j) != (high * 4 + seq))
                def _():
                    remote(
                        wout_ref, wout_all.at[j], wsend.at[0], wrecv.at[j], place.across()
                    ).wait_recv()

            @pl.when(selfish)
            def _():
                wout_own.wait()

            wout_over.start()

        loads[1].wait()
        cot = RingGather(place, cot_ref, cot_all, csend, crecv, True)
        cot.start()
        for c in small_tp:
            c.wait_recv()
        gains = jnp.zeros((grows, 128), f32)
        for t in range(GROUP):
            for d in range(planes):
                gains = gains + small_all[t, d, pl.ds(wrows, grows)].astype(f32)
                flat = columns_of(d, t, shards)
                hg[flat * wrows : (flat + 1) * wrows] = small_all[t, d, pl.ds(0, wrows)]
        gains_ref[...] = gains
        gain_one = jnp.concatenate([gains[i : i + 1] for i in range(gain_rows)], axis=1)
        gain_two = jnp.concatenate(
            [gains[gain_rows + i : gain_rows + i + 1] for i in range(gain_rows)], axis=1
        )
        query_gain = gains[2 * gain_rows : 2 * gain_rows + 1]
        key_gain = gains[2 * gain_rows + 1 : 2 * gain_rows + 2]
        starts = []
        for st in range(streams):
            block = small_all[st * shards, dp, pl.ds(wrows, grows)].astype(f32)
            starts.append(block[2 * gain_rows + 2 : 2 * gain_rows + 3])
            starts_ref[st : st + 1] = starts[st]

        tok.finish()
        step = 32

        def norm(i, _):
            block = i // (rows // step)
            inner = pl.ds(pl.multiple_of(i % (rows // step) * step, step), step)
            value = tok_all[block, inner].astype(f32)
            hid[block, inner] = (value * rms_scale(value) * gain_one).astype(bf16)
            return 0

        lax.fori_loop(0, group_rows // step, norm, 0)
        save = pltpu.make_async_copy(hid, h1_out, osem)
        save.start()
        down_dp.relay(1)
        attn_dp.finish()
        weight = attn_all[...].reshape(width, qkv)
        head = place.head(tp)
        lanes = lax.broadcasted_iota(jnp.int32, (1, 128), 1)

        def rotary(x, gain, s):
            scaled = x * rms_scale(x) * gain
            return (
                scaled * cos_ref[...] + pltpu.roll(scaled, HEAD_SIZE // 2, 1) * sin_ref[...]
            ).astype(bf16)

        for s in range(streams):
            part = pl.ds(s * length, length)
            normed = hid[s * shards : (s + 1) * shards].reshape(length, width)
            raw = jnp.dot(normed, weight, preferred_element_type=f32)
            qkv_ref[part] = raw
            logit = jnp.dot(normed, hg[...], preferred_element_type=f32)
            for g in range(heads):
                at = g * HEAD_SIZE
                low_ref[part, at : at + HEAD_SIZE] = rotary(
                    raw[:, at : at + HEAD_SIZE], query_gain, s
                )
                own = jnp.sum(
                    jnp.where(lanes == head * heads + g, logit, 0.0), axis=1, keepdims=True
                )
                gate_ref[part, at : at + HEAD_SIZE] = jnp.broadcast_to(
                    jax.nn.sigmoid(own), (length, HEAD_SIZE)
                )
            low_ref[part, qcols : qcols + HEAD_SIZE] = rotary(
                raw[:, qcols : qcols + HEAD_SIZE], key_gain, s
            )
            low_ref[part, qcols + HEAD_SIZE :] = raw[:, qcols + HEAD_SIZE :].astype(bf16)
        arrived(ffn)

        def ffn_piece(zp, half, yp):
            return ffn_all.at[zp, half, yp]

        ffn_dp = Spread(
            lambda half: ffn_piece(high, half, y), ffn_piece, ffn_relay, ffsend, ffrecv
        )
        ffn_dp.start_z()
        ffn_dp.start_y()
        block = 128
        for s in range(streams):
            base = s * length
            for r in range(0, length, block):
                keys = r + block
                allowed = document_mask(starts[s], docs, r, block, keys)
                key = low_ref[pl.ds(base, keys), qcols : qcols + HEAD_SIZE]
                value = low_ref[pl.ds(base, keys), qcols + HEAD_SIZE :]
                part = pl.ds(base + r, block)
                for g in range(heads):
                    at = g * HEAD_SIZE
                    scores = (
                        lax.dot_general(
                            low_ref[part, at : at + HEAD_SIZE], key, (((1,), (1,)), ((), ())),
                            preferred_element_type=f32,
                        )
                        * score_scale
                    )
                    scores = jnp.where(allowed, scores, MASK_FILL)
                    weights = jnp.exp(scores - jnp.max(scores, axis=1, keepdims=True))
                    probs = weights / jnp.sum(weights, axis=1, keepdims=True)
                    mixed = jnp.dot(
                        probs.astype(bf16), value, preferred_element_type=f32
                    ).astype(bf16)
                    mixed_ref[part, at : at + HEAD_SIZE] = mixed
                    gated_ref[part, at : at + HEAD_SIZE] = (
                        mixed.astype(f32) * gate_ref[part, at : at + HEAD_SIZE]
                    ).astype(bf16)

        @pl.when(jnp.logical_not(mine))
        def _():
            wout_over.wait_recv()

        wide = 512
        for s in range(streams):
            for c in range(0, width, wide):
                product = jnp.dot(
                    gated_ref[pl.ds(s * length, length)],
                    wout_all[:, :, c : c + wide].reshape(qcols, wide),
                    preferred_element_type=f32,
                )
                partial[s * shards : (s + 1) * shards, :, c : c + wide] = product.astype(
                    bf16
                ).reshape(shards, rows, wide)

        def emit(part, total):
            middle = tok_ref[part].astype(f32) + total
            mid_ref[part] = middle
            held_two[part] = (middle * rms_scale(middle) * gain_two).astype(bf16)

        def first():
            cot.pass_on()
            down_dp.forward(0)
            ffn_dp.relay(0)

        def second():
            cot.step_across()
            down_dp.forward(1)

        ring_scatter(
            place, partial, pair, out, near, far, rsend, rrecv, emit, (first, second)
        )
        two = RingGather(place, held_two, h2_all, gsend, grecv, True)
        two.start()
        ffn_dp.relay(1)
        cot.step_far()
        ffn_dp.forward(0)
        two.pass_on()
        two.step_across()
        two.step_far()
        ffn_dp.forward(1)
        two.finish()
        cot.finish()
        ffn_dp.finish()
        down_dp.finish()
        down_own.wait()
        save.wait()
        for i, c in enumerate(attn):
            if i % GROUP:
                c.wait_send()
        for c in ffn[1:] + small_dp + small_tp:
            c.wait_send()

        @pl.when(jnp.logical_not(selfish))
        def _():
            wout_copies[0].wait_send()

        wout_copies[1].wait_send()

        @pl.when(mine)
        def _():
            wout_over.wait_send()

    pieces = (2, streams, 2, shards * wrows)
    shape = jax.ShapeDtypeStruct
    return pallas(
        body,
        [
            shape((GROUP, rows, width), bf16),
            shape(pieces + (2 * hidden,), bf16),
            shape((planes, brows, width), bf16),
            shape((GROUP, rows, width), bf16),
            shape((GROUP, rows, width), bf16),
            shape((GROUP, planes, srows, 128), bf16),
            shape((grows, 128), f32),
            shape(pieces + (qkv,), bf16),
            shape((planes, wrows, width), bf16),
            shape((group_rows, qkv), f32),
            shape((group_rows, qkv), bf16),
            shape((group_rows, qcols), f32),
            shape((group_rows, qcols), bf16),
            shape((group_rows, qcols), bf16),
            shape((rows, width), f32),
            shape((width, 128), bf16),
            shape((streams, 128), f32),
        ],
        [VMEM] * 3 + [ANY] * len(inputs),
        [ANY] * 5 + [VMEM] * 12,
        [pltpu.VMEM(x.shape, x.dtype) for x in inputs]
        + [
            pltpu.VMEM((GROUP, wrows, 2 * hidden), bf16),
            pltpu.VMEM((2, shards * wrows, qkv), bf16),
            pltpu.VMEM((2, shards * wrows, 2 * hidden), bf16),
            pltpu.VMEM((2, brows // 2, width), bf16),
            pltpu.VMEM((GROUP, rows, width), bf16),
            pltpu.VMEM((GROUP, rows, width), bf16),
            pltpu.VMEM((GROUP, rows, width), bf16),
            pltpu.VMEM((rows, width), bf16),
            DMA((len(inputs),)),
            DMA,
        ]
        + gather_scratch() + gather_scratch() + gather_scratch()
        + [
            DMA((planes,)), DMA((planes,)), DMA((GROUP,)), DMA((GROUP,)),
            DMA((GROUP,)), DMA((GROUP,)), DMA((3 * GROUP,)), DMA((3 * GROUP,)),
            DMA((Spread.SEMS,)), DMA((Spread.SEMS,)), DMA((Spread.SEMS,)), DMA((Spread.SEMS,)),
            DMA((Spread.SEMS + 1,)), DMA((Spread.SEMS,)), DMA((3,)), DMA((5,)),
        ]
        + scatter_scratch(rows, width),
        cid,
        100,
        56,
    )(small, cosine, sine, *inputs)


class PlaceSums:
    SENDS, RECVS = 8, 6

    def __init__(self, piece, got, far, near, relay, send, recv):
        z, low, y = (lax.axis_index(a) for a in ("zh", "st", "y"))
        to_z, to_y = {"zh": 1 - z}, {"y": 1 - y}
        beside, middle = {"st": 1 - low}, {"zh": 1 - z, "st": 1 - low}
        self.outer, self.inner = z == low, z != low
        self.got, self.far, self.near = got, far, near
        self.y_far = remote(piece(1 - z, 1 - y), got.at[0], send.at[0], recv.at[0], to_y)
        self.y_near = remote(piece(z, 1 - y), got.at[1], send.at[1], recv.at[1], to_y)
        self.loads = [
            pltpu.make_async_copy(piece(1 - z, y), far, send.at[2]),
            pltpu.make_async_copy(piece(z, y), near, send.at[3]),
        ]

        def half(ref, h):
            if len(far.shape) == 3:
                return ref.at[h]
            count = far.shape[0] // 2
            return ref.at[pl.ds(h * count, count)]

        self.direct, self.toward, self.onward = [], [], []
        for h in range(2):
            dst = half(got.at[2], h)
            self.direct.append(
                remote(half(far, h), dst, send.at[4 + h], recv.at[2 + h], to_z)
            )
            self.toward.append(
                remote(half(far, h), half(relay, h), send.at[4 + h], recv.at[4 + h], beside)
            )
            self.onward.append(
                remote(half(relay, h), dst, send.at[6 + h], recv.at[2 + h], middle)
            )

    def load(self):
        for c in self.loads:
            c.start()

    def over_z(self):
        self.loads[0].wait()
        self.y_far.wait_recv()
        self.each(lambda at: self.put(at))

        @pl.when(self.outer)
        def _():
            for c in self.toward:
                c.start()

        @pl.when(self.inner)
        def _():
            for c in self.direct:
                c.start()

    def relay(self, half):
        @pl.when(self.inner)
        def _():
            self.toward[half].wait_recv()
            self.onward[half].start()

    def put(self, at):
        self.far[at] = (self.far[at].astype(f32) + self.got[(0,) + at].astype(f32)).astype(bf16)

    def each(self, visit):
        lead, rows = self.far.shape[:-2], self.far.shape[-2]

        def inner(i, _):
            part = pl.ds(pl.multiple_of(i * 32, 32), 32)
            if lead:
                for k in range(lead[0]):
                    visit((k, part))
            else:
                visit((part,))
            return 0

        lax.fori_loop(0, rows // 32, inner, 0)

    def total(self, at):
        return (self.near[at].astype(f32) + self.got[(1,) + at].astype(f32)) + self.got[
            (2,) + at
        ].astype(f32)

    def arrive(self):
        self.loads[1].wait()
        self.y_near.wait_recv()
        for c in self.direct:
            c.wait_recv()

    def drain(self):
        for c in [self.y_far, self.y_near] + self.direct:
            c.wait_send()

        @pl.when(self.inner)
        def _():
            for c in self.onward:
                c.wait_send()


def backward_pass(x, final, middle, tokens, cotangent, gains, headgate, qkv_w, out_w, hidden_one,
                  qkv, low, gate, mixed, gated, starts, down_grad, ffn_grad, docs, shards, cid):
    _, rows, width = x.shape
    planes = 4
    streams = GROUP // shards
    length = rows * shards
    group_rows = rows * GROUP
    qcols = gate.shape[1]
    qkv_cols = qkv.shape[1]
    kcols = (qkv_cols - qcols) // 2
    heads = qcols // HEAD_SIZE
    brows = down_grad.shape[2]
    both = ffn_grad.shape[4]
    hidden = both // 2
    wrows = width // (planes * GROUP)
    gain_rows = width // 128
    score_scale = HEAD_SIZE ** (-0.5)
    cosine, sine = rope_constants(length)
    srows = 24
    inputs = [
        x, middle, tokens, cotangent, headgate, qkv_w, out_w, qkv, low, gate, mixed, gated,
    ]

    def body(
        gains_ref, starts_ref, cos_ref, sin_ref, final_ref, h1_ref, down_ref, ffn_ref,
        i0, i1, i2, i3, i4, i5, i6, i7, i8, i9, i10, i11,
        layer_ref, tgrad_ref, gate_out, up_out, query_out, key_out, value_out, o_out, down_out,
        s_out,
        partial, mid_ref, tok_ref, cot_ref, hg_ref, wq_ref, wout_ref, qkv_ref, low_ref, gate_ref,
        mixed_ref, gated_ref,
        held, db_all, dmid, gq, dgl, dk_acc, dv_acc, dmix, small, stage, s_got, s_held, s_line,
        g_got, g_far, g_near, g_in, d_got, d_far, d_near, q_own, q_got, q_far, q_near, q_in,
        o_own, o_got, o_far, o_near, o_in, g_relay, d_relay, q_relay, o_relay,
        pair, out, near, far, rsend, rrecv, r2send, r2recv, r3send, r3recv, csend, crecv,
        isem, gsend, grecv, dsend, drecv, qsend, qrecv, osend, orecv, gxsend, gxrecv, qxsend,
        qxrecv, oxsend, oxrecv, asend, arecv, bsend, brecv, lsem, turn,
    ):
        sources = [i0, i1, i2, i3, i4, i5, i6, i7, i8, i9, i10, i11]
        targets = [
            partial, mid_ref, tok_ref, cot_ref, hg_ref, wq_ref, wout_ref, qkv_ref, low_ref,
            gate_ref, mixed_ref, gated_ref,
        ]
        place = Place(shards)
        tp, dp, flat = place.tp, place.dp(), place.flat()
        high, y, seq = lax.axis_index("zh"), lax.axis_index("y"), lax.axis_index("seq")
        loads = [
            pltpu.make_async_copy(s, t, isem.at[i])
            for i, (s, t) in enumerate(zip(sources, targets))
        ]
        for c in loads[:4]:
            c.start()
        barrier = pltpu.get_barrier_semaphore()

        def signal(device, semaphore=barrier):
            pl.semaphore_signal(
                semaphore, inc=1, device_id=device, device_id_type=pl.DeviceIdType.MESH
            )

        for device in group_peers(place):
            signal(device)
        for k in range(1, planes):
            signal(place.dp_device((dp + k) % planes))
        owner = place.head(tp) * planes + dp
        source = {"st": lax.axis_index("st"), "seq": high * 2 + y}
        source.update(place.dp_device(seq))

        @pl.when(owner != flat)
        def _():
            signal(source)

        inner = high != lax.axis_index("st")

        @pl.when(inner)
        def _():
            signal({"zh": 1 - high, "st": 1 - lax.axis_index("st")})

        pl.semaphore_wait(
            barrier,
            GROUP + planes - 2 + (owner != flat).astype(jnp.int32) + inner.astype(jnp.int32),
        )

        ffn = PlaceSums(
            lambda zp, yp: ffn_ref.at[zp, :, yp], g_got, g_far, g_near, g_relay, gsend, grecv
        )
        down = PlaceSums(lambda zp, yp: down_ref.at[zp, yp], d_got, d_far, d_near, d_relay, dsend, drecv)
        down.y_far.start()
        ffn.y_far.start()
        ffn.y_near.start()
        down.load()
        ffn.load()
        for c in loads[4:]:
            c.start()

        small[...] = jnp.zeros_like(small)
        gain_all = gains_ref[...]
        gain_one = jnp.concatenate([gain_all[i : i + 1] for i in range(gain_rows)], axis=1)
        gain_two = jnp.concatenate(
            [gain_all[gain_rows + i : gain_rows + i + 1] for i in range(gain_rows)], axis=1
        )
        query_gain = gain_all[2 * gain_rows : 2 * gain_rows + 1]
        key_gain = gain_all[2 * gain_rows + 1 : 2 * gain_rows + 2]
        for c in loads[:4]:
            c.wait()

        def emit_dm(part, total):
            value = mid_ref[part]
            scale = rms_scale(value)
            normed = value * scale
            small[17:18] += jnp.sum(total * normed, axis=0, keepdims=True)
            dm = cot_ref[part].astype(f32) + norm_back(total * gain_two, normed, scale)
            dmid[part] = dm
            held[part] = dm.astype(bf16)

        ring_scatter(place, partial, pair, out, near, far, rsend, rrecv, emit_dm)
        grad = RingGather(place, held, db_all, csend, crecv)
        grad.start()
        h1_all = partial
        load_h1 = pltpu.make_async_copy(h1_ref, h1_all, lsem.at[0])
        load_h1.start()
        down.over_z()
        grad.pass_on()
        down.relay(0)
        grad.step_across()
        down.relay(1)
        grad.step_far()
        for c in loads[4:]:
            c.wait()
        grad.finish()

        lanes = lax.broadcasted_iota(jnp.int32, (1, 128), 1)
        head = place.head(tp)
        for s in range(streams):
            part = pl.ds(s * length, length)
            db = db_all[s * shards : (s + 1) * shards].reshape(length, width)
            da = lax.dot_general(
                db, wout_ref[...], (((1,), (1,)), ((), ())), preferred_element_type=f32
            )
            logits = jnp.zeros((length, 128), f32)
            for g in range(heads):
                at = g * HEAD_SIZE
                piece = da[:, at : at + HEAD_SIZE]
                opened = gate_ref[part, at : at + HEAD_SIZE]
                dmix[part, at : at + HEAD_SIZE] = (piece * opened).astype(bf16)
                own = jnp.sum(
                    piece * mixed_ref[part, at : at + HEAD_SIZE].astype(f32), axis=1,
                    keepdims=True,
                )
                logits = jnp.where(
                    lanes == head * heads + g, own * opened * (1.0 - opened), logits
                )
            dgl[part] = logits.astype(bf16)
        wide = 512
        for c in range(0, width, wide):
            product = lax.dot_general(
                gated_ref[...], db_all[:, :, c : c + wide].reshape(group_rows, wide),
                (((0,), (0,)), ((), ())), preferred_element_type=f32,
            ).astype(bf16)
            for j in range(planes):
                o_own[j // 2, j % 2, :, c : c + wide] = product[j * wrows : (j + 1) * wrows]
        outs = PlaceSums(lambda zp, yp: o_own.at[zp, yp], o_got, o_far, o_near, o_relay, osend, orecv)
        outs.y_far.start()
        outs.load()
        ffn.over_z()

        block = 128
        query_part = jnp.zeros((1, HEAD_SIZE), f32)
        key_part = jnp.zeros((1, HEAD_SIZE), f32)
        for s in range(streams):
            base = s * length
            row = starts_ref[s : s + 1]
            dk_acc[...] = jnp.zeros_like(dk_acc)
            dv_acc[...] = jnp.zeros_like(dv_acc)

            def back(grad_rotated, raw, gain):
                grad_gained = grad_rotated * cos_ref[...] - pltpu.roll(
                    grad_rotated, HEAD_SIZE // 2, 1
                ) * sin_ref[...]
                scale = rms_scale(raw)
                normed = raw * scale
                return (
                    jnp.sum(grad_gained * normed, axis=0, keepdims=True),
                    norm_back(grad_gained * gain, normed, scale).astype(bf16),
                )

            for r in range(0, length, block):
                keys = r + block
                allowed = document_mask(row, docs, r, block, keys)
                key = low_ref[pl.ds(base, keys), qcols : qcols + HEAD_SIZE]
                value = low_ref[pl.ds(base, keys), qcols + HEAD_SIZE :]
                part = pl.ds(base + r, block)
                for g in range(heads):
                    at = g * HEAD_SIZE
                    query = low_ref[part, at : at + HEAD_SIZE]
                    scores = (
                        lax.dot_general(
                            query, key, (((1,), (1,)), ((), ())), preferred_element_type=f32
                        )
                        * score_scale
                    )
                    scores = jnp.where(allowed, scores, MASK_FILL)
                    weights = jnp.exp(scores - jnp.max(scores, axis=1, keepdims=True))
                    probs = weights / jnp.sum(weights, axis=1, keepdims=True)
                    dout = dmix[part, at : at + HEAD_SIZE]
                    dprobs = lax.dot_general(
                        dout, value, (((1,), (1,)), ((), ())), preferred_element_type=f32
                    )
                    delta = jnp.sum(probs * dprobs, axis=1, keepdims=True)
                    dscores = (probs * (dprobs - delta)).astype(bf16)
                    dq = jnp.dot(dscores, key, preferred_element_type=f32) * score_scale
                    gq[part, at : at + HEAD_SIZE] = dq.astype(bf16)
                    dk_acc[0:keys] += lax.dot_general(
                        dscores, query, (((0,), (0,)), ((), ())), preferred_element_type=f32
                    )
                    dv_acc[0:keys] += lax.dot_general(
                        probs.astype(bf16), dout, (((0,), (0,)), ((), ())),
                        preferred_element_type=f32,
                    )
            part = pl.ds(base, length)
            for g in range(heads):
                at = g * HEAD_SIZE
                sums, grads = back(
                    gq[part, at : at + HEAD_SIZE].astype(f32), qkv_ref[part, at : at + HEAD_SIZE],
                    query_gain,
                )
                query_part = query_part + sums
                gq[part, at : at + HEAD_SIZE] = grads
            sums, grads = back(
                (dk_acc[...] * score_scale).astype(bf16).astype(f32),
                qkv_ref[part, qcols : qcols + HEAD_SIZE], key_gain,
            )
            key_part = key_part + sums
            gq[part, qcols : qcols + HEAD_SIZE] = grads
            gq[part, qcols + HEAD_SIZE :] = dv_acc[...].astype(bf16)

        load_h1.wait()
        for n in range(width // 256):
            cols = slice(n * 256, (n + 1) * 256)
            product = lax.dot_general(
                h1_all[:, :, cols].reshape(group_rows, 256), gq[...], (((0,), (0,)), ((), ())),
                preferred_element_type=f32,
            )
            q_own[n // 4, n // 2 % 2, n % 2] = product.astype(bf16)
        qkvs = PlaceSums(lambda zp, yp: q_own.at[zp, :, yp], q_got, q_far, q_near, q_relay, qsend, qrecv)
        qkvs.y_far.start()
        outs.y_near.start()
        qkvs.y_near.start()
        down.y_near.start()
        qkvs.load()
        for c in range(0, width, wide):
            small[0:16, c : c + wide] = lax.dot_general(
                dgl[...], h1_all[:, :, c : c + wide].reshape(group_rows, wide),
                (((0,), (0,)), ((), ())), preferred_element_type=f32,
            )[0:16]

        for s in range(streams):
            part = pl.ds(s * length, length)
            for c in range(0, width, wide):
                product = lax.dot_general(
                    gq[part], wq_ref[c : c + wide], (((1,), (1,)), ((), ())),
                    preferred_element_type=f32,
                ) + lax.dot_general(
                    dgl[part], hg_ref[c : c + wide], (((1,), (1,)), ((), ())),
                    preferred_element_type=f32,
                )
                partial[s * shards : (s + 1) * shards, :, c : c + wide] = product.astype(
                    bf16
                ).reshape(shards, rows, wide)

        def emit_tokens(part, total):
            tok = tok_ref[part].astype(f32)
            scale = rms_scale(tok)
            normed = tok * scale
            small[16:17] += jnp.sum(total * normed, axis=0, keepdims=True)
            tgrad_ref[part] = (
                dmid[part] + norm_back(total * gain_one, normed, scale)
            ).astype(bf16)

        load_final = pltpu.make_async_copy(final_ref, db_all, lsem.at[1])
        load_final.start()
        ffn.relay(0)
        ring_scatter(
            place, partial, pair, out, near, far, r2send, r2recv, emit_tokens,
            (lambda: ffn.relay(1),),
        )
        ring_peers = [place.right(), place.left(), place.partner()]
        for device in ring_peers:
            signal(device, turn)
        outs.over_z()
        qkvs.over_z()

        small[18:19] = jnp.concatenate([query_part] * gain_rows, axis=1)
        small[19:20] = jnp.concatenate([key_part] * gain_rows, axis=1)
        for t in range(GROUP):
            for d in range(planes):
                lane = columns_of(d, t, shards) // 2 * 128
                stage[t, d * srows : (d + 1) * srows] = small[:, lane : lane + 128]
        sums = Exchange(place, stage, s_got, asend, arecv)
        sums.start()

        load_final.wait()
        pl.semaphore_wait(turn, len(ring_peers))

        def emit_layer(part, total):
            layer_ref[part] = (mid_ref[part] + total).astype(bf16)

        def first():
            outs.relay(0)
            outs.relay(1)

        def second():
            qkvs.relay(0)
            qkvs.relay(1)

        ring_scatter(
            place, db_all, pair, out, near, far, r3send, r3recv, emit_layer, (first, second)
        )
        sums.finish()
        s_held[...] = jnp.sum(s_got[...], axis=0).reshape(s_held.shape)
        line_own = pltpu.make_async_copy(s_held.at[dp], s_line.at[dp], bsend.at[0])
        line_own.start()
        lines = []
        for k in range(1, planes):
            to = (dp + k) % planes
            lines.append(
                remote(
                    s_held.at[to], s_line.at[dp], bsend.at[k], brecv.at[k], place.dp_device(to)
                )
            )
            lines[-1].start()

        def scatter_rows(total, ready, send, recv, into):
            def keep(at):
                ready[at] = total(at).astype(bf16)

            copies = []
            for k in range(GROUP):
                peer = (tp + k) % GROUP
                src = ready.at[peer // shards, pl.ds(peer % shards * wrows, wrows)]
                if k == 0:
                    copies.append(pltpu.make_async_copy(src, into.at[tp], send.at[0]))
                else:
                    copies.append(
                        remote(src, into.at[tp], send.at[k], recv.at[k], place.device(peer))
                    )
            return keep, copies

        ffn.arrive()
        keep, ffn_rows = scatter_rows(ffn.total, g_near, gxsend, gxrecv, g_in)
        ffn.each(keep)
        for c in ffn_rows:
            c.start()
        down.arrive()

        def put_down(at):
            down_out[at] = down.total(at)

        down.each(put_down)

        def landed(copies):
            copies[0].wait()
            for c in copies[1:]:
                c.wait_recv()

        landed(ffn_rows)
        for t in range(GROUP):
            for d in range(planes):
                column = columns_of(d, t, shards)
                for m, ref in enumerate((gate_out, up_out)):
                    lane = m * hidden + d * brows
                    for at in range(0, wrows, 32):
                        ref[at : at + 32, column * brows : (column + 1) * brows] = g_in[
                            t, at : at + 32, lane : lane + brows
                        ].astype(f32)
        outs.arrive()

        def keep_out(at):
            o_near[at] = outs.total(at).astype(bf16)

        outs.each(keep_out)
        out_own = pltpu.make_async_copy(o_near, o_in, oxsend)
        out_far = remote(o_near, o_in, oxsend, oxrecv, place.any_device(owner))

        @pl.when(owner == flat)
        def _():
            out_own.start()

        @pl.when(owner != flat)
        def _():
            out_far.start()

        qkvs.arrive()
        keep, qkv_rows = scatter_rows(qkvs.total, q_near, qxsend, qxrecv, q_in)
        qkvs.each(keep)
        for c in qkv_rows:
            c.start()

        landed(qkv_rows)
        for t in range(GROUP):
            home = place.head(t)
            query_out[:, home * qcols : (home + 1) * qcols] = q_in[t, :, :qcols].astype(f32)
            key_out[:, home * kcols : (home + 1) * kcols] = q_in[
                t, :, qcols : qcols + kcols
            ].astype(f32)
            value_out[:, home * kcols : (home + 1) * kcols] = q_in[
                t, :, qcols + kcols :
            ].astype(f32)

        @pl.when(owner == flat)
        def _():
            out_own.wait()

        @pl.when(owner != flat)
        def _():
            out_far.wait()

        o_out[...] = o_in[...].astype(f32)
        for c in lines:
            c.wait_recv()
        line_own.wait()
        s_out[...] = jnp.sum(s_line[...], axis=0)
        for c in lines + ffn_rows[1:] + qkv_rows[1:]:
            c.wait_send()
        for c in (ffn, down, qkvs, outs):
            c.drain()

    shape = jax.ShapeDtypeStruct
    vmem = pltpu.VMEM
    wide_rows = shards * wrows
    return pallas(
        body,
        [
            shape((rows, width), bf16),
            shape((rows, width), bf16),
            shape((wrows, hidden * GROUP), f32),
            shape((wrows, hidden * GROUP), f32),
            shape((wrows, qcols * GROUP), f32),
            shape((wrows, kcols * GROUP), f32),
            shape((wrows, kcols * GROUP), f32),
            shape((wrows, width), f32),
            shape((brows, width), f32),
            shape((srows, 128), f32),
        ],
        [VMEM] * 4 + [ANY] * (4 + len(inputs)),
        [VMEM] * 10,
        [vmem(i.shape, i.dtype) for i in inputs]
        + [
            vmem((rows, width), bf16),
            vmem((GROUP, rows, width), bf16),
            vmem((rows, width), f32),
            vmem((group_rows, qkv_cols), bf16),
            vmem((group_rows, 128), bf16),
            vmem((length, HEAD_SIZE), f32),
            vmem((length, HEAD_SIZE), f32),
            vmem((group_rows, qcols), bf16),
            vmem((srows, width), f32),
            vmem((GROUP, planes * srows, 128), f32),
            vmem((GROUP, planes * srows, 128), f32),
            vmem((planes, srows, 128), f32),
            vmem((planes, srows, 128), f32),
            vmem((3, streams, wide_rows, both), bf16),
            vmem((streams, wide_rows, both), bf16),
            vmem((streams, wide_rows, both), bf16),
            vmem((GROUP, wrows, both), bf16),
            vmem((3, brows, width), bf16),
            vmem((brows, width), bf16),
            vmem((brows, width), bf16),
            vmem((2, streams, 2, wide_rows, qkv_cols), bf16),
            vmem((3, streams, wide_rows, qkv_cols), bf16),
            vmem((streams, wide_rows, qkv_cols), bf16),
            vmem((streams, wide_rows, qkv_cols), bf16),
            vmem((GROUP, wrows, qkv_cols), bf16),
            vmem((2, 2, wrows, width), bf16),
            vmem((3, wrows, width), bf16),
            vmem((wrows, width), bf16),
            vmem((wrows, width), bf16),
            vmem((wrows, width), bf16),
            vmem((streams, wide_rows, both), bf16),
            vmem((brows, width), bf16),
            vmem((streams, wide_rows, qkv_cols), bf16),
            vmem((wrows, width), bf16),
        ]
        + scatter_scratch(rows, width)
        + [DMA((10,)), DMA((10,)), DMA((10,)), DMA((10,))]
        + gather_scratch()
        + [DMA((len(inputs),))]
        + [DMA((PlaceSums.SENDS,)), DMA((PlaceSums.RECVS,))] * 4
        + [DMA((GROUP,)), DMA((GROUP,)), DMA((GROUP,)), DMA((GROUP,)), DMA, DMA]
        + [DMA((GROUP,)), DMA((GROUP,)), DMA((planes,)), DMA((planes,)), DMA((2,))]
        + [pltpu.SemaphoreType.REGULAR],
        cid,
        180,
        62,
    )(gains, starts, cosine, sine, final, hidden_one, down_grad, ffn_grad, *inputs)


def settle(qkv_grad, out_grad, small, qcols, kcols, planes, direct, shards, cid):
    srows = small.shape[1] // planes
    cols = small.shape[2]
    wrows, width = out_grad.shape

    def body(
        q_ref, o_ref, s_ref, query_out, key_out, value_out, o_out, s_out, q_got, o_got, got, held,
        line, qsend, qrecv, osend, orecv, asend, arecv, bsend, brecv,
    ):
        place = Place(shards)
        tp, dp, flat = place.tp, place.dp(), place.flat()
        barrier = pltpu.get_barrier_semaphore()

        def signal(device):
            pl.semaphore_signal(
                barrier, inc=1, device_id=device, device_id_type=pl.DeviceIdType.MESH
            )

        for device in group_peers(place):
            signal(device)
        for k in range(1, planes):
            signal(place.dp_device((dp + k) % planes))
        if direct:
            owner = place.head(tp) * planes + dp
            high, y = lax.axis_index("zh"), lax.axis_index("y")
            source = {"st": lax.axis_index("st"), "seq": high * 2 + y}
            source.update(place.dp_device(lax.axis_index("seq")))

            @pl.when(owner != flat)
            def _():
                signal(source)

            pl.semaphore_wait(barrier, GROUP + planes - 2 + (owner != flat).astype(jnp.int32))
        else:
            pl.semaphore_wait(barrier, GROUP + planes - 2)

        sums = Exchange(place, s_ref, got, asend, arecv)
        sums.start()
        qkv = Exchange(place, q_ref, q_got, qsend, qrecv)
        qkv.start()
        if direct:
            out_own = pltpu.make_async_copy(o_ref, o_got, osend)
            out_far = remote(o_ref, o_got, osend, orecv, place.any_device(owner))

            @pl.when(owner == flat)
            def _():
                out_own.start()

            @pl.when(owner != flat)
            def _():
                out_far.start()

        sums.finish()
        held[...] = jnp.sum(got[...], axis=0).reshape(held.shape)
        line_own = pltpu.make_async_copy(held.at[dp], line.at[dp], bsend.at[0])
        line_own.start()
        lines = []
        for k in range(1, planes):
            to = (dp + k) % planes
            lines.append(
                remote(held.at[to], line.at[dp], bsend.at[k], brecv.at[k], place.dp_device(to))
            )
            lines[-1].start()
        qkv.finish()
        for t in range(GROUP):
            head = place.head(t)
            query_out[:, head * qcols : (head + 1) * qcols] = q_got[t, :, :qcols].astype(f32)
            key_out[:, head * kcols : (head + 1) * kcols] = q_got[
                t, :, qcols : qcols + kcols
            ].astype(f32)
            value_out[:, head * kcols : (head + 1) * kcols] = q_got[t, :, qcols + kcols :].astype(
                f32
            )
        if direct:

            @pl.when(owner == flat)
            def _():
                out_own.wait()

            @pl.when(owner != flat)
            def _():
                out_far.wait()

            o_out[...] = o_got[...].astype(f32)
        else:
            o_out[...] = o_ref[...].astype(f32)
        for c in lines:
            c.wait_recv()
        line_own.wait()
        s_out[...] = jnp.sum(line[...], axis=0)
        for c in lines:
            c.wait_send()

    return pallas(
        body,
        [
            jax.ShapeDtypeStruct((wrows, GROUP * qcols), f32),
            jax.ShapeDtypeStruct((wrows, GROUP * kcols), f32),
            jax.ShapeDtypeStruct((wrows, GROUP * kcols), f32),
            jax.ShapeDtypeStruct((wrows, width), f32),
            jax.ShapeDtypeStruct((srows, cols), f32),
        ],
        [VMEM, VMEM, VMEM],
        [VMEM] * 5,
        [
            pltpu.VMEM(qkv_grad.shape, bf16),
            pltpu.VMEM(out_grad.shape, bf16),
            pltpu.VMEM(small.shape, f32),
            pltpu.VMEM((planes, srows, cols), f32),
            pltpu.VMEM((planes, srows, cols), f32),
            DMA((GROUP,)), DMA((GROUP,)), DMA, DMA,
            DMA((GROUP,)), DMA((GROUP,)), DMA((planes,)), DMA((planes,)),
        ],
        cid,
        20,
    )(qkv_grad, out_grad, small)


def local(
    tokens, doc_starts, attn_gain, query_gain, key_gain, w_query, key_weight, value_weight,
    w_headgate, w_out, ffn_gain, w_gate, w_up, w_down, cotangent,
):
    zs, ys = lax.axis_size("zh"), lax.axis_size("y")
    planes = zs * ys
    direct = zs == 2 and ys == 2
    streams = lax.axis_size("st")
    shards = lax.axis_size("seq")
    devices = planes * GROUP
    rows, width = tokens.shape
    length = rows * shards
    group_rows = rows * GROUP
    wrows = w_query.shape[0]
    brows = w_down.shape[0]
    hidden = brows * planes
    qcols = w_query.shape[1] // GROUP
    kcols = key_weight.shape[1] // GROUP
    group_heads = qcols // HEAD_SIZE
    all_heads = w_headgate.shape[1]
    score_scale = HEAD_SIZE ** (-0.5)
    dp = lax.axis_index(DP)
    tp = lax.axis_index(TP)

    hg = wrows * all_heads
    gcols = query_gain.shape[0]
    at = hg + 2 * wrows
    count = at + 2 * gcols
    sums = -(-count // 1024) * 8
    docs = doc_starts.shape[1]
    qkv_cols = qcols + 2 * kcols
    starts_row = jnp.concatenate(
        [(doc_starts[0] // 128).astype(bf16), (doc_starts[0] % 128).astype(bf16)]
    )
    headgate_rows = jnp.pad(w_headgate, ((0, 0), (0, 128 - all_heads)))
    if direct:
        flat = lax.axis_index(ALL)
        gain_rows = width // 128
        grows = -(-(2 * gain_rows + 3) // 16) * 16
        row_of = lax.broadcasted_iota(jnp.int32, (grows, 128), 0)
        lane_of = lax.broadcasted_iota(jnp.int32, (grows, 128), 1)

        def placed(values, base):
            size = values.shape[0]
            where = (row_of - base) * 128 + lane_of - flat * size
            full = jnp.tile(values, 128 // size)[None]
            return jnp.where((where >= 0) & (where < size), full, 0)

        gain_block = (
            placed(attn_gain, 0) + placed(ffn_gain, gain_rows)
            + placed(query_gain, 2 * gain_rows) + placed(key_gain, 2 * gain_rows + 1)
            + jnp.where(
                row_of == 2 * gain_rows + 2, jnp.pad(starts_row, (0, 128 - 2 * docs))[None], 0
            )
        )
        small = jnp.concatenate([headgate_rows, gain_block])
        (
            cot_all, ffn_w, down_w, hidden_one, hidden_two, small, gains, qkv_w, out_w, qkv,
            low, gate_full, mixed, gated, middle, headgate, starts,
        ) = forward_pass(
            tokens, cotangent, small, w_out, w_query, key_weight, value_weight, w_gate, w_up,
            w_down, docs, shards, 0,
        )
        cot_all = cot_all.reshape(group_rows, width)
        hidden_two = hidden_two.reshape(group_rows, width)
        ffn_w = ffn_w.reshape(width, 2 * hidden)
        down_w = down_w.reshape(hidden, width)
        gate_up = mm(hidden_two, ffn_w)
        gate_pre, up_proj = gate_up[:, :hidden], gate_up[:, hidden:]
        gate_sig = jax.nn.sigmoid(gate_pre)
        inner_act = (gate_pre * gate_sig * up_proj).astype(bf16)
        down_grad = mm_t(inner_act, cot_all).astype(bf16)
        grad_inner = mm_b(cot_all, down_w)
        grad_gate = grad_inner * up_proj * gate_sig * (1.0 + gate_pre * (1.0 - gate_sig))
        grad_up = grad_inner * gate_pre * gate_sig
        grad_gu = jnp.concatenate([grad_gate.astype(bf16), grad_up.astype(bf16)], axis=1)
        ffn_grad = mm_t(hidden_two, grad_gu).astype(bf16)
        places = (GROUP, rows, width)
        (
            layer_out, tokens_grad, gate_grad, up_grad, query_grad, key_grad, value_grad,
            out_grad, down_grad, small_sum,
        ) = backward_pass(
            mm_b(grad_gu, ffn_w).astype(bf16).reshape(places),
            mm(inner_act, down_w).astype(bf16).reshape(places),
            middle, tokens, cotangent, gains, headgate,
            qkv_w.reshape(width, qkv_cols), out_w.reshape(qcols, width), hidden_one, qkv, low,
            gate_full, mixed, gated, starts, down_grad.reshape(zs, ys, brows, width),
            ffn_grad.reshape(zs, streams, ys, shards * wrows, 2 * hidden), docs, shards, 1,
        )
        half = lax.dynamic_slice_in_dim(small_sum, flat % 2 * wrows, wrows, 1)
        return (
            layer_out,
            tokens_grad,
            half[all_heads],
            lax.dynamic_slice_in_dim(small_sum[18], flat * gcols, gcols, 0),
            lax.dynamic_slice_in_dim(small_sum[19], flat * gcols, gcols, 0),
            query_grad,
            key_grad,
            value_grad,
            half[:all_heads].T,
            out_grad,
            half[all_heads + 1],
            gate_grad,
            up_grad,
            down_grad,
        )
    else:
        srows = -(-(wrows + 6) // 16) * 16
        others = [attn_gain, ffn_gain, query_gain, key_gain, starts_row[:docs], starts_row[docs:]]
        small = jnp.concatenate(
            [headgate_rows]
            + [jnp.pad(row, (0, 128 - row.shape[0]))[None] for row in others]
            + [jnp.zeros((srows - wrows - 6, 128), bf16)]
        )
        tokens_all, cot_all, small, qkv_w, ffn_own = front(
            tokens, cotangent, small, w_out, w_query, key_weight, value_weight, w_gate, w_up,
            w_down, planes, False, shards, 0,
        )
        tokens_all = tokens_all.reshape(group_rows, width)
        cot_all = cot_all.reshape(group_rows, width)
        qkv_w = over_dp(qkv_w[0])
        ffn_w = over_dp(ffn_own)
        down_w = lax.all_gather(w_down, DP, axis=0, tiled=True)
        out_w = lax.all_gather(w_out, ALL, axis=0, tiled=True)
        out_w = lax.dynamic_slice_in_dim(out_w, tp * qcols, qcols, 0)
        head = tp
        here = pick(small[::shards], 1, dp)
        starts = here[:, wrows + 4, :docs].astype(jnp.int32) * 128
        starts = starts + here[:, wrows + 5, :docs].astype(jnp.int32)
    small = small.reshape(streams, shards, zs, ys, srows, 128).transpose(2, 0, 3, 1, 4, 5)
    small = small.reshape(devices, srows, 128)
    headgate_all = small[:, :wrows, :all_heads].reshape(width, all_heads)
    if not direct:
        attn_gain_f = small[:, wrows, :wrows].reshape(1, -1).astype(f32)
        ffn_gain_f = small[:, wrows + 1, :wrows].reshape(1, -1).astype(f32)
        query_gain_f = small[:, wrows + 2, :gcols].reshape(-1).astype(f32)
        key_gain_f = small[:, wrows + 3, :gcols].reshape(-1).astype(f32)
    headgate_own = lax.dynamic_slice_in_dim(headgate_all, head * group_heads, group_heads, 1)

    if not direct:
        residual_all = tokens_all.astype(f32)
        hidden_all = (residual_all * rms_scale(residual_all) * attn_gain_f).astype(bf16)
        qkv = mm(hidden_all, qkv_w)
    query_raw = qkv[:, :qcols].reshape(group_rows, group_heads, HEAD_SIZE)
    key_raw = qkv[:, qcols : qcols + kcols].reshape(group_rows, 1, HEAD_SIZE)
    value = qkv[:, qcols + kcols :].astype(bf16).reshape(streams, length, HEAD_SIZE)
    positions = jnp.tile(jnp.arange(length, dtype=jnp.int32), streams)
    cosine, sine = rotary_tables(positions)
    query_scale = rms_scale(query_raw)
    query_normed = query_raw * query_scale
    query = rotate(query_normed * query_gain_f, cosine, sine).astype(bf16)
    query = query.reshape(streams, length, group_heads, HEAD_SIZE)
    key_scale = rms_scale(key_raw)
    key_normed = key_raw * key_scale
    key = rotate(key_normed * key_gain_f, cosine, sine).astype(bf16)
    key = key.reshape(streams, length, HEAD_SIZE)
    stream_pos = jnp.arange(length, dtype=jnp.int32)
    segment = jnp.sum((stream_pos[None, :, None] >= starts[:, None, :]).astype(jnp.int32), axis=2)
    allowed = (stream_pos[:, None] >= stream_pos[None, :])[None] & (
        segment[:, :, None] == segment[:, None, :]
    )
    scores = jnp.einsum("bqgd,bkd->bgqk", query, key, preferred_element_type=f32) * score_scale
    scores = jnp.where(allowed[:, None], scores, MASK_FILL)
    row_max = jnp.max(scores, axis=-1, keepdims=True)
    weights = jnp.exp(scores - row_max)
    probs = weights / jnp.sum(weights, axis=-1, keepdims=True)
    probs_low = probs.astype(bf16)
    if not direct:
        mixed = jnp.einsum(
            "bgqk,bkd->bqgd", probs_low, value, preferred_element_type=f32
        ).astype(bf16)
    mixed_f = mixed.astype(f32).reshape(group_rows, group_heads, HEAD_SIZE)
    if direct:
        head_gate = gate_full.reshape(group_rows, group_heads, HEAD_SIZE)[:, :, :1]
    else:
        head_gate = jax.nn.sigmoid(mm(hidden_all, headgate_own))[:, :, None]
        gated = (mixed_f * head_gate).astype(bf16).reshape(group_rows, qcols)

    def parts(x):
        return x.astype(bf16).reshape(GROUP, rows, width)

    if not direct:
        middle, hidden_two = middle_step(
            parts(mm(gated, out_w)), tokens, ffn_gain_f, None, shards, 2
        )
        hidden_two = hidden_two.reshape(group_rows, width)

    gate_up = mm(hidden_two, ffn_w)
    gate_pre, up_proj = gate_up[:, :hidden], gate_up[:, hidden:]
    gate_sig = jax.nn.sigmoid(gate_pre)
    inner_act = (gate_pre * gate_sig * up_proj).astype(bf16)
    down_grad = mm_t(inner_act, cot_all).astype(bf16).reshape(zs, ys, brows, width)
    if direct:
        down_sum = PlaceSum(down_grad)
        down_sum.over_y()
    else:
        down_grad = scatter_dp(down_grad)
    grad_inner = mm_b(cot_all, down_w)
    grad_gate = (grad_inner * up_proj * gate_sig * (1.0 + gate_pre * (1.0 - gate_sig))).astype(bf16)
    grad_up = (grad_inner * gate_pre * gate_sig).astype(bf16)
    grad_gu = jnp.concatenate([grad_gate, grad_up], axis=1)
    ffn_grad = mm_t(hidden_two, grad_gu).astype(bf16)
    grad_gu, ffn_grad = lax.optimization_barrier((grad_gu, ffn_grad))
    if not direct:
        ffn_grad = scatter_dp(by_place(ffn_grad))
    grad_middle, ffn_gain_part, grad_branch, *ffn_first = middle_back(
        parts(mm_b(grad_gu, ffn_w)), middle, cotangent, ffn_gain_f,
        ffn_grad.reshape(zs, streams, ys, -1, 2 * hidden) if direct else None, shards, 3,
    )
    if direct:
        grad_branch, down_sum.far, down_sum.near, ffn_first = lax.optimization_barrier(
            (grad_branch, down_sum.far, down_sum.near, ffn_first[0])
        )
        down_z = down_sum.over_z()
        ffn_sum = PlaceSum(by_place(ffn_grad))
        ffn_sum.take(ffn_first.reshape(-1, 2 * hidden), None)
        ffn_z = ffn_sum.over_z()
        ffn_sum.near = ffn_sum.over_y_near()
    grad_branch = grad_branch.reshape(group_rows, width)
    layer_out = scatter_sum(parts(mm(inner_act, down_w)), middle, shards, 4)

    out_grad = mm_t(gated, grad_branch).astype(bf16).reshape(zs, ys, wrows, width)
    grad_gated = mm_b(grad_branch, out_w).reshape(group_rows, group_heads, HEAD_SIZE)
    grad_mixed = (grad_gated * head_gate).astype(bf16).reshape(
        streams, length, group_heads, HEAD_SIZE
    )
    gate_flat = head_gate[:, :, 0]
    grad_logit = (
        jnp.sum(grad_gated * mixed_f, axis=-1) * gate_flat * (1.0 - gate_flat)
    ).astype(bf16)
    grad_probs = jnp.einsum("bqgd,bkd->bgqk", grad_mixed, value, preferred_element_type=f32)
    row_delta = jnp.sum(probs * grad_probs, axis=-1, keepdims=True)
    grad_scores = (probs * (grad_probs - row_delta)).astype(bf16)
    grad_query = (
        jnp.einsum("bgqk,bkd->bqgd", grad_scores, key, preferred_element_type=f32) * score_scale
    ).astype(bf16)
    grad_key = (
        jnp.einsum("bgqk,bqgd->bkd", grad_scores, query, preferred_element_type=f32) * score_scale
    ).astype(bf16)
    grad_value = jnp.einsum(
        "bgqk,bqgd->bkd", probs_low, grad_mixed, preferred_element_type=f32
    ).astype(bf16)
    gqn = rotate_back(
        grad_query.astype(f32).reshape(group_rows, group_heads, HEAD_SIZE), cosine, sine
    )
    query_gain_part = jnp.sum(gqn * query_normed, axis=(0, 1))
    grad_query_raw = norm_back(gqn * query_gain_f, query_normed, query_scale).astype(bf16)
    gkn = rotate_back(grad_key.astype(f32).reshape(group_rows, 1, HEAD_SIZE), cosine, sine)
    key_gain_part = jnp.sum(gkn * key_normed, axis=(0, 1))
    grad_key_raw = norm_back(gkn * key_gain_f, key_normed, key_scale).astype(bf16)
    grad_qkv = jnp.concatenate(
        [
            grad_query_raw.reshape(group_rows, qcols),
            grad_key_raw.reshape(group_rows, kcols),
            grad_value.reshape(group_rows, kcols),
        ],
        axis=1,
    )
    qkv_grad = mm_t(hidden_all, grad_qkv).astype(bf16)
    if direct:
        qkv_grad, out_grad, grad_qkv, down_z = lax.optimization_barrier(
            (qkv_grad, out_grad, grad_qkv, down_z)
        )
        down_grad = down_sum.total(down_z)
        qkv_sum, out_sum = PlaceSum(by_place(qkv_grad)), PlaceSum(out_grad)
        qkv_sum.over_y()
        out_sum.over_y()
        qkv_z, out_z = qkv_sum.over_z(), out_sum.over_z()
        ffn_grad = ffn_sum.total(ffn_z)
        qkv_grad, out_grad = qkv_sum.total(qkv_z), out_sum.total(out_z)
    else:
        qkv_grad = scatter_dp(by_place(qkv_grad))
        out_grad = lax.dynamic_update_slice(
            jnp.zeros((width, width), bf16), out_grad.reshape(qcols, width), (tp * qcols, 0)
        )
        out_grad = lax.psum_scatter(out_grad, ALL, scatter_dimension=0, tiled=True)
    tokens_grad, attn_gain_part = tokens_back(
        parts(mm_b(grad_qkv, qkv_w) + mm_b(grad_logit, headgate_own)),
        tokens, grad_middle, attn_gain_f, shards, 5,
    )
    headgate_part = mm_t(hidden_all, grad_logit)
    headgate_part = lax.dynamic_update_slice(
        jnp.zeros((width, all_heads), f32), headgate_part, (0, head * group_heads)
    )

    small_sum = jnp.concatenate(
        [
            headgate_part.reshape(devices, hg),
            attn_gain_part.reshape(devices, wrows),
            ffn_gain_part.reshape(devices, wrows),
            query_gain_part.reshape(devices, gcols),
            key_gain_part.reshape(devices, gcols),
        ],
        axis=1,
    )
    small_sum = jnp.pad(small_sum, ((0, 0), (0, sums * 128 - count)))
    small_sum = small_sum.reshape(zs, streams, ys, shards, sums, 128)
    small_sum = small_sum.transpose(1, 3, 0, 2, 4, 5)
    small_sum = small_sum.reshape(GROUP, planes * sums, 128)

    gate_grad, up_grad = exchange_back(
        ffn_grad.reshape(GROUP, wrows, 2 * hidden), planes, shards, 6
    )
    query_grad, key_grad, value_grad, out_grad, small_sum = settle(
        qkv_grad.reshape(GROUP, wrows, qkv_cols), out_grad, small_sum, qcols, kcols, planes,
        direct, shards, 7,
    )
    small_sum = small_sum.reshape(-1)
    return (
        layer_out,
        tokens_grad,
        small_sum[hg : hg + wrows],
        small_sum[at : at + gcols],
        small_sum[at + gcols : at + 2 * gcols],
        query_grad,
        key_grad,
        value_grad,
        small_sum[:hg].reshape(wrows, all_heads),
        out_grad,
        small_sum[hg + wrows : hg + 2 * wrows],
        gate_grad,
        up_grad,
        down_grad.astype(f32),
    )


def solution(mesh):
    shards = mesh.shape["seq"]
    planes = (2, 2, 2) if shards == 4 and mesh.size == 32 else (1, GROUP // shards, -1)
    grouped = Mesh(mesh.devices.reshape(planes + (shards,)), ALL)
    two = P(ALL, None)
    one = P(ALL)
    return jax.shard_map(
        local,
        mesh=grouped,
        in_specs=(
            two, P(("zh", "st", "y"), None), one, one, one, two, two, two, two, two, one, two, two,
            two, two,
        ),
        out_specs=(two, two, one, one, one, two, two, two, two, two, one, two, two, two),
        check_vma=False,
    )
```

```python
import jax
import jax.numpy as jnp
import numpy as np
from jax import lax
from jax.experimental import pallas as pl
from jax.experimental.pallas import tpu as pltpu
from jax.sharding import Mesh, PartitionSpec as P

QUERY_HEADS = 16
KEY_VALUE_HEADS = 8
HEAD_SIZE = 128
GROUP = 8
NORM_EPS = 1e-06
ROPE_BASE = 1000000.0
MASK_FILL = -1e30

DP = ("zh", "y")
TP = ("st", "seq")
ALL = ("zh", "st", "y", "seq")
f32 = jnp.float32
bf16 = jnp.bfloat16


def rms_scale(vector):
    return lax.rsqrt(jnp.mean(vector * vector, axis=-1, keepdims=True) + NORM_EPS)


def rotary_tables(positions):
    half_width = HEAD_SIZE // 2
    exponent = jnp.arange(half_width, dtype=jnp.int32).astype(f32) * (2.0 / HEAD_SIZE)
    inverse = jnp.power(ROPE_BASE, -exponent)
    angles = positions.astype(f32)[:, None] * inverse[None, :]
    return (jnp.cos(angles)[:, None, :], jnp.sin(angles)[:, None, :])


def rotate(vector, cosine, sine):
    a, b = jnp.split(vector, 2, axis=-1)
    return jnp.concatenate([a * cosine - b * sine, b * cosine + a * sine], axis=-1)


def rotate_back(vector, cosine, sine):
    a, b = jnp.split(vector, 2, axis=-1)
    return jnp.concatenate([a * cosine + b * sine, b * cosine - a * sine], axis=-1)


def norm_back(grad, normed, scale):
    return scale * (grad - normed * jnp.mean(grad * normed, axis=-1, keepdims=True))


def mm(left, right):
    return jnp.dot(left, right, preferred_element_type=f32)


def mm_t(left, right):
    return lax.dot_general(left, right, (((0,), (0,)), ((), ())), preferred_element_type=f32)


def mm_b(left, right):
    return lax.dot_general(left, right, (((1,), (1,)), ((), ())), preferred_element_type=f32)


SWAP = [(0, 1), (1, 0)]


def over_dp(x):
    streams, shards = lax.axis_size("st"), lax.axis_size("seq")
    zs, ys = lax.axis_size("zh"), lax.axis_size("y")
    rows, columns = x.shape[1] * shards, x.shape[2]
    whole = lax.all_gather(x, DP, axis=0, tiled=False)
    whole = whole.reshape(zs, ys, streams, rows, columns).transpose(0, 2, 1, 3, 4)
    return whole.reshape(-1, columns)


def pick(x, axis, index):
    return lax.dynamic_index_in_dim(x, index, axis, keepdims=False)


def plus(left, right):
    return left.astype(f32) + right.astype(f32)


class PlaceSum:
    def __init__(self, x):
        self.x = x
        self.z, self.y = lax.axis_index("zh"), lax.axis_index("y")

    def piece(self, zp, yp):
        return pick(pick(self.x, 0, zp), 0, yp)

    def over_y(self):
        got = lax.ppermute(pick(self.x, 1, 1 - self.y), "y", SWAP)
        self.take(pick(got, 0, 1 - self.z), pick(got, 0, self.z))

    def over_y_near(self):
        return lax.ppermute(self.piece(self.z, 1 - self.y), "y", SWAP)

    def take(self, far, near):
        self.far, self.near = far, near

    def over_z(self):
        far = plus(self.piece(1 - self.z, self.y), self.far).astype(bf16)
        return lax.ppermute(far, "zh", SWAP)

    def total(self, got):
        return (plus(self.piece(self.z, self.y), self.near) + got.astype(f32)).astype(bf16)


def scatter_dp(x):
    zs, ys = x.shape[:2]
    return lax.psum_scatter(
        x.reshape((zs * ys,) + x.shape[2:]), DP, scatter_dimension=0, tiled=False
    )


def by_place(x):
    streams = lax.axis_size("st")
    zs, ys = lax.axis_size("zh"), lax.axis_size("y")
    columns = x.shape[1]
    x = x.reshape(zs, streams, ys, -1, columns).transpose(0, 2, 1, 3, 4)
    return x.reshape(zs, ys, -1, columns)


def pallas(body, out_shape, in_specs, out_specs, scratch, cid, micros, mib=40):
    return pl.pallas_call(
        body,
        out_shape=out_shape,
        in_specs=in_specs,
        out_specs=out_specs,
        scratch_shapes=scratch,
        compiler_params=pltpu.CompilerParams(
            collective_id=cid, has_side_effects=True, vmem_limit_bytes=mib * 1024 * 1024
        ),
        cost_estimate=pl.CostEstimate(
            flops=0, bytes_accessed=int(micros * 3.6e5), transcendentals=0
        ),
    )


ANY = pl.BlockSpec(memory_space=pl.ANY)
VMEM = pl.BlockSpec(memory_space=pltpu.VMEM)
DMA = pltpu.SemaphoreType.DMA


def remote(src, dst, send, recv, device):
    return pltpu.make_async_remote_copy(
        src_ref=src,
        dst_ref=dst,
        send_sem=send,
        recv_sem=recv,
        device_id=device,
        device_id_type=pl.DeviceIdType.MESH,
    )


class Place:
    def __init__(self, shards):
        self.shards = shards
        self.tp = lax.axis_index("st") * shards + lax.axis_index("seq")
        self.core = self.tp % 2
        self.ring = self.turn(self.tp // 2)

    def turn(self, place):
        if self.shards == GROUP:
            return place
        return place + (place // 2) * (1 - 2 * (place % 2))

    def head(self, index):
        if self.shards == GROUP:
            return index
        return index // 4 * 2 + index % 4 // 2 * 4 + index % 2

    def block(self, ahead, other=False):
        ring = self.ring
        if ahead == 1:
            ring = ring + 1 - 2 * (ring % 2)
        elif ahead == 3:
            ring = 3 - ring
        elif ahead == 2:
            ring = (ring + 2) % 4
        core = 1 - self.core if other else self.core
        return self.turn(ring) * 2 + core

    def device(self, index):
        return {"st": index // self.shards, "seq": index % self.shards}

    def dp_device(self, dp):
        ys = lax.axis_size("y")
        return {"zh": dp // ys, "y": dp % ys}

    def any_device(self, flat):
        ys, streams = lax.axis_size("y"), lax.axis_size("st")
        return {
            "zh": flat // (streams * ys * self.shards),
            "st": flat // (ys * self.shards) % streams,
            "y": flat // self.shards % ys,
            "seq": flat % self.shards,
        }

    def flat(self):
        ys, streams = lax.axis_size("y"), lax.axis_size("st")
        z, y = lax.axis_index("zh"), lax.axis_index("y")
        st, seq = lax.axis_index("st"), lax.axis_index("seq")
        return ((z * streams + st) * ys + y) * self.shards + seq

    def dp(self):
        return lax.axis_index("zh") * lax.axis_size("y") + lax.axis_index("y")

    def right(self):
        return self.device(self.block(1))

    def left(self):
        return self.device(self.block(3))

    def across(self):
        return {"y": 1 - lax.axis_index("y")}

    def partner(self):
        return self.device(self.block(0, True))


def greet(devices):
    barrier = pltpu.get_barrier_semaphore()
    for device in devices:
        pl.semaphore_signal(
            barrier, inc=1, device_id=device, device_id_type=pl.DeviceIdType.MESH
        )
    pl.semaphore_wait(barrier, len(devices))


class RingGather:
    SEMS = 11

    def __init__(self, place, own, out, send, recv, one_way=False):
        rows = out.shape[1]
        half = rows // 2
        first, second = pl.ds(0, half), pl.ds(half, half)
        me, near, next_, opposite = (place.block(i) for i in (0, 1, 3, 2))
        to_near, to_next, to_partner = place.device(near), place.device(next_), place.partner()

        def copy(index, src, block, part, device):
            return remote(src, out.at[block, part], send.at[index], recv.at[index], device)

        self.local = pltpu.make_async_copy(own, out.at[me], send.at[self.SEMS])
        self.next = [
            copy(0, own.at[first], me, first, to_next),
            copy(1, own.at[second], me, second, to_next),
        ]
        self.near = [
            copy(2, own.at[first], me, first, to_near),
            copy(3, own.at[second], me, second, to_near),
        ]
        self.mate = remote(own, out.at[me], send.at[4], recv.at[4], to_partner)
        self.on = [copy(5, out.at[next_, first], next_, first, to_near)]
        if one_way:
            self.on.append(copy(6, out.at[next_, second], next_, second, to_near))
        else:
            self.on.append(copy(6, out.at[near, second], near, second, to_next))
        self.one_way = one_way
        self.across = [
            remote(out.at[next_], out.at[next_], send.at[7], recv.at[7], to_partner),
            remote(out.at[near], out.at[near], send.at[8], recv.at[8], to_partner),
            copy(9, out.at[opposite, first], opposite, first, to_partner),
            copy(10, out.at[opposite, second], opposite, second, to_partner),
        ]

    def start(self):
        self.next[0].start()
        self.near[0 if self.one_way else 1].start()
        self.next[1].start()
        self.near[1 if self.one_way else 0].start()
        self.mate.start()
        self.local.start()

    def pass_on(self):
        self.next[0].wait_recv()
        self.on[0].start()
        if self.one_way:
            self.next[1].wait_recv()
        else:
            self.near[1].wait_recv()
        self.on[1].start()

    def step_across(self):
        if not self.one_way:
            self.next[1].wait_recv()
        self.across[0].start()
        self.near[0].wait_recv()
        if self.one_way:
            self.near[1].wait_recv()
        self.across[1].start()

    def step_far(self):
        self.on[0].wait_recv()
        self.across[2].start()
        self.on[1].wait_recv()
        self.across[3].start()

    def finish(self):
        self.mate.wait_recv()
        for c in self.across:
            c.wait_recv()
        for c in self.next + self.near + [self.mate] + self.on + self.across:
            c.wait_send()
        self.local.wait()

    def run(self):
        self.start()
        self.pass_on()
        self.step_across()
        self.step_far()
        self.finish()


def ring_scatter(place, x, pair, out, near, far, send, recv, emit, between=()):
    between = list(between) + [lambda: None] * 3
    rows = x.shape[1]
    half = rows // 2
    step = 32
    to_left, to_right, to_partner = place.left(), place.right(), place.partner()
    swaps = {}
    for q in (2, 1, 3, 0):
        swaps[q] = remote(
            x.at[place.block(q, True)], pair.at[q], send.at[q], recv.at[q], to_partner
        )
        swaps[q].start()

    def add(q, low, high, extra=None):
        block = place.block(q)
        for at in range(low, high, step):
            part = pl.ds(at, step)
            total = x[block, part].astype(f32) + pair[q, part].astype(f32)
            if extra is not None:
                total = total + far[extra, pl.ds(at - low, step)].astype(f32)
            out[q - 1, part] = total.astype(bf16)

    first, second = pl.ds(0, half), pl.ds(half, half)

    def send_to(index, q, part, dst, device):
        c = remote(out.at[q - 1, part], dst, send.at[index], recv.at[index], device)
        c.start()
        return c

    swaps[2].wait_recv()
    add(2, 0, half)
    a = send_to(4, 2, first, far.at[0], to_right)
    add(2, half, rows)
    b = send_to(5, 2, second, far.at[1], to_left)
    swaps[1].wait_recv()
    add(1, 0, half)
    c = send_to(6, 1, first, near.at[0, first], to_right)
    swaps[3].wait_recv()
    add(3, half, rows)
    d = send_to(7, 3, second, near.at[1, second], to_left)
    between[0]()
    a.wait_recv()
    add(3, 0, half, 0)
    e = send_to(8, 3, first, near.at[1, first], to_left)
    b.wait_recv()
    add(1, half, rows, 1)
    g = send_to(9, 1, second, near.at[0, second], to_right)
    between[1]()
    swaps[0].wait_recv()
    own = place.block(0)
    c.wait_recv()
    d.wait_recv()
    e.wait_recv()
    g.wait_recv()
    for at in range(0, rows, step):
        part = pl.ds(at, step)
        emit(
            part,
            (x[own, part].astype(f32) + pair[0, part].astype(f32))
            + (near[0, part].astype(f32) + near[1, part].astype(f32)),
        )
    for copy in list(swaps.values()) + [a, b, c, d, e, g]:
        copy.wait_send()


def scatter_scratch(rows, width):
    return [
        pltpu.VMEM((4, rows, width), bf16),
        pltpu.VMEM((3, rows, width), bf16),
        pltpu.VMEM((2, rows, width), bf16),
        pltpu.VMEM((2, rows // 2, width), bf16),
        DMA((10,)),
        DMA((10,)),
    ]


def gather_scratch():
    return [DMA((RingGather.SEMS + 1,)), DMA((RingGather.SEMS,))]


def scatter_sum(x, base, shards, cid):
    _, rows, width = x.shape

    def body(x_ref, base_ref, out_ref, pair, out, near, far, send, recv):
        place = Place(shards)
        greet([place.right(), place.left(), place.partner()])

        def emit(part, total):
            out_ref[part] = (base_ref[part] + total).astype(bf16)

        ring_scatter(place, x_ref, pair, out, near, far, send, recv, emit)

    return pallas(
        body, jax.ShapeDtypeStruct((rows, width), bf16), [VMEM, VMEM], VMEM,
        scatter_scratch(rows, width), cid, 25,
    )(x, base)


def middle_step(x, tokens, gain, carry, shards, cid):
    _, rows, width = x.shape
    carries = [] if carry is None else [carry]

    def body(x_ref, tok_ref, gain_ref, *refs):
        refs = list(refs)
        carry_ref = refs.pop(0) if carries else None
        mid_ref, all_ref = refs.pop(0), refs.pop(0)
        carry_out = refs.pop(0) if carries else None
        held, pair, out, near, far, send, recv, gsend, grecv, ysend, yrecv = refs
        place = Place(shards)
        greet(
            [place.right(), place.left(), place.partner()]
            + ([place.across()] if carries else [])
        )
        if carries:
            over = remote(carry_ref, carry_out, ysend, yrecv, place.across())
            over.start()

        def emit(part, total):
            middle = tok_ref[part].astype(f32) + total
            mid_ref[part] = middle
            held[part] = (middle * rms_scale(middle) * gain_ref[...]).astype(bf16)

        ring_scatter(place, x_ref, pair, out, near, far, send, recv, emit)
        RingGather(place, held, all_ref, gsend, grecv).run()
        if carries:
            over.wait()

    return pallas(
        body,
        [
            jax.ShapeDtypeStruct((rows, width), f32),
            jax.ShapeDtypeStruct((GROUP, rows, width), bf16),
        ]
        + [jax.ShapeDtypeStruct(c.shape, c.dtype) for c in carries],
        [VMEM, VMEM, VMEM] + [ANY] * len(carries),
        [VMEM, ANY] + [ANY] * len(carries),
        [pltpu.VMEM((rows, width), bf16)] + scatter_scratch(rows, width) + gather_scratch()
        + [DMA, DMA],
        cid,
        50,
    )(x, tokens, gain, *carries)


def middle_back(x, middle, cotangent, gain, grads, shards, cid):
    _, rows, width = x.shape
    carries = [] if grads is None else [grads]

    def body(x_ref, mid_ref, cot_ref, gain_ref, *refs):
        refs = list(refs)
        grads_ref = refs.pop(0) if carries else None
        dm_ref, part_ref, all_ref = refs.pop(0), refs.pop(0), refs.pop(0)
        grads_out = refs.pop(0) if carries else None
        held, pair, out, near, far, send, recv, gsend, grecv, ysend, yrecv = refs
        place = Place(shards)
        greet(
            [place.right(), place.left(), place.partner()]
            + ([place.across()] if carries else [])
        )
        if carries:
            z, y = lax.axis_index("zh"), lax.axis_index("y")
            over = [
                remote(
                    grads_ref.at[1 - z, st, 1 - y], grads_out.at[st], ysend.at[st],
                    yrecv.at[st], place.across(),
                )
                for st in range(grads.shape[1])
            ]
            for c in over:
                c.start()
        part_ref[...] = jnp.zeros_like(part_ref)

        def emit(part, total):
            middle = mid_ref[part]
            scale = rms_scale(middle)
            normed = middle * scale
            part_ref[...] += jnp.sum(total * normed, axis=0, keepdims=True)
            dm = cot_ref[part].astype(f32) + norm_back(total * gain_ref[...], normed, scale)
            dm_ref[part] = dm
            held[part] = dm.astype(bf16)

        ring_scatter(place, x_ref, pair, out, near, far, send, recv, emit)
        RingGather(place, held, all_ref, gsend, grecv).run()
        if carries:
            for c in over:
                c.wait()

    return pallas(
        body,
        [
            jax.ShapeDtypeStruct((rows, width), f32),
            jax.ShapeDtypeStruct((1, width), f32),
            jax.ShapeDtypeStruct((GROUP, rows, width), bf16),
        ]
        + [jax.ShapeDtypeStruct((c.shape[1],) + c.shape[3:], c.dtype) for c in carries],
        [VMEM, VMEM, VMEM, VMEM] + [ANY] * len(carries),
        [VMEM, VMEM, ANY] + [ANY] * len(carries),
        [pltpu.VMEM((rows, width), bf16)] + scatter_scratch(rows, width) + gather_scratch()
        + [DMA((2,)), DMA((2,))],
        cid,
        50,
    )(x, middle, cotangent, gain, *carries)


def tokens_back(x, tokens, dm, gain, shards, cid):
    _, rows, width = x.shape

    def body(
        x_ref, tok_ref, dm_ref, gain_ref, grad_ref, part_ref, pair, out, near, far, send, recv
    ):
        place = Place(shards)
        greet([place.right(), place.left(), place.partner()])
        part_ref[...] = jnp.zeros_like(part_ref)

        def emit(part, total):
            tok = tok_ref[part].astype(f32)
            scale = rms_scale(tok)
            normed = tok * scale
            part_ref[...] += jnp.sum(total * normed, axis=0, keepdims=True)
            grad_ref[part] = (
                dm_ref[part] + norm_back(total * gain_ref[...], normed, scale)
            ).astype(bf16)

        ring_scatter(place, x_ref, pair, out, near, far, send, recv, emit)

    return pallas(
        body,
        (
            jax.ShapeDtypeStruct((rows, width), bf16),
            jax.ShapeDtypeStruct((1, width), f32),
        ),
        [VMEM, VMEM, VMEM, VMEM],
        (VMEM, VMEM),
        scatter_scratch(rows, width),
        cid,
        25,
    )(x, tokens, dm, gain)


class Exchange:
    SEMS = GROUP

    def __init__(self, place, x, out, send, recv):
        self.local = pltpu.make_async_copy(x.at[place.tp], out.at[place.tp], send.at[0])
        self.copies = []
        for k in range(1, GROUP):
            peer = (place.tp + k) % GROUP
            self.copies.append(
                remote(x.at[peer], out.at[place.tp], send.at[k], recv.at[k], place.device(peer))
            )

    def start(self):
        for c in self.copies:
            c.start()
        self.local.start()

    def finish(self):
        for c in self.copies:
            c.wait_recv()
        for c in self.copies:
            c.wait_send()
        self.local.wait()


def group_peers(place):
    return [place.device((place.tp + k) % GROUP) for k in range(1, GROUP)]


def columns_of(dp, t, shards):
    ys, streams = lax.axis_size("y"), lax.axis_size("st")
    z, y = dp // ys, dp % ys
    return ((z * streams + t // shards) * ys + y) * shards + t % shards


def exchange_back(x, planes, shards, cid):
    _, wrows, both = x.shape
    hidden = both // 2
    brows = hidden // planes
    step = min(wrows, 32)

    def body(x_ref, gate_ref, up_ref, got, send, recv):
        place = Place(shards)
        greet(group_peers(place))
        run = Exchange(place, x_ref, got, send, recv)
        run.start()
        run.finish()
        for t in range(GROUP):
            for dp in range(planes):
                flat = columns_of(dp, t, shards)
                for m, out in enumerate((gate_ref, up_ref)):
                    for at in range(0, wrows, step):
                        part = pl.ds(at, step)
                        out[part, flat * brows : (flat + 1) * brows] = got[
                            t, part, m * hidden + dp * brows : m * hidden + (dp + 1) * brows
                        ].astype(f32)

    shape = jax.ShapeDtypeStruct((wrows, hidden * GROUP), f32)
    return pallas(
        body, (shape, shape), [VMEM], (VMEM, VMEM),
        [pltpu.VMEM(x.shape, bf16), DMA((GROUP,)), DMA((GROUP,))], cid, 25,
    )(x)


class PlaceGather:
    SEMS = 5

    def __init__(self, own, out, send, recv, halves):
        z, y = lax.axis_index("zh"), lax.axis_index("y")
        dp, across = z * 2 + y, (1 - z) * 2 + y
        to_z, to_y = {"zh": 1 - z}, {"y": 1 - y}

        def copy(index, src, slot, part, device):
            return remote(
                src.at[part], out.at[slot, part], send.at[index], recv.at[index], device
            )

        first, second = halves
        self.local = pltpu.make_async_copy(own, out.at[dp], send.at[send.shape[0] - 1])
        self.z = [copy(0, own, dp, first, to_z), copy(1, own, dp, second, to_z)]
        self.y = [
            remote(own, out.at[dp], send.at[2], recv.at[2], to_y),
            copy(3, out.at[across], across, first, to_y),
            copy(4, out.at[across], across, second, to_y),
        ]

    def forward(self, half):
        self.z[half].wait_recv()
        self.y[1 + half].start()

    def finish(self):
        for c in self.y:
            c.wait_recv()
        for c in self.z + self.y:
            c.wait_send()


def front(tokens, cotangent, small, w_out, w_query, key_weight, value_weight, w_gate, w_up,
          w_down, planes, direct, shards, cid):
    rows, width = tokens.shape
    wrows = w_out.shape[0]
    srows, scols = small.shape
    brows = w_down.shape[0]
    hidden = brows * planes
    parts = [w_query.shape[1] // GROUP, key_weight.shape[1] // GROUP, value_weight.shape[1] // GROUP]
    qkv = sum(parts)
    slots = planes if direct else 1
    inputs = [tokens, cotangent, w_query, key_weight, value_weight, w_gate, w_up]
    if direct:
        inputs += [w_down, w_out]

    def body(*refs):
        refs = list(refs)

        def take(count):
            taken = refs[:count]
            del refs[:count]
            return taken

        small_ref, = take(1)
        sources = take(len(inputs))
        tok_all, cot_all, small_all, attn_all, ffn_all = take(5)
        down_all, wout_all = take(2) if direct else (None, None)
        held = take(len(inputs))
        (pack, isem, tsend, trecv, csend, crecv, ssend, srecv, psend, precv, fsend, frecv, asend,
         arecv, aasend, aarecv, dsend, drecv, wsend, wrecv) = refs
        place = Place(shards)
        tp, dp, flat = place.tp, place.dp(), place.flat()

        loads = [
            pltpu.make_async_copy(s, h, isem.at[i]) for i, (s, h) in enumerate(zip(sources, held))
        ]
        for i in (2, 3, 4, 0, 5, 6) + ((7, 8) if direct else ()) + (1,):
            loads[i].start()
        tok_ref, cot_ref, wq_ref, wk_ref, wv_ref, wg_ref, wu_ref = held[:7]

        barrier = pltpu.get_barrier_semaphore()

        def signal(device):
            pl.semaphore_signal(
                barrier, inc=1, device_id=device, device_id_type=pl.DeviceIdType.MESH
            )

        for device in group_peers(place):
            signal(device)
        for k in range(1, planes):
            signal(place.dp_device((dp + k) % planes))
        if direct:
            high, low = lax.axis_index("zh"), lax.axis_index("st")
            y, seq = lax.axis_index("y"), lax.axis_index("seq")
            to_seq = high * 2 + y
            from_high, from_y = seq // 2, seq % 2
            selfish = seq == to_seq
            mine = y == from_y
            for j in range(4):

                @pl.when(jnp.logical_and(mine, (from_high * 4 + j) != (high * 4 + seq)))
                def _():
                    signal({"zh": from_high, "seq": jnp.int32(j)})

            pl.semaphore_wait(
                barrier, GROUP - 1 + planes - 1 + 2 - selfish.astype(jnp.int32)
            )
        else:
            pl.semaphore_wait(barrier, GROUP - 1 + planes - 1)

        here = dp if direct else 0
        attn = []
        at = 0
        for i, (ref, cols) in enumerate(zip((wq_ref, wk_ref, wv_ref), parts)):
            loads[2 + i].wait()
            for k in range(GROUP):
                peer = (tp + k) % GROUP
                column = place.head(peer) * cols
                src = ref.at[:, pl.ds(pl.multiple_of(column, cols), cols)]
                dst = attn_all.at[here, tp, :, pl.ds(at, cols)]
                sem = i * GROUP + k
                if k == 0:
                    attn.append(pltpu.make_async_copy(src, dst, asend.at[sem]))
                else:
                    attn.append(
                        remote(src, dst, asend.at[sem], arecv.at[sem], place.device(peer))
                    )
                attn[-1].start()
            at += cols

        small_own = pltpu.make_async_copy(small_ref, small_all.at[tp, dp], ssend.at[0])
        small_own.start()
        small_dp = []
        for k in range(1, planes):
            small_dp.append(
                remote(
                    small_ref, small_all.at[tp, dp], ssend.at[k], srecv.at[k],
                    place.dp_device((dp + k) % planes),
                )
            )
            small_dp[-1].start()

        if direct:
            down_ref, wout_ref = held[7:]
            loads[7].wait()
            half = brows // 2
            down_dp = PlaceGather(
                down_ref, down_all, dsend, drecv, (pl.ds(0, half), pl.ds(half, half))
            )
            down_dp.z[0].start()
        loads[0].wait()
        tok = RingGather(place, tok_ref, tok_all, tsend, trecv, direct)
        tok.start()

        loads[5].wait()
        loads[6].wait()
        for t in range(GROUP):
            for d in range(planes):
                column = columns_of(d, t, shards)
                for m, ref in enumerate((wg_ref, wu_ref)):
                    lane = m * hidden + d * brows
                    pack[t, :, lane : lane + brows] = ref[:, column * brows : (column + 1) * brows]
        ffn = Exchange(place, pack, ffn_all, fsend, frecv)
        ffn.start()

        if direct:
            down_dp.y[0].start()
            down_dp.local.start()
            loads[8].wait()
            wout_copies = [
                remote(
                    wout_ref, wout_all.at[seq], wsend.at[k], wrecv.at[seq],
                    {"zh": z, "seq": to_seq},
                )
                for k, z in enumerate((high, 1 - high))
            ]
            wout_own = pltpu.make_async_copy(wout_ref, wout_all.at[seq], wsend.at[0])
            wout_over = remote(
                wout_all, wout_all, wsend.at[2], wrecv.at[4], place.across()
            )

            @pl.when(selfish)
            def _():
                wout_own.start()

            @pl.when(jnp.logical_not(selfish))
            def _():
                wout_copies[0].start()

            wout_copies[1].start()

        for i in range(3 * GROUP):
            if i % GROUP == 0:
                attn[i].wait()
            else:
                attn[i].wait_recv()
        if direct:
            half = GROUP // 2
            attn_dp = PlaceGather(
                attn_all.at[dp], attn_all, aasend, aarecv, (pl.ds(0, half), pl.ds(half, half))
            )
            attn_dp.z[0].start()
            attn_dp.y[0].start()
            attn_dp.z[1].start()
            down_dp.z[1].start()

        small_own.wait()
        for c in small_dp:
            c.wait_recv()
        small_tp = []
        for k in range(1, GROUP):
            small_tp.append(
                remote(
                    small_all.at[tp], small_all.at[tp], psend.at[k], precv.at[k],
                    place.device((tp + k) % GROUP),
                )
            )
            small_tp[-1].start()

        loads[1].wait()
        cot = RingGather(place, cot_ref, cot_all, csend, crecv, direct)
        tok.pass_on()
        cot.start()
        tok.step_across()
        if direct:
            down_dp.forward(0)

            @pl.when(mine)
            def _():
                for j in range(4):

                    @pl.when((from_high * 4 + j) != (high * 4 + seq))
                    def _():
                        remote(
                            wout_ref, wout_all.at[j], wsend.at[0], wrecv.at[j], place.across()
                        ).wait_recv()

                @pl.when(selfish)
                def _():
                    wout_own.wait()

                wout_over.start()

            attn_dp.forward(0)
        tok.step_far()
        cot.pass_on()
        if direct:
            attn_dp.forward(1)
        cot.step_across()
        if direct:
            down_dp.forward(1)
        cot.step_far()
        tok.finish()
        cot.finish()
        ffn.finish()
        for i in range(3 * GROUP):
            if i % GROUP:
                attn[i].wait_send()
        for c in small_tp:
            c.wait_recv()
        for c in small_dp + small_tp:
            c.wait_send()
        if direct:
            attn_dp.finish()
            down_dp.finish()
            down_dp.local.wait()

            @pl.when(jnp.logical_not(selfish))
            def _():
                wout_copies[0].wait_send()

            wout_copies[1].wait_send()

            @pl.when(mine)
            def _():
                wout_over.wait_send()

            @pl.when(jnp.logical_not(mine))
            def _():
                wout_over.wait_recv()

    shapes = [
        jax.ShapeDtypeStruct((GROUP, rows, width), bf16),
        jax.ShapeDtypeStruct((GROUP, rows, width), bf16),
        jax.ShapeDtypeStruct((GROUP, planes, srows, scols), bf16),
        jax.ShapeDtypeStruct((slots, GROUP, wrows, qkv), bf16),
        jax.ShapeDtypeStruct((GROUP, wrows, 2 * hidden), bf16),
    ]
    if direct:
        shapes += [
            jax.ShapeDtypeStruct((planes, brows, width), bf16),
            jax.ShapeDtypeStruct((planes, wrows, width), bf16),
        ]
    return pallas(
        body,
        shapes,
        [VMEM] + [ANY] * len(inputs),
        [ANY, ANY, VMEM] + [ANY] * (len(shapes) - 3),
        [pltpu.VMEM(x.shape, x.dtype) for x in inputs]
        + [pltpu.VMEM((GROUP, wrows, 2 * hidden), bf16), DMA((len(inputs),))]
        + gather_scratch() + gather_scratch()
        + [
            DMA((planes,)), DMA((planes,)), DMA((GROUP,)), DMA((GROUP,)),
            DMA((GROUP,)), DMA((GROUP,)), DMA((3 * GROUP,)), DMA((3 * GROUP,)),
            DMA((PlaceGather.SEMS,)), DMA((PlaceGather.SEMS,)),
            DMA((PlaceGather.SEMS + 1,)), DMA((PlaceGather.SEMS,)), DMA((3,)), DMA((5,)),
        ],
        cid,
        60,
    )(small, *inputs)


class Spread:
    def __init__(self, own, piece, relay, send, recv):
        z, low, y = (lax.axis_index(a) for a in ("zh", "st", "y"))
        to_z, to_y = {"zh": 1 - z}, {"y": 1 - y}
        beside, middle = {"st": 1 - low}, {"zh": 1 - z, "st": 1 - low}
        self.outer = z == low
        self.inner = z != low
        count = relay.shape[0]
        self.direct, self.toward, self.onward, self.y, self.on = [], [], [], [], []
        for h in range(count):
            at_y, at_on, at_more = count + h, 2 * count + h, 3 * count + h
            here, there = piece(z, h, y), piece(1 - z, h, y)
            self.direct.append(remote(own(h), here, send.at[h], recv.at[h], to_z))
            self.toward.append(
                remote(own(h), relay.at[h], send.at[h], recv.at[at_more], beside)
            )
            self.onward.append(
                remote(relay.at[h], here, send.at[at_more], recv.at[h], middle)
            )
            self.y.append(remote(own(h), here, send.at[at_y], recv.at[at_y], to_y))
            self.on.append(remote(there, there, send.at[at_on], recv.at[at_on], to_y))

    def start_z(self, first=0, last=None):
        @pl.when(self.outer)
        def _():
            for c in self.toward[first:last]:
                c.start()

        @pl.when(self.inner)
        def _():
            for c in self.direct[first:last]:
                c.start()

    def start_y(self):
        for c in self.y:
            c.start()

    def relay(self, half):
        @pl.when(self.inner)
        def _():
            self.toward[half].wait_recv()
            self.onward[half].start()

    def forward(self, half):
        self.direct[half].wait_recv()
        self.on[half].start()

    def finish(self):
        for c in self.y + self.on:
            c.wait_recv()
        for c in self.direct + self.y + self.on:
            c.wait_send()

        @pl.when(self.inner)
        def _():
            for c in self.onward:
                c.wait_send()


def rope_constants(length):
    exponent = np.arange(HEAD_SIZE // 2, dtype=np.float32) * np.float32(2.0 / HEAD_SIZE)
    inverse = np.power(np.float32(ROPE_BASE), -exponent).astype(np.float32)
    angles = np.arange(length, dtype=np.float32)[:, None] * inverse[None, :]
    cosine, sine = np.cos(angles.astype(np.float64)), np.sin(angles.astype(np.float64))
    return (
        jnp.asarray(np.concatenate([cosine, cosine], axis=1).astype(np.float32)),
        jnp.asarray(np.concatenate([-sine, sine], axis=1).astype(np.float32)),
    )


def document_mask(row, docs, low, count, keys):
    at_row = low + lax.broadcasted_iota(jnp.int32, (count, 1), 0)
    at_col = lax.broadcasted_iota(jnp.int32, (1, keys), 1)
    seg_row = jnp.zeros((count, 1), jnp.int32)
    seg_col = jnp.zeros((1, keys), jnp.int32)
    for d in range(docs):
        start = (row[:, d : d + 1] * 128.0 + row[:, docs + d : docs + d + 1]).astype(jnp.int32)
        seg_row = seg_row + jnp.where(at_row >= start, 1, 0)
        seg_col = seg_col + jnp.where(at_col >= start, 1, 0)
    return jnp.logical_and(at_row >= at_col, seg_row == seg_col)


def forward_pass(tokens, cotangent, small, w_out, w_query, key_weight, value_weight, w_gate,
                 w_up, w_down, docs, shards, cid):
    rows, width = tokens.shape
    wrows = w_out.shape[0]
    brows = w_down.shape[0]
    planes = 4
    hidden = brows * planes
    parts = [w_query.shape[1] // GROUP, key_weight.shape[1] // GROUP, value_weight.shape[1] // GROUP]
    qkv = sum(parts)
    qcols = parts[0]
    heads = qcols // HEAD_SIZE
    group_rows = rows * GROUP
    length = rows * shards
    streams = GROUP // shards
    gain_rows = width // 128
    grows = -(-(2 * gain_rows + 3) // 16) * 16
    srows = wrows + grows
    gcols = HEAD_SIZE // (planes * GROUP)
    cosine, sine = rope_constants(length)
    inputs = [tokens, cotangent, w_query, key_weight, value_weight, w_gate, w_up, w_down, w_out]
    score_scale = HEAD_SIZE ** (-0.5)

    def body(
        raw_ref, cos_ref, sin_ref, s0, s1, s2, s3, s4, s5, s6, s7, s8,
        cot_all, ffn_all, down_all, h1_out, h2_all, small_all, gains_ref, attn_all, wout_all,
        qkv_ref, low_ref, gate_ref, mixed_ref, gated_ref, mid_ref, hg, starts_ref,
        h0, h1, h2, h3, h4, h5, h6, h7, h8, small_ref, pack, attn_relay, ffn_relay, down_relay, tok_all, hid, partial, held_two, isem, osem,
        tsend, trecv, csend, crecv, gsend, grecv, ssend, srecv, psend, precv, fsend, frecv, asend,
        arecv, aasend, aarecv, ffsend, ffrecv, dsend, drecv, wsend, wrecv, pair, out, near, far,
        rsend, rrecv,
    ):
        sources = [s0, s1, s2, s3, s4, s5, s6, s7, s8]
        held = [h0, h1, h2, h3, h4, h5, h6, h7, h8]
        place = Place(shards)
        tp, dp = place.tp, place.dp()
        high, low = lax.axis_index("zh"), lax.axis_index("st")
        y, seq = lax.axis_index("y"), lax.axis_index("seq")
        loads = [
            pltpu.make_async_copy(s, h, isem.at[i]) for i, (s, h) in enumerate(zip(sources, held))
        ]
        for i in (2, 3, 4, 8, 0, 5, 6, 7, 1):
            loads[i].start()
        tok_ref, cot_ref, wq_ref, wk_ref, wv_ref, wg_ref, wu_ref, down_ref, wout_ref = held

        barrier = pltpu.get_barrier_semaphore()

        def signal(device):
            pl.semaphore_signal(
                barrier, inc=1, device_id=device, device_id_type=pl.DeviceIdType.MESH
            )

        for device in group_peers(place):
            signal(device)
        for k in range(1, planes):
            signal(place.dp_device((dp + k) % planes))
        to_seq = high * 2 + y
        from_high, from_y = seq // 2, seq % 2
        selfish = seq == to_seq
        mine = y == from_y
        for j in range(4):

            @pl.when(jnp.logical_and(mine, (from_high * 4 + j) != (high * 4 + seq)))
            def _():
                signal({"zh": from_high, "seq": jnp.int32(j)})

        inner = high != low

        @pl.when(inner)
        def _():
            signal({"zh": 1 - high, "st": 1 - low})

        pl.semaphore_wait(
            barrier,
            GROUP - 1 + planes - 1 + 2 - selfish.astype(jnp.int32) + inner.astype(jnp.int32),
        )

        attn = []
        at = 0
        for i, (ref, cols) in enumerate(zip((wq_ref, wk_ref, wv_ref), parts)):
            loads[2 + i].wait()
            for k in range(GROUP):
                peer = (tp + k) % GROUP
                column = place.head(peer) * cols
                src = ref.at[:, pl.ds(pl.multiple_of(column, cols), cols)]
                dst = attn_all.at[high, low, y, pl.ds(seq * wrows, wrows), pl.ds(at, cols)]
                sem = i * GROUP + k
                if k == 0:
                    attn.append(pltpu.make_async_copy(src, dst, asend.at[sem]))
                else:
                    attn.append(
                        remote(src, dst, asend.at[sem], arecv.at[sem], place.device(peer))
                    )
                attn[-1].start()
            at += cols

        small_ref[0:wrows] = raw_ref[0:wrows]
        flat = place.flat()
        block = raw_ref[wrows : wrows + 16].astype(f32)
        row_of = lax.broadcasted_iota(jnp.int32, (grows, 128), 0)
        placed = jnp.zeros((grows, 128), f32)
        per_row = 128 // wrows
        for i, (at, shift) in enumerate(
            (
                (flat // per_row, flat % per_row * wrows),
                (gain_rows + flat // per_row, flat % per_row * wrows),
                (2 * gain_rows, flat * gcols),
                (2 * gain_rows + 1, flat * gcols),
                (2 * gain_rows + 2, 0),
            )
        ):
            row = jnp.broadcast_to(block[i : i + 1], (grows, 128))
            placed = jnp.where(row_of == at, pltpu.roll(row, shift, 1), placed)
        small_ref[wrows:] = placed.astype(bf16)
        small_own = pltpu.make_async_copy(small_ref, small_all.at[tp, dp], ssend.at[0])
        small_own.start()
        small_dp = []
        for k in range(1, planes):
            small_dp.append(
                remote(
                    small_ref, small_all.at[tp, dp], ssend.at[k], srecv.at[k],
                    place.dp_device((dp + k) % planes),
                )
            )
            small_dp[-1].start()

        loads[5].wait()
        loads[6].wait()
        for t in range(GROUP):
            for d in range(planes):
                column = columns_of(d, t, shards)
                for m, ref in enumerate((wg_ref, wu_ref)):
                    lane = m * hidden + d * brows
                    pack[t, :, lane : lane + brows] = ref[:, column * brows : (column + 1) * brows]

        def arrived(copies):
            for i, c in enumerate(copies):
                if i % GROUP == 0:
                    c.wait()
                else:
                    c.wait_recv()

        arrived(attn)

        def attn_piece(zp, half, yp):
            return attn_all.at[zp, half, yp]

        attn_dp = Spread(
            lambda half: attn_piece(high, half, y), attn_piece, attn_relay, aasend, aarecv
        )
        attn_dp.start_z()
        attn_dp.start_y()
        loads[0].wait()
        tok = RingGather(place, tok_ref, tok_all, tsend, trecv, True)
        tok.start()
        small_own.wait()
        for c in small_dp:
            c.wait_recv()
        small_tp = []
        for k in range(1, GROUP):
            small_tp.append(
                remote(
                    small_all.at[tp], small_all.at[tp], psend.at[k], precv.at[k],
                    place.device((tp + k) % GROUP),
                )
            )
            small_tp[-1].start()
        attn_dp.relay(0)
        attn_dp.relay(1)

        loads[7].wait()
        half_rows = brows // 2

        def down_piece(zp, half, yp):
            return down_all.at[zp * 2 + yp, pl.ds(half * half_rows, half_rows)]

        down_dp = Spread(
            lambda half: down_ref.at[pl.ds(half * half_rows, half_rows)], down_piece, down_relay,
            dsend, drecv,
        )
        down_own = pltpu.make_async_copy(down_ref, down_all.at[dp], dsend.at[8])
        down_own.start()
        down_dp.start_z()
        tok.pass_on()
        ffn_dst = ffn_all.at[high, low, y, pl.ds(seq * wrows, wrows)]
        ffn = [pltpu.make_async_copy(pack.at[tp], ffn_dst, fsend.at[0])]
        for k, (ahead, other) in enumerate(
            ((3, False), (3, True), (0, True), (1, False), (1, True), (2, False), (2, True))
        ):
            peer = place.block(ahead, other)
            ffn.append(
                remote(
                    pack.at[peer], ffn_dst, fsend.at[k + 1], frecv.at[k + 1], place.device(peer)
                )
            )
        for c in ffn[:4]:
            c.start()
        loads[8].wait()
        wout_copies = [
            remote(
                wout_ref, wout_all.at[seq], wsend.at[k], wrecv.at[seq], {"zh": z, "seq": to_seq}
            )
            for k, z in enumerate((high, 1 - high))
        ]
        wout_own = pltpu.make_async_copy(wout_ref, wout_all.at[seq], wsend.at[0])
        wout_over = remote(wout_all, wout_all, wsend.at[2], wrecv.at[4], place.across())
        wout_copies[1].start()

        @pl.when(selfish)
        def _():
            wout_own.start()

        @pl.when(jnp.logical_not(selfish))
        def _():
            wout_copies[0].start()

        attn_dp.forward(0)
        attn_dp.forward(1)
        down_dp.start_y()
        tok.step_across()
        down_dp.relay(0)
        tok.step_far()
        for c in ffn[4:]:
            c.start()

        @pl.when(mine)
        def _():
            for j in range(4):

                @pl.when((from_high * 4 + j) != (high * 4 + seq))
                def _():
                    remote(
                        wout_ref, wout_all.at[j], wsend.at[0], wrecv.at[j], place.across()
                    ).wait_recv()

            @pl.when(selfish)
            def _():
                wout_own.wait()

            wout_over.start()

        for c in small_tp:
            c.wait_recv()
        gains = jnp.zeros((grows, 128), f32)
        for t in range(GROUP):
            for d in range(planes):
                gains = gains + small_all[t, d, pl.ds(wrows, grows)].astype(f32)
                flat = columns_of(d, t, shards)
                hg[flat * wrows : (flat + 1) * wrows] = small_all[t, d, pl.ds(0, wrows)]
        gains_ref[...] = gains
        gain_one = jnp.concatenate([gains[i : i + 1] for i in range(gain_rows)], axis=1)
        gain_two = jnp.concatenate(
            [gains[gain_rows + i : gain_rows + i + 1] for i in range(gain_rows)], axis=1
        )
        query_gain = gains[2 * gain_rows : 2 * gain_rows + 1]
        key_gain = gains[2 * gain_rows + 1 : 2 * gain_rows + 2]
        starts = []
        for st in range(streams):
            block = small_all[st * shards, dp, pl.ds(wrows, grows)].astype(f32)
            starts.append(block[2 * gain_rows + 2 : 2 * gain_rows + 3])
            starts_ref[st : st + 1] = starts[st]

        tok.finish()
        step = 32

        def norm(i, _):
            block = i // (rows // step)
            inner = pl.ds(pl.multiple_of(i % (rows // step) * step, step), step)
            value = tok_all[block, inner].astype(f32)
            hid[block, inner] = (value * rms_scale(value) * gain_one).astype(bf16)
            return 0

        lax.fori_loop(0, group_rows // step, norm, 0)
        save = pltpu.make_async_copy(hid, h1_out, osem)
        save.start()
        down_dp.relay(1)
        attn_dp.finish()
        weight = attn_all[...].reshape(width, qkv)
        head = place.head(tp)
        lanes = lax.broadcasted_iota(jnp.int32, (1, 128), 1)

        def rotary(x, gain, s):
            scaled = x * rms_scale(x) * gain
            return (
                scaled * cos_ref[...] + pltpu.roll(scaled, HEAD_SIZE // 2, 1) * sin_ref[...]
            ).astype(bf16)

        for s in range(streams):
            part = pl.ds(s * length, length)
            normed = hid[s * shards : (s + 1) * shards].reshape(length, width)
            raw = jnp.dot(normed, weight, preferred_element_type=f32)
            qkv_ref[part] = raw
            logit = jnp.dot(normed, hg[...], preferred_element_type=f32)
            for g in range(heads):
                at = g * HEAD_SIZE
                low_ref[part, at : at + HEAD_SIZE] = rotary(
                    raw[:, at : at + HEAD_SIZE], query_gain, s
                )
                own = jnp.sum(
                    jnp.where(lanes == head * heads + g, logit, 0.0), axis=1, keepdims=True
                )
                gate_ref[part, at : at + HEAD_SIZE] = jnp.broadcast_to(
                    jax.nn.sigmoid(own), (length, HEAD_SIZE)
                )
            low_ref[part, qcols : qcols + HEAD_SIZE] = rotary(
                raw[:, qcols : qcols + HEAD_SIZE], key_gain, s
            )
            low_ref[part, qcols + HEAD_SIZE :] = raw[:, qcols + HEAD_SIZE :].astype(bf16)
        arrived(ffn)

        quarter = shards * wrows // 2

        def ffn_piece(zp, half, yp):
            return ffn_all.at[zp, half // 2, yp, pl.ds(half % 2 * quarter, quarter)]

        ffn_dp = Spread(
            lambda half: ffn_piece(high, half, y), ffn_piece, ffn_relay, ffsend, ffrecv
        )
        ffn_dp.start_z(0, 2)
        ffn_dp.start_y()
        block = 128
        for s in range(streams):
            base = s * length
            for r in range(0, length, block):
                keys = r + block
                allowed = document_mask(starts[s], docs, r, block, keys)
                key = low_ref[pl.ds(base, keys), qcols : qcols + HEAD_SIZE]
                value = low_ref[pl.ds(base, keys), qcols + HEAD_SIZE :]
                part = pl.ds(base + r, block)
                for g in range(heads):
                    at = g * HEAD_SIZE
                    scores = (
                        lax.dot_general(
                            low_ref[part, at : at + HEAD_SIZE], key, (((1,), (1,)), ((), ())),
                            preferred_element_type=f32,
                        )
                        * score_scale
                    )
                    scores = jnp.where(allowed, scores, MASK_FILL)
                    weights = jnp.exp(scores - jnp.max(scores, axis=1, keepdims=True))
                    probs = weights / jnp.sum(weights, axis=1, keepdims=True)
                    mixed = jnp.dot(
                        probs.astype(bf16), value, preferred_element_type=f32
                    ).astype(bf16)
                    mixed_ref[part, at : at + HEAD_SIZE] = mixed
                    gated_ref[part, at : at + HEAD_SIZE] = (
                        mixed.astype(f32) * gate_ref[part, at : at + HEAD_SIZE]
                    ).astype(bf16)

        @pl.when(jnp.logical_not(mine))
        def _():
            wout_over.wait_recv()

        wide = 512
        for s in range(streams):
            for c in range(0, width, wide):
                product = jnp.dot(
                    gated_ref[pl.ds(s * length, length)],
                    wout_all[:, :, c : c + wide].reshape(qcols, wide),
                    preferred_element_type=f32,
                )
                partial[s * shards : (s + 1) * shards, :, c : c + wide] = product.astype(
                    bf16
                ).reshape(shards, rows, wide)

        def emit(part, total):
            middle = tok_ref[part].astype(f32) + total
            mid_ref[part] = middle
            held_two[part] = (middle * rms_scale(middle) * gain_two).astype(bf16)

        def first():
            ffn_dp.relay(0)
            down_dp.forward(0)

        def second():
            ffn_dp.relay(1)
            ffn_dp.start_z(2, 3)
            down_dp.forward(1)
            ffn_dp.forward(0)

        ring_scatter(
            place, partial, pair, out, near, far, rsend, rrecv, emit, (first, second)
        )
        two = RingGather(place, held_two, h2_all, gsend, grecv, True)
        two.start()
        ffn_dp.forward(1)
        ffn_dp.relay(2)
        two.pass_on()
        ffn_dp.start_z(3, 4)
        loads[1].wait()
        cot = RingGather(place, cot_ref, cot_all, csend, crecv, True)
        cot.start()
        ffn_dp.relay(3)
        two.step_across()
        ffn_dp.forward(2)
        two.step_far()
        cot.pass_on()
        ffn_dp.forward(3)
        cot.step_across()
        cot.step_far()
        two.finish()
        cot.finish()
        ffn_dp.finish()
        down_dp.finish()
        down_own.wait()
        save.wait()
        for i, c in enumerate(attn):
            if i % GROUP:
                c.wait_send()
        for c in ffn[1:] + small_dp + small_tp:
            c.wait_send()

        @pl.when(jnp.logical_not(selfish))
        def _():
            wout_copies[0].wait_send()

        wout_copies[1].wait_send()

        @pl.when(mine)
        def _():
            wout_over.wait_send()

    pieces = (2, streams, 2, shards * wrows)
    shape = jax.ShapeDtypeStruct
    return pallas(
        body,
        [
            shape((GROUP, rows, width), bf16),
            shape(pieces + (2 * hidden,), bf16),
            shape((planes, brows, width), bf16),
            shape((GROUP, rows, width), bf16),
            shape((GROUP, rows, width), bf16),
            shape((GROUP, planes, srows, 128), bf16),
            shape((grows, 128), f32),
            shape(pieces + (qkv,), bf16),
            shape((planes, wrows, width), bf16),
            shape((group_rows, qkv), f32),
            shape((group_rows, qkv), bf16),
            shape((group_rows, qcols), f32),
            shape((group_rows, qcols), bf16),
            shape((group_rows, qcols), bf16),
            shape((rows, width), f32),
            shape((width, 128), bf16),
            shape((streams, 128), f32),
        ],
        [VMEM] * 3 + [ANY] * len(inputs),
        [ANY] * 5 + [VMEM] * 12,
        [pltpu.VMEM(x.shape, x.dtype) for x in inputs]
        + [
            pltpu.VMEM((srows, 128), bf16),
            pltpu.VMEM((GROUP, wrows, 2 * hidden), bf16),
            pltpu.VMEM((2, shards * wrows, qkv), bf16),
            pltpu.VMEM((4, shards * wrows // 2, 2 * hidden), bf16),
            pltpu.VMEM((2, brows // 2, width), bf16),
            pltpu.VMEM((GROUP, rows, width), bf16),
            pltpu.VMEM((GROUP, rows, width), bf16),
            pltpu.VMEM((GROUP, rows, width), bf16),
            pltpu.VMEM((rows, width), bf16),
            DMA((len(inputs),)),
            DMA,
        ]
        + gather_scratch() + gather_scratch() + gather_scratch()
        + [
            DMA((planes,)), DMA((planes,)), DMA((GROUP,)), DMA((GROUP,)),
            DMA((GROUP,)), DMA((GROUP,)), DMA((3 * GROUP,)), DMA((3 * GROUP,)),
            DMA((8,)), DMA((8,)), DMA((16,)), DMA((16,)),
            DMA((9,)), DMA((8,)), DMA((3,)), DMA((5,)),
        ]
        + scatter_scratch(rows, width),
        cid,
        100,
        56,
    )(small, cosine, sine, *inputs)


class PlaceSums:
    SENDS, RECVS = 8, 6

    def __init__(self, piece, got, far, near, relay, send, recv):
        z, low, y = (lax.axis_index(a) for a in ("zh", "st", "y"))
        to_z, to_y = {"zh": 1 - z}, {"y": 1 - y}
        beside, middle = {"st": 1 - low}, {"zh": 1 - z, "st": 1 - low}
        self.outer, self.inner = z == low, z != low
        self.got, self.far, self.near = got, far, near
        self.y_far = remote(piece(1 - z, 1 - y), got.at[0], send.at[0], recv.at[0], to_y)
        self.y_near = remote(piece(z, 1 - y), got.at[1], send.at[1], recv.at[1], to_y)
        self.loads = [
            pltpu.make_async_copy(piece(1 - z, y), far, send.at[2]),
            pltpu.make_async_copy(piece(z, y), near, send.at[3]),
        ]

        def half(ref, h):
            if len(far.shape) == 3:
                return ref.at[h]
            count = far.shape[0] // 2
            return ref.at[pl.ds(h * count, count)]

        self.direct, self.toward, self.onward = [], [], []
        for h in range(2):
            dst = half(got.at[2], h)
            self.direct.append(
                remote(half(far, h), dst, send.at[4 + h], recv.at[2 + h], to_z)
            )
            self.toward.append(
                remote(half(far, h), half(relay, h), send.at[4 + h], recv.at[4 + h], beside)
            )
            self.onward.append(
                remote(half(relay, h), dst, send.at[6 + h], recv.at[2 + h], middle)
            )

    def load(self):
        for c in self.loads:
            c.start()

    def over_z(self, late=False):
        self.loads[0].wait()
        self.y_far.wait_recv()
        self.each(lambda at: self.put(at))
        Spread.start_z(self, 0, 1 if late else 2)

    def start_late(self):
        Spread.start_z(self, 1, 2)

    def relay(self, half):
        @pl.when(self.inner)
        def _():
            self.toward[half].wait_recv()
            self.onward[half].start()

    def put(self, at):
        self.far[at] = (self.far[at].astype(f32) + self.got[(0,) + at].astype(f32)).astype(bf16)

    def each(self, visit):
        lead, rows = self.far.shape[:-2], self.far.shape[-2]

        def inner(i, _):
            part = pl.ds(pl.multiple_of(i * 32, 32), 32)
            if lead:
                for k in range(lead[0]):
                    visit((k, part))
            else:
                visit((part,))
            return 0

        lax.fori_loop(0, rows // 32, inner, 0)

    def total(self, at):
        return (self.near[at].astype(f32) + self.got[(1,) + at].astype(f32)) + self.got[
            (2,) + at
        ].astype(f32)

    def arrive(self):
        self.loads[1].wait()
        self.y_near.wait_recv()
        for c in self.direct:
            c.wait_recv()

    def drain(self):
        for c in [self.y_far, self.y_near] + self.direct:
            c.wait_send()

        @pl.when(self.inner)
        def _():
            for c in self.onward:
                c.wait_send()


def backward_pass(x, final, middle, tokens, cotangent, gains, headgate, qkv_w, out_w, hidden_one,
                  qkv, low, gate, mixed, gated, starts, down_grad, ffn_grad, docs, shards, cid):
    _, rows, width = x.shape
    planes = 4
    streams = GROUP // shards
    length = rows * shards
    group_rows = rows * GROUP
    qcols = gate.shape[1]
    qkv_cols = qkv.shape[1]
    kcols = (qkv_cols - qcols) // 2
    heads = qcols // HEAD_SIZE
    brows = down_grad.shape[2]
    both = ffn_grad.shape[4]
    hidden = both // 2
    wrows = width // (planes * GROUP)
    gain_rows = width // 128
    score_scale = HEAD_SIZE ** (-0.5)
    cosine, sine = rope_constants(length)
    srows = 24
    inputs = [
        x, middle, tokens, cotangent, headgate, qkv_w, out_w, qkv, low, gate, mixed, gated,
    ]

    def body(
        gains_ref, starts_ref, cos_ref, sin_ref, final_ref, h1_ref, down_ref, ffn_ref,
        i0, i1, i2, i3, i4, i5, i6, i7, i8, i9, i10, i11,
        t0, t1, t2, t3, t4, t5, t6, t7, t8, s_out,
        layer_ref, tgrad_ref, gate_out, up_out, query_out, key_out, value_out, o_out, down_out,
        fsem, partial, mid_ref, tok_ref, cot_ref, hg_ref, wq_ref, wout_ref, qkv_ref, low_ref, gate_ref,
        mixed_ref, gated_ref,
        held, db_all, dmid, gq, dgl, dk_acc, dv_acc, dmix, small, stage, s_got, s_held, s_line,
        g_got, g_far, g_near, g_in, d_got, d_far, d_near, q_own, q_got, q_far, q_near, q_in,
        o_own, o_got, o_far, o_near, o_in, g_relay, d_relay, q_relay, o_relay,
        pair, out, near, far, rsend, rrecv, r2send, r2recv, r3send, r3recv, csend, crecv,
        isem, gsend, grecv, dsend, drecv, qsend, qrecv, osend, orecv, gxsend, gxrecv, qxsend,
        qxrecv, oxsend, oxrecv, asend, arecv, bsend, brecv, lsem, turn,
    ):
        sources = [i0, i1, i2, i3, i4, i5, i6, i7, i8, i9, i10, i11]
        targets = [
            partial, mid_ref, tok_ref, cot_ref, hg_ref, wq_ref, wout_ref, qkv_ref, low_ref,
            gate_ref, mixed_ref, gated_ref,
        ]
        finals = [
            pltpu.make_async_copy(ready, target, fsem.at[i])
            for i, (ready, target) in enumerate(
                (
                    (layer_ref, t0), (tgrad_ref, t1), (gate_out, t2), (up_out, t3),
                    (query_out, t4), (key_out, t5), (value_out, t6), (o_out, t7), (down_out, t8),
                )
            )
        ]
        place = Place(shards)
        tp, dp, flat = place.tp, place.dp(), place.flat()
        high, y, seq = lax.axis_index("zh"), lax.axis_index("y"), lax.axis_index("seq")
        loads = [
            pltpu.make_async_copy(s, t, isem.at[i])
            for i, (s, t) in enumerate(zip(sources, targets))
        ]
        for c in loads[:4]:
            c.start()
        barrier = pltpu.get_barrier_semaphore()

        def signal(device, semaphore=barrier):
            pl.semaphore_signal(
                semaphore, inc=1, device_id=device, device_id_type=pl.DeviceIdType.MESH
            )

        for device in group_peers(place):
            signal(device)
        for k in range(1, planes):
            signal(place.dp_device((dp + k) % planes))
        owner = place.head(tp) * planes + dp
        source = {"st": lax.axis_index("st"), "seq": high * 2 + y}
        source.update(place.dp_device(seq))

        @pl.when(owner != flat)
        def _():
            signal(source)

        inner = high != lax.axis_index("st")

        @pl.when(inner)
        def _():
            signal({"zh": 1 - high, "st": 1 - lax.axis_index("st")})

        pl.semaphore_wait(
            barrier,
            GROUP + planes - 2 + (owner != flat).astype(jnp.int32) + inner.astype(jnp.int32),
        )

        ffn = PlaceSums(
            lambda zp, yp: ffn_ref.at[zp, :, yp], g_got, g_far, g_near, g_relay, gsend, grecv
        )
        down = PlaceSums(lambda zp, yp: down_ref.at[zp, yp], d_got, d_far, d_near, d_relay, dsend, drecv)
        down.y_far.start()
        ffn.y_far.start()
        ffn.y_near.start()
        down.load()
        ffn.load()
        for c in loads[4:]:
            c.start()

        small[...] = jnp.zeros_like(small)
        gain_all = gains_ref[...]
        gain_one = jnp.concatenate([gain_all[i : i + 1] for i in range(gain_rows)], axis=1)
        gain_two = jnp.concatenate(
            [gain_all[gain_rows + i : gain_rows + i + 1] for i in range(gain_rows)], axis=1
        )
        query_gain = gain_all[2 * gain_rows : 2 * gain_rows + 1]
        key_gain = gain_all[2 * gain_rows + 1 : 2 * gain_rows + 2]
        for c in loads[:4]:
            c.wait()

        def emit_dm(part, total):
            value = mid_ref[part]
            scale = rms_scale(value)
            normed = value * scale
            small[17:18] += jnp.sum(total * normed, axis=0, keepdims=True)
            dm = cot_ref[part].astype(f32) + norm_back(total * gain_two, normed, scale)
            dmid[part] = dm
            held[part] = dm.astype(bf16)

        ring_scatter(place, partial, pair, out, near, far, rsend, rrecv, emit_dm)
        grad = RingGather(place, held, db_all, csend, crecv)
        grad.start()
        h1_all = partial
        load_h1 = pltpu.make_async_copy(h1_ref, h1_all, lsem.at[0])
        load_h1.start()
        down.over_z()
        grad.pass_on()
        down.relay(0)
        grad.step_across()
        down.relay(1)
        grad.step_far()
        for c in loads[4:]:
            c.wait()
        grad.finish()

        lanes = lax.broadcasted_iota(jnp.int32, (1, 128), 1)
        head = place.head(tp)
        for s in range(streams):
            part = pl.ds(s * length, length)
            db = db_all[s * shards : (s + 1) * shards].reshape(length, width)
            da = lax.dot_general(
                db, wout_ref[...], (((1,), (1,)), ((), ())), preferred_element_type=f32
            )
            logits = jnp.zeros((length, 128), f32)
            for g in range(heads):
                at = g * HEAD_SIZE
                piece = da[:, at : at + HEAD_SIZE]
                opened = gate_ref[part, at : at + HEAD_SIZE]
                dmix[part, at : at + HEAD_SIZE] = (piece * opened).astype(bf16)
                own = jnp.sum(
                    piece * mixed_ref[part, at : at + HEAD_SIZE].astype(f32), axis=1,
                    keepdims=True,
                )
                logits = jnp.where(
                    lanes == head * heads + g, own * opened * (1.0 - opened), logits
                )
            dgl[part] = logits.astype(bf16)
        wide = 512
        for c in range(0, width, wide):
            product = lax.dot_general(
                gated_ref[...], db_all[:, :, c : c + wide].reshape(group_rows, wide),
                (((0,), (0,)), ((), ())), preferred_element_type=f32,
            ).astype(bf16)
            for j in range(planes):
                o_own[j // 2, j % 2, :, c : c + wide] = product[j * wrows : (j + 1) * wrows]
        outs = PlaceSums(lambda zp, yp: o_own.at[zp, yp], o_got, o_far, o_near, o_relay, osend, orecv)
        outs.y_far.start()
        outs.load()
        ffn.over_z(True)

        block = 128
        query_part = jnp.zeros((1, HEAD_SIZE), f32)
        key_part = jnp.zeros((1, HEAD_SIZE), f32)
        for s in range(streams):
            base = s * length
            row = starts_ref[s : s + 1]
            dk_acc[...] = jnp.zeros_like(dk_acc)
            dv_acc[...] = jnp.zeros_like(dv_acc)

            def back(grad_rotated, raw, gain):
                grad_gained = grad_rotated * cos_ref[...] - pltpu.roll(
                    grad_rotated, HEAD_SIZE // 2, 1
                ) * sin_ref[...]
                scale = rms_scale(raw)
                normed = raw * scale
                return (
                    jnp.sum(grad_gained * normed, axis=0, keepdims=True),
                    norm_back(grad_gained * gain, normed, scale).astype(bf16),
                )

            for r in range(0, length, block):
                keys = r + block
                allowed = document_mask(row, docs, r, block, keys)
                key = low_ref[pl.ds(base, keys), qcols : qcols + HEAD_SIZE]
                value = low_ref[pl.ds(base, keys), qcols + HEAD_SIZE :]
                part = pl.ds(base + r, block)
                for g in range(heads):
                    at = g * HEAD_SIZE
                    query = low_ref[part, at : at + HEAD_SIZE]
                    scores = (
                        lax.dot_general(
                            query, key, (((1,), (1,)), ((), ())), preferred_element_type=f32
                        )
                        * score_scale
                    )
                    scores = jnp.where(allowed, scores, MASK_FILL)
                    weights = jnp.exp(scores - jnp.max(scores, axis=1, keepdims=True))
                    probs = weights / jnp.sum(weights, axis=1, keepdims=True)
                    dout = dmix[part, at : at + HEAD_SIZE]
                    dprobs = lax.dot_general(
                        dout, value, (((1,), (1,)), ((), ())), preferred_element_type=f32
                    )
                    delta = jnp.sum(probs * dprobs, axis=1, keepdims=True)
                    dscores = (probs * (dprobs - delta)).astype(bf16)
                    dq = jnp.dot(dscores, key, preferred_element_type=f32) * score_scale
                    gq[part, at : at + HEAD_SIZE] = dq.astype(bf16)
                    dk_acc[0:keys] += lax.dot_general(
                        dscores, query, (((0,), (0,)), ((), ())), preferred_element_type=f32
                    )
                    dv_acc[0:keys] += lax.dot_general(
                        probs.astype(bf16), dout, (((0,), (0,)), ((), ())),
                        preferred_element_type=f32,
                    )
            part = pl.ds(base, length)
            for g in range(heads):
                at = g * HEAD_SIZE
                sums, grads = back(
                    gq[part, at : at + HEAD_SIZE].astype(f32), qkv_ref[part, at : at + HEAD_SIZE],
                    query_gain,
                )
                query_part = query_part + sums
                gq[part, at : at + HEAD_SIZE] = grads
            sums, grads = back(
                (dk_acc[...] * score_scale).astype(bf16).astype(f32),
                qkv_ref[part, qcols : qcols + HEAD_SIZE], key_gain,
            )
            key_part = key_part + sums
            gq[part, qcols : qcols + HEAD_SIZE] = grads
            gq[part, qcols + HEAD_SIZE :] = dv_acc[...].astype(bf16)

        load_h1.wait()
        for n in range(width // 256):
            cols = slice(n * 256, (n + 1) * 256)
            product = lax.dot_general(
                h1_all[:, :, cols].reshape(group_rows, 256), gq[...], (((0,), (0,)), ((), ())),
                preferred_element_type=f32,
            )
            q_own[n // 4, n // 2 % 2, n % 2] = product.astype(bf16)
        qkvs = PlaceSums(lambda zp, yp: q_own.at[zp, :, yp], q_got, q_far, q_near, q_relay, qsend, qrecv)
        qkvs.y_far.start()
        outs.y_near.start()
        qkvs.y_near.start()
        down.y_near.start()
        qkvs.load()
        for c in range(0, width, wide):
            small[0:16, c : c + wide] = lax.dot_general(
                dgl[...], h1_all[:, :, c : c + wide].reshape(group_rows, wide),
                (((0,), (0,)), ((), ())), preferred_element_type=f32,
            )[0:16]

        for s in range(streams):
            part = pl.ds(s * length, length)
            for c in range(0, width, wide):
                product = lax.dot_general(
                    gq[part], wq_ref[c : c + wide], (((1,), (1,)), ((), ())),
                    preferred_element_type=f32,
                ) + lax.dot_general(
                    dgl[part], hg_ref[c : c + wide], (((1,), (1,)), ((), ())),
                    preferred_element_type=f32,
                )
                partial[s * shards : (s + 1) * shards, :, c : c + wide] = product.astype(
                    bf16
                ).reshape(shards, rows, wide)

        def emit_tokens(part, total):
            tok = tok_ref[part].astype(f32)
            scale = rms_scale(tok)
            normed = tok * scale
            small[16:17] += jnp.sum(total * normed, axis=0, keepdims=True)
            tgrad_ref[part] = (
                dmid[part] + norm_back(total * gain_one, normed, scale)
            ).astype(bf16)

        load_final = pltpu.make_async_copy(final_ref, db_all, lsem.at[1])
        load_final.start()
        ring_scatter(
            place, partial, pair, out, near, far, r2send, r2recv, emit_tokens,
            (lambda: ffn.relay(0), ffn.start_late),
        )
        finals[1].start()
        ring_peers = [place.right(), place.left(), place.partner()]
        for device in ring_peers:
            signal(device, turn)
        outs.over_z()
        qkvs.over_z()
        ffn.relay(1)

        small[18:19] = jnp.concatenate([query_part] * gain_rows, axis=1)
        small[19:20] = jnp.concatenate([key_part] * gain_rows, axis=1)
        for t in range(GROUP):
            for d in range(planes):
                lane = columns_of(d, t, shards) // 2 * 128
                stage[t, d * srows : (d + 1) * srows] = small[:, lane : lane + 128]
        sums = Exchange(place, stage, s_got, asend, arecv)
        sums.start()

        load_final.wait()
        pl.semaphore_wait(turn, len(ring_peers))

        def emit_layer(part, total):
            layer_ref[part] = (mid_ref[part] + total).astype(bf16)

        def first():
            outs.relay(0)
            outs.relay(1)

        def scatter_rows(total, ready, send, recv, into):
            def keep(at):
                ready[at] = total(at).astype(bf16)

            copies = []
            for k in range(GROUP):
                peer = (tp + k) % GROUP
                src = ready.at[peer // shards, pl.ds(peer % shards * wrows, wrows)]
                if k == 0:
                    copies.append(pltpu.make_async_copy(src, into.at[tp], send.at[0]))
                else:
                    copies.append(
                        remote(src, into.at[tp], send.at[k], recv.at[k], place.device(peer))
                    )
            return keep, copies

        keep_ffn, ffn_rows = scatter_rows(ffn.total, g_near, gxsend, gxrecv, g_in)

        def second():
            qkvs.relay(0)
            qkvs.relay(1)
            ffn.arrive()
            ffn.each(keep_ffn)
            for c in ffn_rows:
                c.start()

        ring_scatter(
            place, db_all, pair, out, near, far, r3send, r3recv, emit_layer, (first, second)
        )
        finals[0].start()
        sums.finish()
        s_held[...] = jnp.sum(s_got[...], axis=0).reshape(s_held.shape)
        line_own = pltpu.make_async_copy(s_held.at[dp], s_line.at[dp], bsend.at[0])
        line_own.start()
        lines = []
        for k in range(1, planes):
            to = (dp + k) % planes
            lines.append(
                remote(
                    s_held.at[to], s_line.at[dp], bsend.at[k], brecv.at[k], place.dp_device(to)
                )
            )
            lines[-1].start()

        down.arrive()

        def put_down(at):
            down_out[at] = down.total(at)

        down.each(put_down)
        finals[8].start()

        def landed(copies):
            copies[0].wait()
            for c in copies[1:]:
                c.wait_recv()

        landed(ffn_rows)
        for t in range(GROUP):
            for d in range(planes):
                column = columns_of(d, t, shards)
                for m, ref in enumerate((gate_out, up_out)):
                    lane = m * hidden + d * brows
                    for at in range(0, wrows, 32):
                        ref[at : at + 32, column * brows : (column + 1) * brows] = g_in[
                            t, at : at + 32, lane : lane + brows
                        ].astype(f32)
        finals[2].start()
        finals[3].start()

        outs.arrive()

        def keep_out(at):
            o_near[at] = outs.total(at).astype(bf16)

        outs.each(keep_out)
        out_own = pltpu.make_async_copy(o_near, o_in, oxsend)
        out_far = remote(o_near, o_in, oxsend, oxrecv, place.any_device(owner))

        @pl.when(owner == flat)
        def _():
            out_own.start()

        @pl.when(owner != flat)
        def _():
            out_far.start()

        qkvs.arrive()
        keep, qkv_rows = scatter_rows(qkvs.total, q_near, qxsend, qxrecv, q_in)
        qkvs.each(keep)
        for c in qkv_rows:
            c.start()

        landed(qkv_rows)
        for t in range(GROUP):
            home = place.head(t)
            query_out[:, home * qcols : (home + 1) * qcols] = q_in[t, :, :qcols].astype(f32)
            key_out[:, home * kcols : (home + 1) * kcols] = q_in[
                t, :, qcols : qcols + kcols
            ].astype(f32)
            value_out[:, home * kcols : (home + 1) * kcols] = q_in[
                t, :, qcols + kcols :
            ].astype(f32)

        for c in finals[4:7]:
            c.start()

        @pl.when(owner == flat)
        def _():
            out_own.wait()

        @pl.when(owner != flat)
        def _():
            out_far.wait()

        o_out[...] = o_in[...].astype(f32)
        finals[7].start()
        for c in lines:
            c.wait_recv()
        line_own.wait()
        summed = jnp.sum(s_line[...], axis=0)
        per_row = 128 // wrows
        gcols = HEAD_SIZE // (planes * GROUP)
        s_out[...] = jnp.where(
            lax.broadcasted_iota(jnp.int32, (srows, 128), 0) < 18,
            pltpu.roll(summed, (128 - flat % per_row * wrows) % 128, 1),
            pltpu.roll(summed, (128 - flat * gcols) % 128, 1),
        )
        for c in lines + ffn_rows[1:] + qkv_rows[1:]:
            c.wait_send()
        for c in (ffn, down, qkvs, outs):
            c.drain()
        for c in finals:
            c.wait()

    shape = jax.ShapeDtypeStruct
    vmem = pltpu.VMEM
    wide_rows = shards * wrows
    return pallas(
        body,
        [
            shape((rows, width), bf16),
            shape((rows, width), bf16),
            shape((wrows, hidden * GROUP), f32),
            shape((wrows, hidden * GROUP), f32),
            shape((wrows, qcols * GROUP), f32),
            shape((wrows, kcols * GROUP), f32),
            shape((wrows, kcols * GROUP), f32),
            shape((wrows, width), f32),
            shape((brows, width), f32),
            shape((srows, 128), f32),
        ],
        [VMEM] * 4 + [ANY] * (4 + len(inputs)),
        [ANY] * 9 + [VMEM],
        [
            vmem((rows, width), bf16),
            vmem((rows, width), bf16),
            vmem((wrows, hidden * GROUP), f32),
            vmem((wrows, hidden * GROUP), f32),
            vmem((wrows, qcols * GROUP), f32),
            vmem((wrows, kcols * GROUP), f32),
            vmem((wrows, kcols * GROUP), f32),
            vmem((wrows, width), f32),
            vmem((brows, width), f32),
            DMA((9,)),
        ]
        + [vmem(i.shape, i.dtype) for i in inputs]
        + [
            vmem((rows, width), bf16),
            vmem((GROUP, rows, width), bf16),
            vmem((rows, width), f32),
            vmem((group_rows, qkv_cols), bf16),
            vmem((group_rows, 128), bf16),
            vmem((length, HEAD_SIZE), f32),
            vmem((length, HEAD_SIZE), f32),
            vmem((group_rows, qcols), bf16),
            vmem((srows, width), f32),
            vmem((GROUP, planes * srows, 128), f32),
            vmem((GROUP, planes * srows, 128), f32),
            vmem((planes, srows, 128), f32),
            vmem((planes, srows, 128), f32),
            vmem((3, streams, wide_rows, both), bf16),
            vmem((streams, wide_rows, both), bf16),
            vmem((streams, wide_rows, both), bf16),
            vmem((GROUP, wrows, both), bf16),
            vmem((3, brows, width), bf16),
            vmem((brows, width), bf16),
            vmem((brows, width), bf16),
            vmem((2, streams, 2, wide_rows, qkv_cols), bf16),
            vmem((3, streams, wide_rows, qkv_cols), bf16),
            vmem((streams, wide_rows, qkv_cols), bf16),
            vmem((streams, wide_rows, qkv_cols), bf16),
            vmem((GROUP, wrows, qkv_cols), bf16),
            vmem((2, 2, wrows, width), bf16),
            vmem((3, wrows, width), bf16),
            vmem((wrows, width), bf16),
            vmem((wrows, width), bf16),
            vmem((wrows, width), bf16),
            vmem((streams, wide_rows, both), bf16),
            vmem((brows, width), bf16),
            vmem((streams, wide_rows, qkv_cols), bf16),
            vmem((wrows, width), bf16),
        ]
        + scatter_scratch(rows, width)
        + [DMA((10,)), DMA((10,)), DMA((10,)), DMA((10,))]
        + gather_scratch()
        + [DMA((len(inputs),))]
        + [DMA((PlaceSums.SENDS,)), DMA((PlaceSums.RECVS,))] * 4
        + [DMA((GROUP,)), DMA((GROUP,)), DMA((GROUP,)), DMA((GROUP,)), DMA, DMA]
        + [DMA((GROUP,)), DMA((GROUP,)), DMA((planes,)), DMA((planes,)), DMA((2,))]
        + [pltpu.SemaphoreType.REGULAR],
        cid,
        180,
        62,
    )(gains, starts, cosine, sine, final, hidden_one, down_grad, ffn_grad, *inputs)


def store(*arrays):
    count = len(arrays)

    def body(*refs):
        load_sem, store_sem = refs[-2:]
        staged = refs[2 * count : 3 * count]
        loads = [
            pltpu.make_async_copy(refs[i], staged[i], load_sem.at[i]) for i in range(count)
        ]
        stores = [
            pltpu.make_async_copy(staged[i], refs[count + i], store_sem.at[i])
            for i in range(count)
        ]
        for c in loads:
            c.start()
        for load, c in zip(loads, stores):
            load.wait()
            c.start()
        for c in stores:
            c.wait()

    return pl.pallas_call(
        body,
        out_shape=[jax.ShapeDtypeStruct(a.shape, a.dtype) for a in arrays],
        in_specs=[ANY] * count,
        out_specs=[ANY] * count,
        scratch_shapes=[pltpu.VMEM(a.shape, a.dtype) for a in arrays]
        + [DMA((count,)), DMA((count,))],
        compiler_params=pltpu.CompilerParams(vmem_limit_bytes=62 * 1024 * 1024),
    )(*arrays)


def settle(qkv_grad, out_grad, small, qcols, kcols, planes, direct, shards, cid):
    srows = small.shape[1] // planes
    cols = small.shape[2]
    wrows, width = out_grad.shape

    def body(
        q_ref, o_ref, s_ref, query_out, key_out, value_out, o_out, s_out, q_got, o_got, got, held,
        line, qsend, qrecv, osend, orecv, asend, arecv, bsend, brecv,
    ):
        place = Place(shards)
        tp, dp, flat = place.tp, place.dp(), place.flat()
        barrier = pltpu.get_barrier_semaphore()

        def signal(device):
            pl.semaphore_signal(
                barrier, inc=1, device_id=device, device_id_type=pl.DeviceIdType.MESH
            )

        for device in group_peers(place):
            signal(device)
        for k in range(1, planes):
            signal(place.dp_device((dp + k) % planes))
        if direct:
            owner = place.head(tp) * planes + dp
            high, y = lax.axis_index("zh"), lax.axis_index("y")
            source = {"st": lax.axis_index("st"), "seq": high * 2 + y}
            source.update(place.dp_device(lax.axis_index("seq")))

            @pl.when(owner != flat)
            def _():
                signal(source)

            pl.semaphore_wait(barrier, GROUP + planes - 2 + (owner != flat).astype(jnp.int32))
        else:
            pl.semaphore_wait(barrier, GROUP + planes - 2)

        sums = Exchange(place, s_ref, got, asend, arecv)
        sums.start()
        qkv = Exchange(place, q_ref, q_got, qsend, qrecv)
        qkv.start()
        if direct:
            out_own = pltpu.make_async_copy(o_ref, o_got, osend)
            out_far = remote(o_ref, o_got, osend, orecv, place.any_device(owner))

            @pl.when(owner == flat)
            def _():
                out_own.start()

            @pl.when(owner != flat)
            def _():
                out_far.start()

        sums.finish()
        held[...] = jnp.sum(got[...], axis=0).reshape(held.shape)
        line_own = pltpu.make_async_copy(held.at[dp], line.at[dp], bsend.at[0])
        line_own.start()
        lines = []
        for k in range(1, planes):
            to = (dp + k) % planes
            lines.append(
                remote(held.at[to], line.at[dp], bsend.at[k], brecv.at[k], place.dp_device(to))
            )
            lines[-1].start()
        qkv.finish()
        for t in range(GROUP):
            head = place.head(t)
            query_out[:, head * qcols : (head + 1) * qcols] = q_got[t, :, :qcols].astype(f32)
            key_out[:, head * kcols : (head + 1) * kcols] = q_got[
                t, :, qcols : qcols + kcols
            ].astype(f32)
            value_out[:, head * kcols : (head + 1) * kcols] = q_got[t, :, qcols + kcols :].astype(
                f32
            )
        if direct:

            @pl.when(owner == flat)
            def _():
                out_own.wait()

            @pl.when(owner != flat)
            def _():
                out_far.wait()

            o_out[...] = o_got[...].astype(f32)
        else:
            o_out[...] = o_ref[...].astype(f32)
        for c in lines:
            c.wait_recv()
        line_own.wait()
        s_out[...] = jnp.sum(line[...], axis=0)
        for c in lines:
            c.wait_send()

    return pallas(
        body,
        [
            jax.ShapeDtypeStruct((wrows, GROUP * qcols), f32),
            jax.ShapeDtypeStruct((wrows, GROUP * kcols), f32),
            jax.ShapeDtypeStruct((wrows, GROUP * kcols), f32),
            jax.ShapeDtypeStruct((wrows, width), f32),
            jax.ShapeDtypeStruct((srows, cols), f32),
        ],
        [VMEM, VMEM, VMEM],
        [VMEM] * 5,
        [
            pltpu.VMEM(qkv_grad.shape, bf16),
            pltpu.VMEM(out_grad.shape, bf16),
            pltpu.VMEM(small.shape, f32),
            pltpu.VMEM((planes, srows, cols), f32),
            pltpu.VMEM((planes, srows, cols), f32),
            DMA((GROUP,)), DMA((GROUP,)), DMA, DMA,
            DMA((GROUP,)), DMA((GROUP,)), DMA((planes,)), DMA((planes,)),
        ],
        cid,
        20,
    )(qkv_grad, out_grad, small)


def local(
    tokens, doc_starts, attn_gain, query_gain, key_gain, w_query, key_weight, value_weight,
    w_headgate, w_out, ffn_gain, w_gate, w_up, w_down, cotangent,
):
    zs, ys = lax.axis_size("zh"), lax.axis_size("y")
    planes = zs * ys
    direct = zs == 2 and ys == 2
    streams = lax.axis_size("st")
    shards = lax.axis_size("seq")
    devices = planes * GROUP
    rows, width = tokens.shape
    length = rows * shards
    group_rows = rows * GROUP
    wrows = w_query.shape[0]
    brows = w_down.shape[0]
    hidden = brows * planes
    qcols = w_query.shape[1] // GROUP
    kcols = key_weight.shape[1] // GROUP
    group_heads = qcols // HEAD_SIZE
    all_heads = w_headgate.shape[1]
    score_scale = HEAD_SIZE ** (-0.5)
    dp = lax.axis_index(DP)
    tp = lax.axis_index(TP)

    hg = wrows * all_heads
    gcols = query_gain.shape[0]
    at = hg + 2 * wrows
    count = at + 2 * gcols
    sums = -(-count // 1024) * 8
    docs = doc_starts.shape[1]
    qkv_cols = qcols + 2 * kcols
    starts_row = jnp.concatenate(
        [(doc_starts[0] // 128).astype(bf16), (doc_starts[0] % 128).astype(bf16)]
    )
    headgate_rows = jnp.pad(w_headgate, ((0, 0), (0, 128 - all_heads)))
    if direct:
        gain_rows = width // 128
        others = [attn_gain, ffn_gain, query_gain, key_gain, starts_row]
        small = jnp.pad(w_headgate, ((0, 16), (0, 128 - all_heads)))
        for i, row in enumerate(others):
            small = small + jnp.pad(
                row[None], ((wrows + i, 15 - i), (0, 128 - row.shape[0]))
            )
        (
            cot_all, ffn_w, down_w, hidden_one, hidden_two, small, gains, qkv_w, out_w, qkv,
            low, gate_full, mixed, gated, middle, headgate, starts,
        ) = forward_pass(
            tokens, cotangent, small, w_out, w_query, key_weight, value_weight, w_gate, w_up,
            w_down, docs, shards, 0,
        )
        cot_all = cot_all.reshape(group_rows, width)
        hidden_two = hidden_two.reshape(group_rows, width)
        ffn_w = ffn_w.reshape(width, 2 * hidden)
        down_w = down_w.reshape(hidden, width)
        gate_up = mm(hidden_two, ffn_w)
        gate_pre, up_proj = gate_up[:, :hidden], gate_up[:, hidden:]
        gate_sig = jax.nn.sigmoid(gate_pre)
        inner_act = (gate_pre * gate_sig * up_proj).astype(bf16)
        down_grad = mm_t(inner_act, cot_all).astype(bf16)
        grad_inner = mm_b(cot_all, down_w)
        grad_gate = grad_inner * up_proj * gate_sig * (1.0 + gate_pre * (1.0 - gate_sig))
        grad_up = grad_inner * gate_pre * gate_sig
        grad_gu = jnp.concatenate([grad_gate.astype(bf16), grad_up.astype(bf16)], axis=1)
        ffn_grad = mm_t(hidden_two, grad_gu).astype(bf16)
        places = (GROUP, rows, width)
        (
            layer_out, tokens_grad, gate_grad, up_grad, query_grad, key_grad, value_grad,
            out_grad, down_grad, small_sum,
        ) = backward_pass(
            mm_b(grad_gu, ffn_w).astype(bf16).reshape(places),
            mm(inner_act, down_w).astype(bf16).reshape(places),
            middle, tokens, cotangent, gains, headgate,
            qkv_w.reshape(width, qkv_cols), out_w.reshape(qcols, width), hidden_one, qkv, low,
            gate_full, mixed, gated, starts, down_grad.reshape(zs, ys, brows, width),
            ffn_grad.reshape(zs, streams, ys, shards * wrows, 2 * hidden), docs, shards, 1,
        )
        (
            layer_out, tokens_grad, gate_grad, up_grad, query_grad, key_grad, value_grad,
            out_grad, down_grad,
        ) = store(
            layer_out, tokens_grad, gate_grad, up_grad, query_grad, key_grad, value_grad,
            out_grad, down_grad,
        )
        return (
            layer_out,
            tokens_grad,
            small_sum[all_heads, :wrows],
            small_sum[18, :gcols],
            small_sum[19, :gcols],
            query_grad,
            key_grad,
            value_grad,
            small_sum[:all_heads, :wrows].T,
            out_grad,
            small_sum[all_heads + 1, :wrows],
            gate_grad,
            up_grad,
            down_grad,
        )
    else:
        srows = -(-(wrows + 6) // 16) * 16
        others = [attn_gain, ffn_gain, query_gain, key_gain, starts_row[:docs], starts_row[docs:]]
        small = jnp.concatenate(
            [headgate_rows]
            + [jnp.pad(row, (0, 128 - row.shape[0]))[None] for row in others]
            + [jnp.zeros((srows - wrows - 6, 128), bf16)]
        )
        tokens_all, cot_all, small, qkv_w, ffn_own = front(
            tokens, cotangent, small, w_out, w_query, key_weight, value_weight, w_gate, w_up,
            w_down, planes, False, shards, 0,
        )
        tokens_all = tokens_all.reshape(group_rows, width)
        cot_all = cot_all.reshape(group_rows, width)
        qkv_w = over_dp(qkv_w[0])
        ffn_w = over_dp(ffn_own)
        down_w = lax.all_gather(w_down, DP, axis=0, tiled=True)
        out_w = lax.all_gather(w_out, ALL, axis=0, tiled=True)
        out_w = lax.dynamic_slice_in_dim(out_w, tp * qcols, qcols, 0)
        head = tp
        here = pick(small[::shards], 1, dp)
        starts = here[:, wrows + 4, :docs].astype(jnp.int32) * 128
        starts = starts + here[:, wrows + 5, :docs].astype(jnp.int32)
    small = small.reshape(streams, shards, zs, ys, srows, 128).transpose(2, 0, 3, 1, 4, 5)
    small = small.reshape(devices, srows, 128)
    headgate_all = small[:, :wrows, :all_heads].reshape(width, all_heads)
    if not direct:
        attn_gain_f = small[:, wrows, :wrows].reshape(1, -1).astype(f32)
        ffn_gain_f = small[:, wrows + 1, :wrows].reshape(1, -1).astype(f32)
        query_gain_f = small[:, wrows + 2, :gcols].reshape(-1).astype(f32)
        key_gain_f = small[:, wrows + 3, :gcols].reshape(-1).astype(f32)
    headgate_own = lax.dynamic_slice_in_dim(headgate_all, head * group_heads, group_heads, 1)

    if not direct:
        residual_all = tokens_all.astype(f32)
        hidden_all = (residual_all * rms_scale(residual_all) * attn_gain_f).astype(bf16)
        qkv = mm(hidden_all, qkv_w)
    query_raw = qkv[:, :qcols].reshape(group_rows, group_heads, HEAD_SIZE)
    key_raw = qkv[:, qcols : qcols + kcols].reshape(group_rows, 1, HEAD_SIZE)
    value = qkv[:, qcols + kcols :].astype(bf16).reshape(streams, length, HEAD_SIZE)
    positions = jnp.tile(jnp.arange(length, dtype=jnp.int32), streams)
    cosine, sine = rotary_tables(positions)
    query_scale = rms_scale(query_raw)
    query_normed = query_raw * query_scale
    query = rotate(query_normed * query_gain_f, cosine, sine).astype(bf16)
    query = query.reshape(streams, length, group_heads, HEAD_SIZE)
    key_scale = rms_scale(key_raw)
    key_normed = key_raw * key_scale
    key = rotate(key_normed * key_gain_f, cosine, sine).astype(bf16)
    key = key.reshape(streams, length, HEAD_SIZE)
    stream_pos = jnp.arange(length, dtype=jnp.int32)
    segment = jnp.sum((stream_pos[None, :, None] >= starts[:, None, :]).astype(jnp.int32), axis=2)
    allowed = (stream_pos[:, None] >= stream_pos[None, :])[None] & (
        segment[:, :, None] == segment[:, None, :]
    )
    scores = jnp.einsum("bqgd,bkd->bgqk", query, key, preferred_element_type=f32) * score_scale
    scores = jnp.where(allowed[:, None], scores, MASK_FILL)
    row_max = jnp.max(scores, axis=-1, keepdims=True)
    weights = jnp.exp(scores - row_max)
    probs = weights / jnp.sum(weights, axis=-1, keepdims=True)
    probs_low = probs.astype(bf16)
    if not direct:
        mixed = jnp.einsum(
            "bgqk,bkd->bqgd", probs_low, value, preferred_element_type=f32
        ).astype(bf16)
    mixed_f = mixed.astype(f32).reshape(group_rows, group_heads, HEAD_SIZE)
    if direct:
        head_gate = gate_full.reshape(group_rows, group_heads, HEAD_SIZE)[:, :, :1]
    else:
        head_gate = jax.nn.sigmoid(mm(hidden_all, headgate_own))[:, :, None]
        gated = (mixed_f * head_gate).astype(bf16).reshape(group_rows, qcols)

    def parts(x):
        return x.astype(bf16).reshape(GROUP, rows, width)

    if not direct:
        middle, hidden_two = middle_step(
            parts(mm(gated, out_w)), tokens, ffn_gain_f, None, shards, 2
        )
        hidden_two = hidden_two.reshape(group_rows, width)

    gate_up = mm(hidden_two, ffn_w)
    gate_pre, up_proj = gate_up[:, :hidden], gate_up[:, hidden:]
    gate_sig = jax.nn.sigmoid(gate_pre)
    inner_act = (gate_pre * gate_sig * up_proj).astype(bf16)
    down_grad = mm_t(inner_act, cot_all).astype(bf16).reshape(zs, ys, brows, width)
    if direct:
        down_sum = PlaceSum(down_grad)
        down_sum.over_y()
    else:
        down_grad = scatter_dp(down_grad)
    grad_inner = mm_b(cot_all, down_w)
    grad_gate = (grad_inner * up_proj * gate_sig * (1.0 + gate_pre * (1.0 - gate_sig))).astype(bf16)
    grad_up = (grad_inner * gate_pre * gate_sig).astype(bf16)
    grad_gu = jnp.concatenate([grad_gate, grad_up], axis=1)
    ffn_grad = mm_t(hidden_two, grad_gu).astype(bf16)
    grad_gu, ffn_grad = lax.optimization_barrier((grad_gu, ffn_grad))
    if not direct:
        ffn_grad = scatter_dp(by_place(ffn_grad))
    grad_middle, ffn_gain_part, grad_branch, *ffn_first = middle_back(
        parts(mm_b(grad_gu, ffn_w)), middle, cotangent, ffn_gain_f,
        ffn_grad.reshape(zs, streams, ys, -1, 2 * hidden) if direct else None, shards, 3,
    )
    if direct:
        grad_branch, down_sum.far, down_sum.near, ffn_first = lax.optimization_barrier(
            (grad_branch, down_sum.far, down_sum.near, ffn_first[0])
        )
        down_z = down_sum.over_z()
        ffn_sum = PlaceSum(by_place(ffn_grad))
        ffn_sum.take(ffn_first.reshape(-1, 2 * hidden), None)
        ffn_z = ffn_sum.over_z()
        ffn_sum.near = ffn_sum.over_y_near()
    grad_branch = grad_branch.reshape(group_rows, width)
    layer_out = scatter_sum(parts(mm(inner_act, down_w)), middle, shards, 4)

    out_grad = mm_t(gated, grad_branch).astype(bf16).reshape(zs, ys, wrows, width)
    grad_gated = mm_b(grad_branch, out_w).reshape(group_rows, group_heads, HEAD_SIZE)
    grad_mixed = (grad_gated * head_gate).astype(bf16).reshape(
        streams, length, group_heads, HEAD_SIZE
    )
    gate_flat = head_gate[:, :, 0]
    grad_logit = (
        jnp.sum(grad_gated * mixed_f, axis=-1) * gate_flat * (1.0 - gate_flat)
    ).astype(bf16)
    grad_probs = jnp.einsum("bqgd,bkd->bgqk", grad_mixed, value, preferred_element_type=f32)
    row_delta = jnp.sum(probs * grad_probs, axis=-1, keepdims=True)
    grad_scores = (probs * (grad_probs - row_delta)).astype(bf16)
    grad_query = (
        jnp.einsum("bgqk,bkd->bqgd", grad_scores, key, preferred_element_type=f32) * score_scale
    ).astype(bf16)
    grad_key = (
        jnp.einsum("bgqk,bqgd->bkd", grad_scores, query, preferred_element_type=f32) * score_scale
    ).astype(bf16)
    grad_value = jnp.einsum(
        "bgqk,bqgd->bkd", probs_low, grad_mixed, preferred_element_type=f32
    ).astype(bf16)
    gqn = rotate_back(
        grad_query.astype(f32).reshape(group_rows, group_heads, HEAD_SIZE), cosine, sine
    )
    query_gain_part = jnp.sum(gqn * query_normed, axis=(0, 1))
    grad_query_raw = norm_back(gqn * query_gain_f, query_normed, query_scale).astype(bf16)
    gkn = rotate_back(grad_key.astype(f32).reshape(group_rows, 1, HEAD_SIZE), cosine, sine)
    key_gain_part = jnp.sum(gkn * key_normed, axis=(0, 1))
    grad_key_raw = norm_back(gkn * key_gain_f, key_normed, key_scale).astype(bf16)
    grad_qkv = jnp.concatenate(
        [
            grad_query_raw.reshape(group_rows, qcols),
            grad_key_raw.reshape(group_rows, kcols),
            grad_value.reshape(group_rows, kcols),
        ],
        axis=1,
    )
    qkv_grad = mm_t(hidden_all, grad_qkv).astype(bf16)
    if direct:
        qkv_grad, out_grad, grad_qkv, down_z = lax.optimization_barrier(
            (qkv_grad, out_grad, grad_qkv, down_z)
        )
        down_grad = down_sum.total(down_z)
        qkv_sum, out_sum = PlaceSum(by_place(qkv_grad)), PlaceSum(out_grad)
        qkv_sum.over_y()
        out_sum.over_y()
        qkv_z, out_z = qkv_sum.over_z(), out_sum.over_z()
        ffn_grad = ffn_sum.total(ffn_z)
        qkv_grad, out_grad = qkv_sum.total(qkv_z), out_sum.total(out_z)
    else:
        qkv_grad = scatter_dp(by_place(qkv_grad))
        out_grad = lax.dynamic_update_slice(
            jnp.zeros((width, width), bf16), out_grad.reshape(qcols, width), (tp * qcols, 0)
        )
        out_grad = lax.psum_scatter(out_grad, ALL, scatter_dimension=0, tiled=True)
    tokens_grad, attn_gain_part = tokens_back(
        parts(mm_b(grad_qkv, qkv_w) + mm_b(grad_logit, headgate_own)),
        tokens, grad_middle, attn_gain_f, shards, 5,
    )
    headgate_part = mm_t(hidden_all, grad_logit)
    headgate_part = lax.dynamic_update_slice(
        jnp.zeros((width, all_heads), f32), headgate_part, (0, head * group_heads)
    )

    small_sum = jnp.concatenate(
        [
            headgate_part.reshape(devices, hg),
            attn_gain_part.reshape(devices, wrows),
            ffn_gain_part.reshape(devices, wrows),
            query_gain_part.reshape(devices, gcols),
            key_gain_part.reshape(devices, gcols),
        ],
        axis=1,
    )
    small_sum = jnp.pad(small_sum, ((0, 0), (0, sums * 128 - count)))
    small_sum = small_sum.reshape(zs, streams, ys, shards, sums, 128)
    small_sum = small_sum.transpose(1, 3, 0, 2, 4, 5)
    small_sum = small_sum.reshape(GROUP, planes * sums, 128)

    gate_grad, up_grad = exchange_back(
        ffn_grad.reshape(GROUP, wrows, 2 * hidden), planes, shards, 6
    )
    query_grad, key_grad, value_grad, out_grad, small_sum = settle(
        qkv_grad.reshape(GROUP, wrows, qkv_cols), out_grad, small_sum, qcols, kcols, planes,
        direct, shards, 7,
    )
    small_sum = small_sum.reshape(-1)
    return (
        layer_out,
        tokens_grad,
        small_sum[hg : hg + wrows],
        small_sum[at : at + gcols],
        small_sum[at + gcols : at + 2 * gcols],
        query_grad,
        key_grad,
        value_grad,
        small_sum[:hg].reshape(wrows, all_heads),
        out_grad,
        small_sum[hg + wrows : hg + 2 * wrows],
        gate_grad,
        up_grad,
        down_grad.astype(f32),
    )


def solution(mesh):
    shards = mesh.shape["seq"]
    planes = (2, 2, 2) if shards == 4 and mesh.size == 32 else (1, GROUP // shards, -1)
    grouped = Mesh(mesh.devices.reshape(planes + (shards,)), ALL)
    two = P(ALL, None)
    one = P(ALL)
    return jax.shard_map(
        local,
        mesh=grouped,
        in_specs=(
            two, P(("zh", "st", "y"), None), one, one, one, two, two, two, two, two, one, two, two,
            two, two,
        ),
        out_specs=(two, two, one, one, one, two, two, two, two, two, one, two, two, two),
        check_vma=False,
    )
```

```python
import jax
import jax.numpy as jnp
import numpy as np
from jax import lax
from jax.experimental import pallas as pl
from jax.experimental.pallas import tpu as pltpu
from jax.sharding import Mesh, PartitionSpec as P

QUERY_HEADS = 16
KEY_VALUE_HEADS = 8
HEAD_SIZE = 128
GROUP = 8
NORM_EPS = 1e-06
ROPE_BASE = 1000000.0
MASK_FILL = -1e30

DP = ("zh", "y")
TP = ("st", "seq")
ALL = ("zh", "st", "y", "seq")
f32 = jnp.float32
bf16 = jnp.bfloat16


def rms_scale(vector):
    return lax.rsqrt(jnp.mean(vector * vector, axis=-1, keepdims=True) + NORM_EPS)


def rotary_tables(positions):
    half_width = HEAD_SIZE // 2
    exponent = jnp.arange(half_width, dtype=jnp.int32).astype(f32) * (2.0 / HEAD_SIZE)
    inverse = jnp.power(ROPE_BASE, -exponent)
    angles = positions.astype(f32)[:, None] * inverse[None, :]
    return (jnp.cos(angles)[:, None, :], jnp.sin(angles)[:, None, :])


def rotate(vector, cosine, sine):
    a, b = jnp.split(vector, 2, axis=-1)
    return jnp.concatenate([a * cosine - b * sine, b * cosine + a * sine], axis=-1)


def rotate_back(vector, cosine, sine):
    a, b = jnp.split(vector, 2, axis=-1)
    return jnp.concatenate([a * cosine + b * sine, b * cosine - a * sine], axis=-1)


def norm_back(grad, normed, scale):
    return scale * (grad - normed * jnp.mean(grad * normed, axis=-1, keepdims=True))


def mm(left, right):
    return jnp.dot(left, right, preferred_element_type=f32)


def mm_t(left, right):
    return lax.dot_general(left, right, (((0,), (0,)), ((), ())), preferred_element_type=f32)


def mm_b(left, right):
    return lax.dot_general(left, right, (((1,), (1,)), ((), ())), preferred_element_type=f32)


SWAP = [(0, 1), (1, 0)]


def over_dp(x):
    streams, shards = lax.axis_size("st"), lax.axis_size("seq")
    zs, ys = lax.axis_size("zh"), lax.axis_size("y")
    rows, columns = x.shape[1] * shards, x.shape[2]
    whole = lax.all_gather(x, DP, axis=0, tiled=False)
    whole = whole.reshape(zs, ys, streams, rows, columns).transpose(0, 2, 1, 3, 4)
    return whole.reshape(-1, columns)


def pick(x, axis, index):
    return lax.dynamic_index_in_dim(x, index, axis, keepdims=False)


def plus(left, right):
    return left.astype(f32) + right.astype(f32)


class PlaceSum:
    def __init__(self, x):
        self.x = x
        self.z, self.y = lax.axis_index("zh"), lax.axis_index("y")

    def piece(self, zp, yp):
        return pick(pick(self.x, 0, zp), 0, yp)

    def over_y(self):
        got = lax.ppermute(pick(self.x, 1, 1 - self.y), "y", SWAP)
        self.take(pick(got, 0, 1 - self.z), pick(got, 0, self.z))

    def over_y_near(self):
        return lax.ppermute(self.piece(self.z, 1 - self.y), "y", SWAP)

    def take(self, far, near):
        self.far, self.near = far, near

    def over_z(self):
        far = plus(self.piece(1 - self.z, self.y), self.far).astype(bf16)
        return lax.ppermute(far, "zh", SWAP)

    def total(self, got):
        return (plus(self.piece(self.z, self.y), self.near) + got.astype(f32)).astype(bf16)


def scatter_dp(x):
    zs, ys = x.shape[:2]
    return lax.psum_scatter(
        x.reshape((zs * ys,) + x.shape[2:]), DP, scatter_dimension=0, tiled=False
    )


def by_place(x):
    streams = lax.axis_size("st")
    zs, ys = lax.axis_size("zh"), lax.axis_size("y")
    columns = x.shape[1]
    x = x.reshape(zs, streams, ys, -1, columns).transpose(0, 2, 1, 3, 4)
    return x.reshape(zs, ys, -1, columns)


def pallas(body, out_shape, in_specs, out_specs, scratch, cid, micros, mib=40):
    return pl.pallas_call(
        body,
        out_shape=out_shape,
        in_specs=in_specs,
        out_specs=out_specs,
        scratch_shapes=scratch,
        compiler_params=pltpu.CompilerParams(
            collective_id=cid, has_side_effects=True, vmem_limit_bytes=mib * 1024 * 1024
        ),
        cost_estimate=pl.CostEstimate(
            flops=0, bytes_accessed=int(micros * 3.6e5), transcendentals=0
        ),
    )


ANY = pl.BlockSpec(memory_space=pl.ANY)
VMEM = pl.BlockSpec(memory_space=pltpu.VMEM)
DMA = pltpu.SemaphoreType.DMA


def remote(src, dst, send, recv, device):
    return pltpu.make_async_remote_copy(
        src_ref=src,
        dst_ref=dst,
        send_sem=send,
        recv_sem=recv,
        device_id=device,
        device_id_type=pl.DeviceIdType.MESH,
    )


class Place:
    def __init__(self, shards):
        self.shards = shards
        self.tp = lax.axis_index("st") * shards + lax.axis_index("seq")
        self.core = self.tp % 2
        self.ring = self.turn(self.tp // 2)

    def turn(self, place):
        if self.shards == GROUP:
            return place
        return place + (place // 2) * (1 - 2 * (place % 2))

    def head(self, index):
        if self.shards == GROUP:
            return index
        return index // 4 * 2 + index % 4 // 2 * 4 + index % 2

    def block(self, ahead, other=False):
        ring = self.ring
        if ahead == 1:
            ring = ring + 1 - 2 * (ring % 2)
        elif ahead == 3:
            ring = 3 - ring
        elif ahead == 2:
            ring = (ring + 2) % 4
        core = 1 - self.core if other else self.core
        return self.turn(ring) * 2 + core

    def device(self, index):
        return {"st": index // self.shards, "seq": index % self.shards}

    def dp_device(self, dp):
        ys = lax.axis_size("y")
        return {"zh": dp // ys, "y": dp % ys}

    def any_device(self, flat):
        ys, streams = lax.axis_size("y"), lax.axis_size("st")
        return {
            "zh": flat // (streams * ys * self.shards),
            "st": flat // (ys * self.shards) % streams,
            "y": flat // self.shards % ys,
            "seq": flat % self.shards,
        }

    def flat(self):
        ys, streams = lax.axis_size("y"), lax.axis_size("st")
        z, y = lax.axis_index("zh"), lax.axis_index("y")
        st, seq = lax.axis_index("st"), lax.axis_index("seq")
        return ((z * streams + st) * ys + y) * self.shards + seq

    def dp(self):
        return lax.axis_index("zh") * lax.axis_size("y") + lax.axis_index("y")

    def right(self):
        return self.device(self.block(1))

    def left(self):
        return self.device(self.block(3))

    def across(self):
        return {"y": 1 - lax.axis_index("y")}

    def partner(self):
        return self.device(self.block(0, True))


def greet(devices):
    barrier = pltpu.get_barrier_semaphore()
    for device in devices:
        pl.semaphore_signal(
            barrier, inc=1, device_id=device, device_id_type=pl.DeviceIdType.MESH
        )
    pl.semaphore_wait(barrier, len(devices))


class RingGather:
    SEMS = 11

    def __init__(self, place, own, out, send, recv, one_way=False):
        rows = out.shape[1]
        half = rows // 2
        first, second = pl.ds(0, half), pl.ds(half, half)
        me, near, next_, opposite = (place.block(i) for i in (0, 1, 3, 2))
        to_near, to_next, to_partner = place.device(near), place.device(next_), place.partner()

        def copy(index, src, block, part, device):
            return remote(src, out.at[block, part], send.at[index], recv.at[index], device)

        self.local = pltpu.make_async_copy(own, out.at[me], send.at[self.SEMS])
        self.next = [
            copy(0, own.at[first], me, first, to_next),
            copy(1, own.at[second], me, second, to_next),
        ]
        self.near = [
            copy(2, own.at[first], me, first, to_near),
            copy(3, own.at[second], me, second, to_near),
        ]
        self.mate = remote(own, out.at[me], send.at[4], recv.at[4], to_partner)
        self.on = [copy(5, out.at[next_, first], next_, first, to_near)]
        if one_way:
            self.on.append(copy(6, out.at[next_, second], next_, second, to_near))
        else:
            self.on.append(copy(6, out.at[near, second], near, second, to_next))
        self.one_way = one_way
        self.across = [
            remote(out.at[next_], out.at[next_], send.at[7], recv.at[7], to_partner),
            remote(out.at[near], out.at[near], send.at[8], recv.at[8], to_partner),
            copy(9, out.at[opposite, first], opposite, first, to_partner),
            copy(10, out.at[opposite, second], opposite, second, to_partner),
        ]

    def start(self):
        self.next[0].start()
        self.near[0 if self.one_way else 1].start()
        self.next[1].start()
        self.near[1 if self.one_way else 0].start()
        self.mate.start()
        self.local.start()

    def pass_on(self):
        self.next[0].wait_recv()
        self.on[0].start()
        if self.one_way:
            self.next[1].wait_recv()
        else:
            self.near[1].wait_recv()
        self.on[1].start()

    def step_across(self):
        if not self.one_way:
            self.next[1].wait_recv()
        self.across[0].start()
        self.near[0].wait_recv()
        if self.one_way:
            self.near[1].wait_recv()
        self.across[1].start()

    def step_far(self):
        self.on[0].wait_recv()
        self.across[2].start()
        self.on[1].wait_recv()
        self.across[3].start()

    def finish(self):
        self.mate.wait_recv()
        for c in self.across:
            c.wait_recv()
        for c in self.next + self.near + [self.mate] + self.on + self.across:
            c.wait_send()
        self.local.wait()

    def run(self):
        self.start()
        self.pass_on()
        self.step_across()
        self.step_far()
        self.finish()


def ring_scatter(place, x, pair, out, near, far, send, recv, emit, between=()):
    between = list(between) + [lambda: None] * 3
    rows = x.shape[1]
    half = rows // 2
    step = 32
    to_left, to_right, to_partner = place.left(), place.right(), place.partner()
    swaps = {}
    for q in (2, 1, 3, 0):
        swaps[q] = remote(
            x.at[place.block(q, True)], pair.at[q], send.at[q], recv.at[q], to_partner
        )
        swaps[q].start()

    def add(q, low, high, extra=None):
        block = place.block(q)

        def one(i, _):
            part = pl.ds(pl.multiple_of(low + i * step, step), step)
            total = x[block, part].astype(f32) + pair[q, part].astype(f32)
            if extra is not None:
                inner = pl.ds(pl.multiple_of(i * step, step), step)
                total = total + far[extra, inner].astype(f32)
            out[q - 1, part] = total.astype(bf16)
            return 0

        lax.fori_loop(0, (high - low) // step, one, 0)

    first, second = pl.ds(0, half), pl.ds(half, half)

    def send_to(index, q, part, dst, device):
        c = remote(out.at[q - 1, part], dst, send.at[index], recv.at[index], device)
        c.start()
        return c

    swaps[2].wait_recv()
    add(2, 0, half)
    a = send_to(4, 2, first, far.at[0], to_right)
    add(2, half, rows)
    b = send_to(5, 2, second, far.at[1], to_left)
    swaps[1].wait_recv()
    add(1, 0, half)
    c = send_to(6, 1, first, near.at[0, first], to_right)
    swaps[3].wait_recv()
    add(3, half, rows)
    d = send_to(7, 3, second, near.at[1, second], to_left)
    between[0]()
    a.wait_recv()
    add(3, 0, half, 0)
    e = send_to(8, 3, first, near.at[1, first], to_left)
    b.wait_recv()
    add(1, half, rows, 1)
    g = send_to(9, 1, second, near.at[0, second], to_right)
    between[1]()
    swaps[0].wait_recv()
    own = place.block(0)
    c.wait_recv()
    d.wait_recv()
    e.wait_recv()
    g.wait_recv()

    def last(i, _):
        part = pl.ds(pl.multiple_of(i * step, step), step)
        emit(
            part,
            (x[own, part].astype(f32) + pair[0, part].astype(f32))
            + (near[0, part].astype(f32) + near[1, part].astype(f32)),
        )
        return 0

    lax.fori_loop(0, rows // step, last, 0)
    for copy in list(swaps.values()) + [a, b, c, d, e, g]:
        copy.wait_send()


def scatter_scratch(rows, width):
    return [
        pltpu.VMEM((4, rows, width), bf16),
        pltpu.VMEM((3, rows, width), bf16),
        pltpu.VMEM((2, rows, width), bf16),
        pltpu.VMEM((2, rows // 2, width), bf16),
        DMA((10,)),
        DMA((10,)),
    ]


def gather_scratch():
    return [DMA((RingGather.SEMS + 1,)), DMA((RingGather.SEMS,))]


def scatter_sum(x, base, shards, cid):
    _, rows, width = x.shape

    def body(x_ref, base_ref, out_ref, pair, out, near, far, send, recv):
        place = Place(shards)
        greet([place.right(), place.left(), place.partner()])

        def emit(part, total):
            out_ref[part] = (base_ref[part] + total).astype(bf16)

        ring_scatter(place, x_ref, pair, out, near, far, send, recv, emit)

    return pallas(
        body, jax.ShapeDtypeStruct((rows, width), bf16), [VMEM, VMEM], VMEM,
        scatter_scratch(rows, width), cid, 25,
    )(x, base)


def middle_step(x, tokens, gain, carry, shards, cid):
    _, rows, width = x.shape
    carries = [] if carry is None else [carry]

    def body(x_ref, tok_ref, gain_ref, *refs):
        refs = list(refs)
        carry_ref = refs.pop(0) if carries else None
        mid_ref, all_ref = refs.pop(0), refs.pop(0)
        carry_out = refs.pop(0) if carries else None
        held, pair, out, near, far, send, recv, gsend, grecv, ysend, yrecv = refs
        place = Place(shards)
        greet(
            [place.right(), place.left(), place.partner()]
            + ([place.across()] if carries else [])
        )
        if carries:
            over = remote(carry_ref, carry_out, ysend, yrecv, place.across())
            over.start()

        def emit(part, total):
            middle = tok_ref[part].astype(f32) + total
            mid_ref[part] = middle
            held[part] = (middle * rms_scale(middle) * gain_ref[...]).astype(bf16)

        ring_scatter(place, x_ref, pair, out, near, far, send, recv, emit)
        RingGather(place, held, all_ref, gsend, grecv).run()
        if carries:
            over.wait()

    return pallas(
        body,
        [
            jax.ShapeDtypeStruct((rows, width), f32),
            jax.ShapeDtypeStruct((GROUP, rows, width), bf16),
        ]
        + [jax.ShapeDtypeStruct(c.shape, c.dtype) for c in carries],
        [VMEM, VMEM, VMEM] + [ANY] * len(carries),
        [VMEM, ANY] + [ANY] * len(carries),
        [pltpu.VMEM((rows, width), bf16)] + scatter_scratch(rows, width) + gather_scratch()
        + [DMA, DMA],
        cid,
        50,
    )(x, tokens, gain, *carries)


def middle_back(x, middle, cotangent, gain, grads, shards, cid):
    _, rows, width = x.shape
    carries = [] if grads is None else [grads]

    def body(x_ref, mid_ref, cot_ref, gain_ref, *refs):
        refs = list(refs)
        grads_ref = refs.pop(0) if carries else None
        dm_ref, part_ref, all_ref = refs.pop(0), refs.pop(0), refs.pop(0)
        grads_out = refs.pop(0) if carries else None
        held, pair, out, near, far, send, recv, gsend, grecv, ysend, yrecv = refs
        place = Place(shards)
        greet(
            [place.right(), place.left(), place.partner()]
            + ([place.across()] if carries else [])
        )
        if carries:
            z, y = lax.axis_index("zh"), lax.axis_index("y")
            over = [
                remote(
                    grads_ref.at[1 - z, st, 1 - y], grads_out.at[st], ysend.at[st],
                    yrecv.at[st], place.across(),
                )
                for st in range(grads.shape[1])
            ]
            for c in over:
                c.start()
        part_ref[...] = jnp.zeros_like(part_ref)

        def emit(part, total):
            middle = mid_ref[part]
            scale = rms_scale(middle)
            normed = middle * scale
            part_ref[...] += jnp.sum(total * normed, axis=0, keepdims=True)
            dm = cot_ref[part].astype(f32) + norm_back(total * gain_ref[...], normed, scale)
            dm_ref[part] = dm
            held[part] = dm.astype(bf16)

        ring_scatter(place, x_ref, pair, out, near, far, send, recv, emit)
        RingGather(place, held, all_ref, gsend, grecv).run()
        if carries:
            for c in over:
                c.wait()

    return pallas(
        body,
        [
            jax.ShapeDtypeStruct((rows, width), f32),
            jax.ShapeDtypeStruct((1, width), f32),
            jax.ShapeDtypeStruct((GROUP, rows, width), bf16),
        ]
        + [jax.ShapeDtypeStruct((c.shape[1],) + c.shape[3:], c.dtype) for c in carries],
        [VMEM, VMEM, VMEM, VMEM] + [ANY] * len(carries),
        [VMEM, VMEM, ANY] + [ANY] * len(carries),
        [pltpu.VMEM((rows, width), bf16)] + scatter_scratch(rows, width) + gather_scratch()
        + [DMA((2,)), DMA((2,))],
        cid,
        50,
    )(x, middle, cotangent, gain, *carries)


def tokens_back(x, tokens, dm, gain, shards, cid):
    _, rows, width = x.shape

    def body(
        x_ref, tok_ref, dm_ref, gain_ref, grad_ref, part_ref, pair, out, near, far, send, recv
    ):
        place = Place(shards)
        greet([place.right(), place.left(), place.partner()])
        part_ref[...] = jnp.zeros_like(part_ref)

        def emit(part, total):
            tok = tok_ref[part].astype(f32)
            scale = rms_scale(tok)
            normed = tok * scale
            part_ref[...] += jnp.sum(total * normed, axis=0, keepdims=True)
            grad_ref[part] = (
                dm_ref[part] + norm_back(total * gain_ref[...], normed, scale)
            ).astype(bf16)

        ring_scatter(place, x_ref, pair, out, near, far, send, recv, emit)

    return pallas(
        body,
        (
            jax.ShapeDtypeStruct((rows, width), bf16),
            jax.ShapeDtypeStruct((1, width), f32),
        ),
        [VMEM, VMEM, VMEM, VMEM],
        (VMEM, VMEM),
        scatter_scratch(rows, width),
        cid,
        25,
    )(x, tokens, dm, gain)


class Exchange:
    SEMS = GROUP

    def __init__(self, place, x, out, send, recv):
        self.local = pltpu.make_async_copy(x.at[place.tp], out.at[place.tp], send.at[0])
        self.copies = []
        for k in range(1, GROUP):
            peer = (place.tp + k) % GROUP
            self.copies.append(
                remote(x.at[peer], out.at[place.tp], send.at[k], recv.at[k], place.device(peer))
            )

    def start(self):
        for c in self.copies:
            c.start()
        self.local.start()

    def finish(self):
        for c in self.copies:
            c.wait_recv()
        for c in self.copies:
            c.wait_send()
        self.local.wait()


def group_peers(place):
    return [place.device((place.tp + k) % GROUP) for k in range(1, GROUP)]


def columns_of(dp, t, shards):
    ys, streams = lax.axis_size("y"), lax.axis_size("st")
    z, y = dp // ys, dp % ys
    return ((z * streams + t // shards) * ys + y) * shards + t % shards


def exchange_back(x, planes, shards, cid):
    _, wrows, both = x.shape
    hidden = both // 2
    brows = hidden // planes
    step = min(wrows, 32)

    def body(x_ref, gate_ref, up_ref, got, send, recv):
        place = Place(shards)
        greet(group_peers(place))
        run = Exchange(place, x_ref, got, send, recv)
        run.start()
        run.finish()
        for t in range(GROUP):
            for dp in range(planes):
                flat = columns_of(dp, t, shards)
                for m, out in enumerate((gate_ref, up_ref)):
                    for at in range(0, wrows, step):
                        part = pl.ds(at, step)
                        out[part, flat * brows : (flat + 1) * brows] = got[
                            t, part, m * hidden + dp * brows : m * hidden + (dp + 1) * brows
                        ].astype(f32)

    shape = jax.ShapeDtypeStruct((wrows, hidden * GROUP), f32)
    return pallas(
        body, (shape, shape), [VMEM], (VMEM, VMEM),
        [pltpu.VMEM(x.shape, bf16), DMA((GROUP,)), DMA((GROUP,))], cid, 25,
    )(x)


class PlaceGather:
    SEMS = 5

    def __init__(self, own, out, send, recv, halves):
        z, y = lax.axis_index("zh"), lax.axis_index("y")
        dp, across = z * 2 + y, (1 - z) * 2 + y
        to_z, to_y = {"zh": 1 - z}, {"y": 1 - y}

        def copy(index, src, slot, part, device):
            return remote(
                src.at[part], out.at[slot, part], send.at[index], recv.at[index], device
            )

        first, second = halves
        self.local = pltpu.make_async_copy(own, out.at[dp], send.at[send.shape[0] - 1])
        self.z = [copy(0, own, dp, first, to_z), copy(1, own, dp, second, to_z)]
        self.y = [
            remote(own, out.at[dp], send.at[2], recv.at[2], to_y),
            copy(3, out.at[across], across, first, to_y),
            copy(4, out.at[across], across, second, to_y),
        ]

    def forward(self, half):
        self.z[half].wait_recv()
        self.y[1 + half].start()

    def finish(self):
        for c in self.y:
            c.wait_recv()
        for c in self.z + self.y:
            c.wait_send()


def front(tokens, cotangent, small, w_out, w_query, key_weight, value_weight, w_gate, w_up,
          w_down, planes, direct, shards, cid):
    rows, width = tokens.shape
    wrows = w_out.shape[0]
    srows, scols = small.shape
    brows = w_down.shape[0]
    hidden = brows * planes
    parts = [w_query.shape[1] // GROUP, key_weight.shape[1] // GROUP, value_weight.shape[1] // GROUP]
    qkv = sum(parts)
    slots = planes if direct else 1
    inputs = [tokens, cotangent, w_query, key_weight, value_weight, w_gate, w_up]
    if direct:
        inputs += [w_down, w_out]

    def body(*refs):
        refs = list(refs)

        def take(count):
            taken = refs[:count]
            del refs[:count]
            return taken

        small_ref, = take(1)
        sources = take(len(inputs))
        tok_all, cot_all, small_all, attn_all, ffn_all = take(5)
        down_all, wout_all = take(2) if direct else (None, None)
        held = take(len(inputs))
        (pack, isem, tsend, trecv, csend, crecv, ssend, srecv, psend, precv, fsend, frecv, asend,
         arecv, aasend, aarecv, dsend, drecv, wsend, wrecv) = refs
        place = Place(shards)
        tp, dp, flat = place.tp, place.dp(), place.flat()

        loads = [
            pltpu.make_async_copy(s, h, isem.at[i]) for i, (s, h) in enumerate(zip(sources, held))
        ]
        for i in (2, 3, 4, 0, 5, 6) + ((7, 8) if direct else ()) + (1,):
            loads[i].start()
        tok_ref, cot_ref, wq_ref, wk_ref, wv_ref, wg_ref, wu_ref = held[:7]

        barrier = pltpu.get_barrier_semaphore()

        def signal(device):
            pl.semaphore_signal(
                barrier, inc=1, device_id=device, device_id_type=pl.DeviceIdType.MESH
            )

        for device in group_peers(place):
            signal(device)
        for k in range(1, planes):
            signal(place.dp_device((dp + k) % planes))
        if direct:
            high, low = lax.axis_index("zh"), lax.axis_index("st")
            y, seq = lax.axis_index("y"), lax.axis_index("seq")
            to_seq = high * 2 + y
            from_high, from_y = seq // 2, seq % 2
            selfish = seq == to_seq
            mine = y == from_y
            for j in range(4):

                @pl.when(jnp.logical_and(mine, (from_high * 4 + j) != (high * 4 + seq)))
                def _():
                    signal({"zh": from_high, "seq": jnp.int32(j)})

            pl.semaphore_wait(
                barrier, GROUP - 1 + planes - 1 + 2 - selfish.astype(jnp.int32)
            )
        else:
            pl.semaphore_wait(barrier, GROUP - 1 + planes - 1)

        here = dp if direct else 0
        attn = []
        at = 0
        for i, (ref, cols) in enumerate(zip((wq_ref, wk_ref, wv_ref), parts)):
            loads[2 + i].wait()
            for k in range(GROUP):
                peer = (tp + k) % GROUP
                column = place.head(peer) * cols
                src = ref.at[:, pl.ds(pl.multiple_of(column, cols), cols)]
                dst = attn_all.at[here, tp, :, pl.ds(at, cols)]
                sem = i * GROUP + k
                if k == 0:
                    attn.append(pltpu.make_async_copy(src, dst, asend.at[sem]))
                else:
                    attn.append(
                        remote(src, dst, asend.at[sem], arecv.at[sem], place.device(peer))
                    )
                attn[-1].start()
            at += cols

        small_own = pltpu.make_async_copy(small_ref, small_all.at[tp, dp], ssend.at[0])
        small_own.start()
        small_dp = []
        for k in range(1, planes):
            small_dp.append(
                remote(
                    small_ref, small_all.at[tp, dp], ssend.at[k], srecv.at[k],
                    place.dp_device((dp + k) % planes),
                )
            )
            small_dp[-1].start()

        if direct:
            down_ref, wout_ref = held[7:]
            loads[7].wait()
            half = brows // 2
            down_dp = PlaceGather(
                down_ref, down_all, dsend, drecv, (pl.ds(0, half), pl.ds(half, half))
            )
            down_dp.z[0].start()
        loads[0].wait()
        tok = RingGather(place, tok_ref, tok_all, tsend, trecv, direct)
        tok.start()

        loads[5].wait()
        loads[6].wait()
        for t in range(GROUP):
            for d in range(planes):
                column = columns_of(d, t, shards)
                for m, ref in enumerate((wg_ref, wu_ref)):
                    lane = m * hidden + d * brows
                    pack[t, :, lane : lane + brows] = ref[:, column * brows : (column + 1) * brows]
        ffn = Exchange(place, pack, ffn_all, fsend, frecv)
        ffn.start()

        if direct:
            down_dp.y[0].start()
            down_dp.local.start()
            loads[8].wait()
            wout_copies = [
                remote(
                    wout_ref, wout_all.at[seq], wsend.at[k], wrecv.at[seq],
                    {"zh": z, "seq": to_seq},
                )
                for k, z in enumerate((high, 1 - high))
            ]
            wout_own = pltpu.make_async_copy(wout_ref, wout_all.at[seq], wsend.at[0])
            wout_over = remote(
                wout_all, wout_all, wsend.at[2], wrecv.at[4], place.across()
            )

            @pl.when(selfish)
            def _():
                wout_own.start()

            @pl.when(jnp.logical_not(selfish))
            def _():
                wout_copies[0].start()

            wout_copies[1].start()

        for i in range(3 * GROUP):
            if i % GROUP == 0:
                attn[i].wait()
            else:
                attn[i].wait_recv()
        if direct:
            half = GROUP // 2
            attn_dp = PlaceGather(
                attn_all.at[dp], attn_all, aasend, aarecv, (pl.ds(0, half), pl.ds(half, half))
            )
            attn_dp.z[0].start()
            attn_dp.y[0].start()
            attn_dp.z[1].start()
            down_dp.z[1].start()

        small_own.wait()
        for c in small_dp:
            c.wait_recv()
        small_tp = []
        for k in range(1, GROUP):
            small_tp.append(
                remote(
                    small_all.at[tp], small_all.at[tp], psend.at[k], precv.at[k],
                    place.device((tp + k) % GROUP),
                )
            )
            small_tp[-1].start()

        loads[1].wait()
        cot = RingGather(place, cot_ref, cot_all, csend, crecv, direct)
        tok.pass_on()
        cot.start()
        tok.step_across()
        if direct:
            down_dp.forward(0)

            @pl.when(mine)
            def _():
                for j in range(4):

                    @pl.when((from_high * 4 + j) != (high * 4 + seq))
                    def _():
                        remote(
                            wout_ref, wout_all.at[j], wsend.at[0], wrecv.at[j], place.across()
                        ).wait_recv()

                @pl.when(selfish)
                def _():
                    wout_own.wait()

                wout_over.start()

            attn_dp.forward(0)
        tok.step_far()
        cot.pass_on()
        if direct:
            attn_dp.forward(1)
        cot.step_across()
        if direct:
            down_dp.forward(1)
        cot.step_far()
        tok.finish()
        cot.finish()
        ffn.finish()
        for i in range(3 * GROUP):
            if i % GROUP:
                attn[i].wait_send()
        for c in small_tp:
            c.wait_recv()
        for c in small_dp + small_tp:
            c.wait_send()
        if direct:
            attn_dp.finish()
            down_dp.finish()
            down_dp.local.wait()

            @pl.when(jnp.logical_not(selfish))
            def _():
                wout_copies[0].wait_send()

            wout_copies[1].wait_send()

            @pl.when(mine)
            def _():
                wout_over.wait_send()

            @pl.when(jnp.logical_not(mine))
            def _():
                wout_over.wait_recv()

    shapes = [
        jax.ShapeDtypeStruct((GROUP, rows, width), bf16),
        jax.ShapeDtypeStruct((GROUP, rows, width), bf16),
        jax.ShapeDtypeStruct((GROUP, planes, srows, scols), bf16),
        jax.ShapeDtypeStruct((slots, GROUP, wrows, qkv), bf16),
        jax.ShapeDtypeStruct((GROUP, wrows, 2 * hidden), bf16),
    ]
    if direct:
        shapes += [
            jax.ShapeDtypeStruct((planes, brows, width), bf16),
            jax.ShapeDtypeStruct((planes, wrows, width), bf16),
        ]
    return pallas(
        body,
        shapes,
        [VMEM] + [ANY] * len(inputs),
        [ANY, ANY, VMEM] + [ANY] * (len(shapes) - 3),
        [pltpu.VMEM(x.shape, x.dtype) for x in inputs]
        + [pltpu.VMEM((GROUP, wrows, 2 * hidden), bf16), DMA((len(inputs),))]
        + gather_scratch() + gather_scratch()
        + [
            DMA((planes,)), DMA((planes,)), DMA((GROUP,)), DMA((GROUP,)),
            DMA((GROUP,)), DMA((GROUP,)), DMA((3 * GROUP,)), DMA((3 * GROUP,)),
            DMA((PlaceGather.SEMS,)), DMA((PlaceGather.SEMS,)),
            DMA((PlaceGather.SEMS + 1,)), DMA((PlaceGather.SEMS,)), DMA((3,)), DMA((5,)),
        ],
        cid,
        60,
    )(small, *inputs)


class Spread:
    def __init__(self, own, piece, relay, send, recv):
        z, low, y = (lax.axis_index(a) for a in ("zh", "st", "y"))
        to_z, to_y = {"zh": 1 - z}, {"y": 1 - y}
        beside, middle = {"st": 1 - low}, {"zh": 1 - z, "st": 1 - low}
        self.outer = z == low
        self.inner = z != low
        count = relay.shape[0]
        self.direct, self.toward, self.onward, self.y, self.on = [], [], [], [], []
        for h in range(count):
            at_y, at_on, at_more = count + h, 2 * count + h, 3 * count + h
            here, there = piece(z, h, y), piece(1 - z, h, y)
            self.direct.append(remote(own(h), here, send.at[h], recv.at[h], to_z))
            self.toward.append(
                remote(own(h), relay.at[h], send.at[h], recv.at[at_more], beside)
            )
            self.onward.append(
                remote(relay.at[h], here, send.at[at_more], recv.at[h], middle)
            )
            self.y.append(remote(own(h), here, send.at[at_y], recv.at[at_y], to_y))
            self.on.append(remote(there, there, send.at[at_on], recv.at[at_on], to_y))

    def start_z(self, first=0, last=None):
        @pl.when(self.outer)
        def _():
            for c in self.toward[first:last]:
                c.start()

        @pl.when(self.inner)
        def _():
            for c in self.direct[first:last]:
                c.start()

    def start_y(self):
        for c in self.y:
            c.start()

    def relay(self, half):
        @pl.when(self.inner)
        def _():
            self.toward[half].wait_recv()
            self.onward[half].start()

    def forward(self, half):
        self.direct[half].wait_recv()
        self.on[half].start()

    def finish(self):
        for c in self.y + self.on:
            c.wait_recv()
        for c in self.direct + self.y + self.on:
            c.wait_send()

        @pl.when(self.inner)
        def _():
            for c in self.onward:
                c.wait_send()


def rope_constants(length):
    exponent = np.arange(HEAD_SIZE // 2, dtype=np.float32) * np.float32(2.0 / HEAD_SIZE)
    inverse = np.power(np.float32(ROPE_BASE), -exponent).astype(np.float32)
    angles = np.arange(length, dtype=np.float32)[:, None] * inverse[None, :]
    cosine, sine = np.cos(angles.astype(np.float64)), np.sin(angles.astype(np.float64))
    return (
        jnp.asarray(np.concatenate([cosine, cosine], axis=1).astype(np.float32)),
        jnp.asarray(np.concatenate([-sine, sine], axis=1).astype(np.float32)),
    )


def document_mask(row, docs, low, count, keys):
    at_row = low + lax.broadcasted_iota(jnp.int32, (count, 1), 0)
    at_col = lax.broadcasted_iota(jnp.int32, (1, keys), 1)
    seg_row = jnp.zeros((count, 1), jnp.int32)
    seg_col = jnp.zeros((1, keys), jnp.int32)
    for d in range(docs):
        start = (row[:, d : d + 1] * 128.0 + row[:, docs + d : docs + d + 1]).astype(jnp.int32)
        seg_row = seg_row + jnp.where(at_row >= start, 1, 0)
        seg_col = seg_col + jnp.where(at_col >= start, 1, 0)
    return jnp.logical_and(at_row >= at_col, seg_row == seg_col)


def forward_pass(tokens, cotangent, small, w_out, w_query, key_weight, value_weight, w_gate,
                 w_up, w_down, docs, shards, cid):
    rows, width = tokens.shape
    wrows = w_out.shape[0]
    brows = w_down.shape[0]
    planes = 4
    hidden = brows * planes
    parts = [w_query.shape[1] // GROUP, key_weight.shape[1] // GROUP, value_weight.shape[1] // GROUP]
    qkv = sum(parts)
    qcols = parts[0]
    heads = qcols // HEAD_SIZE
    group_rows = rows * GROUP
    length = rows * shards
    streams = GROUP // shards
    gain_rows = width // 128
    grows = -(-(2 * gain_rows + 3) // 16) * 16
    srows = wrows + grows
    gcols = HEAD_SIZE // (planes * GROUP)
    cosine, sine = rope_constants(length)
    inputs = [tokens, cotangent, w_query, key_weight, value_weight, w_gate, w_up, w_down, w_out]
    score_scale = HEAD_SIZE ** (-0.5)

    def body(
        raw_ref, cos_ref, sin_ref, s0, s1, s2, s3, s4, s5, s6, s7, s8,
        cot_all, ffn_all, down_all, h1_out, h2_all, small_all, gains_ref, attn_all, wout_all,
        qkv_ref, low_ref, gate_ref, mixed_ref, gated_ref, mid_ref, hg, starts_ref,
        h0, h1, h2, h3, h4, h5, h6, h7, h8, small_ref, pack, attn_relay, ffn_relay, down_relay, tok_all, hid, partial, held_two, isem, osem,
        tsend, trecv, csend, crecv, gsend, grecv, ssend, srecv, psend, precv, fsend, frecv, asend,
        arecv, aasend, aarecv, ffsend, ffrecv, dsend, drecv, wsend, wrecv, pair, out, near, far,
        rsend, rrecv,
    ):
        sources = [s0, s1, s2, s3, s4, s5, s6, s7, s8]
        held = [h0, h1, h2, h3, h4, h5, h6, h7, h8]
        place = Place(shards)
        tp, dp = place.tp, place.dp()
        high, low = lax.axis_index("zh"), lax.axis_index("st")
        y, seq = lax.axis_index("y"), lax.axis_index("seq")
        loads = [
            pltpu.make_async_copy(s, h, isem.at[i]) for i, (s, h) in enumerate(zip(sources, held))
        ]
        for i in (2, 3, 4, 8, 0, 5, 6, 7, 1):
            loads[i].start()
        tok_ref, cot_ref, wq_ref, wk_ref, wv_ref, wg_ref, wu_ref, down_ref, wout_ref = held

        barrier = pltpu.get_barrier_semaphore()

        def signal(device):
            pl.semaphore_signal(
                barrier, inc=1, device_id=device, device_id_type=pl.DeviceIdType.MESH
            )

        for device in group_peers(place):
            signal(device)
        for k in range(1, planes):
            signal(place.dp_device((dp + k) % planes))
        to_seq = high * 2 + y
        from_high, from_y = seq // 2, seq % 2
        selfish = seq == to_seq
        mine = y == from_y
        for j in range(4):

            @pl.when(jnp.logical_and(mine, (from_high * 4 + j) != (high * 4 + seq)))
            def _():
                signal({"zh": from_high, "seq": jnp.int32(j)})

        inner = high != low

        @pl.when(inner)
        def _():
            signal({"zh": 1 - high, "st": 1 - low})

        pl.semaphore_wait(
            barrier,
            GROUP - 1 + planes - 1 + 2 - selfish.astype(jnp.int32) + inner.astype(jnp.int32),
        )

        attn = []
        at = 0
        for i, (ref, cols) in enumerate(zip((wq_ref, wk_ref, wv_ref), parts)):
            loads[2 + i].wait()
            for k in range(GROUP):
                peer = (tp + k) % GROUP
                column = place.head(peer) * cols
                src = ref.at[:, pl.ds(pl.multiple_of(column, cols), cols)]
                dst = attn_all.at[high, low, y, pl.ds(seq * wrows, wrows), pl.ds(at, cols)]
                sem = i * GROUP + k
                if k == 0:
                    attn.append(pltpu.make_async_copy(src, dst, asend.at[sem]))
                else:
                    attn.append(
                        remote(src, dst, asend.at[sem], arecv.at[sem], place.device(peer))
                    )
                attn[-1].start()
            at += cols

        small_ref[0:wrows] = raw_ref[0:wrows]
        flat = place.flat()
        block = raw_ref[wrows : wrows + 16].astype(f32)
        row_of = lax.broadcasted_iota(jnp.int32, (grows, 128), 0)
        placed = jnp.zeros((grows, 128), f32)
        per_row = 128 // wrows
        for i, (at, shift) in enumerate(
            (
                (flat // per_row, flat % per_row * wrows),
                (gain_rows + flat // per_row, flat % per_row * wrows),
                (2 * gain_rows, flat * gcols),
                (2 * gain_rows + 1, flat * gcols),
                (2 * gain_rows + 2, 0),
            )
        ):
            row = jnp.broadcast_to(block[i : i + 1], (grows, 128))
            placed = jnp.where(row_of == at, pltpu.roll(row, shift, 1), placed)
        small_ref[wrows:] = placed.astype(bf16)
        small_own = pltpu.make_async_copy(small_ref, small_all.at[tp, dp], ssend.at[0])
        small_own.start()
        small_dp = []
        for k in range(1, planes):
            small_dp.append(
                remote(
                    small_ref, small_all.at[tp, dp], ssend.at[k], srecv.at[k],
                    place.dp_device((dp + k) % planes),
                )
            )
            small_dp[-1].start()

        loads[5].wait()
        loads[6].wait()
        def pack_rows(i, _):
            part = pl.ds(pl.multiple_of(i * 16, 16), 16)
            for t in range(GROUP):
                for d in range(planes):
                    column = columns_of(d, t, shards)
                    for m, ref in enumerate((wg_ref, wu_ref)):
                        lane = m * hidden + d * brows
                        pack[t, part, lane : lane + brows] = ref[
                            part, column * brows : (column + 1) * brows
                        ]
            return 0

        lax.fori_loop(0, wrows // 16, pack_rows, 0)

        def arrived(copies):
            for i, c in enumerate(copies):
                if i % GROUP == 0:
                    c.wait()
                else:
                    c.wait_recv()

        arrived(attn)

        def attn_piece(zp, half, yp):
            return attn_all.at[zp, half, yp]

        attn_dp = Spread(
            lambda half: attn_piece(high, half, y), attn_piece, attn_relay, aasend, aarecv
        )
        attn_dp.start_z()
        attn_dp.start_y()
        loads[0].wait()
        tok = RingGather(place, tok_ref, tok_all, tsend, trecv, True)
        tok.start()
        small_own.wait()
        for c in small_dp:
            c.wait_recv()
        small_tp = []
        for k in range(1, GROUP):
            small_tp.append(
                remote(
                    small_all.at[tp], small_all.at[tp], psend.at[k], precv.at[k],
                    place.device((tp + k) % GROUP),
                )
            )
            small_tp[-1].start()
        attn_dp.relay(0)
        attn_dp.relay(1)

        loads[7].wait()
        half_rows = brows // 2

        def down_piece(zp, half, yp):
            return down_all.at[zp * 2 + yp, pl.ds(half * half_rows, half_rows)]

        down_dp = Spread(
            lambda half: down_ref.at[pl.ds(half * half_rows, half_rows)], down_piece, down_relay,
            dsend, drecv,
        )
        down_own = pltpu.make_async_copy(down_ref, down_all.at[dp], dsend.at[8])
        down_own.start()
        down_dp.start_z()
        tok.pass_on()
        ffn_dst = ffn_all.at[high, low, y, pl.ds(seq * wrows, wrows)]
        ffn = [pltpu.make_async_copy(pack.at[tp], ffn_dst, fsend.at[0])]
        for k, (ahead, other) in enumerate(
            ((3, False), (3, True), (0, True), (1, False), (1, True), (2, False), (2, True))
        ):
            peer = place.block(ahead, other)
            ffn.append(
                remote(
                    pack.at[peer], ffn_dst, fsend.at[k + 1], frecv.at[k + 1], place.device(peer)
                )
            )
        for c in ffn[:4]:
            c.start()
        loads[8].wait()
        wout_copies = [
            remote(
                wout_ref, wout_all.at[seq], wsend.at[k], wrecv.at[seq], {"zh": z, "seq": to_seq}
            )
            for k, z in enumerate((high, 1 - high))
        ]
        wout_own = pltpu.make_async_copy(wout_ref, wout_all.at[seq], wsend.at[0])
        wout_over = remote(wout_all, wout_all, wsend.at[2], wrecv.at[4], place.across())
        wout_copies[1].start()

        @pl.when(selfish)
        def _():
            wout_own.start()

        @pl.when(jnp.logical_not(selfish))
        def _():
            wout_copies[0].start()

        attn_dp.forward(0)
        attn_dp.forward(1)
        down_dp.start_y()
        tok.step_across()
        down_dp.relay(0)
        tok.step_far()
        for c in ffn[4:]:
            c.start()

        @pl.when(mine)
        def _():
            for j in range(4):

                @pl.when((from_high * 4 + j) != (high * 4 + seq))
                def _():
                    remote(
                        wout_ref, wout_all.at[j], wsend.at[0], wrecv.at[j], place.across()
                    ).wait_recv()

            @pl.when(selfish)
            def _():
                wout_own.wait()

            wout_over.start()

        for c in small_tp:
            c.wait_recv()
        gains = jnp.zeros((grows, 128), f32)
        for t in range(GROUP):
            for d in range(planes):
                gains = gains + small_all[t, d, pl.ds(wrows, grows)].astype(f32)
                flat = columns_of(d, t, shards)
                hg[flat * wrows : (flat + 1) * wrows] = small_all[t, d, pl.ds(0, wrows)]
        gains_ref[...] = gains
        gain_one = jnp.concatenate([gains[i : i + 1] for i in range(gain_rows)], axis=1)
        gain_two = jnp.concatenate(
            [gains[gain_rows + i : gain_rows + i + 1] for i in range(gain_rows)], axis=1
        )
        query_gain = gains[2 * gain_rows : 2 * gain_rows + 1]
        key_gain = gains[2 * gain_rows + 1 : 2 * gain_rows + 2]
        starts = []
        for st in range(streams):
            block = small_all[st * shards, dp, pl.ds(wrows, grows)].astype(f32)
            starts.append(block[2 * gain_rows + 2 : 2 * gain_rows + 3])
            starts_ref[st : st + 1] = starts[st]

        tok.finish()
        step = 32

        def norm(i, _):
            block = i // (rows // step)
            inner = pl.ds(pl.multiple_of(i % (rows // step) * step, step), step)
            value = tok_all[block, inner].astype(f32)
            hid[block, inner] = (value * rms_scale(value) * gain_one).astype(bf16)
            return 0

        lax.fori_loop(0, group_rows // step, norm, 0)
        save = pltpu.make_async_copy(hid, h1_out, osem)
        save.start()
        down_dp.relay(1)
        attn_dp.finish()
        weight = attn_all[...].reshape(width, qkv)
        head = place.head(tp)
        lanes = lax.broadcasted_iota(jnp.int32, (1, 128), 1)

        def rotary(x, gain, s):
            scaled = x * rms_scale(x) * gain
            return (
                scaled * cos_ref[...] + pltpu.roll(scaled, HEAD_SIZE // 2, 1) * sin_ref[...]
            ).astype(bf16)

        def project(s, _):
            part = pl.ds(pl.multiple_of(s * length, length), length)
            normed = hid[pl.ds(s * shards, shards)].reshape(length, width)
            raw = jnp.dot(normed, weight, preferred_element_type=f32)
            qkv_ref[part] = raw
            logit = jnp.dot(normed, hg[...], preferred_element_type=f32)
            for g in range(heads):
                at = g * HEAD_SIZE
                low_ref[part, at : at + HEAD_SIZE] = rotary(
                    raw[:, at : at + HEAD_SIZE], query_gain, s
                )
                own = jnp.sum(
                    jnp.where(lanes == head * heads + g, logit, 0.0), axis=1, keepdims=True
                )
                gate_ref[part, at : at + HEAD_SIZE] = jnp.broadcast_to(
                    jax.nn.sigmoid(own), (length, HEAD_SIZE)
                )
            low_ref[part, qcols : qcols + HEAD_SIZE] = rotary(
                raw[:, qcols : qcols + HEAD_SIZE], key_gain, s
            )
            low_ref[part, qcols + HEAD_SIZE :] = raw[:, qcols + HEAD_SIZE :].astype(bf16)
            return 0

        lax.fori_loop(0, streams, project, 0)
        arrived(ffn)

        quarter = shards * wrows // 2

        def ffn_piece(zp, half, yp):
            return ffn_all.at[zp, half // 2, yp, pl.ds(half % 2 * quarter, quarter)]

        ffn_dp = Spread(
            lambda half: ffn_piece(high, half, y), ffn_piece, ffn_relay, ffsend, ffrecv
        )
        ffn_dp.start_z(0, 2)
        ffn_dp.start_y()
        block = 128
        def attend(s, _):
            base = pl.multiple_of(s * length, length)
            row = starts_ref[pl.ds(s, 1)]
            for r in range(0, length, block):
                keys = r + block
                allowed = document_mask(row, docs, r, block, keys)
                key = low_ref[pl.ds(base, keys), qcols : qcols + HEAD_SIZE]
                value = low_ref[pl.ds(base, keys), qcols + HEAD_SIZE :]
                part = pl.ds(base + r, block)
                for g in range(heads):
                    at = g * HEAD_SIZE
                    scores = (
                        lax.dot_general(
                            low_ref[part, at : at + HEAD_SIZE], key, (((1,), (1,)), ((), ())),
                            preferred_element_type=f32,
                        )
                        * score_scale
                    )
                    scores = jnp.where(allowed, scores, MASK_FILL)
                    weights = jnp.exp(scores - jnp.max(scores, axis=1, keepdims=True))
                    probs = weights / jnp.sum(weights, axis=1, keepdims=True)
                    mixed = jnp.dot(
                        probs.astype(bf16), value, preferred_element_type=f32
                    ).astype(bf16)
                    mixed_ref[part, at : at + HEAD_SIZE] = mixed
                    gated_ref[part, at : at + HEAD_SIZE] = (
                        mixed.astype(f32) * gate_ref[part, at : at + HEAD_SIZE]
                    ).astype(bf16)
            return 0

        lax.fori_loop(0, streams, attend, 0)

        @pl.when(jnp.logical_not(mine))
        def _():
            wout_over.wait_recv()

        wide = 512
        def give(i, _):
            s = i // (width // wide)
            cols = pl.ds(pl.multiple_of(i % (width // wide) * wide, wide), wide)
            product = jnp.dot(
                gated_ref[pl.ds(pl.multiple_of(s * length, length), length)],
                wout_all[:, :, cols].reshape(qcols, wide),
                preferred_element_type=f32,
            )
            partial[pl.ds(s * shards, shards), :, cols] = product.astype(bf16).reshape(
                shards, rows, wide
            )
            return 0

        lax.fori_loop(0, streams * (width // wide), give, 0)

        def emit(part, total):
            middle = tok_ref[part].astype(f32) + total
            mid_ref[part] = middle
            held_two[part] = (middle * rms_scale(middle) * gain_two).astype(bf16)

        def first():
            ffn_dp.relay(0)
            down_dp.forward(0)

        def second():
            ffn_dp.relay(1)
            ffn_dp.start_z(2, 3)
            down_dp.forward(1)
            ffn_dp.forward(0)

        ring_scatter(
            place, partial, pair, out, near, far, rsend, rrecv, emit, (first, second)
        )
        two = RingGather(place, held_two, h2_all, gsend, grecv, True)
        two.start()
        ffn_dp.forward(1)
        ffn_dp.relay(2)
        two.pass_on()
        ffn_dp.start_z(3, 4)
        loads[1].wait()
        cot = RingGather(place, cot_ref, cot_all, csend, crecv, True)
        cot.start()
        ffn_dp.relay(3)
        two.step_across()
        ffn_dp.forward(2)
        two.step_far()
        cot.pass_on()
        ffn_dp.forward(3)
        cot.step_across()
        cot.step_far()
        two.finish()
        cot.finish()
        ffn_dp.finish()
        down_dp.finish()
        down_own.wait()
        save.wait()
        for i, c in enumerate(attn):
            if i % GROUP:
                c.wait_send()
        for c in ffn[1:] + small_dp + small_tp:
            c.wait_send()

        @pl.when(jnp.logical_not(selfish))
        def _():
            wout_copies[0].wait_send()

        wout_copies[1].wait_send()

        @pl.when(mine)
        def _():
            wout_over.wait_send()

    pieces = (2, streams, 2, shards * wrows)
    shape = jax.ShapeDtypeStruct
    return pallas(
        body,
        [
            shape((GROUP, rows, width), bf16),
            shape(pieces + (2 * hidden,), bf16),
            shape((planes, brows, width), bf16),
            shape((GROUP, rows, width), bf16),
            shape((GROUP, rows, width), bf16),
            shape((GROUP, planes, srows, 128), bf16),
            shape((grows, 128), f32),
            shape(pieces + (qkv,), bf16),
            shape((planes, wrows, width), bf16),
            shape((group_rows, qkv), f32),
            shape((group_rows, qkv), bf16),
            shape((group_rows, qcols), f32),
            shape((group_rows, qcols), bf16),
            shape((group_rows, qcols), bf16),
            shape((rows, width), f32),
            shape((width, 128), bf16),
            shape((streams, 128), f32),
        ],
        [VMEM] * 3 + [ANY] * len(inputs),
        [ANY] * 5 + [VMEM] * 12,
        [pltpu.VMEM(x.shape, x.dtype) for x in inputs]
        + [
            pltpu.VMEM((srows, 128), bf16),
            pltpu.VMEM((GROUP, wrows, 2 * hidden), bf16),
            pltpu.VMEM((2, shards * wrows, qkv), bf16),
            pltpu.VMEM((4, shards * wrows // 2, 2 * hidden), bf16),
            pltpu.VMEM((2, brows // 2, width), bf16),
            pltpu.VMEM((GROUP, rows, width), bf16),
            pltpu.VMEM((GROUP, rows, width), bf16),
            pltpu.VMEM((GROUP, rows, width), bf16),
            pltpu.VMEM((rows, width), bf16),
            DMA((len(inputs),)),
            DMA,
        ]
        + gather_scratch() + gather_scratch() + gather_scratch()
        + [
            DMA((planes,)), DMA((planes,)), DMA((GROUP,)), DMA((GROUP,)),
            DMA((GROUP,)), DMA((GROUP,)), DMA((3 * GROUP,)), DMA((3 * GROUP,)),
            DMA((8,)), DMA((8,)), DMA((16,)), DMA((16,)),
            DMA((9,)), DMA((8,)), DMA((3,)), DMA((5,)),
        ]
        + scatter_scratch(rows, width),
        cid,
        100,
        56,
    )(small, cosine, sine, *inputs)


class PlaceSums:
    SENDS, RECVS = 8, 6

    def __init__(self, piece, got, far, near, relay, send, recv):
        z, low, y = (lax.axis_index(a) for a in ("zh", "st", "y"))
        to_z, to_y = {"zh": 1 - z}, {"y": 1 - y}
        beside, middle = {"st": 1 - low}, {"zh": 1 - z, "st": 1 - low}
        self.outer, self.inner = z == low, z != low
        self.got, self.far, self.near = got, far, near
        self.y_far = remote(piece(1 - z, 1 - y), got.at[0], send.at[0], recv.at[0], to_y)
        self.y_near = remote(piece(z, 1 - y), got.at[1], send.at[1], recv.at[1], to_y)
        self.loads = [
            pltpu.make_async_copy(piece(1 - z, y), far, send.at[2]),
            pltpu.make_async_copy(piece(z, y), near, send.at[3]),
        ]

        def half(ref, h):
            if len(far.shape) == 3:
                return ref.at[h]
            count = far.shape[0] // 2
            return ref.at[pl.ds(h * count, count)]

        self.direct, self.toward, self.onward = [], [], []
        for h in range(2):
            dst = half(got.at[2], h)
            self.direct.append(
                remote(half(far, h), dst, send.at[4 + h], recv.at[2 + h], to_z)
            )
            self.toward.append(
                remote(half(far, h), half(relay, h), send.at[4 + h], recv.at[4 + h], beside)
            )
            self.onward.append(
                remote(half(relay, h), dst, send.at[6 + h], recv.at[2 + h], middle)
            )

    def load(self):
        for c in self.loads:
            c.start()

    def over_z(self, late=False):
        self.loads[0].wait()
        self.y_far.wait_recv()
        self.each(lambda at: self.put(at))
        Spread.start_z(self, 0, 1 if late else 2)

    def start_late(self):
        Spread.start_z(self, 1, 2)

    def relay(self, half):
        @pl.when(self.inner)
        def _():
            self.toward[half].wait_recv()
            self.onward[half].start()

    def put(self, at):
        self.far[at] = (self.far[at].astype(f32) + self.got[(0,) + at].astype(f32)).astype(bf16)

    def each(self, visit):
        lead, rows = self.far.shape[:-2], self.far.shape[-2]

        def inner(i, _):
            part = pl.ds(pl.multiple_of(i * 32, 32), 32)
            if lead:
                for k in range(lead[0]):
                    visit((k, part))
            else:
                visit((part,))
            return 0

        lax.fori_loop(0, rows // 32, inner, 0)

    def total(self, at):
        return (self.near[at].astype(f32) + self.got[(1,) + at].astype(f32)) + self.got[
            (2,) + at
        ].astype(f32)

    def arrive(self):
        self.loads[1].wait()
        self.y_near.wait_recv()
        for c in self.direct:
            c.wait_recv()

    def drain(self):
        for c in [self.y_far, self.y_near] + self.direct:
            c.wait_send()

        @pl.when(self.inner)
        def _():
            for c in self.onward:
                c.wait_send()


def backward_pass(x, final, middle, tokens, cotangent, gains, headgate, qkv_w, out_w, hidden_one,
                  qkv, low, gate, mixed, gated, starts, down_grad, ffn_grad, docs, shards, cid):
    _, rows, width = x.shape
    planes = 4
    streams = GROUP // shards
    length = rows * shards
    group_rows = rows * GROUP
    qcols = gate.shape[1]
    qkv_cols = qkv.shape[1]
    kcols = (qkv_cols - qcols) // 2
    heads = qcols // HEAD_SIZE
    brows = down_grad.shape[2]
    both = ffn_grad.shape[4]
    hidden = both // 2
    wrows = width // (planes * GROUP)
    gain_rows = width // 128
    score_scale = HEAD_SIZE ** (-0.5)
    cosine, sine = rope_constants(length)
    srows = 24
    inputs = [
        x, middle, tokens, cotangent, headgate, qkv_w, out_w, qkv, low, gate, mixed, gated,
    ]

    def body(
        gains_ref, starts_ref, cos_ref, sin_ref, final_ref, h1_ref, down_ref, ffn_ref,
        i0, i1, i2, i3, i4, i5, i6, i7, i8, i9, i10, i11,
        t0, t1, t2, t3, t4, t5, t6, t7, t8, s_out,
        layer_ref, tgrad_ref, gate_out, up_out, query_out, key_out, value_out, o_out, down_out,
        fsem, partial, mid_ref, tok_ref, cot_ref, hg_ref, wq_ref, wout_ref, qkv_ref, low_ref, gate_ref,
        mixed_ref, gated_ref,
        held, db_all, dmid, gq, dgl, dk_acc, dv_acc, dmix, small, stage, s_got, s_held, s_line,
        g_got, g_far, g_near, g_in, d_got, d_far, d_near, q_own, q_got, q_far, q_near, q_in,
        o_own, o_got, o_far, o_near, o_in, g_relay, d_relay, q_relay, o_relay,
        pair, out, near, far, rsend, rrecv, r2send, r2recv, r3send, r3recv, csend, crecv,
        isem, gsend, grecv, dsend, drecv, qsend, qrecv, osend, orecv, gxsend, gxrecv, qxsend,
        qxrecv, oxsend, oxrecv, asend, arecv, bsend, brecv, lsem, turn,
    ):
        sources = [i0, i1, i2, i3, i4, i5, i6, i7, i8, i9, i10, i11]
        targets = [
            partial, mid_ref, tok_ref, cot_ref, hg_ref, wq_ref, wout_ref, qkv_ref, low_ref,
            gate_ref, mixed_ref, gated_ref,
        ]
        finals = [
            pltpu.make_async_copy(ready, target, fsem.at[i])
            for i, (ready, target) in enumerate(
                (
                    (layer_ref, t0), (tgrad_ref, t1), (gate_out, t2), (up_out, t3),
                    (query_out, t4), (key_out, t5), (value_out, t6), (o_out, t7), (down_out, t8),
                )
            )
        ]
        place = Place(shards)
        tp, dp, flat = place.tp, place.dp(), place.flat()
        high, y, seq = lax.axis_index("zh"), lax.axis_index("y"), lax.axis_index("seq")
        loads = [
            pltpu.make_async_copy(s, t, isem.at[i])
            for i, (s, t) in enumerate(zip(sources, targets))
        ]
        for c in loads[:4]:
            c.start()
        barrier = pltpu.get_barrier_semaphore()

        def signal(device, semaphore=barrier):
            pl.semaphore_signal(
                semaphore, inc=1, device_id=device, device_id_type=pl.DeviceIdType.MESH
            )

        for device in group_peers(place):
            signal(device)
        for k in range(1, planes):
            signal(place.dp_device((dp + k) % planes))
        owner = place.head(tp) * planes + dp
        source = {"st": lax.axis_index("st"), "seq": high * 2 + y}
        source.update(place.dp_device(seq))

        @pl.when(owner != flat)
        def _():
            signal(source)

        inner = high != lax.axis_index("st")

        @pl.when(inner)
        def _():
            signal({"zh": 1 - high, "st": 1 - lax.axis_index("st")})

        pl.semaphore_wait(
            barrier,
            GROUP + planes - 2 + (owner != flat).astype(jnp.int32) + inner.astype(jnp.int32),
        )

        ffn = PlaceSums(
            lambda zp, yp: ffn_ref.at[zp, :, yp], g_got, g_far, g_near, g_relay, gsend, grecv
        )
        down = PlaceSums(lambda zp, yp: down_ref.at[zp, yp], d_got, d_far, d_near, d_relay, dsend, drecv)
        down.y_far.start()
        ffn.y_far.start()
        ffn.y_near.start()
        down.load()
        ffn.load()
        for c in loads[4:]:
            c.start()

        small[...] = jnp.zeros_like(small)
        gain_all = gains_ref[...]
        gain_one = jnp.concatenate([gain_all[i : i + 1] for i in range(gain_rows)], axis=1)
        gain_two = jnp.concatenate(
            [gain_all[gain_rows + i : gain_rows + i + 1] for i in range(gain_rows)], axis=1
        )
        query_gain = gain_all[2 * gain_rows : 2 * gain_rows + 1]
        key_gain = gain_all[2 * gain_rows + 1 : 2 * gain_rows + 2]
        for c in loads[:4]:
            c.wait()

        def emit_dm(part, total):
            value = mid_ref[part]
            scale = rms_scale(value)
            normed = value * scale
            small[17:18] += jnp.sum(total * normed, axis=0, keepdims=True)
            dm = cot_ref[part].astype(f32) + norm_back(total * gain_two, normed, scale)
            dmid[part] = dm
            held[part] = dm.astype(bf16)

        ring_scatter(place, partial, pair, out, near, far, rsend, rrecv, emit_dm)
        grad = RingGather(place, held, db_all, csend, crecv)
        grad.start()
        h1_all = partial
        load_h1 = pltpu.make_async_copy(h1_ref, h1_all, lsem.at[0])
        load_h1.start()
        down.over_z()
        grad.pass_on()
        down.relay(0)
        grad.step_across()
        down.relay(1)
        grad.step_far()
        for c in loads[4:]:
            c.wait()
        grad.finish()

        lanes = lax.broadcasted_iota(jnp.int32, (1, 128), 1)
        head = place.head(tp)
        def open_out(s, _):
            part = pl.ds(pl.multiple_of(s * length, length), length)
            db = db_all[pl.ds(s * shards, shards)].reshape(length, width)
            da = lax.dot_general(
                db, wout_ref[...], (((1,), (1,)), ((), ())), preferred_element_type=f32
            )
            logits = jnp.zeros((length, 128), f32)
            for g in range(heads):
                at = g * HEAD_SIZE
                piece = da[:, at : at + HEAD_SIZE]
                opened = gate_ref[part, at : at + HEAD_SIZE]
                dmix[part, at : at + HEAD_SIZE] = (piece * opened).astype(bf16)
                own = jnp.sum(
                    piece * mixed_ref[part, at : at + HEAD_SIZE].astype(f32), axis=1,
                    keepdims=True,
                )
                logits = jnp.where(
                    lanes == head * heads + g, own * opened * (1.0 - opened), logits
                )
            dgl[part] = logits.astype(bf16)
            return 0

        lax.fori_loop(0, streams, open_out, 0)
        wide = 512
        def out_grad(i, _):
            cols = pl.ds(pl.multiple_of(i * wide, wide), wide)
            product = lax.dot_general(
                gated_ref[...], db_all[:, :, cols].reshape(group_rows, wide),
                (((0,), (0,)), ((), ())), preferred_element_type=f32,
            ).astype(bf16)
            for j in range(planes):
                o_own[j // 2, j % 2, :, cols] = product[j * wrows : (j + 1) * wrows]
            return 0

        lax.fori_loop(0, width // wide, out_grad, 0)
        outs = PlaceSums(lambda zp, yp: o_own.at[zp, yp], o_got, o_far, o_near, o_relay, osend, orecv)
        outs.y_far.start()
        outs.load()
        ffn.over_z(True)

        block = 128

        def attend_back(s, carried):
            query_part, key_part = carried
            base = pl.multiple_of(s * length, length)
            row = starts_ref[pl.ds(s, 1)]
            dk_acc[...] = jnp.zeros_like(dk_acc)
            dv_acc[...] = jnp.zeros_like(dv_acc)

            def back(grad_rotated, raw, gain):
                grad_gained = grad_rotated * cos_ref[...] - pltpu.roll(
                    grad_rotated, HEAD_SIZE // 2, 1
                ) * sin_ref[...]
                scale = rms_scale(raw)
                normed = raw * scale
                return (
                    jnp.sum(grad_gained * normed, axis=0, keepdims=True),
                    norm_back(grad_gained * gain, normed, scale).astype(bf16),
                )

            for r in range(0, length, block):
                keys = r + block
                allowed = document_mask(row, docs, r, block, keys)
                key = low_ref[pl.ds(base, keys), qcols : qcols + HEAD_SIZE]
                value = low_ref[pl.ds(base, keys), qcols + HEAD_SIZE :]
                part = pl.ds(base + r, block)
                for g in range(heads):
                    at = g * HEAD_SIZE
                    query = low_ref[part, at : at + HEAD_SIZE]
                    scores = (
                        lax.dot_general(
                            query, key, (((1,), (1,)), ((), ())), preferred_element_type=f32
                        )
                        * score_scale
                    )
                    scores = jnp.where(allowed, scores, MASK_FILL)
                    weights = jnp.exp(scores - jnp.max(scores, axis=1, keepdims=True))
                    probs = weights / jnp.sum(weights, axis=1, keepdims=True)
                    dout = dmix[part, at : at + HEAD_SIZE]
                    dprobs = lax.dot_general(
                        dout, value, (((1,), (1,)), ((), ())), preferred_element_type=f32
                    )
                    delta = jnp.sum(probs * dprobs, axis=1, keepdims=True)
                    dscores = (probs * (dprobs - delta)).astype(bf16)
                    dq = jnp.dot(dscores, key, preferred_element_type=f32) * score_scale
                    gq[part, at : at + HEAD_SIZE] = dq.astype(bf16)
                    dk_acc[0:keys] += lax.dot_general(
                        dscores, query, (((0,), (0,)), ((), ())), preferred_element_type=f32
                    )
                    dv_acc[0:keys] += lax.dot_general(
                        probs.astype(bf16), dout, (((0,), (0,)), ((), ())),
                        preferred_element_type=f32,
                    )
            part = pl.ds(base, length)
            for g in range(heads):
                at = g * HEAD_SIZE
                sums, grads = back(
                    gq[part, at : at + HEAD_SIZE].astype(f32), qkv_ref[part, at : at + HEAD_SIZE],
                    query_gain,
                )
                query_part = query_part + sums
                gq[part, at : at + HEAD_SIZE] = grads
            sums, grads = back(
                (dk_acc[...] * score_scale).astype(bf16).astype(f32),
                qkv_ref[part, qcols : qcols + HEAD_SIZE], key_gain,
            )
            key_part = key_part + sums
            gq[part, qcols : qcols + HEAD_SIZE] = grads
            gq[part, qcols + HEAD_SIZE :] = dv_acc[...].astype(bf16)
            return query_part, key_part

        query_part, key_part = lax.fori_loop(
            0, streams, attend_back,
            (jnp.zeros((1, HEAD_SIZE), f32), jnp.zeros((1, HEAD_SIZE), f32)),
        )

        load_h1.wait()
        def qkv_grad(n, _):
            cols = pl.ds(pl.multiple_of(n * 256, 256), 256)
            product = lax.dot_general(
                h1_all[:, :, cols].reshape(group_rows, 256), gq[...], (((0,), (0,)), ((), ())),
                preferred_element_type=f32,
            )
            q_own[n // 4, n // 2 % 2, n % 2] = product.astype(bf16)
            return 0

        lax.fori_loop(0, width // 256, qkv_grad, 0)
        qkvs = PlaceSums(lambda zp, yp: q_own.at[zp, :, yp], q_got, q_far, q_near, q_relay, qsend, qrecv)
        qkvs.y_far.start()
        outs.y_near.start()
        qkvs.y_near.start()
        down.y_near.start()
        qkvs.load()
        def headgate_grad(i, _):
            cols = pl.ds(pl.multiple_of(i * wide, wide), wide)
            small[0:16, cols] = lax.dot_general(
                dgl[...], h1_all[:, :, cols].reshape(group_rows, wide),
                (((0,), (0,)), ((), ())), preferred_element_type=f32,
            )[0:16]
            return 0

        lax.fori_loop(0, width // wide, headgate_grad, 0)

        def dh1(i, _):
            s = i // (width // wide)
            at = pl.multiple_of(i % (width // wide) * wide, wide)
            part, cols = pl.ds(pl.multiple_of(s * length, length), length), pl.ds(at, wide)
            product = lax.dot_general(
                gq[part], wq_ref[cols], (((1,), (1,)), ((), ())), preferred_element_type=f32
            ) + lax.dot_general(
                dgl[part], hg_ref[cols], (((1,), (1,)), ((), ())), preferred_element_type=f32
            )
            partial[pl.ds(s * shards, shards), :, cols] = product.astype(bf16).reshape(
                shards, rows, wide
            )
            return 0

        lax.fori_loop(0, streams * (width // wide), dh1, 0)

        def emit_tokens(part, total):
            tok = tok_ref[part].astype(f32)
            scale = rms_scale(tok)
            normed = tok * scale
            small[16:17] += jnp.sum(total * normed, axis=0, keepdims=True)
            tgrad_ref[part] = (
                dmid[part] + norm_back(total * gain_one, normed, scale)
            ).astype(bf16)

        load_final = pltpu.make_async_copy(final_ref, db_all, lsem.at[1])
        load_final.start()
        ring_scatter(
            place, partial, pair, out, near, far, r2send, r2recv, emit_tokens,
            (lambda: ffn.relay(0), ffn.start_late),
        )
        finals[1].start()
        ring_peers = [place.right(), place.left(), place.partner()]
        for device in ring_peers:
            signal(device, turn)
        outs.over_z()
        qkvs.over_z()
        ffn.relay(1)

        small[18:19] = jnp.concatenate([query_part] * gain_rows, axis=1)
        small[19:20] = jnp.concatenate([key_part] * gain_rows, axis=1)
        for t in range(GROUP):
            for d in range(planes):
                lane = columns_of(d, t, shards) // 2 * 128
                stage[t, d * srows : (d + 1) * srows] = small[:, lane : lane + 128]
        sums = Exchange(place, stage, s_got, asend, arecv)
        sums.start()

        load_final.wait()
        pl.semaphore_wait(turn, len(ring_peers))

        def emit_layer(part, total):
            layer_ref[part] = (mid_ref[part] + total).astype(bf16)

        def first():
            outs.relay(0)
            outs.relay(1)

        def scatter_rows(total, ready, send, recv, into):
            def keep(at):
                ready[at] = total(at).astype(bf16)

            copies = []
            for k in range(GROUP):
                peer = (tp + k) % GROUP
                src = ready.at[peer // shards, pl.ds(peer % shards * wrows, wrows)]
                if k == 0:
                    copies.append(pltpu.make_async_copy(src, into.at[tp], send.at[0]))
                else:
                    copies.append(
                        remote(src, into.at[tp], send.at[k], recv.at[k], place.device(peer))
                    )
            return keep, copies

        keep_ffn, ffn_rows = scatter_rows(ffn.total, g_near, gxsend, gxrecv, g_in)

        def second():
            qkvs.relay(0)
            qkvs.relay(1)
            ffn.arrive()
            ffn.each(keep_ffn)
            for c in ffn_rows:
                c.start()

        ring_scatter(
            place, db_all, pair, out, near, far, r3send, r3recv, emit_layer, (first, second)
        )
        finals[0].start()
        sums.finish()
        s_held[...] = jnp.sum(s_got[...], axis=0).reshape(s_held.shape)
        line_own = pltpu.make_async_copy(s_held.at[dp], s_line.at[dp], bsend.at[0])
        line_own.start()
        lines = []
        for k in range(1, planes):
            to = (dp + k) % planes
            lines.append(
                remote(
                    s_held.at[to], s_line.at[dp], bsend.at[k], brecv.at[k], place.dp_device(to)
                )
            )
            lines[-1].start()

        down.arrive()

        def put_down(at):
            down_out[at] = down.total(at)

        down.each(put_down)
        finals[8].start()

        def landed(copies):
            copies[0].wait()
            for c in copies[1:]:
                c.wait_recv()

        landed(ffn_rows)
        def unpack_rows(i, _):
            part = pl.ds(pl.multiple_of(i * 16, 16), 16)
            for t in range(GROUP):
                for d in range(planes):
                    column = columns_of(d, t, shards)
                    for m, ref in enumerate((gate_out, up_out)):
                        lane = m * hidden + d * brows
                        ref[part, column * brows : (column + 1) * brows] = g_in[
                            t, part, lane : lane + brows
                        ].astype(f32)
            return 0

        lax.fori_loop(0, wrows // 16, unpack_rows, 0)
        finals[2].start()
        finals[3].start()

        outs.arrive()

        def keep_out(at):
            o_near[at] = outs.total(at).astype(bf16)

        outs.each(keep_out)
        out_own = pltpu.make_async_copy(o_near, o_in, oxsend)
        out_far = remote(o_near, o_in, oxsend, oxrecv, place.any_device(owner))

        @pl.when(owner == flat)
        def _():
            out_own.start()

        @pl.when(owner != flat)
        def _():
            out_far.start()

        qkvs.arrive()
        keep, qkv_rows = scatter_rows(qkvs.total, q_near, qxsend, qxrecv, q_in)
        qkvs.each(keep)
        for c in qkv_rows:
            c.start()

        landed(qkv_rows)
        for t in range(GROUP):
            home = place.head(t)
            query_out[:, home * qcols : (home + 1) * qcols] = q_in[t, :, :qcols].astype(f32)
            key_out[:, home * kcols : (home + 1) * kcols] = q_in[
                t, :, qcols : qcols + kcols
            ].astype(f32)
            value_out[:, home * kcols : (home + 1) * kcols] = q_in[
                t, :, qcols + kcols :
            ].astype(f32)

        for c in finals[4:7]:
            c.start()

        @pl.when(owner == flat)
        def _():
            out_own.wait()

        @pl.when(owner != flat)
        def _():
            out_far.wait()

        o_out[...] = o_in[...].astype(f32)
        finals[7].start()
        for c in lines:
            c.wait_recv()
        line_own.wait()
        summed = jnp.sum(s_line[...], axis=0)
        per_row = 128 // wrows
        gcols = HEAD_SIZE // (planes * GROUP)
        s_out[...] = jnp.where(
            lax.broadcasted_iota(jnp.int32, (srows, 128), 0) < 18,
            pltpu.roll(summed, (128 - flat % per_row * wrows) % 128, 1),
            pltpu.roll(summed, (128 - flat * gcols) % 128, 1),
        )
        for c in lines + ffn_rows[1:] + qkv_rows[1:]:
            c.wait_send()
        for c in (ffn, down, qkvs, outs):
            c.drain()
        for c in finals:
            c.wait()

    shape = jax.ShapeDtypeStruct
    vmem = pltpu.VMEM
    wide_rows = shards * wrows
    return pallas(
        body,
        [
            shape((rows, width), bf16),
            shape((rows, width), bf16),
            shape((wrows, hidden * GROUP), f32),
            shape((wrows, hidden * GROUP), f32),
            shape((wrows, qcols * GROUP), f32),
            shape((wrows, kcols * GROUP), f32),
            shape((wrows, kcols * GROUP), f32),
            shape((wrows, width), f32),
            shape((brows, width), f32),
            shape((srows, 128), f32),
        ],
        [VMEM] * 4 + [ANY] * (4 + len(inputs)),
        [ANY] * 9 + [VMEM],
        [
            vmem((rows, width), bf16),
            vmem((rows, width), bf16),
            vmem((wrows, hidden * GROUP), f32),
            vmem((wrows, hidden * GROUP), f32),
            vmem((wrows, qcols * GROUP), f32),
            vmem((wrows, kcols * GROUP), f32),
            vmem((wrows, kcols * GROUP), f32),
            vmem((wrows, width), f32),
            vmem((brows, width), f32),
            DMA((9,)),
        ]
        + [vmem(i.shape, i.dtype) for i in inputs]
        + [
            vmem((rows, width), bf16),
            vmem((GROUP, rows, width), bf16),
            vmem((rows, width), f32),
            vmem((group_rows, qkv_cols), bf16),
            vmem((group_rows, 128), bf16),
            vmem((length, HEAD_SIZE), f32),
            vmem((length, HEAD_SIZE), f32),
            vmem((group_rows, qcols), bf16),
            vmem((srows, width), f32),
            vmem((GROUP, planes * srows, 128), f32),
            vmem((GROUP, planes * srows, 128), f32),
            vmem((planes, srows, 128), f32),
            vmem((planes, srows, 128), f32),
            vmem((3, streams, wide_rows, both), bf16),
            vmem((streams, wide_rows, both), bf16),
            vmem((streams, wide_rows, both), bf16),
            vmem((GROUP, wrows, both), bf16),
            vmem((3, brows, width), bf16),
            vmem((brows, width), bf16),
            vmem((brows, width), bf16),
            vmem((2, streams, 2, wide_rows, qkv_cols), bf16),
            vmem((3, streams, wide_rows, qkv_cols), bf16),
            vmem((streams, wide_rows, qkv_cols), bf16),
            vmem((streams, wide_rows, qkv_cols), bf16),
            vmem((GROUP, wrows, qkv_cols), bf16),
            vmem((2, 2, wrows, width), bf16),
            vmem((3, wrows, width), bf16),
            vmem((wrows, width), bf16),
            vmem((wrows, width), bf16),
            vmem((wrows, width), bf16),
            vmem((streams, wide_rows, both), bf16),
            vmem((brows, width), bf16),
            vmem((streams, wide_rows, qkv_cols), bf16),
            vmem((wrows, width), bf16),
        ]
        + scatter_scratch(rows, width)
        + [DMA((10,)), DMA((10,)), DMA((10,)), DMA((10,))]
        + gather_scratch()
        + [DMA((len(inputs),))]
        + [DMA((PlaceSums.SENDS,)), DMA((PlaceSums.RECVS,))] * 4
        + [DMA((GROUP,)), DMA((GROUP,)), DMA((GROUP,)), DMA((GROUP,)), DMA, DMA]
        + [DMA((GROUP,)), DMA((GROUP,)), DMA((planes,)), DMA((planes,)), DMA((2,))]
        + [pltpu.SemaphoreType.REGULAR],
        cid,
        180,
        62,
    )(gains, starts, cosine, sine, final, hidden_one, down_grad, ffn_grad, *inputs)


def store(*arrays):
    count = len(arrays)

    def body(*refs):
        load_sem, store_sem = refs[-2:]
        staged = refs[2 * count : 3 * count]
        loads = [
            pltpu.make_async_copy(refs[i], staged[i], load_sem.at[i]) for i in range(count)
        ]
        stores = [
            pltpu.make_async_copy(staged[i], refs[count + i], store_sem.at[i])
            for i in range(count)
        ]
        for c in loads:
            c.start()
        for load, c in zip(loads, stores):
            load.wait()
            c.start()
        for c in stores:
            c.wait()

    return pl.pallas_call(
        body,
        out_shape=[jax.ShapeDtypeStruct(a.shape, a.dtype) for a in arrays],
        in_specs=[ANY] * count,
        out_specs=[ANY] * count,
        scratch_shapes=[pltpu.VMEM(a.shape, a.dtype) for a in arrays]
        + [DMA((count,)), DMA((count,))],
        compiler_params=pltpu.CompilerParams(vmem_limit_bytes=62 * 1024 * 1024),
    )(*arrays)


def settle(qkv_grad, out_grad, small, qcols, kcols, planes, direct, shards, cid):
    srows = small.shape[1] // planes
    cols = small.shape[2]
    wrows, width = out_grad.shape

    def body(
        q_ref, o_ref, s_ref, query_out, key_out, value_out, o_out, s_out, q_got, o_got, got, held,
        line, qsend, qrecv, osend, orecv, asend, arecv, bsend, brecv,
    ):
        place = Place(shards)
        tp, dp, flat = place.tp, place.dp(), place.flat()
        barrier = pltpu.get_barrier_semaphore()

        def signal(device):
            pl.semaphore_signal(
                barrier, inc=1, device_id=device, device_id_type=pl.DeviceIdType.MESH
            )

        for device in group_peers(place):
            signal(device)
        for k in range(1, planes):
            signal(place.dp_device((dp + k) % planes))
        if direct:
            owner = place.head(tp) * planes + dp
            high, y = lax.axis_index("zh"), lax.axis_index("y")
            source = {"st": lax.axis_index("st"), "seq": high * 2 + y}
            source.update(place.dp_device(lax.axis_index("seq")))

            @pl.when(owner != flat)
            def _():
                signal(source)

            pl.semaphore_wait(barrier, GROUP + planes - 2 + (owner != flat).astype(jnp.int32))
        else:
            pl.semaphore_wait(barrier, GROUP + planes - 2)

        sums = Exchange(place, s_ref, got, asend, arecv)
        sums.start()
        qkv = Exchange(place, q_ref, q_got, qsend, qrecv)
        qkv.start()
        if direct:
            out_own = pltpu.make_async_copy(o_ref, o_got, osend)
            out_far = remote(o_ref, o_got, osend, orecv, place.any_device(owner))

            @pl.when(owner == flat)
            def _():
                out_own.start()

            @pl.when(owner != flat)
            def _():
                out_far.start()

        sums.finish()
        held[...] = jnp.sum(got[...], axis=0).reshape(held.shape)
        line_own = pltpu.make_async_copy(held.at[dp], line.at[dp], bsend.at[0])
        line_own.start()
        lines = []
        for k in range(1, planes):
            to = (dp + k) % planes
            lines.append(
                remote(held.at[to], line.at[dp], bsend.at[k], brecv.at[k], place.dp_device(to))
            )
            lines[-1].start()
        qkv.finish()
        for t in range(GROUP):
            head = place.head(t)
            query_out[:, head * qcols : (head + 1) * qcols] = q_got[t, :, :qcols].astype(f32)
            key_out[:, head * kcols : (head + 1) * kcols] = q_got[
                t, :, qcols : qcols + kcols
            ].astype(f32)
            value_out[:, head * kcols : (head + 1) * kcols] = q_got[t, :, qcols + kcols :].astype(
                f32
            )
        if direct:

            @pl.when(owner == flat)
            def _():
                out_own.wait()

            @pl.when(owner != flat)
            def _():
                out_far.wait()

            o_out[...] = o_got[...].astype(f32)
        else:
            o_out[...] = o_ref[...].astype(f32)
        for c in lines:
            c.wait_recv()
        line_own.wait()
        s_out[...] = jnp.sum(line[...], axis=0)
        for c in lines:
            c.wait_send()

    return pallas(
        body,
        [
            jax.ShapeDtypeStruct((wrows, GROUP * qcols), f32),
            jax.ShapeDtypeStruct((wrows, GROUP * kcols), f32),
            jax.ShapeDtypeStruct((wrows, GROUP * kcols), f32),
            jax.ShapeDtypeStruct((wrows, width), f32),
            jax.ShapeDtypeStruct((srows, cols), f32),
        ],
        [VMEM, VMEM, VMEM],
        [VMEM] * 5,
        [
            pltpu.VMEM(qkv_grad.shape, bf16),
            pltpu.VMEM(out_grad.shape, bf16),
            pltpu.VMEM(small.shape, f32),
            pltpu.VMEM((planes, srows, cols), f32),
            pltpu.VMEM((planes, srows, cols), f32),
            DMA((GROUP,)), DMA((GROUP,)), DMA, DMA,
            DMA((GROUP,)), DMA((GROUP,)), DMA((planes,)), DMA((planes,)),
        ],
        cid,
        20,
    )(qkv_grad, out_grad, small)


def local(
    tokens, doc_starts, attn_gain, query_gain, key_gain, w_query, key_weight, value_weight,
    w_headgate, w_out, ffn_gain, w_gate, w_up, w_down, cotangent,
):
    zs, ys = lax.axis_size("zh"), lax.axis_size("y")
    planes = zs * ys
    direct = zs == 2 and ys == 2
    streams = lax.axis_size("st")
    shards = lax.axis_size("seq")
    devices = planes * GROUP
    rows, width = tokens.shape
    length = rows * shards
    group_rows = rows * GROUP
    wrows = w_query.shape[0]
    brows = w_down.shape[0]
    hidden = brows * planes
    qcols = w_query.shape[1] // GROUP
    kcols = key_weight.shape[1] // GROUP
    group_heads = qcols // HEAD_SIZE
    all_heads = w_headgate.shape[1]
    score_scale = HEAD_SIZE ** (-0.5)
    dp = lax.axis_index(DP)
    tp = lax.axis_index(TP)

    hg = wrows * all_heads
    gcols = query_gain.shape[0]
    at = hg + 2 * wrows
    count = at + 2 * gcols
    sums = -(-count // 1024) * 8
    docs = doc_starts.shape[1]
    qkv_cols = qcols + 2 * kcols
    starts_row = jnp.concatenate(
        [(doc_starts[0] // 128).astype(bf16), (doc_starts[0] % 128).astype(bf16)]
    )
    headgate_rows = jnp.pad(w_headgate, ((0, 0), (0, 128 - all_heads)))
    if direct:
        gain_rows = width // 128
        others = [attn_gain, ffn_gain, query_gain, key_gain, starts_row]
        small = jnp.pad(w_headgate, ((0, 16), (0, 128 - all_heads)))
        for i, row in enumerate(others):
            small = small + jnp.pad(
                row[None], ((wrows + i, 15 - i), (0, 128 - row.shape[0]))
            )
        (
            cot_all, ffn_w, down_w, hidden_one, hidden_two, small, gains, qkv_w, out_w, qkv,
            low, gate_full, mixed, gated, middle, headgate, starts,
        ) = forward_pass(
            tokens, cotangent, small, w_out, w_query, key_weight, value_weight, w_gate, w_up,
            w_down, docs, shards, 0,
        )
        cot_all = cot_all.reshape(group_rows, width)
        hidden_two = hidden_two.reshape(group_rows, width)
        ffn_w = ffn_w.reshape(width, 2 * hidden)
        down_w = down_w.reshape(hidden, width)
        gate_up = mm(hidden_two, ffn_w)
        gate_pre, up_proj = gate_up[:, :hidden], gate_up[:, hidden:]
        gate_sig = jax.nn.sigmoid(gate_pre)
        inner_act = (gate_pre * gate_sig * up_proj).astype(bf16)
        down_grad = mm_t(inner_act, cot_all).astype(bf16)
        grad_inner = mm_b(cot_all, down_w)
        grad_gate = grad_inner * up_proj * gate_sig * (1.0 + gate_pre * (1.0 - gate_sig))
        grad_up = grad_inner * gate_pre * gate_sig
        grad_gu = jnp.concatenate([grad_gate.astype(bf16), grad_up.astype(bf16)], axis=1)
        ffn_grad = mm_t(hidden_two, grad_gu).astype(bf16)
        places = (GROUP, rows, width)
        (
            layer_out, tokens_grad, gate_grad, up_grad, query_grad, key_grad, value_grad,
            out_grad, down_grad, small_sum,
        ) = backward_pass(
            mm_b(grad_gu, ffn_w).astype(bf16).reshape(places),
            mm(inner_act, down_w).astype(bf16).reshape(places),
            middle, tokens, cotangent, gains, headgate,
            qkv_w.reshape(width, qkv_cols), out_w.reshape(qcols, width), hidden_one, qkv, low,
            gate_full, mixed, gated, starts, down_grad.reshape(zs, ys, brows, width),
            ffn_grad.reshape(zs, streams, ys, shards * wrows, 2 * hidden), docs, shards, 1,
        )
        (
            layer_out, tokens_grad, gate_grad, up_grad, query_grad, key_grad, value_grad,
            out_grad, down_grad,
        ) = store(
            layer_out, tokens_grad, gate_grad, up_grad, query_grad, key_grad, value_grad,
            out_grad, down_grad,
        )
        return (
            layer_out,
            tokens_grad,
            small_sum[all_heads, :wrows],
            small_sum[18, :gcols],
            small_sum[19, :gcols],
            query_grad,
            key_grad,
            value_grad,
            small_sum[:all_heads, :wrows].T,
            out_grad,
            small_sum[all_heads + 1, :wrows],
            gate_grad,
            up_grad,
            down_grad,
        )
    else:
        srows = -(-(wrows + 6) // 16) * 16
        others = [attn_gain, ffn_gain, query_gain, key_gain, starts_row[:docs], starts_row[docs:]]
        small = jnp.concatenate(
            [headgate_rows]
            + [jnp.pad(row, (0, 128 - row.shape[0]))[None] for row in others]
            + [jnp.zeros((srows - wrows - 6, 128), bf16)]
        )
        tokens_all, cot_all, small, qkv_w, ffn_own = front(
            tokens, cotangent, small, w_out, w_query, key_weight, value_weight, w_gate, w_up,
            w_down, planes, False, shards, 0,
        )
        tokens_all = tokens_all.reshape(group_rows, width)
        cot_all = cot_all.reshape(group_rows, width)
        qkv_w = over_dp(qkv_w[0])
        ffn_w = over_dp(ffn_own)
        down_w = lax.all_gather(w_down, DP, axis=0, tiled=True)
        out_w = lax.all_gather(w_out, ALL, axis=0, tiled=True)
        out_w = lax.dynamic_slice_in_dim(out_w, tp * qcols, qcols, 0)
        head = tp
        here = pick(small[::shards], 1, dp)
        starts = here[:, wrows + 4, :docs].astype(jnp.int32) * 128
        starts = starts + here[:, wrows + 5, :docs].astype(jnp.int32)
    small = small.reshape(streams, shards, zs, ys, srows, 128).transpose(2, 0, 3, 1, 4, 5)
    small = small.reshape(devices, srows, 128)
    headgate_all = small[:, :wrows, :all_heads].reshape(width, all_heads)
    if not direct:
        attn_gain_f = small[:, wrows, :wrows].reshape(1, -1).astype(f32)
        ffn_gain_f = small[:, wrows + 1, :wrows].reshape(1, -1).astype(f32)
        query_gain_f = small[:, wrows + 2, :gcols].reshape(-1).astype(f32)
        key_gain_f = small[:, wrows + 3, :gcols].reshape(-1).astype(f32)
    headgate_own = lax.dynamic_slice_in_dim(headgate_all, head * group_heads, group_heads, 1)

    if not direct:
        residual_all = tokens_all.astype(f32)
        hidden_all = (residual_all * rms_scale(residual_all) * attn_gain_f).astype(bf16)
        qkv = mm(hidden_all, qkv_w)
    query_raw = qkv[:, :qcols].reshape(group_rows, group_heads, HEAD_SIZE)
    key_raw = qkv[:, qcols : qcols + kcols].reshape(group_rows, 1, HEAD_SIZE)
    value = qkv[:, qcols + kcols :].astype(bf16).reshape(streams, length, HEAD_SIZE)
    positions = jnp.tile(jnp.arange(length, dtype=jnp.int32), streams)
    cosine, sine = rotary_tables(positions)
    query_scale = rms_scale(query_raw)
    query_normed = query_raw * query_scale
    query = rotate(query_normed * query_gain_f, cosine, sine).astype(bf16)
    query = query.reshape(streams, length, group_heads, HEAD_SIZE)
    key_scale = rms_scale(key_raw)
    key_normed = key_raw * key_scale
    key = rotate(key_normed * key_gain_f, cosine, sine).astype(bf16)
    key = key.reshape(streams, length, HEAD_SIZE)
    stream_pos = jnp.arange(length, dtype=jnp.int32)
    segment = jnp.sum((stream_pos[None, :, None] >= starts[:, None, :]).astype(jnp.int32), axis=2)
    allowed = (stream_pos[:, None] >= stream_pos[None, :])[None] & (
        segment[:, :, None] == segment[:, None, :]
    )
    scores = jnp.einsum("bqgd,bkd->bgqk", query, key, preferred_element_type=f32) * score_scale
    scores = jnp.where(allowed[:, None], scores, MASK_FILL)
    row_max = jnp.max(scores, axis=-1, keepdims=True)
    weights = jnp.exp(scores - row_max)
    probs = weights / jnp.sum(weights, axis=-1, keepdims=True)
    probs_low = probs.astype(bf16)
    if not direct:
        mixed = jnp.einsum(
            "bgqk,bkd->bqgd", probs_low, value, preferred_element_type=f32
        ).astype(bf16)
    mixed_f = mixed.astype(f32).reshape(group_rows, group_heads, HEAD_SIZE)
    if direct:
        head_gate = gate_full.reshape(group_rows, group_heads, HEAD_SIZE)[:, :, :1]
    else:
        head_gate = jax.nn.sigmoid(mm(hidden_all, headgate_own))[:, :, None]
        gated = (mixed_f * head_gate).astype(bf16).reshape(group_rows, qcols)

    def parts(x):
        return x.astype(bf16).reshape(GROUP, rows, width)

    if not direct:
        middle, hidden_two = middle_step(
            parts(mm(gated, out_w)), tokens, ffn_gain_f, None, shards, 2
        )
        hidden_two = hidden_two.reshape(group_rows, width)

    gate_up = mm(hidden_two, ffn_w)
    gate_pre, up_proj = gate_up[:, :hidden], gate_up[:, hidden:]
    gate_sig = jax.nn.sigmoid(gate_pre)
    inner_act = (gate_pre * gate_sig * up_proj).astype(bf16)
    down_grad = mm_t(inner_act, cot_all).astype(bf16).reshape(zs, ys, brows, width)
    if direct:
        down_sum = PlaceSum(down_grad)
        down_sum.over_y()
    else:
        down_grad = scatter_dp(down_grad)
    grad_inner = mm_b(cot_all, down_w)
    grad_gate = (grad_inner * up_proj * gate_sig * (1.0 + gate_pre * (1.0 - gate_sig))).astype(bf16)
    grad_up = (grad_inner * gate_pre * gate_sig).astype(bf16)
    grad_gu = jnp.concatenate([grad_gate, grad_up], axis=1)
    ffn_grad = mm_t(hidden_two, grad_gu).astype(bf16)
    grad_gu, ffn_grad = lax.optimization_barrier((grad_gu, ffn_grad))
    if not direct:
        ffn_grad = scatter_dp(by_place(ffn_grad))
    grad_middle, ffn_gain_part, grad_branch, *ffn_first = middle_back(
        parts(mm_b(grad_gu, ffn_w)), middle, cotangent, ffn_gain_f,
        ffn_grad.reshape(zs, streams, ys, -1, 2 * hidden) if direct else None, shards, 3,
    )
    if direct:
        grad_branch, down_sum.far, down_sum.near, ffn_first = lax.optimization_barrier(
            (grad_branch, down_sum.far, down_sum.near, ffn_first[0])
        )
        down_z = down_sum.over_z()
        ffn_sum = PlaceSum(by_place(ffn_grad))
        ffn_sum.take(ffn_first.reshape(-1, 2 * hidden), None)
        ffn_z = ffn_sum.over_z()
        ffn_sum.near = ffn_sum.over_y_near()
    grad_branch = grad_branch.reshape(group_rows, width)
    layer_out = scatter_sum(parts(mm(inner_act, down_w)), middle, shards, 4)

    out_grad = mm_t(gated, grad_branch).astype(bf16).reshape(zs, ys, wrows, width)
    grad_gated = mm_b(grad_branch, out_w).reshape(group_rows, group_heads, HEAD_SIZE)
    grad_mixed = (grad_gated * head_gate).astype(bf16).reshape(
        streams, length, group_heads, HEAD_SIZE
    )
    gate_flat = head_gate[:, :, 0]
    grad_logit = (
        jnp.sum(grad_gated * mixed_f, axis=-1) * gate_flat * (1.0 - gate_flat)
    ).astype(bf16)
    grad_probs = jnp.einsum("bqgd,bkd->bgqk", grad_mixed, value, preferred_element_type=f32)
    row_delta = jnp.sum(probs * grad_probs, axis=-1, keepdims=True)
    grad_scores = (probs * (grad_probs - row_delta)).astype(bf16)
    grad_query = (
        jnp.einsum("bgqk,bkd->bqgd", grad_scores, key, preferred_element_type=f32) * score_scale
    ).astype(bf16)
    grad_key = (
        jnp.einsum("bgqk,bqgd->bkd", grad_scores, query, preferred_element_type=f32) * score_scale
    ).astype(bf16)
    grad_value = jnp.einsum(
        "bgqk,bqgd->bkd", probs_low, grad_mixed, preferred_element_type=f32
    ).astype(bf16)
    gqn = rotate_back(
        grad_query.astype(f32).reshape(group_rows, group_heads, HEAD_SIZE), cosine, sine
    )
    query_gain_part = jnp.sum(gqn * query_normed, axis=(0, 1))
    grad_query_raw = norm_back(gqn * query_gain_f, query_normed, query_scale).astype(bf16)
    gkn = rotate_back(grad_key.astype(f32).reshape(group_rows, 1, HEAD_SIZE), cosine, sine)
    key_gain_part = jnp.sum(gkn * key_normed, axis=(0, 1))
    grad_key_raw = norm_back(gkn * key_gain_f, key_normed, key_scale).astype(bf16)
    grad_qkv = jnp.concatenate(
        [
            grad_query_raw.reshape(group_rows, qcols),
            grad_key_raw.reshape(group_rows, kcols),
            grad_value.reshape(group_rows, kcols),
        ],
        axis=1,
    )
    qkv_grad = mm_t(hidden_all, grad_qkv).astype(bf16)
    if direct:
        qkv_grad, out_grad, grad_qkv, down_z = lax.optimization_barrier(
            (qkv_grad, out_grad, grad_qkv, down_z)
        )
        down_grad = down_sum.total(down_z)
        qkv_sum, out_sum = PlaceSum(by_place(qkv_grad)), PlaceSum(out_grad)
        qkv_sum.over_y()
        out_sum.over_y()
        qkv_z, out_z = qkv_sum.over_z(), out_sum.over_z()
        ffn_grad = ffn_sum.total(ffn_z)
        qkv_grad, out_grad = qkv_sum.total(qkv_z), out_sum.total(out_z)
    else:
        qkv_grad = scatter_dp(by_place(qkv_grad))
        out_grad = lax.dynamic_update_slice(
            jnp.zeros((width, width), bf16), out_grad.reshape(qcols, width), (tp * qcols, 0)
        )
        out_grad = lax.psum_scatter(out_grad, ALL, scatter_dimension=0, tiled=True)
    tokens_grad, attn_gain_part = tokens_back(
        parts(mm_b(grad_qkv, qkv_w) + mm_b(grad_logit, headgate_own)),
        tokens, grad_middle, attn_gain_f, shards, 5,
    )
    headgate_part = mm_t(hidden_all, grad_logit)
    headgate_part = lax.dynamic_update_slice(
        jnp.zeros((width, all_heads), f32), headgate_part, (0, head * group_heads)
    )

    small_sum = jnp.concatenate(
        [
            headgate_part.reshape(devices, hg),
            attn_gain_part.reshape(devices, wrows),
            ffn_gain_part.reshape(devices, wrows),
            query_gain_part.reshape(devices, gcols),
            key_gain_part.reshape(devices, gcols),
        ],
        axis=1,
    )
    small_sum = jnp.pad(small_sum, ((0, 0), (0, sums * 128 - count)))
    small_sum = small_sum.reshape(zs, streams, ys, shards, sums, 128)
    small_sum = small_sum.transpose(1, 3, 0, 2, 4, 5)
    small_sum = small_sum.reshape(GROUP, planes * sums, 128)

    gate_grad, up_grad = exchange_back(
        ffn_grad.reshape(GROUP, wrows, 2 * hidden), planes, shards, 6
    )
    query_grad, key_grad, value_grad, out_grad, small_sum = settle(
        qkv_grad.reshape(GROUP, wrows, qkv_cols), out_grad, small_sum, qcols, kcols, planes,
        direct, shards, 7,
    )
    small_sum = small_sum.reshape(-1)
    return (
        layer_out,
        tokens_grad,
        small_sum[hg : hg + wrows],
        small_sum[at : at + gcols],
        small_sum[at + gcols : at + 2 * gcols],
        query_grad,
        key_grad,
        value_grad,
        small_sum[:hg].reshape(wrows, all_heads),
        out_grad,
        small_sum[hg + wrows : hg + 2 * wrows],
        gate_grad,
        up_grad,
        down_grad.astype(f32),
    )


def solution(mesh):
    shards = mesh.shape["seq"]
    planes = (2, 2, 2) if shards == 4 and mesh.size == 32 else (1, GROUP // shards, -1)
    grouped = Mesh(mesh.devices.reshape(planes + (shards,)), ALL)
    two = P(ALL, None)
    one = P(ALL)
    return jax.shard_map(
        local,
        mesh=grouped,
        in_specs=(
            two, P(("zh", "st", "y"), None), one, one, one, two, two, two, two, two, one, two, two,
            two, two,
        ),
        out_specs=(two, two, one, one, one, two, two, two, two, two, one, two, two, two),
        check_vma=False,
    )
```

```python
import jax
import jax.numpy as jnp
import numpy as np
from jax import lax
from jax.experimental import pallas as pl
from jax.experimental.pallas import tpu as pltpu
from jax.sharding import Mesh, PartitionSpec as P

QUERY_HEADS = 16
KEY_VALUE_HEADS = 8
HEAD_SIZE = 128
GROUP = 8
NORM_EPS = 1e-06
ROPE_BASE = 1000000.0
MASK_FILL = -1e30

DP = ("zh", "y")
TP = ("st", "seq")
ALL = ("zh", "st", "y", "seq")
f32 = jnp.float32
bf16 = jnp.bfloat16


def rms_scale(vector):
    return lax.rsqrt(jnp.mean(vector * vector, axis=-1, keepdims=True) + NORM_EPS)


def rotary_tables(positions):
    half_width = HEAD_SIZE // 2
    exponent = jnp.arange(half_width, dtype=jnp.int32).astype(f32) * (2.0 / HEAD_SIZE)
    inverse = jnp.power(ROPE_BASE, -exponent)
    angles = positions.astype(f32)[:, None] * inverse[None, :]
    return (jnp.cos(angles)[:, None, :], jnp.sin(angles)[:, None, :])


def rotate(vector, cosine, sine):
    a, b = jnp.split(vector, 2, axis=-1)
    return jnp.concatenate([a * cosine - b * sine, b * cosine + a * sine], axis=-1)


def rotate_back(vector, cosine, sine):
    a, b = jnp.split(vector, 2, axis=-1)
    return jnp.concatenate([a * cosine + b * sine, b * cosine - a * sine], axis=-1)


def norm_back(grad, normed, scale):
    return scale * (grad - normed * jnp.mean(grad * normed, axis=-1, keepdims=True))


def mm(left, right):
    return jnp.dot(left, right, preferred_element_type=f32)


def mm_t(left, right):
    return lax.dot_general(left, right, (((0,), (0,)), ((), ())), preferred_element_type=f32)


def mm_b(left, right):
    return lax.dot_general(left, right, (((1,), (1,)), ((), ())), preferred_element_type=f32)


SWAP = [(0, 1), (1, 0)]


def over_dp(x):
    streams, shards = lax.axis_size("st"), lax.axis_size("seq")
    zs, ys = lax.axis_size("zh"), lax.axis_size("y")
    rows, columns = x.shape[1] * shards, x.shape[2]
    whole = lax.all_gather(x, DP, axis=0, tiled=False)
    whole = whole.reshape(zs, ys, streams, rows, columns).transpose(0, 2, 1, 3, 4)
    return whole.reshape(-1, columns)


def pick(x, axis, index):
    return lax.dynamic_index_in_dim(x, index, axis, keepdims=False)


def plus(left, right):
    return left.astype(f32) + right.astype(f32)


class PlaceSum:
    def __init__(self, x):
        self.x = x
        self.z, self.y = lax.axis_index("zh"), lax.axis_index("y")

    def piece(self, zp, yp):
        return pick(pick(self.x, 0, zp), 0, yp)

    def over_y(self):
        got = lax.ppermute(pick(self.x, 1, 1 - self.y), "y", SWAP)
        self.take(pick(got, 0, 1 - self.z), pick(got, 0, self.z))

    def over_y_near(self):
        return lax.ppermute(self.piece(self.z, 1 - self.y), "y", SWAP)

    def take(self, far, near):
        self.far, self.near = far, near

    def over_z(self):
        far = plus(self.piece(1 - self.z, self.y), self.far).astype(bf16)
        return lax.ppermute(far, "zh", SWAP)

    def total(self, got):
        return (plus(self.piece(self.z, self.y), self.near) + got.astype(f32)).astype(bf16)


def scatter_dp(x):
    zs, ys = x.shape[:2]
    return lax.psum_scatter(
        x.reshape((zs * ys,) + x.shape[2:]), DP, scatter_dimension=0, tiled=False
    )


def by_place(x):
    streams = lax.axis_size("st")
    zs, ys = lax.axis_size("zh"), lax.axis_size("y")
    columns = x.shape[1]
    x = x.reshape(zs, streams, ys, -1, columns).transpose(0, 2, 1, 3, 4)
    return x.reshape(zs, ys, -1, columns)


def pallas(body, out_shape, in_specs, out_specs, scratch, cid, micros, mib=40):
    return pl.pallas_call(
        body,
        out_shape=out_shape,
        in_specs=in_specs,
        out_specs=out_specs,
        scratch_shapes=scratch,
        compiler_params=pltpu.CompilerParams(
            collective_id=cid, has_side_effects=True, vmem_limit_bytes=mib * 1024 * 1024
        ),
        cost_estimate=pl.CostEstimate(
            flops=0, bytes_accessed=int(micros * 3.6e5), transcendentals=0
        ),
    )


ANY = pl.BlockSpec(memory_space=pl.ANY)
VMEM = pl.BlockSpec(memory_space=pltpu.VMEM)
DMA = pltpu.SemaphoreType.DMA


def remote(src, dst, send, recv, device):
    return pltpu.make_async_remote_copy(
        src_ref=src,
        dst_ref=dst,
        send_sem=send,
        recv_sem=recv,
        device_id=device,
        device_id_type=pl.DeviceIdType.MESH,
    )


class Place:
    def __init__(self, shards):
        self.shards = shards
        self.tp = lax.axis_index("st") * shards + lax.axis_index("seq")
        self.core = self.tp % 2
        self.ring = self.turn(self.tp // 2)

    def turn(self, place):
        if self.shards == GROUP:
            return place
        return place + (place // 2) * (1 - 2 * (place % 2))

    def head(self, index):
        if self.shards == GROUP:
            return index
        return index // 4 * 2 + index % 4 // 2 * 4 + index % 2

    def block(self, ahead, other=False):
        ring = self.ring
        if ahead == 1:
            ring = ring + 1 - 2 * (ring % 2)
        elif ahead == 3:
            ring = 3 - ring
        elif ahead == 2:
            ring = (ring + 2) % 4
        core = 1 - self.core if other else self.core
        return self.turn(ring) * 2 + core

    def device(self, index):
        return {"st": index // self.shards, "seq": index % self.shards}

    def dp_device(self, dp):
        ys = lax.axis_size("y")
        return {"zh": dp // ys, "y": dp % ys}

    def any_device(self, flat):
        ys, streams = lax.axis_size("y"), lax.axis_size("st")
        return {
            "zh": flat // (streams * ys * self.shards),
            "st": flat // (ys * self.shards) % streams,
            "y": flat // self.shards % ys,
            "seq": flat % self.shards,
        }

    def flat(self):
        ys, streams = lax.axis_size("y"), lax.axis_size("st")
        z, y = lax.axis_index("zh"), lax.axis_index("y")
        st, seq = lax.axis_index("st"), lax.axis_index("seq")
        return ((z * streams + st) * ys + y) * self.shards + seq

    def dp(self):
        return lax.axis_index("zh") * lax.axis_size("y") + lax.axis_index("y")

    def right(self):
        return self.device(self.block(1))

    def left(self):
        return self.device(self.block(3))

    def across(self):
        return {"y": 1 - lax.axis_index("y")}

    def partner(self):
        return self.device(self.block(0, True))


def greet(devices):
    barrier = pltpu.get_barrier_semaphore()
    for device in devices:
        pl.semaphore_signal(
            barrier, inc=1, device_id=device, device_id_type=pl.DeviceIdType.MESH
        )
    pl.semaphore_wait(barrier, len(devices))


class RingGather:
    SEMS = 11

    def __init__(self, place, own, out, send, recv, one_way=False):
        rows = out.shape[1]
        half = rows // 2
        first, second = pl.ds(0, half), pl.ds(half, half)
        me, near, next_, opposite = (place.block(i) for i in (0, 1, 3, 2))
        to_near, to_next, to_partner = place.device(near), place.device(next_), place.partner()

        def copy(index, src, block, part, device):
            return remote(src, out.at[block, part], send.at[index], recv.at[index], device)

        self.local = pltpu.make_async_copy(own, out.at[me], send.at[self.SEMS])
        self.next = [
            copy(0, own.at[first], me, first, to_next),
            copy(1, own.at[second], me, second, to_next),
        ]
        self.near = [
            copy(2, own.at[first], me, first, to_near),
            copy(3, own.at[second], me, second, to_near),
        ]
        self.mate = remote(own, out.at[me], send.at[4], recv.at[4], to_partner)
        self.on = [copy(5, out.at[next_, first], next_, first, to_near)]
        if one_way:
            self.on.append(copy(6, out.at[next_, second], next_, second, to_near))
        else:
            self.on.append(copy(6, out.at[near, second], near, second, to_next))
        self.one_way = one_way
        self.across = [
            remote(out.at[next_], out.at[next_], send.at[7], recv.at[7], to_partner),
            remote(out.at[near], out.at[near], send.at[8], recv.at[8], to_partner),
            copy(9, out.at[opposite, first], opposite, first, to_partner),
            copy(10, out.at[opposite, second], opposite, second, to_partner),
        ]

    def start(self):
        self.next[0].start()
        self.near[0 if self.one_way else 1].start()
        self.next[1].start()
        self.near[1 if self.one_way else 0].start()
        self.mate.start()
        self.local.start()

    def pass_on(self):
        self.next[0].wait_recv()
        self.on[0].start()
        if self.one_way:
            self.next[1].wait_recv()
        else:
            self.near[1].wait_recv()
        self.on[1].start()

    def step_across(self):
        if not self.one_way:
            self.next[1].wait_recv()
        self.across[0].start()
        self.near[0].wait_recv()
        if self.one_way:
            self.near[1].wait_recv()
        self.across[1].start()

    def step_far(self):
        self.on[0].wait_recv()
        self.across[2].start()
        self.on[1].wait_recv()
        self.across[3].start()

    def finish(self):
        self.mate.wait_recv()
        for c in self.across:
            c.wait_recv()
        for c in self.next + self.near + [self.mate] + self.on + self.across:
            c.wait_send()
        self.local.wait()

    def run(self):
        self.start()
        self.pass_on()
        self.step_across()
        self.step_far()
        self.finish()


def ring_scatter(place, x, pair, out, near, far, send, recv, emit, between=()):
    between = list(between) + [lambda: None] * 3
    rows = x.shape[1]
    half = rows // 2
    step = 32
    to_left, to_right, to_partner = place.left(), place.right(), place.partner()
    swaps = {}
    for q in (2, 1, 3, 0):
        swaps[q] = remote(
            x.at[place.block(q, True)], pair.at[q], send.at[q], recv.at[q], to_partner
        )
        swaps[q].start()

    def add(q, low, high, extra=None):
        block = place.block(q)

        def one(i, _):
            part = pl.ds(pl.multiple_of(low + i * step, step), step)
            total = x[block, part].astype(f32) + pair[q, part].astype(f32)
            if extra is not None:
                inner = pl.ds(pl.multiple_of(i * step, step), step)
                total = total + far[extra, inner].astype(f32)
            out[q - 1, part] = total.astype(bf16)
            return 0

        lax.fori_loop(0, (high - low) // step, one, 0)

    first, second = pl.ds(0, half), pl.ds(half, half)

    def send_to(index, q, part, dst, device):
        c = remote(out.at[q - 1, part], dst, send.at[index], recv.at[index], device)
        c.start()
        return c

    swaps[2].wait_recv()
    add(2, 0, half)
    a = send_to(4, 2, first, far.at[0], to_right)
    add(2, half, rows)
    b = send_to(5, 2, second, far.at[1], to_left)
    swaps[1].wait_recv()
    add(1, 0, half)
    c = send_to(6, 1, first, near.at[0, first], to_right)
    swaps[3].wait_recv()
    add(3, half, rows)
    d = send_to(7, 3, second, near.at[1, second], to_left)
    between[0]()
    a.wait_recv()
    add(3, 0, half, 0)
    e = send_to(8, 3, first, near.at[1, first], to_left)
    b.wait_recv()
    add(1, half, rows, 1)
    g = send_to(9, 1, second, near.at[0, second], to_right)
    between[1]()
    swaps[0].wait_recv()
    own = place.block(0)
    c.wait_recv()
    d.wait_recv()
    e.wait_recv()
    g.wait_recv()

    def last(i, _):
        part = pl.ds(pl.multiple_of(i * step, step), step)
        emit(
            part,
            (x[own, part].astype(f32) + pair[0, part].astype(f32))
            + (near[0, part].astype(f32) + near[1, part].astype(f32)),
        )
        return 0

    lax.fori_loop(0, rows // step, last, 0)
    for copy in list(swaps.values()) + [a, b, c, d, e, g]:
        copy.wait_send()


def scatter_scratch(rows, width):
    return [
        pltpu.VMEM((4, rows, width), bf16),
        pltpu.VMEM((3, rows, width), bf16),
        pltpu.VMEM((2, rows, width), bf16),
        pltpu.VMEM((2, rows // 2, width), bf16),
        DMA((10,)),
        DMA((10,)),
    ]


def gather_scratch():
    return [DMA((RingGather.SEMS + 1,)), DMA((RingGather.SEMS,))]


def scatter_sum(x, base, shards, cid):
    _, rows, width = x.shape

    def body(x_ref, base_ref, out_ref, pair, out, near, far, send, recv):
        place = Place(shards)
        greet([place.right(), place.left(), place.partner()])

        def emit(part, total):
            out_ref[part] = (base_ref[part] + total).astype(bf16)

        ring_scatter(place, x_ref, pair, out, near, far, send, recv, emit)

    return pallas(
        body, jax.ShapeDtypeStruct((rows, width), bf16), [VMEM, VMEM], VMEM,
        scatter_scratch(rows, width), cid, 25,
    )(x, base)


def middle_step(x, tokens, gain, carry, shards, cid):
    _, rows, width = x.shape
    carries = [] if carry is None else [carry]

    def body(x_ref, tok_ref, gain_ref, *refs):
        refs = list(refs)
        carry_ref = refs.pop(0) if carries else None
        mid_ref, all_ref = refs.pop(0), refs.pop(0)
        carry_out = refs.pop(0) if carries else None
        held, pair, out, near, far, send, recv, gsend, grecv, ysend, yrecv = refs
        place = Place(shards)
        greet(
            [place.right(), place.left(), place.partner()]
            + ([place.across()] if carries else [])
        )
        if carries:
            over = remote(carry_ref, carry_out, ysend, yrecv, place.across())
            over.start()

        def emit(part, total):
            middle = tok_ref[part].astype(f32) + total
            mid_ref[part] = middle
            held[part] = (middle * rms_scale(middle) * gain_ref[...]).astype(bf16)

        ring_scatter(place, x_ref, pair, out, near, far, send, recv, emit)
        RingGather(place, held, all_ref, gsend, grecv).run()
        if carries:
            over.wait()

    return pallas(
        body,
        [
            jax.ShapeDtypeStruct((rows, width), f32),
            jax.ShapeDtypeStruct((GROUP, rows, width), bf16),
        ]
        + [jax.ShapeDtypeStruct(c.shape, c.dtype) for c in carries],
        [VMEM, VMEM, VMEM] + [ANY] * len(carries),
        [VMEM, ANY] + [ANY] * len(carries),
        [pltpu.VMEM((rows, width), bf16)] + scatter_scratch(rows, width) + gather_scratch()
        + [DMA, DMA],
        cid,
        50,
    )(x, tokens, gain, *carries)


def middle_back(x, middle, cotangent, gain, grads, shards, cid):
    _, rows, width = x.shape
    carries = [] if grads is None else [grads]

    def body(x_ref, mid_ref, cot_ref, gain_ref, *refs):
        refs = list(refs)
        grads_ref = refs.pop(0) if carries else None
        dm_ref, part_ref, all_ref = refs.pop(0), refs.pop(0), refs.pop(0)
        grads_out = refs.pop(0) if carries else None
        held, pair, out, near, far, send, recv, gsend, grecv, ysend, yrecv = refs
        place = Place(shards)
        greet(
            [place.right(), place.left(), place.partner()]
            + ([place.across()] if carries else [])
        )
        if carries:
            z, y = lax.axis_index("zh"), lax.axis_index("y")
            over = [
                remote(
                    grads_ref.at[1 - z, st, 1 - y], grads_out.at[st], ysend.at[st],
                    yrecv.at[st], place.across(),
                )
                for st in range(grads.shape[1])
            ]
            for c in over:
                c.start()
        part_ref[...] = jnp.zeros_like(part_ref)

        def emit(part, total):
            middle = mid_ref[part]
            scale = rms_scale(middle)
            normed = middle * scale
            part_ref[...] += jnp.sum(total * normed, axis=0, keepdims=True)
            dm = cot_ref[part].astype(f32) + norm_back(total * gain_ref[...], normed, scale)
            dm_ref[part] = dm
            held[part] = dm.astype(bf16)

        ring_scatter(place, x_ref, pair, out, near, far, send, recv, emit)
        RingGather(place, held, all_ref, gsend, grecv).run()
        if carries:
            for c in over:
                c.wait()

    return pallas(
        body,
        [
            jax.ShapeDtypeStruct((rows, width), f32),
            jax.ShapeDtypeStruct((1, width), f32),
            jax.ShapeDtypeStruct((GROUP, rows, width), bf16),
        ]
        + [jax.ShapeDtypeStruct((c.shape[1],) + c.shape[3:], c.dtype) for c in carries],
        [VMEM, VMEM, VMEM, VMEM] + [ANY] * len(carries),
        [VMEM, VMEM, ANY] + [ANY] * len(carries),
        [pltpu.VMEM((rows, width), bf16)] + scatter_scratch(rows, width) + gather_scratch()
        + [DMA((2,)), DMA((2,))],
        cid,
        50,
    )(x, middle, cotangent, gain, *carries)


def tokens_back(x, tokens, dm, gain, shards, cid):
    _, rows, width = x.shape

    def body(
        x_ref, tok_ref, dm_ref, gain_ref, grad_ref, part_ref, pair, out, near, far, send, recv
    ):
        place = Place(shards)
        greet([place.right(), place.left(), place.partner()])
        part_ref[...] = jnp.zeros_like(part_ref)

        def emit(part, total):
            tok = tok_ref[part].astype(f32)
            scale = rms_scale(tok)
            normed = tok * scale
            part_ref[...] += jnp.sum(total * normed, axis=0, keepdims=True)
            grad_ref[part] = (
                dm_ref[part] + norm_back(total * gain_ref[...], normed, scale)
            ).astype(bf16)

        ring_scatter(place, x_ref, pair, out, near, far, send, recv, emit)

    return pallas(
        body,
        (
            jax.ShapeDtypeStruct((rows, width), bf16),
            jax.ShapeDtypeStruct((1, width), f32),
        ),
        [VMEM, VMEM, VMEM, VMEM],
        (VMEM, VMEM),
        scatter_scratch(rows, width),
        cid,
        25,
    )(x, tokens, dm, gain)


class Exchange:
    SEMS = GROUP

    def __init__(self, place, x, out, send, recv):
        self.local = pltpu.make_async_copy(x.at[place.tp], out.at[place.tp], send.at[0])
        self.copies = []
        for k in range(1, GROUP):
            peer = (place.tp + k) % GROUP
            self.copies.append(
                remote(x.at[peer], out.at[place.tp], send.at[k], recv.at[k], place.device(peer))
            )

    def start(self):
        for c in self.copies:
            c.start()
        self.local.start()

    def finish(self):
        for c in self.copies:
            c.wait_recv()
        for c in self.copies:
            c.wait_send()
        self.local.wait()


def group_peers(place):
    return [place.device((place.tp + k) % GROUP) for k in range(1, GROUP)]


def columns_of(dp, t, shards):
    ys, streams = lax.axis_size("y"), lax.axis_size("st")
    z, y = dp // ys, dp % ys
    return ((z * streams + t // shards) * ys + y) * shards + t % shards


def exchange_back(x, planes, shards, cid):
    _, wrows, both = x.shape
    hidden = both // 2
    brows = hidden // planes
    step = min(wrows, 32)

    def body(x_ref, gate_ref, up_ref, got, send, recv):
        place = Place(shards)
        greet(group_peers(place))
        run = Exchange(place, x_ref, got, send, recv)
        run.start()
        run.finish()
        for t in range(GROUP):
            for dp in range(planes):
                flat = columns_of(dp, t, shards)
                for m, out in enumerate((gate_ref, up_ref)):
                    for at in range(0, wrows, step):
                        part = pl.ds(at, step)
                        out[part, flat * brows : (flat + 1) * brows] = got[
                            t, part, m * hidden + dp * brows : m * hidden + (dp + 1) * brows
                        ].astype(f32)

    shape = jax.ShapeDtypeStruct((wrows, hidden * GROUP), f32)
    return pallas(
        body, (shape, shape), [VMEM], (VMEM, VMEM),
        [pltpu.VMEM(x.shape, bf16), DMA((GROUP,)), DMA((GROUP,))], cid, 25,
    )(x)


class PlaceGather:
    SEMS = 5

    def __init__(self, own, out, send, recv, halves):
        z, y = lax.axis_index("zh"), lax.axis_index("y")
        dp, across = z * 2 + y, (1 - z) * 2 + y
        to_z, to_y = {"zh": 1 - z}, {"y": 1 - y}

        def copy(index, src, slot, part, device):
            return remote(
                src.at[part], out.at[slot, part], send.at[index], recv.at[index], device
            )

        first, second = halves
        self.local = pltpu.make_async_copy(own, out.at[dp], send.at[send.shape[0] - 1])
        self.z = [copy(0, own, dp, first, to_z), copy(1, own, dp, second, to_z)]
        self.y = [
            remote(own, out.at[dp], send.at[2], recv.at[2], to_y),
            copy(3, out.at[across], across, first, to_y),
            copy(4, out.at[across], across, second, to_y),
        ]

    def forward(self, half):
        self.z[half].wait_recv()
        self.y[1 + half].start()

    def finish(self):
        for c in self.y:
            c.wait_recv()
        for c in self.z + self.y:
            c.wait_send()


def front(tokens, cotangent, small, w_out, w_query, key_weight, value_weight, w_gate, w_up,
          w_down, planes, direct, shards, cid):
    rows, width = tokens.shape
    wrows = w_out.shape[0]
    srows, scols = small.shape
    brows = w_down.shape[0]
    hidden = brows * planes
    parts = [w_query.shape[1] // GROUP, key_weight.shape[1] // GROUP, value_weight.shape[1] // GROUP]
    qkv = sum(parts)
    slots = planes if direct else 1
    inputs = [tokens, cotangent, w_query, key_weight, value_weight, w_gate, w_up]
    if direct:
        inputs += [w_down, w_out]

    def body(*refs):
        refs = list(refs)

        def take(count):
            taken = refs[:count]
            del refs[:count]
            return taken

        small_ref, = take(1)
        sources = take(len(inputs))
        tok_all, cot_all, small_all, attn_all, ffn_all = take(5)
        down_all, wout_all = take(2) if direct else (None, None)
        held = take(len(inputs))
        (pack, isem, tsend, trecv, csend, crecv, ssend, srecv, psend, precv, fsend, frecv, asend,
         arecv, aasend, aarecv, dsend, drecv, wsend, wrecv) = refs
        place = Place(shards)
        tp, dp, flat = place.tp, place.dp(), place.flat()

        loads = [
            pltpu.make_async_copy(s, h, isem.at[i]) for i, (s, h) in enumerate(zip(sources, held))
        ]
        for i in (2, 3, 4, 0, 5, 6) + ((7, 8) if direct else ()) + (1,):
            loads[i].start()
        tok_ref, cot_ref, wq_ref, wk_ref, wv_ref, wg_ref, wu_ref = held[:7]

        barrier = pltpu.get_barrier_semaphore()

        def signal(device):
            pl.semaphore_signal(
                barrier, inc=1, device_id=device, device_id_type=pl.DeviceIdType.MESH
            )

        for device in group_peers(place):
            signal(device)
        for k in range(1, planes):
            signal(place.dp_device((dp + k) % planes))
        if direct:
            high, low = lax.axis_index("zh"), lax.axis_index("st")
            y, seq = lax.axis_index("y"), lax.axis_index("seq")
            to_seq = high * 2 + y
            from_high, from_y = seq // 2, seq % 2
            selfish = seq == to_seq
            mine = y == from_y
            for j in range(4):

                @pl.when(jnp.logical_and(mine, (from_high * 4 + j) != (high * 4 + seq)))
                def _():
                    signal({"zh": from_high, "seq": jnp.int32(j)})

            pl.semaphore_wait(
                barrier, GROUP - 1 + planes - 1 + 2 - selfish.astype(jnp.int32)
            )
        else:
            pl.semaphore_wait(barrier, GROUP - 1 + planes - 1)

        here = dp if direct else 0
        attn = []
        at = 0
        for i, (ref, cols) in enumerate(zip((wq_ref, wk_ref, wv_ref), parts)):
            loads[2 + i].wait()
            for k in range(GROUP):
                peer = (tp + k) % GROUP
                column = place.head(peer) * cols
                src = ref.at[:, pl.ds(pl.multiple_of(column, cols), cols)]
                dst = attn_all.at[here, tp, :, pl.ds(at, cols)]
                sem = i * GROUP + k
                if k == 0:
                    attn.append(pltpu.make_async_copy(src, dst, asend.at[sem]))
                else:
                    attn.append(
                        remote(src, dst, asend.at[sem], arecv.at[sem], place.device(peer))
                    )
                attn[-1].start()
            at += cols

        small_own = pltpu.make_async_copy(small_ref, small_all.at[tp, dp], ssend.at[0])
        small_own.start()
        small_dp = []
        for k in range(1, planes):
            small_dp.append(
                remote(
                    small_ref, small_all.at[tp, dp], ssend.at[k], srecv.at[k],
                    place.dp_device((dp + k) % planes),
                )
            )
            small_dp[-1].start()

        if direct:
            down_ref, wout_ref = held[7:]
            loads[7].wait()
            half = brows // 2
            down_dp = PlaceGather(
                down_ref, down_all, dsend, drecv, (pl.ds(0, half), pl.ds(half, half))
            )
            down_dp.z[0].start()
        loads[0].wait()
        tok = RingGather(place, tok_ref, tok_all, tsend, trecv, direct)
        tok.start()

        loads[5].wait()
        loads[6].wait()
        for t in range(GROUP):
            for d in range(planes):
                column = columns_of(d, t, shards)
                for m, ref in enumerate((wg_ref, wu_ref)):
                    lane = m * hidden + d * brows
                    pack[t, :, lane : lane + brows] = ref[:, column * brows : (column + 1) * brows]
        ffn = Exchange(place, pack, ffn_all, fsend, frecv)
        ffn.start()

        if direct:
            down_dp.y[0].start()
            down_dp.local.start()
            loads[8].wait()
            wout_copies = [
                remote(
                    wout_ref, wout_all.at[seq], wsend.at[k], wrecv.at[seq],
                    {"zh": z, "seq": to_seq},
                )
                for k, z in enumerate((high, 1 - high))
            ]
            wout_own = pltpu.make_async_copy(wout_ref, wout_all.at[seq], wsend.at[0])
            wout_over = remote(
                wout_all, wout_all, wsend.at[2], wrecv.at[4], place.across()
            )

            @pl.when(selfish)
            def _():
                wout_own.start()

            @pl.when(jnp.logical_not(selfish))
            def _():
                wout_copies[0].start()

            wout_copies[1].start()

        for i in range(3 * GROUP):
            if i % GROUP == 0:
                attn[i].wait()
            else:
                attn[i].wait_recv()
        if direct:
            half = GROUP // 2
            attn_dp = PlaceGather(
                attn_all.at[dp], attn_all, aasend, aarecv, (pl.ds(0, half), pl.ds(half, half))
            )
            attn_dp.z[0].start()
            attn_dp.y[0].start()
            attn_dp.z[1].start()
            down_dp.z[1].start()

        small_own.wait()
        for c in small_dp:
            c.wait_recv()
        small_tp = []
        for k in range(1, GROUP):
            small_tp.append(
                remote(
                    small_all.at[tp], small_all.at[tp], psend.at[k], precv.at[k],
                    place.device((tp + k) % GROUP),
                )
            )
            small_tp[-1].start()

        loads[1].wait()
        cot = RingGather(place, cot_ref, cot_all, csend, crecv, direct)
        tok.pass_on()
        cot.start()
        tok.step_across()
        if direct:
            down_dp.forward(0)

            @pl.when(mine)
            def _():
                for j in range(4):

                    @pl.when((from_high * 4 + j) != (high * 4 + seq))
                    def _():
                        remote(
                            wout_ref, wout_all.at[j], wsend.at[0], wrecv.at[j], place.across()
                        ).wait_recv()

                @pl.when(selfish)
                def _():
                    wout_own.wait()

                wout_over.start()

            attn_dp.forward(0)
        tok.step_far()
        cot.pass_on()
        if direct:
            attn_dp.forward(1)
        cot.step_across()
        if direct:
            down_dp.forward(1)
        cot.step_far()
        tok.finish()
        cot.finish()
        ffn.finish()
        for i in range(3 * GROUP):
            if i % GROUP:
                attn[i].wait_send()
        for c in small_tp:
            c.wait_recv()
        for c in small_dp + small_tp:
            c.wait_send()
        if direct:
            attn_dp.finish()
            down_dp.finish()
            down_dp.local.wait()

            @pl.when(jnp.logical_not(selfish))
            def _():
                wout_copies[0].wait_send()

            wout_copies[1].wait_send()

            @pl.when(mine)
            def _():
                wout_over.wait_send()

            @pl.when(jnp.logical_not(mine))
            def _():
                wout_over.wait_recv()

    shapes = [
        jax.ShapeDtypeStruct((GROUP, rows, width), bf16),
        jax.ShapeDtypeStruct((GROUP, rows, width), bf16),
        jax.ShapeDtypeStruct((GROUP, planes, srows, scols), bf16),
        jax.ShapeDtypeStruct((slots, GROUP, wrows, qkv), bf16),
        jax.ShapeDtypeStruct((GROUP, wrows, 2 * hidden), bf16),
    ]
    if direct:
        shapes += [
            jax.ShapeDtypeStruct((planes, brows, width), bf16),
            jax.ShapeDtypeStruct((planes, wrows, width), bf16),
        ]
    return pallas(
        body,
        shapes,
        [VMEM] + [ANY] * len(inputs),
        [ANY, ANY, VMEM] + [ANY] * (len(shapes) - 3),
        [pltpu.VMEM(x.shape, x.dtype) for x in inputs]
        + [pltpu.VMEM((GROUP, wrows, 2 * hidden), bf16), DMA((len(inputs),))]
        + gather_scratch() + gather_scratch()
        + [
            DMA((planes,)), DMA((planes,)), DMA((GROUP,)), DMA((GROUP,)),
            DMA((GROUP,)), DMA((GROUP,)), DMA((3 * GROUP,)), DMA((3 * GROUP,)),
            DMA((PlaceGather.SEMS,)), DMA((PlaceGather.SEMS,)),
            DMA((PlaceGather.SEMS + 1,)), DMA((PlaceGather.SEMS,)), DMA((3,)), DMA((5,)),
        ],
        cid,
        60,
    )(small, *inputs)


class Spread:
    def __init__(self, own, piece, relay, send, recv):
        z, low, y = (lax.axis_index(a) for a in ("zh", "st", "y"))
        to_z, to_y = {"zh": 1 - z}, {"y": 1 - y}
        beside, middle = {"st": 1 - low}, {"zh": 1 - z, "st": 1 - low}
        self.outer = z == low
        self.inner = z != low
        count = relay.shape[0]
        self.direct, self.toward, self.onward, self.y, self.on = [], [], [], [], []
        for h in range(count):
            at_y, at_on, at_more = count + h, 2 * count + h, 3 * count + h
            here, there = piece(z, h, y), piece(1 - z, h, y)
            self.direct.append(remote(own(h), here, send.at[h], recv.at[h], to_z))
            self.toward.append(
                remote(own(h), relay.at[h], send.at[h], recv.at[at_more], beside)
            )
            self.onward.append(
                remote(relay.at[h], here, send.at[at_more], recv.at[h], middle)
            )
            self.y.append(remote(own(h), here, send.at[at_y], recv.at[at_y], to_y))
            self.on.append(remote(there, there, send.at[at_on], recv.at[at_on], to_y))

    def start_z(self, first=0, last=None):
        @pl.when(self.outer)
        def _():
            for c in self.toward[first:last]:
                c.start()

        @pl.when(self.inner)
        def _():
            for c in self.direct[first:last]:
                c.start()

    def start_y(self):
        for c in self.y:
            c.start()

    def relay(self, half):
        @pl.when(self.inner)
        def _():
            self.toward[half].wait_recv()
            self.onward[half].start()

    def forward(self, half):
        self.direct[half].wait_recv()
        self.on[half].start()

    def finish(self):
        for c in self.y + self.on:
            c.wait_recv()
        for c in self.direct + self.y + self.on:
            c.wait_send()

        @pl.when(self.inner)
        def _():
            for c in self.onward:
                c.wait_send()


def rope_constants(length):
    exponent = np.arange(HEAD_SIZE // 2, dtype=np.float32) * np.float32(2.0 / HEAD_SIZE)
    inverse = np.power(np.float32(ROPE_BASE), -exponent).astype(np.float32)
    angles = np.arange(length, dtype=np.float32)[:, None] * inverse[None, :]
    cosine, sine = np.cos(angles.astype(np.float64)), np.sin(angles.astype(np.float64))
    return (
        jnp.asarray(np.concatenate([cosine, cosine], axis=1).astype(np.float32)),
        jnp.asarray(np.concatenate([-sine, sine], axis=1).astype(np.float32)),
    )


def document_mask(row, docs, low, count, keys):
    at_row = low + lax.broadcasted_iota(jnp.int32, (count, 1), 0)
    at_col = lax.broadcasted_iota(jnp.int32, (1, keys), 1)
    seg_row = jnp.zeros((count, 1), jnp.int32)
    seg_col = jnp.zeros((1, keys), jnp.int32)
    for d in range(docs):
        start = (row[:, d : d + 1] * 128.0 + row[:, docs + d : docs + d + 1]).astype(jnp.int32)
        seg_row = seg_row + jnp.where(at_row >= start, 1, 0)
        seg_col = seg_col + jnp.where(at_col >= start, 1, 0)
    return jnp.logical_and(at_row >= at_col, seg_row == seg_col)


def forward_pass(tokens, cotangent, small, w_out, w_query, key_weight, value_weight, w_gate,
                 w_up, w_down, docs, shards, cid):
    rows, width = tokens.shape
    wrows = w_out.shape[0]
    brows = w_down.shape[0]
    planes = 4
    hidden = brows * planes
    parts = [w_query.shape[1] // GROUP, key_weight.shape[1] // GROUP, value_weight.shape[1] // GROUP]
    qkv = sum(parts)
    qcols = parts[0]
    heads = qcols // HEAD_SIZE
    group_rows = rows * GROUP
    length = rows * shards
    streams = GROUP // shards
    gain_rows = width // 128
    grows = -(-(2 * gain_rows + 3) // 16) * 16
    srows = wrows + grows
    gcols = HEAD_SIZE // (planes * GROUP)
    cosine, sine = rope_constants(length)
    inputs = [tokens, cotangent, w_query, key_weight, value_weight, w_gate, w_up, w_down, w_out]
    score_scale = HEAD_SIZE ** (-0.5)

    def body(
        raw_ref, cos_ref, sin_ref, s0, s1, s2, s3, s4, s5, s6, s7, s8,
        cot_all, ffn_all, down_all, h1_out, h2_all, small_all, gains_ref, attn_all, wout_all,
        qkv_ref, low_ref, gate_ref, mixed_ref, gated_ref, mid_ref, hg, starts_ref,
        h0, h1, h2, h3, h4, h5, h6, h7, h8, small_ref, pack, attn_relay, ffn_relay, down_relay, tok_all, hid, partial, held_two, isem, osem,
        tsend, trecv, csend, crecv, gsend, grecv, ssend, srecv, psend, precv, fsend, frecv, asend,
        arecv, aasend, aarecv, ffsend, ffrecv, dsend, drecv, wsend, wrecv, pair, out, near, far,
        rsend, rrecv,
    ):
        sources = [s0, s1, s2, s3, s4, s5, s6, s7, s8]
        held = [h0, h1, h2, h3, h4, h5, h6, h7, h8]
        place = Place(shards)
        tp, dp = place.tp, place.dp()
        high, low = lax.axis_index("zh"), lax.axis_index("st")
        y, seq = lax.axis_index("y"), lax.axis_index("seq")
        loads = [
            pltpu.make_async_copy(s, h, isem.at[i]) for i, (s, h) in enumerate(zip(sources, held))
        ]
        for i in (2, 3, 4, 8, 0, 5, 6, 7, 1):
            loads[i].start()
        tok_ref, cot_ref, wq_ref, wk_ref, wv_ref, wg_ref, wu_ref, down_ref, wout_ref = held

        barrier = pltpu.get_barrier_semaphore()

        def signal(device):
            pl.semaphore_signal(
                barrier, inc=1, device_id=device, device_id_type=pl.DeviceIdType.MESH
            )

        for device in group_peers(place):
            signal(device)
        for k in range(1, planes):
            signal(place.dp_device((dp + k) % planes))
        to_seq = high * 2 + y
        from_high, from_y = seq // 2, seq % 2
        selfish = seq == to_seq
        mine = y == from_y
        for j in range(4):

            @pl.when(jnp.logical_and(mine, (from_high * 4 + j) != (high * 4 + seq)))
            def _():
                signal({"zh": from_high, "seq": jnp.int32(j)})

        inner = high != low

        @pl.when(inner)
        def _():
            signal({"zh": 1 - high, "st": 1 - low})

        pl.semaphore_wait(
            barrier,
            GROUP - 1 + planes - 1 + 2 - selfish.astype(jnp.int32) + inner.astype(jnp.int32),
        )

        attn = []
        at = 0
        for i, (ref, cols) in enumerate(zip((wq_ref, wk_ref, wv_ref), parts)):
            loads[2 + i].wait()
            for k in range(GROUP):
                peer = (tp + k) % GROUP
                column = place.head(peer) * cols
                src = ref.at[:, pl.ds(pl.multiple_of(column, cols), cols)]
                dst = attn_all.at[high, low, y, pl.ds(seq * wrows, wrows), pl.ds(at, cols)]
                sem = i * GROUP + k
                if k == 0:
                    attn.append(pltpu.make_async_copy(src, dst, asend.at[sem]))
                else:
                    attn.append(
                        remote(src, dst, asend.at[sem], arecv.at[sem], place.device(peer))
                    )
                attn[-1].start()
            at += cols

        small_ref[0:wrows] = raw_ref[0:wrows]
        flat = place.flat()
        block = raw_ref[wrows : wrows + 16].astype(f32)
        row_of = lax.broadcasted_iota(jnp.int32, (grows, 128), 0)
        placed = jnp.zeros((grows, 128), f32)
        per_row = 128 // wrows
        for i, (at, shift) in enumerate(
            (
                (flat // per_row, flat % per_row * wrows),
                (gain_rows + flat // per_row, flat % per_row * wrows),
                (2 * gain_rows, flat * gcols),
                (2 * gain_rows + 1, flat * gcols),
                (2 * gain_rows + 2, 0),
            )
        ):
            row = jnp.broadcast_to(block[i : i + 1], (grows, 128))
            placed = jnp.where(row_of == at, pltpu.roll(row, shift, 1), placed)
        small_ref[wrows:] = placed.astype(bf16)
        small_own = pltpu.make_async_copy(small_ref, small_all.at[tp, dp], ssend.at[0])
        small_own.start()
        small_dp = []
        for k in range(1, planes):
            small_dp.append(
                remote(
                    small_ref, small_all.at[tp, dp], ssend.at[k], srecv.at[k],
                    place.dp_device((dp + k) % planes),
                )
            )
            small_dp[-1].start()

        loads[5].wait()
        loads[6].wait()
        def pack_rows(i, _):
            part = pl.ds(pl.multiple_of(i * 16, 16), 16)
            for t in range(GROUP):
                for d in range(planes):
                    column = columns_of(d, t, shards)
                    for m, ref in enumerate((wg_ref, wu_ref)):
                        lane = m * hidden + d * brows
                        pack[t, part, lane : lane + brows] = ref[
                            part, column * brows : (column + 1) * brows
                        ]
            return 0

        lax.fori_loop(0, wrows // 16, pack_rows, 0)

        def arrived(copies):
            for i, c in enumerate(copies):
                if i % GROUP == 0:
                    c.wait()
                else:
                    c.wait_recv()

        arrived(attn)

        def attn_piece(zp, half, yp):
            return attn_all.at[zp, half, yp]

        attn_dp = Spread(
            lambda half: attn_piece(high, half, y), attn_piece, attn_relay, aasend, aarecv
        )
        attn_dp.start_z()
        attn_dp.start_y()
        loads[0].wait()
        tok = RingGather(place, tok_ref, tok_all, tsend, trecv, True)
        tok.start()
        small_own.wait()
        for c in small_dp:
            c.wait_recv()
        small_tp = []
        for k in range(1, GROUP):
            small_tp.append(
                remote(
                    small_all.at[tp], small_all.at[tp], psend.at[k], precv.at[k],
                    place.device((tp + k) % GROUP),
                )
            )
            small_tp[-1].start()
        attn_dp.relay(0)
        attn_dp.relay(1)

        loads[7].wait()
        half_rows = brows // 2

        def down_piece(zp, half, yp):
            return down_all.at[zp * 2 + yp, pl.ds(half * half_rows, half_rows)]

        down_dp = Spread(
            lambda half: down_ref.at[pl.ds(half * half_rows, half_rows)], down_piece, down_relay,
            dsend, drecv,
        )
        down_own = pltpu.make_async_copy(down_ref, down_all.at[dp], dsend.at[8])
        down_own.start()
        down_dp.start_z()
        tok.pass_on()
        ffn_dst = ffn_all.at[high, low, y, pl.ds(seq * wrows, wrows)]
        ffn = [pltpu.make_async_copy(pack.at[tp], ffn_dst, fsend.at[0])]
        for k, (ahead, other) in enumerate(
            ((3, False), (3, True), (0, True), (1, False), (1, True), (2, False), (2, True))
        ):
            peer = place.block(ahead, other)
            ffn.append(
                remote(
                    pack.at[peer], ffn_dst, fsend.at[k + 1], frecv.at[k + 1], place.device(peer)
                )
            )
        for c in ffn[:4]:
            c.start()
        loads[8].wait()
        wout_copies = [
            remote(
                wout_ref, wout_all.at[seq], wsend.at[k], wrecv.at[seq], {"zh": z, "seq": to_seq}
            )
            for k, z in enumerate((high, 1 - high))
        ]
        wout_own = pltpu.make_async_copy(wout_ref, wout_all.at[seq], wsend.at[0])
        wout_over = remote(wout_all, wout_all, wsend.at[2], wrecv.at[4], place.across())
        wout_copies[1].start()

        @pl.when(selfish)
        def _():
            wout_own.start()

        @pl.when(jnp.logical_not(selfish))
        def _():
            wout_copies[0].start()

        attn_dp.forward(0)
        attn_dp.forward(1)
        down_dp.start_y()
        tok.step_across()
        down_dp.relay(0)
        tok.step_far()
        for c in ffn[4:]:
            c.start()

        @pl.when(mine)
        def _():
            for j in range(4):

                @pl.when((from_high * 4 + j) != (high * 4 + seq))
                def _():
                    remote(
                        wout_ref, wout_all.at[j], wsend.at[0], wrecv.at[j], place.across()
                    ).wait_recv()

            @pl.when(selfish)
            def _():
                wout_own.wait()

            wout_over.start()

        for c in small_tp:
            c.wait_recv()
        gains = jnp.zeros((grows, 128), f32)
        for t in range(GROUP):
            for d in range(planes):
                gains = gains + small_all[t, d, pl.ds(wrows, grows)].astype(f32)
                flat = columns_of(d, t, shards)
                hg[flat * wrows : (flat + 1) * wrows] = small_all[t, d, pl.ds(0, wrows)]
        gains_ref[...] = gains
        gain_one = jnp.concatenate([gains[i : i + 1] for i in range(gain_rows)], axis=1)
        gain_two = jnp.concatenate(
            [gains[gain_rows + i : gain_rows + i + 1] for i in range(gain_rows)], axis=1
        )
        query_gain = gains[2 * gain_rows : 2 * gain_rows + 1]
        key_gain = gains[2 * gain_rows + 1 : 2 * gain_rows + 2]
        starts = []
        for st in range(streams):
            block = small_all[st * shards, dp, pl.ds(wrows, grows)].astype(f32)
            starts.append(block[2 * gain_rows + 2 : 2 * gain_rows + 3])
            starts_ref[st : st + 1] = starts[st]

        tok.finish()
        step = 32

        def norm(i, _):
            block = i // (rows // step)
            inner = pl.ds(pl.multiple_of(i % (rows // step) * step, step), step)
            value = tok_all[block, inner].astype(f32)
            hid[block, inner] = (value * rms_scale(value) * gain_one).astype(bf16)
            return 0

        lax.fori_loop(0, group_rows // step, norm, 0)
        save = pltpu.make_async_copy(hid, h1_out, osem)
        save.start()
        down_dp.relay(1)
        attn_dp.finish()
        weight = attn_all[...].reshape(width, qkv)
        head = place.head(tp)
        lanes = lax.broadcasted_iota(jnp.int32, (1, 128), 1)

        def rotary(x, gain, s):
            scaled = x * rms_scale(x) * gain
            return (
                scaled * cos_ref[...] + pltpu.roll(scaled, HEAD_SIZE // 2, 1) * sin_ref[...]
            ).astype(bf16)

        def project(s, _):
            part = pl.ds(pl.multiple_of(s * length, length), length)
            normed = hid[pl.ds(s * shards, shards)].reshape(length, width)
            raw = jnp.dot(normed, weight, preferred_element_type=f32)
            qkv_ref[part] = raw
            logit = jnp.dot(normed, hg[...], preferred_element_type=f32)
            for g in range(heads):
                at = g * HEAD_SIZE
                low_ref[part, at : at + HEAD_SIZE] = rotary(
                    raw[:, at : at + HEAD_SIZE], query_gain, s
                )
                own = jnp.sum(
                    jnp.where(lanes == head * heads + g, logit, 0.0), axis=1, keepdims=True
                )
                gate_ref[part, at : at + HEAD_SIZE] = jnp.broadcast_to(
                    jax.nn.sigmoid(own), (length, HEAD_SIZE)
                )
            low_ref[part, qcols : qcols + HEAD_SIZE] = rotary(
                raw[:, qcols : qcols + HEAD_SIZE], key_gain, s
            )
            low_ref[part, qcols + HEAD_SIZE :] = raw[:, qcols + HEAD_SIZE :].astype(bf16)
            return 0

        lax.fori_loop(0, streams, project, 0)
        arrived(ffn)

        quarter = shards * wrows // 2

        def ffn_piece(zp, half, yp):
            return ffn_all.at[zp, half // 2, yp, pl.ds(half % 2 * quarter, quarter)]

        ffn_dp = Spread(
            lambda half: ffn_piece(high, half, y), ffn_piece, ffn_relay, ffsend, ffrecv
        )
        ffn_dp.start_z(0, 2)
        ffn_dp.start_y()
        block = 128
        def attend(s, _):
            base = pl.multiple_of(s * length, length)
            row = starts_ref[pl.ds(s, 1)]
            for r in range(0, length, block):
                keys = r + block
                allowed = document_mask(row, docs, r, block, keys)
                key = low_ref[pl.ds(base, keys), qcols : qcols + HEAD_SIZE]
                value = low_ref[pl.ds(base, keys), qcols + HEAD_SIZE :]
                part = pl.ds(base + r, block)
                for g in range(heads):
                    at = g * HEAD_SIZE
                    scores = (
                        lax.dot_general(
                            low_ref[part, at : at + HEAD_SIZE], key, (((1,), (1,)), ((), ())),
                            preferred_element_type=f32,
                        )
                        * score_scale
                    )
                    scores = jnp.where(allowed, scores, MASK_FILL)
                    weights = jnp.exp(scores - jnp.max(scores, axis=1, keepdims=True))
                    probs = weights / jnp.sum(weights, axis=1, keepdims=True)
                    mixed = jnp.dot(
                        probs.astype(bf16), value, preferred_element_type=f32
                    ).astype(bf16)
                    mixed_ref[part, at : at + HEAD_SIZE] = mixed
                    gated_ref[part, at : at + HEAD_SIZE] = (
                        mixed.astype(f32) * gate_ref[part, at : at + HEAD_SIZE]
                    ).astype(bf16)
            return 0

        lax.fori_loop(0, streams, attend, 0)

        @pl.when(jnp.logical_not(mine))
        def _():
            wout_over.wait_recv()

        wide = 512
        def give(i, _):
            s = i // (width // wide)
            cols = pl.ds(pl.multiple_of(i % (width // wide) * wide, wide), wide)
            product = jnp.dot(
                gated_ref[pl.ds(pl.multiple_of(s * length, length), length)],
                wout_all[:, :, cols].reshape(qcols, wide),
                preferred_element_type=f32,
            )
            partial[pl.ds(s * shards, shards), :, cols] = product.astype(bf16).reshape(
                shards, rows, wide
            )
            return 0

        lax.fori_loop(0, streams * (width // wide), give, 0)

        def emit(part, total):
            middle = tok_ref[part].astype(f32) + total
            mid_ref[part] = middle
            held_two[part] = (middle * rms_scale(middle) * gain_two).astype(bf16)

        def first():
            ffn_dp.relay(0)
            down_dp.forward(0)

        def second():
            ffn_dp.relay(1)
            ffn_dp.start_z(2, 3)
            down_dp.forward(1)
            ffn_dp.forward(0)

        ring_scatter(
            place, partial, pair, out, near, far, rsend, rrecv, emit, (first, second)
        )
        two = RingGather(place, held_two, h2_all, gsend, grecv, True)
        two.start()
        ffn_dp.forward(1)
        ffn_dp.relay(2)
        two.pass_on()
        ffn_dp.start_z(3, 4)
        loads[1].wait()
        cot = RingGather(place, cot_ref, cot_all, csend, crecv, True)
        cot.start()
        ffn_dp.relay(3)
        two.step_across()
        ffn_dp.forward(2)
        two.step_far()
        cot.pass_on()
        ffn_dp.forward(3)
        cot.step_across()
        cot.step_far()
        two.finish()
        cot.finish()
        ffn_dp.finish()
        down_dp.finish()
        down_own.wait()
        save.wait()
        for i, c in enumerate(attn):
            if i % GROUP:
                c.wait_send()
        for c in ffn[1:] + small_dp + small_tp:
            c.wait_send()

        @pl.when(jnp.logical_not(selfish))
        def _():
            wout_copies[0].wait_send()

        wout_copies[1].wait_send()

        @pl.when(mine)
        def _():
            wout_over.wait_send()

    pieces = (2, streams, 2, shards * wrows)
    shape = jax.ShapeDtypeStruct
    return pallas(
        body,
        [
            shape((GROUP, rows, width), bf16),
            shape(pieces + (2 * hidden,), bf16),
            shape((planes, brows, width), bf16),
            shape((GROUP, rows, width), bf16),
            shape((GROUP, rows, width), bf16),
            shape((GROUP, planes, srows, 128), bf16),
            shape((grows, 128), f32),
            shape(pieces + (qkv,), bf16),
            shape((planes, wrows, width), bf16),
            shape((group_rows, qkv), f32),
            shape((group_rows, qkv), bf16),
            shape((group_rows, qcols), f32),
            shape((group_rows, qcols), bf16),
            shape((group_rows, qcols), bf16),
            shape((rows, width), f32),
            shape((width, 128), bf16),
            shape((streams, 128), f32),
        ],
        [VMEM] * 3 + [ANY] * len(inputs),
        [ANY] * 5 + [VMEM] * 12,
        [pltpu.VMEM(x.shape, x.dtype) for x in inputs]
        + [
            pltpu.VMEM((srows, 128), bf16),
            pltpu.VMEM((GROUP, wrows, 2 * hidden), bf16),
            pltpu.VMEM((2, shards * wrows, qkv), bf16),
            pltpu.VMEM((4, shards * wrows // 2, 2 * hidden), bf16),
            pltpu.VMEM((2, brows // 2, width), bf16),
            pltpu.VMEM((GROUP, rows, width), bf16),
            pltpu.VMEM((GROUP, rows, width), bf16),
            pltpu.VMEM((GROUP, rows, width), bf16),
            pltpu.VMEM((rows, width), bf16),
            DMA((len(inputs),)),
            DMA,
        ]
        + gather_scratch() + gather_scratch() + gather_scratch()
        + [
            DMA((planes,)), DMA((planes,)), DMA((GROUP,)), DMA((GROUP,)),
            DMA((GROUP,)), DMA((GROUP,)), DMA((3 * GROUP,)), DMA((3 * GROUP,)),
            DMA((8,)), DMA((8,)), DMA((16,)), DMA((16,)),
            DMA((9,)), DMA((8,)), DMA((3,)), DMA((5,)),
        ]
        + scatter_scratch(rows, width),
        cid,
        100,
        56,
    )(small, cosine, sine, *inputs)


class PlaceSums:
    SENDS, RECVS = 8, 6

    def __init__(self, piece, got, far, near, relay, send, recv):
        z, low, y = (lax.axis_index(a) for a in ("zh", "st", "y"))
        to_z, to_y = {"zh": 1 - z}, {"y": 1 - y}
        beside, middle = {"st": 1 - low}, {"zh": 1 - z, "st": 1 - low}
        self.outer, self.inner = z == low, z != low
        self.got, self.far, self.near = got, far, near
        self.y_far = remote(piece(1 - z, 1 - y), got.at[0], send.at[0], recv.at[0], to_y)
        self.y_near = remote(piece(z, 1 - y), got.at[1], send.at[1], recv.at[1], to_y)
        self.loads = [
            pltpu.make_async_copy(piece(1 - z, y), far, send.at[2]),
            pltpu.make_async_copy(piece(z, y), near, send.at[3]),
        ]

        def half(ref, h):
            if len(far.shape) == 3:
                return ref.at[h]
            count = far.shape[0] // 2
            return ref.at[pl.ds(h * count, count)]

        self.direct, self.toward, self.onward = [], [], []
        for h in range(2):
            dst = half(got.at[2], h)
            self.direct.append(
                remote(half(far, h), dst, send.at[4 + h], recv.at[2 + h], to_z)
            )
            self.toward.append(
                remote(half(far, h), half(relay, h), send.at[4 + h], recv.at[4 + h], beside)
            )
            self.onward.append(
                remote(half(relay, h), dst, send.at[6 + h], recv.at[2 + h], middle)
            )

    def load(self):
        for c in self.loads:
            c.start()

    def over_z(self, late=False):
        self.loads[0].wait()
        self.y_far.wait_recv()
        self.each(lambda at: self.put(at))
        Spread.start_z(self, 0, 1 if late else 2)

    def start_late(self):
        Spread.start_z(self, 1, 2)

    def relay(self, half):
        @pl.when(self.inner)
        def _():
            self.toward[half].wait_recv()
            self.onward[half].start()

    def put(self, at):
        self.far[at] = (self.far[at].astype(f32) + self.got[(0,) + at].astype(f32)).astype(bf16)

    def each(self, visit):
        lead, rows = self.far.shape[:-2], self.far.shape[-2]

        def inner(i, _):
            part = pl.ds(pl.multiple_of(i * 32, 32), 32)
            if lead:
                for k in range(lead[0]):
                    visit((k, part))
            else:
                visit((part,))
            return 0

        lax.fori_loop(0, rows // 32, inner, 0)

    def total(self, at):
        return (self.near[at].astype(f32) + self.got[(1,) + at].astype(f32)) + self.got[
            (2,) + at
        ].astype(f32)

    def arrive(self):
        self.loads[1].wait()
        self.y_near.wait_recv()
        for c in self.direct:
            c.wait_recv()

    def drain(self):
        for c in [self.y_far, self.y_near] + self.direct:
            c.wait_send()

        @pl.when(self.inner)
        def _():
            for c in self.onward:
                c.wait_send()


def backward_pass(x, act, down_w, middle, tokens, cotangent, gains, headgate, qkv_w, out_w, hidden_one,
                  qkv, low, gate, mixed, gated, starts, down_grad, ffn_grad, docs, shards, cid):
    _, rows, width = x.shape
    planes = 4
    streams = GROUP // shards
    length = rows * shards
    group_rows = rows * GROUP
    qcols = gate.shape[1]
    qkv_cols = qkv.shape[1]
    kcols = (qkv_cols - qcols) // 2
    heads = qcols // HEAD_SIZE
    brows = down_grad.shape[2]
    both = ffn_grad.shape[4]
    hidden = both // 2
    wrows = width // (planes * GROUP)
    gain_rows = width // 128
    score_scale = HEAD_SIZE ** (-0.5)
    cosine, sine = rope_constants(length)
    srows = 24
    inputs = [
        x, middle, tokens, cotangent, headgate, qkv_w, out_w, qkv, low, gate, mixed, gated,
    ]

    def body(
        gains_ref, starts_ref, cos_ref, sin_ref, act_in, dw_in, h1_ref, down_ref, ffn_ref,
        i0, i1, i2, i3, i4, i5, i6, i7, i8, i9, i10, i11,
        t0, t1, t2, t3, t4, t5, t6, t7, t8, s_out, final_ref,
        layer_ref, tgrad_ref, gate_out, up_out, query_out, key_out, value_out, o_out, down_out,
        fsem, dw_ref, product_ref, act_sem, dw_sem, product_sem, partial, mid_ref, tok_ref, cot_ref, hg_ref, wq_ref, wout_ref, qkv_ref, low_ref, gate_ref,
        mixed_ref, gated_ref,
        held, db_all, dmid, gq, dgl, dk_acc, dv_acc, dmix, small, stage, s_got, s_held, s_line,
        g_got, g_far, g_near, g_in, d_got, d_far, d_near, q_own, q_got, q_far, q_near, q_in,
        o_own, o_got, o_far, o_near, o_in, g_relay, d_relay, q_relay, o_relay,
        pair, out, near, far, rsend, rrecv, r2send, r2recv, r3send, r3recv, csend, crecv,
        isem, gsend, grecv, dsend, drecv, qsend, qrecv, osend, orecv, gxsend, gxrecv, qxsend,
        qxrecv, oxsend, oxrecv, asend, arecv, bsend, brecv, lsem, turn,
    ):
        sources = [i0, i1, i2, i3, i4, i5, i6, i7, i8, i9, i10, i11]
        targets = [
            partial, mid_ref, tok_ref, cot_ref, hg_ref, wq_ref, wout_ref, qkv_ref, low_ref,
            gate_ref, mixed_ref, gated_ref,
        ]
        finals = [
            pltpu.make_async_copy(ready, target, fsem.at[i])
            for i, (ready, target) in enumerate(
                (
                    (layer_ref, t0), (tgrad_ref, t1), (gate_out, t2), (up_out, t3),
                    (query_out, t4), (key_out, t5), (value_out, t6), (o_out, t7), (down_out, t8),
                )
            )
        ]
        place = Place(shards)
        tp, dp, flat = place.tp, place.dp(), place.flat()
        high, y, seq = lax.axis_index("zh"), lax.axis_index("y"), lax.axis_index("seq")
        loads = [
            pltpu.make_async_copy(s, t, isem.at[i])
            for i, (s, t) in enumerate(zip(sources, targets))
        ]
        for c in loads[:4]:
            c.start()
        load_act = [
            pltpu.make_async_copy(act_in.at[:, pl.ds(0, qkv_cols)], gq, act_sem.at[0]),
            pltpu.make_async_copy(act_in.at[:, pl.ds(qkv_cols, qcols)], dmix, act_sem.at[1]),
        ]
        for c in load_act:
            c.start()
        barrier = pltpu.get_barrier_semaphore()

        def signal(device, semaphore=barrier):
            pl.semaphore_signal(
                semaphore, inc=1, device_id=device, device_id_type=pl.DeviceIdType.MESH
            )

        for device in group_peers(place):
            signal(device)
        for k in range(1, planes):
            signal(place.dp_device((dp + k) % planes))
        owner = place.head(tp) * planes + dp
        source = {"st": lax.axis_index("st"), "seq": high * 2 + y}
        source.update(place.dp_device(seq))

        @pl.when(owner != flat)
        def _():
            signal(source)

        inner = high != lax.axis_index("st")

        @pl.when(inner)
        def _():
            signal({"zh": 1 - high, "st": 1 - lax.axis_index("st")})

        pl.semaphore_wait(
            barrier,
            GROUP + planes - 2 + (owner != flat).astype(jnp.int32) + inner.astype(jnp.int32),
        )

        ffn = PlaceSums(
            lambda zp, yp: ffn_ref.at[zp, :, yp], g_got, g_far, g_near, g_relay, gsend, grecv
        )
        down = PlaceSums(lambda zp, yp: down_ref.at[zp, yp], d_got, d_far, d_near, d_relay, dsend, drecv)
        down.y_far.start()
        ffn.y_far.start()
        ffn.y_near.start()
        down.load()
        ffn.load()
        for c in loads[4:]:
            c.start()

        small[...] = jnp.zeros_like(small)
        gain_all = gains_ref[...]
        gain_one = jnp.concatenate([gain_all[i : i + 1] for i in range(gain_rows)], axis=1)
        gain_two = jnp.concatenate(
            [gain_all[gain_rows + i : gain_rows + i + 1] for i in range(gain_rows)], axis=1
        )
        query_gain = gain_all[2 * gain_rows : 2 * gain_rows + 1]
        key_gain = gain_all[2 * gain_rows + 1 : 2 * gain_rows + 2]
        for c in loads[:4]:
            c.wait()

        def emit_dm(part, total):
            value = mid_ref[part]
            scale = rms_scale(value)
            normed = value * scale
            small[17:18] += jnp.sum(total * normed, axis=0, keepdims=True)
            dm = cot_ref[part].astype(f32) + norm_back(total * gain_two, normed, scale)
            dmid[part] = dm
            held[part] = dm.astype(bf16)

        ring_scatter(place, partial, pair, out, near, far, rsend, rrecv, emit_dm)
        grad = RingGather(place, held, db_all, csend, crecv)
        grad.start()
        h1_all = partial
        load_h1 = pltpu.make_async_copy(h1_ref, h1_all, lsem.at[0])
        load_h1.start()

        for c in load_act:
            c.wait()
        fine = dw_ref.shape[2]
        blocks = width // fine

        def columns(i):
            return pl.ds(pl.multiple_of(i * fine, fine), fine)

        def weight_load(i):
            return pltpu.make_async_copy(
                dw_in.at[:, columns(i)], dw_ref.at[i % 2], dw_sem.at[i % 2]
            )

        def product_store(i):
            return pltpu.make_async_copy(
                product_ref.at[i % 2], final_ref.at[:, :, columns(i)], product_sem.at[i % 2]
            )

        weight_load(0).start()

        def down_product(i, _):
            @pl.when(i + 1 < blocks)
            def _():
                weight_load(i + 1).start()

            weight_load(i).wait()

            @pl.when(i >= 2)
            def _():
                product_store(i - 2).wait()

            product = jnp.dot(
                gq[...], dw_ref[i % 2, 0:qkv_cols], preferred_element_type=f32
            ) + jnp.dot(dmix[...], dw_ref[i % 2, qkv_cols:], preferred_element_type=f32)
            product_ref[i % 2] = product.astype(bf16).reshape(GROUP, rows, fine)
            product_store(i).start()
            return 0

        lax.fori_loop(0, blocks, down_product, 0)
        for i in (blocks - 2, blocks - 1):
            product_store(i).wait()
        down.over_z()
        grad.pass_on()
        down.relay(0)
        grad.step_across()
        down.relay(1)
        grad.step_far()
        for c in loads[4:]:
            c.wait()
        grad.finish()

        lanes = lax.broadcasted_iota(jnp.int32, (1, 128), 1)
        head = place.head(tp)
        def open_out(s, _):
            part = pl.ds(pl.multiple_of(s * length, length), length)
            db = db_all[pl.ds(s * shards, shards)].reshape(length, width)
            da = lax.dot_general(
                db, wout_ref[...], (((1,), (1,)), ((), ())), preferred_element_type=f32
            )
            logits = jnp.zeros((length, 128), f32)
            for g in range(heads):
                at = g * HEAD_SIZE
                piece = da[:, at : at + HEAD_SIZE]
                opened = gate_ref[part, at : at + HEAD_SIZE]
                dmix[part, at : at + HEAD_SIZE] = (piece * opened).astype(bf16)
                own = jnp.sum(
                    piece * mixed_ref[part, at : at + HEAD_SIZE].astype(f32), axis=1,
                    keepdims=True,
                )
                logits = jnp.where(
                    lanes == head * heads + g, own * opened * (1.0 - opened), logits
                )
            dgl[part] = logits.astype(bf16)
            return 0

        lax.fori_loop(0, streams, open_out, 0)
        wide = 512
        def out_grad(i, _):
            cols = pl.ds(pl.multiple_of(i * wide, wide), wide)
            product = lax.dot_general(
                gated_ref[...], db_all[:, :, cols].reshape(group_rows, wide),
                (((0,), (0,)), ((), ())), preferred_element_type=f32,
            ).astype(bf16)
            for j in range(planes):
                o_own[j // 2, j % 2, :, cols] = product[j * wrows : (j + 1) * wrows]
            return 0

        lax.fori_loop(0, width // wide, out_grad, 0)
        outs = PlaceSums(lambda zp, yp: o_own.at[zp, yp], o_got, o_far, o_near, o_relay, osend, orecv)
        outs.y_far.start()
        outs.load()
        ffn.over_z(True)

        block = 128

        def attend_back(s, carried):
            query_part, key_part = carried
            base = pl.multiple_of(s * length, length)
            row = starts_ref[pl.ds(s, 1)]
            dk_acc[...] = jnp.zeros_like(dk_acc)
            dv_acc[...] = jnp.zeros_like(dv_acc)

            def back(grad_rotated, raw, gain):
                grad_gained = grad_rotated * cos_ref[...] - pltpu.roll(
                    grad_rotated, HEAD_SIZE // 2, 1
                ) * sin_ref[...]
                scale = rms_scale(raw)
                normed = raw * scale
                return (
                    jnp.sum(grad_gained * normed, axis=0, keepdims=True),
                    norm_back(grad_gained * gain, normed, scale).astype(bf16),
                )

            for r in range(0, length, block):
                keys = r + block
                allowed = document_mask(row, docs, r, block, keys)
                key = low_ref[pl.ds(base, keys), qcols : qcols + HEAD_SIZE]
                value = low_ref[pl.ds(base, keys), qcols + HEAD_SIZE :]
                part = pl.ds(base + r, block)
                for g in range(heads):
                    at = g * HEAD_SIZE
                    query = low_ref[part, at : at + HEAD_SIZE]
                    scores = (
                        lax.dot_general(
                            query, key, (((1,), (1,)), ((), ())), preferred_element_type=f32
                        )
                        * score_scale
                    )
                    scores = jnp.where(allowed, scores, MASK_FILL)
                    weights = jnp.exp(scores - jnp.max(scores, axis=1, keepdims=True))
                    probs = weights / jnp.sum(weights, axis=1, keepdims=True)
                    dout = dmix[part, at : at + HEAD_SIZE]
                    dprobs = lax.dot_general(
                        dout, value, (((1,), (1,)), ((), ())), preferred_element_type=f32
                    )
                    delta = jnp.sum(probs * dprobs, axis=1, keepdims=True)
                    dscores = (probs * (dprobs - delta)).astype(bf16)
                    dq = jnp.dot(dscores, key, preferred_element_type=f32) * score_scale
                    gq[part, at : at + HEAD_SIZE] = dq.astype(bf16)
                    dk_acc[0:keys] += lax.dot_general(
                        dscores, query, (((0,), (0,)), ((), ())), preferred_element_type=f32
                    )
                    dv_acc[0:keys] += lax.dot_general(
                        probs.astype(bf16), dout, (((0,), (0,)), ((), ())),
                        preferred_element_type=f32,
                    )
            part = pl.ds(base, length)
            for g in range(heads):
                at = g * HEAD_SIZE
                sums, grads = back(
                    gq[part, at : at + HEAD_SIZE].astype(f32), qkv_ref[part, at : at + HEAD_SIZE],
                    query_gain,
                )
                query_part = query_part + sums
                gq[part, at : at + HEAD_SIZE] = grads
            sums, grads = back(
                (dk_acc[...] * score_scale).astype(bf16).astype(f32),
                qkv_ref[part, qcols : qcols + HEAD_SIZE], key_gain,
            )
            key_part = key_part + sums
            gq[part, qcols : qcols + HEAD_SIZE] = grads
            gq[part, qcols + HEAD_SIZE :] = dv_acc[...].astype(bf16)
            return query_part, key_part

        query_part, key_part = lax.fori_loop(
            0, streams, attend_back,
            (jnp.zeros((1, HEAD_SIZE), f32), jnp.zeros((1, HEAD_SIZE), f32)),
        )

        load_h1.wait()
        def qkv_grad(n, _):
            cols = pl.ds(pl.multiple_of(n * 256, 256), 256)
            product = lax.dot_general(
                h1_all[:, :, cols].reshape(group_rows, 256), gq[...], (((0,), (0,)), ((), ())),
                preferred_element_type=f32,
            )
            q_own[n // 4, n // 2 % 2, n % 2] = product.astype(bf16)
            return 0

        lax.fori_loop(0, width // 256, qkv_grad, 0)
        qkvs = PlaceSums(lambda zp, yp: q_own.at[zp, :, yp], q_got, q_far, q_near, q_relay, qsend, qrecv)
        qkvs.y_far.start()
        outs.y_near.start()
        qkvs.y_near.start()
        down.y_near.start()
        qkvs.load()
        def headgate_grad(i, _):
            cols = pl.ds(pl.multiple_of(i * wide, wide), wide)
            small[0:16, cols] = lax.dot_general(
                dgl[...], h1_all[:, :, cols].reshape(group_rows, wide),
                (((0,), (0,)), ((), ())), preferred_element_type=f32,
            )[0:16]
            return 0

        lax.fori_loop(0, width // wide, headgate_grad, 0)

        def dh1(i, _):
            s = i // (width // wide)
            at = pl.multiple_of(i % (width // wide) * wide, wide)
            part, cols = pl.ds(pl.multiple_of(s * length, length), length), pl.ds(at, wide)
            product = lax.dot_general(
                gq[part], wq_ref[cols], (((1,), (1,)), ((), ())), preferred_element_type=f32
            ) + lax.dot_general(
                dgl[part], hg_ref[cols], (((1,), (1,)), ((), ())), preferred_element_type=f32
            )
            partial[pl.ds(s * shards, shards), :, cols] = product.astype(bf16).reshape(
                shards, rows, wide
            )
            return 0

        lax.fori_loop(0, streams * (width // wide), dh1, 0)

        def emit_tokens(part, total):
            tok = tok_ref[part].astype(f32)
            scale = rms_scale(tok)
            normed = tok * scale
            small[16:17] += jnp.sum(total * normed, axis=0, keepdims=True)
            tgrad_ref[part] = (
                dmid[part] + norm_back(total * gain_one, normed, scale)
            ).astype(bf16)

        load_final = pltpu.make_async_copy(final_ref, db_all, lsem.at[1])
        load_final.start()
        ring_scatter(
            place, partial, pair, out, near, far, r2send, r2recv, emit_tokens,
            (lambda: ffn.relay(0), ffn.start_late),
        )
        finals[1].start()
        ring_peers = [place.right(), place.left(), place.partner()]
        for device in ring_peers:
            signal(device, turn)
        outs.over_z()
        qkvs.over_z()
        ffn.relay(1)

        small[18:19] = jnp.concatenate([query_part] * gain_rows, axis=1)
        small[19:20] = jnp.concatenate([key_part] * gain_rows, axis=1)
        for t in range(GROUP):
            for d in range(planes):
                lane = columns_of(d, t, shards) // 2 * 128
                stage[t, d * srows : (d + 1) * srows] = small[:, lane : lane + 128]
        sums = Exchange(place, stage, s_got, asend, arecv)
        sums.start()

        load_final.wait()
        pl.semaphore_wait(turn, len(ring_peers))

        def emit_layer(part, total):
            layer_ref[part] = (mid_ref[part] + total).astype(bf16)

        def first():
            outs.relay(0)
            outs.relay(1)

        def scatter_rows(total, ready, send, recv, into):
            def keep(at):
                ready[at] = total(at).astype(bf16)

            copies = []
            for k in range(GROUP):
                peer = (tp + k) % GROUP
                src = ready.at[peer // shards, pl.ds(peer % shards * wrows, wrows)]
                if k == 0:
                    copies.append(pltpu.make_async_copy(src, into.at[tp], send.at[0]))
                else:
                    copies.append(
                        remote(src, into.at[tp], send.at[k], recv.at[k], place.device(peer))
                    )
            return keep, copies

        keep_ffn, ffn_rows = scatter_rows(ffn.total, g_near, gxsend, gxrecv, g_in)

        def second():
            qkvs.relay(0)
            qkvs.relay(1)
            ffn.arrive()
            ffn.each(keep_ffn)
            for c in ffn_rows:
                c.start()

        ring_scatter(
            place, db_all, pair, out, near, far, r3send, r3recv, emit_layer, (first, second)
        )
        finals[0].start()
        sums.finish()
        s_held[...] = jnp.sum(s_got[...], axis=0).reshape(s_held.shape)
        line_own = pltpu.make_async_copy(s_held.at[dp], s_line.at[dp], bsend.at[0])
        line_own.start()
        lines = []
        for k in range(1, planes):
            to = (dp + k) % planes
            lines.append(
                remote(
                    s_held.at[to], s_line.at[dp], bsend.at[k], brecv.at[k], place.dp_device(to)
                )
            )
            lines[-1].start()

        down.arrive()

        def put_down(at):
            down_out[at] = down.total(at)

        down.each(put_down)
        finals[8].start()

        def landed(copies):
            copies[0].wait()
            for c in copies[1:]:
                c.wait_recv()

        landed(ffn_rows)
        def unpack_rows(i, _):
            part = pl.ds(pl.multiple_of(i * 16, 16), 16)
            for t in range(GROUP):
                for d in range(planes):
                    column = columns_of(d, t, shards)
                    for m, ref in enumerate((gate_out, up_out)):
                        lane = m * hidden + d * brows
                        ref[part, column * brows : (column + 1) * brows] = g_in[
                            t, part, lane : lane + brows
                        ].astype(f32)
            return 0

        lax.fori_loop(0, wrows // 16, unpack_rows, 0)
        finals[2].start()
        finals[3].start()

        outs.arrive()

        def keep_out(at):
            o_near[at] = outs.total(at).astype(bf16)

        outs.each(keep_out)
        out_own = pltpu.make_async_copy(o_near, o_in, oxsend)
        out_far = remote(o_near, o_in, oxsend, oxrecv, place.any_device(owner))

        @pl.when(owner == flat)
        def _():
            out_own.start()

        @pl.when(owner != flat)
        def _():
            out_far.start()

        qkvs.arrive()
        keep, qkv_rows = scatter_rows(qkvs.total, q_near, qxsend, qxrecv, q_in)
        qkvs.each(keep)
        for c in qkv_rows:
            c.start()

        landed(qkv_rows)
        for t in range(GROUP):
            home = place.head(t)
            query_out[:, home * qcols : (home + 1) * qcols] = q_in[t, :, :qcols].astype(f32)
            key_out[:, home * kcols : (home + 1) * kcols] = q_in[
                t, :, qcols : qcols + kcols
            ].astype(f32)
            value_out[:, home * kcols : (home + 1) * kcols] = q_in[
                t, :, qcols + kcols :
            ].astype(f32)

        for c in finals[4:7]:
            c.start()

        @pl.when(owner == flat)
        def _():
            out_own.wait()

        @pl.when(owner != flat)
        def _():
            out_far.wait()

        o_out[...] = o_in[...].astype(f32)
        finals[7].start()
        for c in lines:
            c.wait_recv()
        line_own.wait()
        summed = jnp.sum(s_line[...], axis=0)
        per_row = 128 // wrows
        gcols = HEAD_SIZE // (planes * GROUP)
        s_out[...] = jnp.where(
            lax.broadcasted_iota(jnp.int32, (srows, 128), 0) < 18,
            pltpu.roll(summed, (128 - flat % per_row * wrows) % 128, 1),
            pltpu.roll(summed, (128 - flat * gcols) % 128, 1),
        )
        for c in lines + ffn_rows[1:] + qkv_rows[1:]:
            c.wait_send()
        for c in (ffn, down, qkvs, outs):
            c.drain()
        for c in finals:
            c.wait()

    shape = jax.ShapeDtypeStruct
    vmem = pltpu.VMEM
    wide_rows = shards * wrows
    return pallas(
        body,
        [
            shape((rows, width), bf16),
            shape((rows, width), bf16),
            shape((wrows, hidden * GROUP), f32),
            shape((wrows, hidden * GROUP), f32),
            shape((wrows, qcols * GROUP), f32),
            shape((wrows, kcols * GROUP), f32),
            shape((wrows, kcols * GROUP), f32),
            shape((wrows, width), f32),
            shape((brows, width), f32),
            shape((srows, 128), f32),
            shape((GROUP, rows, width), bf16),
        ],
        [VMEM] * 4 + [ANY] * (5 + len(inputs)),
        [ANY] * 9 + [VMEM, ANY],
        [
            vmem((rows, width), bf16),
            vmem((rows, width), bf16),
            vmem((wrows, hidden * GROUP), f32),
            vmem((wrows, hidden * GROUP), f32),
            vmem((wrows, qcols * GROUP), f32),
            vmem((wrows, kcols * GROUP), f32),
            vmem((wrows, kcols * GROUP), f32),
            vmem((wrows, width), f32),
            vmem((brows, width), f32),
            DMA((9,)),
            vmem((2, act.shape[1], 256), bf16),
            vmem((2, GROUP, rows, 256), bf16),
            DMA((2,)), DMA((2,)), DMA((2,)),
        ]
        + [vmem(i.shape, i.dtype) for i in inputs]
        + [
            vmem((rows, width), bf16),
            vmem((GROUP, rows, width), bf16),
            vmem((rows, width), f32),
            vmem((group_rows, qkv_cols), bf16),
            vmem((group_rows, 128), bf16),
            vmem((length, HEAD_SIZE), f32),
            vmem((length, HEAD_SIZE), f32),
            vmem((group_rows, qcols), bf16),
            vmem((srows, width), f32),
            vmem((GROUP, planes * srows, 128), f32),
            vmem((GROUP, planes * srows, 128), f32),
            vmem((planes, srows, 128), f32),
            vmem((planes, srows, 128), f32),
            vmem((3, streams, wide_rows, both), bf16),
            vmem((streams, wide_rows, both), bf16),
            vmem((streams, wide_rows, both), bf16),
            vmem((GROUP, wrows, both), bf16),
            vmem((3, brows, width), bf16),
            vmem((brows, width), bf16),
            vmem((brows, width), bf16),
            vmem((2, streams, 2, wide_rows, qkv_cols), bf16),
            vmem((3, streams, wide_rows, qkv_cols), bf16),
            vmem((streams, wide_rows, qkv_cols), bf16),
            vmem((streams, wide_rows, qkv_cols), bf16),
            vmem((GROUP, wrows, qkv_cols), bf16),
            vmem((2, 2, wrows, width), bf16),
            vmem((3, wrows, width), bf16),
            vmem((wrows, width), bf16),
            vmem((wrows, width), bf16),
            vmem((wrows, width), bf16),
            vmem((streams, wide_rows, both), bf16),
            vmem((brows, width), bf16),
            vmem((streams, wide_rows, qkv_cols), bf16),
            vmem((wrows, width), bf16),
        ]
        + scatter_scratch(rows, width)
        + [DMA((10,)), DMA((10,)), DMA((10,)), DMA((10,))]
        + gather_scratch()
        + [DMA((len(inputs),))]
        + [DMA((PlaceSums.SENDS,)), DMA((PlaceSums.RECVS,))] * 4
        + [DMA((GROUP,)), DMA((GROUP,)), DMA((GROUP,)), DMA((GROUP,)), DMA, DMA]
        + [DMA((GROUP,)), DMA((GROUP,)), DMA((planes,)), DMA((planes,)), DMA((2,))]
        + [pltpu.SemaphoreType.REGULAR],
        cid,
        180,
        63,
    )(gains, starts, cosine, sine, act, down_w, hidden_one, down_grad, ffn_grad, *inputs)


def store(*arrays):
    count = len(arrays)

    def body(*refs):
        load_sem, store_sem = refs[-2:]
        staged = refs[2 * count : 3 * count]
        loads = [
            pltpu.make_async_copy(refs[i], staged[i], load_sem.at[i]) for i in range(count)
        ]
        stores = [
            pltpu.make_async_copy(staged[i], refs[count + i], store_sem.at[i])
            for i in range(count)
        ]
        for c in loads:
            c.start()
        for load, c in zip(loads, stores):
            load.wait()
            c.start()
        for c in stores:
            c.wait()

    return pl.pallas_call(
        body,
        out_shape=[jax.ShapeDtypeStruct(a.shape, a.dtype) for a in arrays],
        in_specs=[ANY] * count,
        out_specs=[ANY] * count,
        scratch_shapes=[pltpu.VMEM(a.shape, a.dtype) for a in arrays]
        + [DMA((count,)), DMA((count,))],
        compiler_params=pltpu.CompilerParams(vmem_limit_bytes=62 * 1024 * 1024),
    )(*arrays)


def settle(qkv_grad, out_grad, small, qcols, kcols, planes, direct, shards, cid):
    srows = small.shape[1] // planes
    cols = small.shape[2]
    wrows, width = out_grad.shape

    def body(
        q_ref, o_ref, s_ref, query_out, key_out, value_out, o_out, s_out, q_got, o_got, got, held,
        line, qsend, qrecv, osend, orecv, asend, arecv, bsend, brecv,
    ):
        place = Place(shards)
        tp, dp, flat = place.tp, place.dp(), place.flat()
        barrier = pltpu.get_barrier_semaphore()

        def signal(device):
            pl.semaphore_signal(
                barrier, inc=1, device_id=device, device_id_type=pl.DeviceIdType.MESH
            )

        for device in group_peers(place):
            signal(device)
        for k in range(1, planes):
            signal(place.dp_device((dp + k) % planes))
        if direct:
            owner = place.head(tp) * planes + dp
            high, y = lax.axis_index("zh"), lax.axis_index("y")
            source = {"st": lax.axis_index("st"), "seq": high * 2 + y}
            source.update(place.dp_device(lax.axis_index("seq")))

            @pl.when(owner != flat)
            def _():
                signal(source)

            pl.semaphore_wait(barrier, GROUP + planes - 2 + (owner != flat).astype(jnp.int32))
        else:
            pl.semaphore_wait(barrier, GROUP + planes - 2)

        sums = Exchange(place, s_ref, got, asend, arecv)
        sums.start()
        qkv = Exchange(place, q_ref, q_got, qsend, qrecv)
        qkv.start()
        if direct:
            out_own = pltpu.make_async_copy(o_ref, o_got, osend)
            out_far = remote(o_ref, o_got, osend, orecv, place.any_device(owner))

            @pl.when(owner == flat)
            def _():
                out_own.start()

            @pl.when(owner != flat)
            def _():
                out_far.start()

        sums.finish()
        held[...] = jnp.sum(got[...], axis=0).reshape(held.shape)
        line_own = pltpu.make_async_copy(held.at[dp], line.at[dp], bsend.at[0])
        line_own.start()
        lines = []
        for k in range(1, planes):
            to = (dp + k) % planes
            lines.append(
                remote(held.at[to], line.at[dp], bsend.at[k], brecv.at[k], place.dp_device(to))
            )
            lines[-1].start()
        qkv.finish()
        for t in range(GROUP):
            head = place.head(t)
            query_out[:, head * qcols : (head + 1) * qcols] = q_got[t, :, :qcols].astype(f32)
            key_out[:, head * kcols : (head + 1) * kcols] = q_got[
                t, :, qcols : qcols + kcols
            ].astype(f32)
            value_out[:, head * kcols : (head + 1) * kcols] = q_got[t, :, qcols + kcols :].astype(
                f32
            )
        if direct:

            @pl.when(owner == flat)
            def _():
                out_own.wait()

            @pl.when(owner != flat)
            def _():
                out_far.wait()

            o_out[...] = o_got[...].astype(f32)
        else:
            o_out[...] = o_ref[...].astype(f32)
        for c in lines:
            c.wait_recv()
        line_own.wait()
        s_out[...] = jnp.sum(line[...], axis=0)
        for c in lines:
            c.wait_send()

    return pallas(
        body,
        [
            jax.ShapeDtypeStruct((wrows, GROUP * qcols), f32),
            jax.ShapeDtypeStruct((wrows, GROUP * kcols), f32),
            jax.ShapeDtypeStruct((wrows, GROUP * kcols), f32),
            jax.ShapeDtypeStruct((wrows, width), f32),
            jax.ShapeDtypeStruct((srows, cols), f32),
        ],
        [VMEM, VMEM, VMEM],
        [VMEM] * 5,
        [
            pltpu.VMEM(qkv_grad.shape, bf16),
            pltpu.VMEM(out_grad.shape, bf16),
            pltpu.VMEM(small.shape, f32),
            pltpu.VMEM((planes, srows, cols), f32),
            pltpu.VMEM((planes, srows, cols), f32),
            DMA((GROUP,)), DMA((GROUP,)), DMA, DMA,
            DMA((GROUP,)), DMA((GROUP,)), DMA((planes,)), DMA((planes,)),
        ],
        cid,
        20,
    )(qkv_grad, out_grad, small)


def local(
    tokens, doc_starts, attn_gain, query_gain, key_gain, w_query, key_weight, value_weight,
    w_headgate, w_out, ffn_gain, w_gate, w_up, w_down, cotangent,
):
    zs, ys = lax.axis_size("zh"), lax.axis_size("y")
    planes = zs * ys
    direct = zs == 2 and ys == 2
    streams = lax.axis_size("st")
    shards = lax.axis_size("seq")
    devices = planes * GROUP
    rows, width = tokens.shape
    length = rows * shards
    group_rows = rows * GROUP
    wrows = w_query.shape[0]
    brows = w_down.shape[0]
    hidden = brows * planes
    qcols = w_query.shape[1] // GROUP
    kcols = key_weight.shape[1] // GROUP
    group_heads = qcols // HEAD_SIZE
    all_heads = w_headgate.shape[1]
    score_scale = HEAD_SIZE ** (-0.5)
    dp = lax.axis_index(DP)
    tp = lax.axis_index(TP)

    hg = wrows * all_heads
    gcols = query_gain.shape[0]
    at = hg + 2 * wrows
    count = at + 2 * gcols
    sums = -(-count // 1024) * 8
    docs = doc_starts.shape[1]
    qkv_cols = qcols + 2 * kcols
    starts_row = jnp.concatenate(
        [(doc_starts[0] // 128).astype(bf16), (doc_starts[0] % 128).astype(bf16)]
    )
    headgate_rows = jnp.pad(w_headgate, ((0, 0), (0, 128 - all_heads)))
    if direct:
        gain_rows = width // 128
        others = [attn_gain, ffn_gain, query_gain, key_gain, starts_row]
        small = jnp.pad(w_headgate, ((0, 16), (0, 128 - all_heads)))
        for i, row in enumerate(others):
            small = small + jnp.pad(
                row[None], ((wrows + i, 15 - i), (0, 128 - row.shape[0]))
            )
        (
            cot_all, ffn_w, down_w, hidden_one, hidden_two, small, gains, qkv_w, out_w, qkv,
            low, gate_full, mixed, gated, middle, headgate, starts,
        ) = forward_pass(
            tokens, cotangent, small, w_out, w_query, key_weight, value_weight, w_gate, w_up,
            w_down, docs, shards, 0,
        )
        cot_all = cot_all.reshape(group_rows, width)
        hidden_two = hidden_two.reshape(group_rows, width)
        ffn_w = ffn_w.reshape(width, 2 * hidden)
        down_w = down_w.reshape(hidden, width)
        gate_up = mm(hidden_two, ffn_w)
        gate_pre, up_proj = gate_up[:, :hidden], gate_up[:, hidden:]
        gate_sig = jax.nn.sigmoid(gate_pre)
        inner_act = (gate_pre * gate_sig * up_proj).astype(bf16)
        down_grad = mm_t(inner_act, cot_all).astype(bf16)
        grad_inner = mm_b(cot_all, down_w)
        grad_gate = grad_inner * up_proj * gate_sig * (1.0 + gate_pre * (1.0 - gate_sig))
        grad_up = grad_inner * gate_pre * gate_sig
        grad_gu = jnp.concatenate([grad_gate.astype(bf16), grad_up.astype(bf16)], axis=1)
        ffn_grad = mm_t(hidden_two, grad_gu).astype(bf16)
        places = (GROUP, rows, width)
        (
            layer_out, tokens_grad, gate_grad, up_grad, query_grad, key_grad, value_grad,
            out_grad, down_grad, small_sum, _,
        ) = backward_pass(
            mm_b(grad_gu, ffn_w).astype(bf16).reshape(places),
            inner_act, down_w, middle, tokens, cotangent, gains, headgate,
            qkv_w.reshape(width, qkv_cols), out_w.reshape(qcols, width), hidden_one, qkv, low,
            gate_full, mixed, gated, starts, down_grad.reshape(zs, ys, brows, width),
            ffn_grad.reshape(zs, streams, ys, shards * wrows, 2 * hidden), docs, shards, 1,
        )
        (
            layer_out, tokens_grad, gate_grad, up_grad, query_grad, key_grad, value_grad,
            out_grad, down_grad,
        ) = store(
            layer_out, tokens_grad, gate_grad, up_grad, query_grad, key_grad, value_grad,
            out_grad, down_grad,
        )
        return (
            layer_out,
            tokens_grad,
            small_sum[all_heads, :wrows],
            small_sum[18, :gcols],
            small_sum[19, :gcols],
            query_grad,
            key_grad,
            value_grad,
            small_sum[:all_heads, :wrows].T,
            out_grad,
            small_sum[all_heads + 1, :wrows],
            gate_grad,
            up_grad,
            down_grad,
        )
    else:
        srows = -(-(wrows + 6) // 16) * 16
        others = [attn_gain, ffn_gain, query_gain, key_gain, starts_row[:docs], starts_row[docs:]]
        small = jnp.concatenate(
            [headgate_rows]
            + [jnp.pad(row, (0, 128 - row.shape[0]))[None] for row in others]
            + [jnp.zeros((srows - wrows - 6, 128), bf16)]
        )
        tokens_all, cot_all, small, qkv_w, ffn_own = front(
            tokens, cotangent, small, w_out, w_query, key_weight, value_weight, w_gate, w_up,
            w_down, planes, False, shards, 0,
        )
        tokens_all = tokens_all.reshape(group_rows, width)
        cot_all = cot_all.reshape(group_rows, width)
        qkv_w = over_dp(qkv_w[0])
        ffn_w = over_dp(ffn_own)
        down_w = lax.all_gather(w_down, DP, axis=0, tiled=True)
        out_w = lax.all_gather(w_out, ALL, axis=0, tiled=True)
        out_w = lax.dynamic_slice_in_dim(out_w, tp * qcols, qcols, 0)
        head = tp
        here = pick(small[::shards], 1, dp)
        starts = here[:, wrows + 4, :docs].astype(jnp.int32) * 128
        starts = starts + here[:, wrows + 5, :docs].astype(jnp.int32)
    small = small.reshape(streams, shards, zs, ys, srows, 128).transpose(2, 0, 3, 1, 4, 5)
    small = small.reshape(devices, srows, 128)
    headgate_all = small[:, :wrows, :all_heads].reshape(width, all_heads)
    if not direct:
        attn_gain_f = small[:, wrows, :wrows].reshape(1, -1).astype(f32)
        ffn_gain_f = small[:, wrows + 1, :wrows].reshape(1, -1).astype(f32)
        query_gain_f = small[:, wrows + 2, :gcols].reshape(-1).astype(f32)
        key_gain_f = small[:, wrows + 3, :gcols].reshape(-1).astype(f32)
    headgate_own = lax.dynamic_slice_in_dim(headgate_all, head * group_heads, group_heads, 1)

    if not direct:
        residual_all = tokens_all.astype(f32)
        hidden_all = (residual_all * rms_scale(residual_all) * attn_gain_f).astype(bf16)
        qkv = mm(hidden_all, qkv_w)
    query_raw = qkv[:, :qcols].reshape(group_rows, group_heads, HEAD_SIZE)
    key_raw = qkv[:, qcols : qcols + kcols].reshape(group_rows, 1, HEAD_SIZE)
    value = qkv[:, qcols + kcols :].astype(bf16).reshape(streams, length, HEAD_SIZE)
    positions = jnp.tile(jnp.arange(length, dtype=jnp.int32), streams)
    cosine, sine = rotary_tables(positions)
    query_scale = rms_scale(query_raw)
    query_normed = query_raw * query_scale
    query = rotate(query_normed * query_gain_f, cosine, sine).astype(bf16)
    query = query.reshape(streams, length, group_heads, HEAD_SIZE)
    key_scale = rms_scale(key_raw)
    key_normed = key_raw * key_scale
    key = rotate(key_normed * key_gain_f, cosine, sine).astype(bf16)
    key = key.reshape(streams, length, HEAD_SIZE)
    stream_pos = jnp.arange(length, dtype=jnp.int32)
    segment = jnp.sum((stream_pos[None, :, None] >= starts[:, None, :]).astype(jnp.int32), axis=2)
    allowed = (stream_pos[:, None] >= stream_pos[None, :])[None] & (
        segment[:, :, None] == segment[:, None, :]
    )
    scores = jnp.einsum("bqgd,bkd->bgqk", query, key, preferred_element_type=f32) * score_scale
    scores = jnp.where(allowed[:, None], scores, MASK_FILL)
    row_max = jnp.max(scores, axis=-1, keepdims=True)
    weights = jnp.exp(scores - row_max)
    probs = weights / jnp.sum(weights, axis=-1, keepdims=True)
    probs_low = probs.astype(bf16)
    if not direct:
        mixed = jnp.einsum(
            "bgqk,bkd->bqgd", probs_low, value, preferred_element_type=f32
        ).astype(bf16)
    mixed_f = mixed.astype(f32).reshape(group_rows, group_heads, HEAD_SIZE)
    if direct:
        head_gate = gate_full.reshape(group_rows, group_heads, HEAD_SIZE)[:, :, :1]
    else:
        head_gate = jax.nn.sigmoid(mm(hidden_all, headgate_own))[:, :, None]
        gated = (mixed_f * head_gate).astype(bf16).reshape(group_rows, qcols)

    def parts(x):
        return x.astype(bf16).reshape(GROUP, rows, width)

    if not direct:
        middle, hidden_two = middle_step(
            parts(mm(gated, out_w)), tokens, ffn_gain_f, None, shards, 2
        )
        hidden_two = hidden_two.reshape(group_rows, width)

    gate_up = mm(hidden_two, ffn_w)
    gate_pre, up_proj = gate_up[:, :hidden], gate_up[:, hidden:]
    gate_sig = jax.nn.sigmoid(gate_pre)
    inner_act = (gate_pre * gate_sig * up_proj).astype(bf16)
    down_grad = mm_t(inner_act, cot_all).astype(bf16).reshape(zs, ys, brows, width)
    if direct:
        down_sum = PlaceSum(down_grad)
        down_sum.over_y()
    else:
        down_grad = scatter_dp(down_grad)
    grad_inner = mm_b(cot_all, down_w)
    grad_gate = (grad_inner * up_proj * gate_sig * (1.0 + gate_pre * (1.0 - gate_sig))).astype(bf16)
    grad_up = (grad_inner * gate_pre * gate_sig).astype(bf16)
    grad_gu = jnp.concatenate([grad_gate, grad_up], axis=1)
    ffn_grad = mm_t(hidden_two, grad_gu).astype(bf16)
    grad_gu, ffn_grad = lax.optimization_barrier((grad_gu, ffn_grad))
    if not direct:
        ffn_grad = scatter_dp(by_place(ffn_grad))
    grad_middle, ffn_gain_part, grad_branch, *ffn_first = middle_back(
        parts(mm_b(grad_gu, ffn_w)), middle, cotangent, ffn_gain_f,
        ffn_grad.reshape(zs, streams, ys, -1, 2 * hidden) if direct else None, shards, 3,
    )
    if direct:
        grad_branch, down_sum.far, down_sum.near, ffn_first = lax.optimization_barrier(
            (grad_branch, down_sum.far, down_sum.near, ffn_first[0])
        )
        down_z = down_sum.over_z()
        ffn_sum = PlaceSum(by_place(ffn_grad))
        ffn_sum.take(ffn_first.reshape(-1, 2 * hidden), None)
        ffn_z = ffn_sum.over_z()
        ffn_sum.near = ffn_sum.over_y_near()
    grad_branch = grad_branch.reshape(group_rows, width)
    layer_out = scatter_sum(parts(mm(inner_act, down_w)), middle, shards, 4)

    out_grad = mm_t(gated, grad_branch).astype(bf16).reshape(zs, ys, wrows, width)
    grad_gated = mm_b(grad_branch, out_w).reshape(group_rows, group_heads, HEAD_SIZE)
    grad_mixed = (grad_gated * head_gate).astype(bf16).reshape(
        streams, length, group_heads, HEAD_SIZE
    )
    gate_flat = head_gate[:, :, 0]
    grad_logit = (
        jnp.sum(grad_gated * mixed_f, axis=-1) * gate_flat * (1.0 - gate_flat)
    ).astype(bf16)
    grad_probs = jnp.einsum("bqgd,bkd->bgqk", grad_mixed, value, preferred_element_type=f32)
    row_delta = jnp.sum(probs * grad_probs, axis=-1, keepdims=True)
    grad_scores = (probs * (grad_probs - row_delta)).astype(bf16)
    grad_query = (
        jnp.einsum("bgqk,bkd->bqgd", grad_scores, key, preferred_element_type=f32) * score_scale
    ).astype(bf16)
    grad_key = (
        jnp.einsum("bgqk,bqgd->bkd", grad_scores, query, preferred_element_type=f32) * score_scale
    ).astype(bf16)
    grad_value = jnp.einsum(
        "bgqk,bqgd->bkd", probs_low, grad_mixed, preferred_element_type=f32
    ).astype(bf16)
    gqn = rotate_back(
        grad_query.astype(f32).reshape(group_rows, group_heads, HEAD_SIZE), cosine, sine
    )
    query_gain_part = jnp.sum(gqn * query_normed, axis=(0, 1))
    grad_query_raw = norm_back(gqn * query_gain_f, query_normed, query_scale).astype(bf16)
    gkn = rotate_back(grad_key.astype(f32).reshape(group_rows, 1, HEAD_SIZE), cosine, sine)
    key_gain_part = jnp.sum(gkn * key_normed, axis=(0, 1))
    grad_key_raw = norm_back(gkn * key_gain_f, key_normed, key_scale).astype(bf16)
    grad_qkv = jnp.concatenate(
        [
            grad_query_raw.reshape(group_rows, qcols),
            grad_key_raw.reshape(group_rows, kcols),
            grad_value.reshape(group_rows, kcols),
        ],
        axis=1,
    )
    qkv_grad = mm_t(hidden_all, grad_qkv).astype(bf16)
    if direct:
        qkv_grad, out_grad, grad_qkv, down_z = lax.optimization_barrier(
            (qkv_grad, out_grad, grad_qkv, down_z)
        )
        down_grad = down_sum.total(down_z)
        qkv_sum, out_sum = PlaceSum(by_place(qkv_grad)), PlaceSum(out_grad)
        qkv_sum.over_y()
        out_sum.over_y()
        qkv_z, out_z = qkv_sum.over_z(), out_sum.over_z()
        ffn_grad = ffn_sum.total(ffn_z)
        qkv_grad, out_grad = qkv_sum.total(qkv_z), out_sum.total(out_z)
    else:
        qkv_grad = scatter_dp(by_place(qkv_grad))
        out_grad = lax.dynamic_update_slice(
            jnp.zeros((width, width), bf16), out_grad.reshape(qcols, width), (tp * qcols, 0)
        )
        out_grad = lax.psum_scatter(out_grad, ALL, scatter_dimension=0, tiled=True)
    tokens_grad, attn_gain_part = tokens_back(
        parts(mm_b(grad_qkv, qkv_w) + mm_b(grad_logit, headgate_own)),
        tokens, grad_middle, attn_gain_f, shards, 5,
    )
    headgate_part = mm_t(hidden_all, grad_logit)
    headgate_part = lax.dynamic_update_slice(
        jnp.zeros((width, all_heads), f32), headgate_part, (0, head * group_heads)
    )

    small_sum = jnp.concatenate(
        [
            headgate_part.reshape(devices, hg),
            attn_gain_part.reshape(devices, wrows),
            ffn_gain_part.reshape(devices, wrows),
            query_gain_part.reshape(devices, gcols),
            key_gain_part.reshape(devices, gcols),
        ],
        axis=1,
    )
    small_sum = jnp.pad(small_sum, ((0, 0), (0, sums * 128 - count)))
    small_sum = small_sum.reshape(zs, streams, ys, shards, sums, 128)
    small_sum = small_sum.transpose(1, 3, 0, 2, 4, 5)
    small_sum = small_sum.reshape(GROUP, planes * sums, 128)

    gate_grad, up_grad = exchange_back(
        ffn_grad.reshape(GROUP, wrows, 2 * hidden), planes, shards, 6
    )
    query_grad, key_grad, value_grad, out_grad, small_sum = settle(
        qkv_grad.reshape(GROUP, wrows, qkv_cols), out_grad, small_sum, qcols, kcols, planes,
        direct, shards, 7,
    )
    small_sum = small_sum.reshape(-1)
    return (
        layer_out,
        tokens_grad,
        small_sum[hg : hg + wrows],
        small_sum[at : at + gcols],
        small_sum[at + gcols : at + 2 * gcols],
        query_grad,
        key_grad,
        value_grad,
        small_sum[:hg].reshape(wrows, all_heads),
        out_grad,
        small_sum[hg + wrows : hg + 2 * wrows],
        gate_grad,
        up_grad,
        down_grad.astype(f32),
    )


def solution(mesh):
    shards = mesh.shape["seq"]
    planes = (2, 2, 2) if shards == 4 and mesh.size == 32 else (1, GROUP // shards, -1)
    grouped = Mesh(mesh.devices.reshape(planes + (shards,)), ALL)
    two = P(ALL, None)
    one = P(ALL)
    return jax.shard_map(
        local,
        mesh=grouped,
        in_specs=(
            two, P(("zh", "st", "y"), None), one, one, one, two, two, two, two, two, one, two, two,
            two, two,
        ),
        out_specs=(two, two, one, one, one, two, two, two, two, two, one, two, two, two),
        check_vma=False,
    )
```

```python
import jax
import jax.numpy as jnp
import numpy as np
from jax import lax
from jax.experimental import pallas as pl
from jax.experimental.pallas import tpu as pltpu
from jax.sharding import Mesh, PartitionSpec as P

QUERY_HEADS = 16
KEY_VALUE_HEADS = 8
HEAD_SIZE = 128
GROUP = 8
NORM_EPS = 1e-06
ROPE_BASE = 1000000.0
MASK_FILL = -1e30

DP = ("zh", "y")
TP = ("st", "seq")
ALL = ("zh", "st", "y", "seq")
f32 = jnp.float32
bf16 = jnp.bfloat16


def rms_scale(vector):
    return lax.rsqrt(jnp.mean(vector * vector, axis=-1, keepdims=True) + NORM_EPS)


def rotary_tables(positions):
    half_width = HEAD_SIZE // 2
    exponent = jnp.arange(half_width, dtype=jnp.int32).astype(f32) * (2.0 / HEAD_SIZE)
    inverse = jnp.power(ROPE_BASE, -exponent)
    angles = positions.astype(f32)[:, None] * inverse[None, :]
    return (jnp.cos(angles)[:, None, :], jnp.sin(angles)[:, None, :])


def rotate(vector, cosine, sine):
    a, b = jnp.split(vector, 2, axis=-1)
    return jnp.concatenate([a * cosine - b * sine, b * cosine + a * sine], axis=-1)


def rotate_back(vector, cosine, sine):
    a, b = jnp.split(vector, 2, axis=-1)
    return jnp.concatenate([a * cosine + b * sine, b * cosine - a * sine], axis=-1)


def norm_back(grad, normed, scale):
    return scale * (grad - normed * jnp.mean(grad * normed, axis=-1, keepdims=True))


def mm(left, right):
    return jnp.dot(left, right, preferred_element_type=f32)


def mm_t(left, right):
    return lax.dot_general(left, right, (((0,), (0,)), ((), ())), preferred_element_type=f32)


def mm_b(left, right):
    return lax.dot_general(left, right, (((1,), (1,)), ((), ())), preferred_element_type=f32)


SWAP = [(0, 1), (1, 0)]


def over_dp(x):
    streams, shards = lax.axis_size("st"), lax.axis_size("seq")
    zs, ys = lax.axis_size("zh"), lax.axis_size("y")
    rows, columns = x.shape[1] * shards, x.shape[2]
    whole = lax.all_gather(x, DP, axis=0, tiled=False)
    whole = whole.reshape(zs, ys, streams, rows, columns).transpose(0, 2, 1, 3, 4)
    return whole.reshape(-1, columns)


def pick(x, axis, index):
    return lax.dynamic_index_in_dim(x, index, axis, keepdims=False)


def plus(left, right):
    return left.astype(f32) + right.astype(f32)


class PlaceSum:
    def __init__(self, x):
        self.x = x
        self.z, self.y = lax.axis_index("zh"), lax.axis_index("y")

    def piece(self, zp, yp):
        return pick(pick(self.x, 0, zp), 0, yp)

    def over_y(self):
        got = lax.ppermute(pick(self.x, 1, 1 - self.y), "y", SWAP)
        self.take(pick(got, 0, 1 - self.z), pick(got, 0, self.z))

    def over_y_near(self):
        return lax.ppermute(self.piece(self.z, 1 - self.y), "y", SWAP)

    def take(self, far, near):
        self.far, self.near = far, near

    def over_z(self):
        far = plus(self.piece(1 - self.z, self.y), self.far).astype(bf16)
        return lax.ppermute(far, "zh", SWAP)

    def total(self, got):
        return (plus(self.piece(self.z, self.y), self.near) + got.astype(f32)).astype(bf16)


def scatter_dp(x):
    zs, ys = x.shape[:2]
    return lax.psum_scatter(
        x.reshape((zs * ys,) + x.shape[2:]), DP, scatter_dimension=0, tiled=False
    )


def by_place(x):
    streams = lax.axis_size("st")
    zs, ys = lax.axis_size("zh"), lax.axis_size("y")
    columns = x.shape[1]
    x = x.reshape(zs, streams, ys, -1, columns).transpose(0, 2, 1, 3, 4)
    return x.reshape(zs, ys, -1, columns)


def pallas(body, out_shape, in_specs, out_specs, scratch, cid, micros, mib=40):
    return pl.pallas_call(
        body,
        out_shape=out_shape,
        in_specs=in_specs,
        out_specs=out_specs,
        scratch_shapes=scratch,
        compiler_params=pltpu.CompilerParams(
            collective_id=cid, has_side_effects=True, vmem_limit_bytes=mib * 1024 * 1024
        ),
        cost_estimate=pl.CostEstimate(
            flops=0, bytes_accessed=int(micros * 3.6e5), transcendentals=0
        ),
    )


ANY = pl.BlockSpec(memory_space=pl.ANY)
VMEM = pl.BlockSpec(memory_space=pltpu.VMEM)
DMA = pltpu.SemaphoreType.DMA


def remote(src, dst, send, recv, device):
    return pltpu.make_async_remote_copy(
        src_ref=src,
        dst_ref=dst,
        send_sem=send,
        recv_sem=recv,
        device_id=device,
        device_id_type=pl.DeviceIdType.MESH,
    )


class Place:
    def __init__(self, shards):
        self.shards = shards
        self.tp = lax.axis_index("st") * shards + lax.axis_index("seq")
        self.core = self.tp % 2
        self.ring = self.turn(self.tp // 2)

    def turn(self, place):
        if self.shards == GROUP:
            return place
        return place + (place // 2) * (1 - 2 * (place % 2))

    def head(self, index):
        if self.shards == GROUP:
            return index
        return index // 4 * 2 + index % 4 // 2 * 4 + index % 2

    def block(self, ahead, other=False):
        ring = self.ring
        if ahead == 1:
            ring = ring + 1 - 2 * (ring % 2)
        elif ahead == 3:
            ring = 3 - ring
        elif ahead == 2:
            ring = (ring + 2) % 4
        core = 1 - self.core if other else self.core
        return self.turn(ring) * 2 + core

    def device(self, index):
        return {"st": index // self.shards, "seq": index % self.shards}

    def dp_device(self, dp):
        ys = lax.axis_size("y")
        return {"zh": dp // ys, "y": dp % ys}

    def any_device(self, flat):
        ys, streams = lax.axis_size("y"), lax.axis_size("st")
        return {
            "zh": flat // (streams * ys * self.shards),
            "st": flat // (ys * self.shards) % streams,
            "y": flat // self.shards % ys,
            "seq": flat % self.shards,
        }

    def flat(self):
        ys, streams = lax.axis_size("y"), lax.axis_size("st")
        z, y = lax.axis_index("zh"), lax.axis_index("y")
        st, seq = lax.axis_index("st"), lax.axis_index("seq")
        return ((z * streams + st) * ys + y) * self.shards + seq

    def dp(self):
        return lax.axis_index("zh") * lax.axis_size("y") + lax.axis_index("y")

    def right(self):
        return self.device(self.block(1))

    def left(self):
        return self.device(self.block(3))

    def across(self):
        return {"y": 1 - lax.axis_index("y")}

    def partner(self):
        return self.device(self.block(0, True))


def greet(devices):
    barrier = pltpu.get_barrier_semaphore()
    for device in devices:
        pl.semaphore_signal(
            barrier, inc=1, device_id=device, device_id_type=pl.DeviceIdType.MESH
        )
    pl.semaphore_wait(barrier, len(devices))


class RingGather:
    SEMS = 11

    def __init__(self, place, own, out, send, recv, one_way=False):
        rows = out.shape[1]
        half = rows // 2
        first, second = pl.ds(0, half), pl.ds(half, half)
        me, near, next_, opposite = (place.block(i) for i in (0, 1, 3, 2))
        to_near, to_next, to_partner = place.device(near), place.device(next_), place.partner()

        def copy(index, src, block, part, device):
            return remote(src, out.at[block, part], send.at[index], recv.at[index], device)

        self.local = pltpu.make_async_copy(own, out.at[me], send.at[self.SEMS])
        self.next = [
            copy(0, own.at[first], me, first, to_next),
            copy(1, own.at[second], me, second, to_next),
        ]
        self.near = [
            copy(2, own.at[first], me, first, to_near),
            copy(3, own.at[second], me, second, to_near),
        ]
        self.mate = remote(own, out.at[me], send.at[4], recv.at[4], to_partner)
        self.on = [copy(5, out.at[next_, first], next_, first, to_near)]
        if one_way:
            self.on.append(copy(6, out.at[next_, second], next_, second, to_near))
        else:
            self.on.append(copy(6, out.at[near, second], near, second, to_next))
        self.one_way = one_way
        self.across = [
            remote(out.at[next_], out.at[next_], send.at[7], recv.at[7], to_partner),
            remote(out.at[near], out.at[near], send.at[8], recv.at[8], to_partner),
            copy(9, out.at[opposite, first], opposite, first, to_partner),
            copy(10, out.at[opposite, second], opposite, second, to_partner),
        ]

    def start(self):
        self.next[0].start()
        self.near[0 if self.one_way else 1].start()
        self.next[1].start()
        self.near[1 if self.one_way else 0].start()
        self.mate.start()
        self.local.start()

    def pass_on(self):
        self.next[0].wait_recv()
        self.on[0].start()
        if self.one_way:
            self.next[1].wait_recv()
        else:
            self.near[1].wait_recv()
        self.on[1].start()

    def step_across(self):
        if not self.one_way:
            self.next[1].wait_recv()
        self.across[0].start()
        self.near[0].wait_recv()
        if self.one_way:
            self.near[1].wait_recv()
        self.across[1].start()

    def step_far(self):
        self.on[0].wait_recv()
        self.across[2].start()
        self.on[1].wait_recv()
        self.across[3].start()

    def finish(self):
        self.mate.wait_recv()
        for c in self.across:
            c.wait_recv()
        for c in self.next + self.near + [self.mate] + self.on + self.across:
            c.wait_send()
        self.local.wait()

    def run(self):
        self.start()
        self.pass_on()
        self.step_across()
        self.step_far()
        self.finish()


def ring_scatter(place, x, pair, out, near, far, send, recv, emit, between=()):
    between = list(between) + [lambda: None] * 3
    rows = x.shape[1]
    half = rows // 2
    step = 32
    to_left, to_right, to_partner = place.left(), place.right(), place.partner()
    swaps = {}
    for q in (2, 1, 3, 0):
        swaps[q] = remote(
            x.at[place.block(q, True)], pair.at[q], send.at[q], recv.at[q], to_partner
        )
        swaps[q].start()

    def add(q, low, high, extra=None):
        block = place.block(q)

        def one(i, _):
            part = pl.ds(pl.multiple_of(low + i * step, step), step)
            total = x[block, part].astype(f32) + pair[q, part].astype(f32)
            if extra is not None:
                inner = pl.ds(pl.multiple_of(i * step, step), step)
                total = total + far[extra, inner].astype(f32)
            out[q - 1, part] = total.astype(bf16)
            return 0

        lax.fori_loop(0, (high - low) // step, one, 0)

    first, second = pl.ds(0, half), pl.ds(half, half)

    def send_to(index, q, part, dst, device):
        c = remote(out.at[q - 1, part], dst, send.at[index], recv.at[index], device)
        c.start()
        return c

    swaps[2].wait_recv()
    add(2, 0, half)
    a = send_to(4, 2, first, far.at[0], to_right)
    add(2, half, rows)
    b = send_to(5, 2, second, far.at[1], to_left)
    swaps[1].wait_recv()
    add(1, 0, half)
    c = send_to(6, 1, first, near.at[0, first], to_right)
    swaps[3].wait_recv()
    add(3, half, rows)
    d = send_to(7, 3, second, near.at[1, second], to_left)
    between[0]()
    a.wait_recv()
    add(3, 0, half, 0)
    e = send_to(8, 3, first, near.at[1, first], to_left)
    b.wait_recv()
    add(1, half, rows, 1)
    g = send_to(9, 1, second, near.at[0, second], to_right)
    between[1]()
    swaps[0].wait_recv()
    own = place.block(0)
    c.wait_recv()
    d.wait_recv()
    e.wait_recv()
    g.wait_recv()

    def last(i, _):
        part = pl.ds(pl.multiple_of(i * step, step), step)
        emit(
            part,
            (x[own, part].astype(f32) + pair[0, part].astype(f32))
            + (near[0, part].astype(f32) + near[1, part].astype(f32)),
        )
        return 0

    lax.fori_loop(0, rows // step, last, 0)
    for copy in list(swaps.values()) + [a, b, c, d, e, g]:
        copy.wait_send()


def scatter_scratch(rows, width):
    return [
        pltpu.VMEM((4, rows, width), bf16),
        pltpu.VMEM((3, rows, width), bf16),
        pltpu.VMEM((2, rows, width), bf16),
        pltpu.VMEM((2, rows // 2, width), bf16),
        DMA((10,)),
        DMA((10,)),
    ]


def gather_scratch():
    return [DMA((RingGather.SEMS + 1,)), DMA((RingGather.SEMS,))]


def scatter_sum(x, base, shards, cid):
    _, rows, width = x.shape

    def body(x_ref, base_ref, out_ref, pair, out, near, far, send, recv):
        place = Place(shards)
        greet([place.right(), place.left(), place.partner()])

        def emit(part, total):
            out_ref[part] = (base_ref[part] + total).astype(bf16)

        ring_scatter(place, x_ref, pair, out, near, far, send, recv, emit)

    return pallas(
        body, jax.ShapeDtypeStruct((rows, width), bf16), [VMEM, VMEM], VMEM,
        scatter_scratch(rows, width), cid, 25,
    )(x, base)


def middle_step(x, tokens, gain, carry, shards, cid):
    _, rows, width = x.shape
    carries = [] if carry is None else [carry]

    def body(x_ref, tok_ref, gain_ref, *refs):
        refs = list(refs)
        carry_ref = refs.pop(0) if carries else None
        mid_ref, all_ref = refs.pop(0), refs.pop(0)
        carry_out = refs.pop(0) if carries else None
        held, pair, out, near, far, send, recv, gsend, grecv, ysend, yrecv = refs
        place = Place(shards)
        greet(
            [place.right(), place.left(), place.partner()]
            + ([place.across()] if carries else [])
        )
        if carries:
            over = remote(carry_ref, carry_out, ysend, yrecv, place.across())
            over.start()

        def emit(part, total):
            middle = tok_ref[part].astype(f32) + total
            mid_ref[part] = middle
            held[part] = (middle * rms_scale(middle) * gain_ref[...]).astype(bf16)

        ring_scatter(place, x_ref, pair, out, near, far, send, recv, emit)
        RingGather(place, held, all_ref, gsend, grecv).run()
        if carries:
            over.wait()

    return pallas(
        body,
        [
            jax.ShapeDtypeStruct((rows, width), f32),
            jax.ShapeDtypeStruct((GROUP, rows, width), bf16),
        ]
        + [jax.ShapeDtypeStruct(c.shape, c.dtype) for c in carries],
        [VMEM, VMEM, VMEM] + [ANY] * len(carries),
        [VMEM, ANY] + [ANY] * len(carries),
        [pltpu.VMEM((rows, width), bf16)] + scatter_scratch(rows, width) + gather_scratch()
        + [DMA, DMA],
        cid,
        50,
    )(x, tokens, gain, *carries)


def middle_back(x, middle, cotangent, gain, grads, shards, cid):
    _, rows, width = x.shape
    carries = [] if grads is None else [grads]

    def body(x_ref, mid_ref, cot_ref, gain_ref, *refs):
        refs = list(refs)
        grads_ref = refs.pop(0) if carries else None
        dm_ref, part_ref, all_ref = refs.pop(0), refs.pop(0), refs.pop(0)
        grads_out = refs.pop(0) if carries else None
        held, pair, out, near, far, send, recv, gsend, grecv, ysend, yrecv = refs
        place = Place(shards)
        greet(
            [place.right(), place.left(), place.partner()]
            + ([place.across()] if carries else [])
        )
        if carries:
            z, y = lax.axis_index("zh"), lax.axis_index("y")
            over = [
                remote(
                    grads_ref.at[1 - z, st, 1 - y], grads_out.at[st], ysend.at[st],
                    yrecv.at[st], place.across(),
                )
                for st in range(grads.shape[1])
            ]
            for c in over:
                c.start()
        part_ref[...] = jnp.zeros_like(part_ref)

        def emit(part, total):
            middle = mid_ref[part]
            scale = rms_scale(middle)
            normed = middle * scale
            part_ref[...] += jnp.sum(total * normed, axis=0, keepdims=True)
            dm = cot_ref[part].astype(f32) + norm_back(total * gain_ref[...], normed, scale)
            dm_ref[part] = dm
            held[part] = dm.astype(bf16)

        ring_scatter(place, x_ref, pair, out, near, far, send, recv, emit)
        RingGather(place, held, all_ref, gsend, grecv).run()
        if carries:
            for c in over:
                c.wait()

    return pallas(
        body,
        [
            jax.ShapeDtypeStruct((rows, width), f32),
            jax.ShapeDtypeStruct((1, width), f32),
            jax.ShapeDtypeStruct((GROUP, rows, width), bf16),
        ]
        + [jax.ShapeDtypeStruct((c.shape[1],) + c.shape[3:], c.dtype) for c in carries],
        [VMEM, VMEM, VMEM, VMEM] + [ANY] * len(carries),
        [VMEM, VMEM, ANY] + [ANY] * len(carries),
        [pltpu.VMEM((rows, width), bf16)] + scatter_scratch(rows, width) + gather_scratch()
        + [DMA((2,)), DMA((2,))],
        cid,
        50,
    )(x, middle, cotangent, gain, *carries)


def tokens_back(x, tokens, dm, gain, shards, cid):
    _, rows, width = x.shape

    def body(
        x_ref, tok_ref, dm_ref, gain_ref, grad_ref, part_ref, pair, out, near, far, send, recv
    ):
        place = Place(shards)
        greet([place.right(), place.left(), place.partner()])
        part_ref[...] = jnp.zeros_like(part_ref)

        def emit(part, total):
            tok = tok_ref[part].astype(f32)
            scale = rms_scale(tok)
            normed = tok * scale
            part_ref[...] += jnp.sum(total * normed, axis=0, keepdims=True)
            grad_ref[part] = (
                dm_ref[part] + norm_back(total * gain_ref[...], normed, scale)
            ).astype(bf16)

        ring_scatter(place, x_ref, pair, out, near, far, send, recv, emit)

    return pallas(
        body,
        (
            jax.ShapeDtypeStruct((rows, width), bf16),
            jax.ShapeDtypeStruct((1, width), f32),
        ),
        [VMEM, VMEM, VMEM, VMEM],
        (VMEM, VMEM),
        scatter_scratch(rows, width),
        cid,
        25,
    )(x, tokens, dm, gain)


class Exchange:
    SEMS = GROUP

    def __init__(self, place, x, out, send, recv):
        self.local = pltpu.make_async_copy(x.at[place.tp], out.at[place.tp], send.at[0])
        self.copies = []
        for k in range(1, GROUP):
            peer = (place.tp + k) % GROUP
            self.copies.append(
                remote(x.at[peer], out.at[place.tp], send.at[k], recv.at[k], place.device(peer))
            )

    def start(self):
        for c in self.copies:
            c.start()
        self.local.start()

    def finish(self):
        for c in self.copies:
            c.wait_recv()
        for c in self.copies:
            c.wait_send()
        self.local.wait()


def group_peers(place):
    return [place.device((place.tp + k) % GROUP) for k in range(1, GROUP)]


def columns_of(dp, t, shards):
    ys, streams = lax.axis_size("y"), lax.axis_size("st")
    z, y = dp // ys, dp % ys
    return ((z * streams + t // shards) * ys + y) * shards + t % shards


def exchange_back(x, planes, shards, cid):
    _, wrows, both = x.shape
    hidden = both // 2
    brows = hidden // planes
    step = min(wrows, 32)

    def body(x_ref, gate_ref, up_ref, got, send, recv):
        place = Place(shards)
        greet(group_peers(place))
        run = Exchange(place, x_ref, got, send, recv)
        run.start()
        run.finish()
        for t in range(GROUP):
            for dp in range(planes):
                flat = columns_of(dp, t, shards)
                for m, out in enumerate((gate_ref, up_ref)):
                    for at in range(0, wrows, step):
                        part = pl.ds(at, step)
                        out[part, flat * brows : (flat + 1) * brows] = got[
                            t, part, m * hidden + dp * brows : m * hidden + (dp + 1) * brows
                        ].astype(f32)

    shape = jax.ShapeDtypeStruct((wrows, hidden * GROUP), f32)
    return pallas(
        body, (shape, shape), [VMEM], (VMEM, VMEM),
        [pltpu.VMEM(x.shape, bf16), DMA((GROUP,)), DMA((GROUP,))], cid, 25,
    )(x)


class PlaceGather:
    SEMS = 5

    def __init__(self, own, out, send, recv, halves):
        z, y = lax.axis_index("zh"), lax.axis_index("y")
        dp, across = z * 2 + y, (1 - z) * 2 + y
        to_z, to_y = {"zh": 1 - z}, {"y": 1 - y}

        def copy(index, src, slot, part, device):
            return remote(
                src.at[part], out.at[slot, part], send.at[index], recv.at[index], device
            )

        first, second = halves
        self.local = pltpu.make_async_copy(own, out.at[dp], send.at[send.shape[0] - 1])
        self.z = [copy(0, own, dp, first, to_z), copy(1, own, dp, second, to_z)]
        self.y = [
            remote(own, out.at[dp], send.at[2], recv.at[2], to_y),
            copy(3, out.at[across], across, first, to_y),
            copy(4, out.at[across], across, second, to_y),
        ]

    def forward(self, half):
        self.z[half].wait_recv()
        self.y[1 + half].start()

    def finish(self):
        for c in self.y:
            c.wait_recv()
        for c in self.z + self.y:
            c.wait_send()


def front(tokens, cotangent, small, w_out, w_query, key_weight, value_weight, w_gate, w_up,
          w_down, planes, direct, shards, cid):
    rows, width = tokens.shape
    wrows = w_out.shape[0]
    srows, scols = small.shape
    brows = w_down.shape[0]
    hidden = brows * planes
    parts = [w_query.shape[1] // GROUP, key_weight.shape[1] // GROUP, value_weight.shape[1] // GROUP]
    qkv = sum(parts)
    slots = planes if direct else 1
    inputs = [tokens, cotangent, w_query, key_weight, value_weight, w_gate, w_up]
    if direct:
        inputs += [w_down, w_out]

    def body(*refs):
        refs = list(refs)

        def take(count):
            taken = refs[:count]
            del refs[:count]
            return taken

        small_ref, = take(1)
        sources = take(len(inputs))
        tok_all, cot_all, small_all, attn_all, ffn_all = take(5)
        down_all, wout_all = take(2) if direct else (None, None)
        held = take(len(inputs))
        (pack, isem, tsend, trecv, csend, crecv, ssend, srecv, psend, precv, fsend, frecv, asend,
         arecv, aasend, aarecv, dsend, drecv, wsend, wrecv) = refs
        place = Place(shards)
        tp, dp, flat = place.tp, place.dp(), place.flat()

        loads = [
            pltpu.make_async_copy(s, h, isem.at[i]) for i, (s, h) in enumerate(zip(sources, held))
        ]
        for i in (2, 3, 4, 0, 5, 6) + ((7, 8) if direct else ()) + (1,):
            loads[i].start()
        tok_ref, cot_ref, wq_ref, wk_ref, wv_ref, wg_ref, wu_ref = held[:7]

        barrier = pltpu.get_barrier_semaphore()

        def signal(device):
            pl.semaphore_signal(
                barrier, inc=1, device_id=device, device_id_type=pl.DeviceIdType.MESH
            )

        for device in group_peers(place):
            signal(device)
        for k in range(1, planes):
            signal(place.dp_device((dp + k) % planes))
        if direct:
            high, low = lax.axis_index("zh"), lax.axis_index("st")
            y, seq = lax.axis_index("y"), lax.axis_index("seq")
            to_seq = high * 2 + y
            from_high, from_y = seq // 2, seq % 2
            selfish = seq == to_seq
            mine = y == from_y
            for j in range(4):

                @pl.when(jnp.logical_and(mine, (from_high * 4 + j) != (high * 4 + seq)))
                def _():
                    signal({"zh": from_high, "seq": jnp.int32(j)})

            pl.semaphore_wait(
                barrier, GROUP - 1 + planes - 1 + 2 - selfish.astype(jnp.int32)
            )
        else:
            pl.semaphore_wait(barrier, GROUP - 1 + planes - 1)

        here = dp if direct else 0
        attn = []
        at = 0
        for i, (ref, cols) in enumerate(zip((wq_ref, wk_ref, wv_ref), parts)):
            loads[2 + i].wait()
            for k in range(GROUP):
                peer = (tp + k) % GROUP
                column = place.head(peer) * cols
                src = ref.at[:, pl.ds(pl.multiple_of(column, cols), cols)]
                dst = attn_all.at[here, tp, :, pl.ds(at, cols)]
                sem = i * GROUP + k
                if k == 0:
                    attn.append(pltpu.make_async_copy(src, dst, asend.at[sem]))
                else:
                    attn.append(
                        remote(src, dst, asend.at[sem], arecv.at[sem], place.device(peer))
                    )
                attn[-1].start()
            at += cols

        small_own = pltpu.make_async_copy(small_ref, small_all.at[tp, dp], ssend.at[0])
        small_own.start()
        small_dp = []
        for k in range(1, planes):
            small_dp.append(
                remote(
                    small_ref, small_all.at[tp, dp], ssend.at[k], srecv.at[k],
                    place.dp_device((dp + k) % planes),
                )
            )
            small_dp[-1].start()

        if direct:
            down_ref, wout_ref = held[7:]
            loads[7].wait()
            half = brows // 2
            down_dp = PlaceGather(
                down_ref, down_all, dsend, drecv, (pl.ds(0, half), pl.ds(half, half))
            )
            down_dp.z[0].start()
        loads[0].wait()
        tok = RingGather(place, tok_ref, tok_all, tsend, trecv, direct)
        tok.start()

        loads[5].wait()
        loads[6].wait()
        for t in range(GROUP):
            for d in range(planes):
                column = columns_of(d, t, shards)
                for m, ref in enumerate((wg_ref, wu_ref)):
                    lane = m * hidden + d * brows
                    pack[t, :, lane : lane + brows] = ref[:, column * brows : (column + 1) * brows]
        ffn = Exchange(place, pack, ffn_all, fsend, frecv)
        ffn.start()

        if direct:
            down_dp.y[0].start()
            down_dp.local.start()
            loads[8].wait()
            wout_copies = [
                remote(
                    wout_ref, wout_all.at[seq], wsend.at[k], wrecv.at[seq],
                    {"zh": z, "seq": to_seq},
                )
                for k, z in enumerate((high, 1 - high))
            ]
            wout_own = pltpu.make_async_copy(wout_ref, wout_all.at[seq], wsend.at[0])
            wout_over = remote(
                wout_all, wout_all, wsend.at[2], wrecv.at[4], place.across()
            )

            @pl.when(selfish)
            def _():
                wout_own.start()

            @pl.when(jnp.logical_not(selfish))
            def _():
                wout_copies[0].start()

            wout_copies[1].start()

        for i in range(3 * GROUP):
            if i % GROUP == 0:
                attn[i].wait()
            else:
                attn[i].wait_recv()
        if direct:
            half = GROUP // 2
            attn_dp = PlaceGather(
                attn_all.at[dp], attn_all, aasend, aarecv, (pl.ds(0, half), pl.ds(half, half))
            )
            attn_dp.z[0].start()
            attn_dp.y[0].start()
            attn_dp.z[1].start()
            down_dp.z[1].start()

        small_own.wait()
        for c in small_dp:
            c.wait_recv()
        small_tp = []
        for k in range(1, GROUP):
            small_tp.append(
                remote(
                    small_all.at[tp], small_all.at[tp], psend.at[k], precv.at[k],
                    place.device((tp + k) % GROUP),
                )
            )
            small_tp[-1].start()

        loads[1].wait()
        cot = RingGather(place, cot_ref, cot_all, csend, crecv, direct)
        tok.pass_on()
        cot.start()
        tok.step_across()
        if direct:
            down_dp.forward(0)

            @pl.when(mine)
            def _():
                for j in range(4):

                    @pl.when((from_high * 4 + j) != (high * 4 + seq))
                    def _():
                        remote(
                            wout_ref, wout_all.at[j], wsend.at[0], wrecv.at[j], place.across()
                        ).wait_recv()

                @pl.when(selfish)
                def _():
                    wout_own.wait()

                wout_over.start()

            attn_dp.forward(0)
        tok.step_far()
        cot.pass_on()
        if direct:
            attn_dp.forward(1)
        cot.step_across()
        if direct:
            down_dp.forward(1)
        cot.step_far()
        tok.finish()
        cot.finish()
        ffn.finish()
        for i in range(3 * GROUP):
            if i % GROUP:
                attn[i].wait_send()
        for c in small_tp:
            c.wait_recv()
        for c in small_dp + small_tp:
            c.wait_send()
        if direct:
            attn_dp.finish()
            down_dp.finish()
            down_dp.local.wait()

            @pl.when(jnp.logical_not(selfish))
            def _():
                wout_copies[0].wait_send()

            wout_copies[1].wait_send()

            @pl.when(mine)
            def _():
                wout_over.wait_send()

            @pl.when(jnp.logical_not(mine))
            def _():
                wout_over.wait_recv()

    shapes = [
        jax.ShapeDtypeStruct((GROUP, rows, width), bf16),
        jax.ShapeDtypeStruct((GROUP, rows, width), bf16),
        jax.ShapeDtypeStruct((GROUP, planes, srows, scols), bf16),
        jax.ShapeDtypeStruct((slots, GROUP, wrows, qkv), bf16),
        jax.ShapeDtypeStruct((GROUP, wrows, 2 * hidden), bf16),
    ]
    if direct:
        shapes += [
            jax.ShapeDtypeStruct((planes, brows, width), bf16),
            jax.ShapeDtypeStruct((planes, wrows, width), bf16),
        ]
    return pallas(
        body,
        shapes,
        [VMEM] + [ANY] * len(inputs),
        [ANY, ANY, VMEM] + [ANY] * (len(shapes) - 3),
        [pltpu.VMEM(x.shape, x.dtype) for x in inputs]
        + [pltpu.VMEM((GROUP, wrows, 2 * hidden), bf16), DMA((len(inputs),))]
        + gather_scratch() + gather_scratch()
        + [
            DMA((planes,)), DMA((planes,)), DMA((GROUP,)), DMA((GROUP,)),
            DMA((GROUP,)), DMA((GROUP,)), DMA((3 * GROUP,)), DMA((3 * GROUP,)),
            DMA((PlaceGather.SEMS,)), DMA((PlaceGather.SEMS,)),
            DMA((PlaceGather.SEMS + 1,)), DMA((PlaceGather.SEMS,)), DMA((3,)), DMA((5,)),
        ],
        cid,
        60,
    )(small, *inputs)


class Spread:
    def __init__(self, own, piece, relay, send, recv):
        z, low, y = (lax.axis_index(a) for a in ("zh", "st", "y"))
        to_z, to_y = {"zh": 1 - z}, {"y": 1 - y}
        beside, middle = {"st": 1 - low}, {"zh": 1 - z, "st": 1 - low}
        self.outer = z == low
        self.inner = z != low
        count = relay.shape[0]
        self.direct, self.toward, self.onward, self.y, self.on = [], [], [], [], []
        for h in range(count):
            at_y, at_on, at_more = count + h, 2 * count + h, 3 * count + h
            here, there = piece(z, h, y), piece(1 - z, h, y)
            self.direct.append(remote(own(h), here, send.at[h], recv.at[h], to_z))
            self.toward.append(
                remote(own(h), relay.at[h], send.at[h], recv.at[at_more], beside)
            )
            self.onward.append(
                remote(relay.at[h], here, send.at[at_more], recv.at[h], middle)
            )
            self.y.append(remote(own(h), here, send.at[at_y], recv.at[at_y], to_y))
            self.on.append(remote(there, there, send.at[at_on], recv.at[at_on], to_y))

    def start_z(self, first=0, last=None):
        @pl.when(self.outer)
        def _():
            for c in self.toward[first:last]:
                c.start()

        @pl.when(self.inner)
        def _():
            for c in self.direct[first:last]:
                c.start()

    def start_y(self):
        for c in self.y:
            c.start()

    def relay(self, half):
        @pl.when(self.inner)
        def _():
            self.toward[half].wait_recv()
            self.onward[half].start()

    def forward(self, half):
        self.direct[half].wait_recv()
        self.on[half].start()

    def finish(self):
        for c in self.y + self.on:
            c.wait_recv()
        for c in self.direct + self.y + self.on:
            c.wait_send()

        @pl.when(self.inner)
        def _():
            for c in self.onward:
                c.wait_send()


def rope_constants(length):
    exponent = np.arange(HEAD_SIZE // 2, dtype=np.float32) * np.float32(2.0 / HEAD_SIZE)
    inverse = np.power(np.float32(ROPE_BASE), -exponent).astype(np.float32)
    angles = np.arange(length, dtype=np.float32)[:, None] * inverse[None, :]
    cosine, sine = np.cos(angles.astype(np.float64)), np.sin(angles.astype(np.float64))
    return (
        jnp.asarray(np.concatenate([cosine, cosine], axis=1).astype(np.float32)),
        jnp.asarray(np.concatenate([-sine, sine], axis=1).astype(np.float32)),
    )


def document_mask(row, docs, low, count, keys):
    at_row = low + lax.broadcasted_iota(jnp.int32, (count, 1), 0)
    at_col = lax.broadcasted_iota(jnp.int32, (1, keys), 1)
    seg_row = jnp.zeros((count, 1), jnp.int32)
    seg_col = jnp.zeros((1, keys), jnp.int32)
    for d in range(docs):
        start = (row[:, d : d + 1] * 128.0 + row[:, docs + d : docs + d + 1]).astype(jnp.int32)
        seg_row = seg_row + jnp.where(at_row >= start, 1, 0)
        seg_col = seg_col + jnp.where(at_col >= start, 1, 0)
    return jnp.logical_and(at_row >= at_col, seg_row == seg_col)


def forward_pass(tokens, cotangent, small, w_out, w_query, key_weight, value_weight, w_gate,
                 w_up, w_down, docs, shards, cid):
    rows, width = tokens.shape
    wrows = w_out.shape[0]
    brows = w_down.shape[0]
    planes = 4
    hidden = brows * planes
    parts = [w_query.shape[1] // GROUP, key_weight.shape[1] // GROUP, value_weight.shape[1] // GROUP]
    qkv = sum(parts)
    qcols = parts[0]
    heads = qcols // HEAD_SIZE
    group_rows = rows * GROUP
    length = rows * shards
    streams = GROUP // shards
    gain_rows = width // 128
    grows = -(-(2 * gain_rows + 3) // 16) * 16
    srows = wrows + grows
    gcols = HEAD_SIZE // (planes * GROUP)
    cosine, sine = rope_constants(length)
    inputs = [tokens, cotangent, w_query, key_weight, value_weight, w_gate, w_up, w_down, w_out]
    score_scale = HEAD_SIZE ** (-0.5)

    def body(
        raw_ref, cos_ref, sin_ref, s0, s1, s2, s3, s4, s5, s6, s7, s8,
        cot_all, ffn_all, down_all, h1_out, h2_all, small_all, gains_ref, attn_all, wout_all,
        qkv_ref, low_ref, gate_ref, mixed_ref, gated_ref, mid_ref, hg, starts_ref,
        h0, h1, h2, h3, h4, h5, h6, h7, h8, small_ref, pack, attn_relay, ffn_relay, down_relay, tok_all, hid, partial, held_two, isem, osem,
        tsend, trecv, csend, crecv, gsend, grecv, ssend, srecv, psend, precv, fsend, frecv, asend,
        arecv, aasend, aarecv, ffsend, ffrecv, dsend, drecv, wsend, wrecv, pair, out, near, far,
        rsend, rrecv,
    ):
        sources = [s0, s1, s2, s3, s4, s5, s6, s7, s8]
        held = [h0, h1, h2, h3, h4, h5, h6, h7, h8]
        place = Place(shards)
        tp, dp = place.tp, place.dp()
        high, low = lax.axis_index("zh"), lax.axis_index("st")
        y, seq = lax.axis_index("y"), lax.axis_index("seq")
        loads = [
            pltpu.make_async_copy(s, h, isem.at[i]) for i, (s, h) in enumerate(zip(sources, held))
        ]
        for i in (2, 3, 4, 8, 0, 5, 6, 7, 1):
            loads[i].start()
        tok_ref, cot_ref, wq_ref, wk_ref, wv_ref, wg_ref, wu_ref, down_ref, wout_ref = held

        barrier = pltpu.get_barrier_semaphore()

        def signal(device):
            pl.semaphore_signal(
                barrier, inc=1, device_id=device, device_id_type=pl.DeviceIdType.MESH
            )

        for device in group_peers(place):
            signal(device)
        for k in range(1, planes):
            signal(place.dp_device((dp + k) % planes))
        to_seq = high * 2 + y
        from_high, from_y = seq // 2, seq % 2
        selfish = seq == to_seq
        mine = y == from_y
        for j in range(4):

            @pl.when(jnp.logical_and(mine, (from_high * 4 + j) != (high * 4 + seq)))
            def _():
                signal({"zh": from_high, "seq": jnp.int32(j)})

        inner = high != low

        @pl.when(inner)
        def _():
            signal({"zh": 1 - high, "st": 1 - low})

        pl.semaphore_wait(
            barrier,
            GROUP - 1 + planes - 1 + 2 - selfish.astype(jnp.int32) + inner.astype(jnp.int32),
        )

        attn = []
        at = 0
        for i, (ref, cols) in enumerate(zip((wq_ref, wk_ref, wv_ref), parts)):
            loads[2 + i].wait()
            for k in range(GROUP):
                peer = (tp + k) % GROUP
                column = place.head(peer) * cols
                src = ref.at[:, pl.ds(pl.multiple_of(column, cols), cols)]
                dst = attn_all.at[high, low, y, pl.ds(seq * wrows, wrows), pl.ds(at, cols)]
                sem = i * GROUP + k
                if k == 0:
                    attn.append(pltpu.make_async_copy(src, dst, asend.at[sem]))
                else:
                    attn.append(
                        remote(src, dst, asend.at[sem], arecv.at[sem], place.device(peer))
                    )
                attn[-1].start()
            at += cols

        small_ref[0:wrows] = raw_ref[0:wrows]
        flat = place.flat()
        block = raw_ref[wrows : wrows + 16].astype(f32)
        row_of = lax.broadcasted_iota(jnp.int32, (grows, 128), 0)
        placed = jnp.zeros((grows, 128), f32)
        per_row = 128 // wrows
        for i, (at, shift) in enumerate(
            (
                (flat // per_row, flat % per_row * wrows),
                (gain_rows + flat // per_row, flat % per_row * wrows),
                (2 * gain_rows, flat * gcols),
                (2 * gain_rows + 1, flat * gcols),
                (2 * gain_rows + 2, 0),
            )
        ):
            row = jnp.broadcast_to(block[i : i + 1], (grows, 128))
            placed = jnp.where(row_of == at, pltpu.roll(row, shift, 1), placed)
        small_ref[wrows:] = placed.astype(bf16)
        small_own = pltpu.make_async_copy(small_ref, small_all.at[tp, dp], ssend.at[0])
        small_own.start()
        small_dp = []
        for k in range(1, planes):
            small_dp.append(
                remote(
                    small_ref, small_all.at[tp, dp], ssend.at[k], srecv.at[k],
                    place.dp_device((dp + k) % planes),
                )
            )
            small_dp[-1].start()

        loads[5].wait()
        loads[6].wait()
        def pack_rows(i, _):
            part = pl.ds(pl.multiple_of(i * 16, 16), 16)
            for t in range(GROUP):
                for d in range(planes):
                    column = columns_of(d, t, shards)
                    for m, ref in enumerate((wg_ref, wu_ref)):
                        lane = m * hidden + d * brows
                        pack[t, part, lane : lane + brows] = ref[
                            part, column * brows : (column + 1) * brows
                        ]
            return 0

        lax.fori_loop(0, wrows // 16, pack_rows, 0)

        def arrived(copies):
            for i, c in enumerate(copies):
                if i % GROUP == 0:
                    c.wait()
                else:
                    c.wait_recv()

        arrived(attn)

        def attn_piece(zp, half, yp):
            return attn_all.at[zp, half, yp]

        attn_dp = Spread(
            lambda half: attn_piece(high, half, y), attn_piece, attn_relay, aasend, aarecv
        )
        attn_dp.start_z()
        attn_dp.start_y()
        loads[0].wait()
        tok = RingGather(place, tok_ref, tok_all, tsend, trecv, True)
        tok.start()
        small_own.wait()
        for c in small_dp:
            c.wait_recv()
        small_tp = []
        for k in range(1, GROUP):
            small_tp.append(
                remote(
                    small_all.at[tp], small_all.at[tp], psend.at[k], precv.at[k],
                    place.device((tp + k) % GROUP),
                )
            )
            small_tp[-1].start()
        attn_dp.relay(0)
        attn_dp.relay(1)

        loads[7].wait()
        half_rows = brows // 2

        def down_piece(zp, half, yp):
            return down_all.at[zp * 2 + yp, pl.ds(half * half_rows, half_rows)]

        down_dp = Spread(
            lambda half: down_ref.at[pl.ds(half * half_rows, half_rows)], down_piece, down_relay,
            dsend, drecv,
        )
        down_own = pltpu.make_async_copy(down_ref, down_all.at[dp], dsend.at[8])
        down_own.start()
        down_dp.start_z()
        tok.pass_on()
        ffn_dst = ffn_all.at[high, low, y, pl.ds(seq * wrows, wrows)]
        ffn = [pltpu.make_async_copy(pack.at[tp], ffn_dst, fsend.at[0])]
        for k, (ahead, other) in enumerate(
            ((3, False), (3, True), (0, True), (1, False), (1, True), (2, False), (2, True))
        ):
            peer = place.block(ahead, other)
            ffn.append(
                remote(
                    pack.at[peer], ffn_dst, fsend.at[k + 1], frecv.at[k + 1], place.device(peer)
                )
            )
        for c in ffn[:4]:
            c.start()
        loads[8].wait()
        wout_copies = [
            remote(
                wout_ref, wout_all.at[seq], wsend.at[k], wrecv.at[seq], {"zh": z, "seq": to_seq}
            )
            for k, z in enumerate((high, 1 - high))
        ]
        wout_own = pltpu.make_async_copy(wout_ref, wout_all.at[seq], wsend.at[0])
        wout_over = remote(wout_all, wout_all, wsend.at[2], wrecv.at[4], place.across())
        wout_copies[1].start()

        @pl.when(selfish)
        def _():
            wout_own.start()

        @pl.when(jnp.logical_not(selfish))
        def _():
            wout_copies[0].start()

        attn_dp.forward(0)
        attn_dp.forward(1)
        down_dp.start_y()
        tok.step_across()
        down_dp.relay(0)
        tok.step_far()
        for c in ffn[4:]:
            c.start()

        @pl.when(mine)
        def _():
            for j in range(4):

                @pl.when((from_high * 4 + j) != (high * 4 + seq))
                def _():
                    remote(
                        wout_ref, wout_all.at[j], wsend.at[0], wrecv.at[j], place.across()
                    ).wait_recv()

            @pl.when(selfish)
            def _():
                wout_own.wait()

            wout_over.start()

        for c in small_tp:
            c.wait_recv()
        gains = jnp.zeros((grows, 128), f32)
        for t in range(GROUP):
            for d in range(planes):
                gains = gains + small_all[t, d, pl.ds(wrows, grows)].astype(f32)
                flat = columns_of(d, t, shards)
                hg[flat * wrows : (flat + 1) * wrows] = small_all[t, d, pl.ds(0, wrows)]
        gains_ref[...] = gains
        gain_one = jnp.concatenate([gains[i : i + 1] for i in range(gain_rows)], axis=1)
        gain_two = jnp.concatenate(
            [gains[gain_rows + i : gain_rows + i + 1] for i in range(gain_rows)], axis=1
        )
        query_gain = gains[2 * gain_rows : 2 * gain_rows + 1]
        key_gain = gains[2 * gain_rows + 1 : 2 * gain_rows + 2]
        starts = []
        for st in range(streams):
            block = small_all[st * shards, dp, pl.ds(wrows, grows)].astype(f32)
            starts.append(block[2 * gain_rows + 2 : 2 * gain_rows + 3])
            starts_ref[st : st + 1] = starts[st]

        tok.finish()
        step = 32

        def norm(i, _):
            block = i // (rows // step)
            inner = pl.ds(pl.multiple_of(i % (rows // step) * step, step), step)
            value = tok_all[block, inner].astype(f32)
            hid[block, inner] = (value * rms_scale(value) * gain_one).astype(bf16)
            return 0

        lax.fori_loop(0, group_rows // step, norm, 0)
        save = pltpu.make_async_copy(hid, h1_out, osem)
        save.start()
        down_dp.relay(1)
        attn_dp.finish()
        weight = attn_all[...].reshape(width, qkv)
        head = place.head(tp)
        lanes = lax.broadcasted_iota(jnp.int32, (1, 128), 1)

        def rotary(x, gain, s):
            scaled = x * rms_scale(x) * gain
            return (
                scaled * cos_ref[...] + pltpu.roll(scaled, HEAD_SIZE // 2, 1) * sin_ref[...]
            ).astype(bf16)

        def project(s, _):
            part = pl.ds(pl.multiple_of(s * length, length), length)
            normed = hid[pl.ds(s * shards, shards)].reshape(length, width)
            raw = jnp.dot(normed, weight, preferred_element_type=f32)
            qkv_ref[part] = raw
            logit = jnp.dot(normed, hg[...], preferred_element_type=f32)
            for g in range(heads):
                at = g * HEAD_SIZE
                low_ref[part, at : at + HEAD_SIZE] = rotary(
                    raw[:, at : at + HEAD_SIZE], query_gain, s
                )
                own = jnp.sum(
                    jnp.where(lanes == head * heads + g, logit, 0.0), axis=1, keepdims=True
                )
                gate_ref[part, at : at + HEAD_SIZE] = jnp.broadcast_to(
                    jax.nn.sigmoid(own), (length, HEAD_SIZE)
                )
            low_ref[part, qcols : qcols + HEAD_SIZE] = rotary(
                raw[:, qcols : qcols + HEAD_SIZE], key_gain, s
            )
            low_ref[part, qcols + HEAD_SIZE :] = raw[:, qcols + HEAD_SIZE :].astype(bf16)
            return 0

        lax.fori_loop(0, streams, project, 0)
        arrived(ffn)

        quarter = shards * wrows // 2

        def ffn_piece(zp, half, yp):
            return ffn_all.at[zp, half // 2, yp, pl.ds(half % 2 * quarter, quarter)]

        ffn_dp = Spread(
            lambda half: ffn_piece(high, half, y), ffn_piece, ffn_relay, ffsend, ffrecv
        )
        ffn_dp.start_z(0, 2)
        ffn_dp.start_y()
        block = 128
        def attend(s, _):
            base = pl.multiple_of(s * length, length)
            row = starts_ref[pl.ds(s, 1)]
            for r in range(0, length, block):
                keys = r + block
                allowed = document_mask(row, docs, r, block, keys)
                key = low_ref[pl.ds(base, keys), qcols : qcols + HEAD_SIZE]
                value = low_ref[pl.ds(base, keys), qcols + HEAD_SIZE :]
                part = pl.ds(base + r, block)
                for g in range(heads):
                    at = g * HEAD_SIZE
                    scores = (
                        lax.dot_general(
                            low_ref[part, at : at + HEAD_SIZE], key, (((1,), (1,)), ((), ())),
                            preferred_element_type=f32,
                        )
                        * score_scale
                    )
                    scores = jnp.where(allowed, scores, MASK_FILL)
                    weights = jnp.exp(scores - jnp.max(scores, axis=1, keepdims=True))
                    probs = weights / jnp.sum(weights, axis=1, keepdims=True)
                    mixed = jnp.dot(
                        probs.astype(bf16), value, preferred_element_type=f32
                    ).astype(bf16)
                    mixed_ref[part, at : at + HEAD_SIZE] = mixed
                    gated_ref[part, at : at + HEAD_SIZE] = (
                        mixed.astype(f32) * gate_ref[part, at : at + HEAD_SIZE]
                    ).astype(bf16)
            return 0

        lax.fori_loop(0, streams, attend, 0)

        @pl.when(jnp.logical_not(mine))
        def _():
            wout_over.wait_recv()

        wide = 512
        def give(i, _):
            s = i // (width // wide)
            cols = pl.ds(pl.multiple_of(i % (width // wide) * wide, wide), wide)
            product = jnp.dot(
                gated_ref[pl.ds(pl.multiple_of(s * length, length), length)],
                wout_all[:, :, cols].reshape(qcols, wide),
                preferred_element_type=f32,
            )
            partial[pl.ds(s * shards, shards), :, cols] = product.astype(bf16).reshape(
                shards, rows, wide
            )
            return 0

        lax.fori_loop(0, streams * (width // wide), give, 0)

        def emit(part, total):
            middle = tok_ref[part].astype(f32) + total
            mid_ref[part] = middle
            held_two[part] = (middle * rms_scale(middle) * gain_two).astype(bf16)

        def first():
            ffn_dp.relay(0)
            down_dp.forward(0)

        def second():
            ffn_dp.relay(1)
            ffn_dp.start_z(2, 3)
            down_dp.forward(1)
            ffn_dp.forward(0)

        ring_scatter(
            place, partial, pair, out, near, far, rsend, rrecv, emit, (first, second)
        )
        two = RingGather(place, held_two, h2_all, gsend, grecv, True)
        two.start()
        ffn_dp.forward(1)
        ffn_dp.relay(2)
        two.pass_on()
        ffn_dp.start_z(3, 4)
        loads[1].wait()
        cot = RingGather(place, cot_ref, cot_all, csend, crecv, True)
        cot.start()
        ffn_dp.relay(3)
        two.step_across()
        ffn_dp.forward(2)
        two.step_far()
        cot.pass_on()
        ffn_dp.forward(3)
        cot.step_across()
        cot.step_far()
        two.finish()
        cot.finish()
        ffn_dp.finish()
        down_dp.finish()
        down_own.wait()
        save.wait()
        for i, c in enumerate(attn):
            if i % GROUP:
                c.wait_send()
        for c in ffn[1:] + small_dp + small_tp:
            c.wait_send()

        @pl.when(jnp.logical_not(selfish))
        def _():
            wout_copies[0].wait_send()

        wout_copies[1].wait_send()

        @pl.when(mine)
        def _():
            wout_over.wait_send()

    pieces = (2, streams, 2, shards * wrows)
    shape = jax.ShapeDtypeStruct
    return pallas(
        body,
        [
            shape((GROUP, rows, width), bf16),
            shape(pieces + (2 * hidden,), bf16),
            shape((planes, brows, width), bf16),
            shape((GROUP, rows, width), bf16),
            shape((GROUP, rows, width), bf16),
            shape((GROUP, planes, srows, 128), bf16),
            shape((grows, 128), f32),
            shape(pieces + (qkv,), bf16),
            shape((planes, wrows, width), bf16),
            shape((group_rows, qkv), f32),
            shape((group_rows, qkv), bf16),
            shape((group_rows, qcols), f32),
            shape((group_rows, qcols), bf16),
            shape((group_rows, qcols), bf16),
            shape((rows, width), f32),
            shape((width, 128), bf16),
            shape((streams, 128), f32),
        ],
        [VMEM] * 3 + [ANY] * len(inputs),
        [ANY] * 5 + [VMEM] * 12,
        [pltpu.VMEM(x.shape, x.dtype) for x in inputs]
        + [
            pltpu.VMEM((srows, 128), bf16),
            pltpu.VMEM((GROUP, wrows, 2 * hidden), bf16),
            pltpu.VMEM((2, shards * wrows, qkv), bf16),
            pltpu.VMEM((4, shards * wrows // 2, 2 * hidden), bf16),
            pltpu.VMEM((2, brows // 2, width), bf16),
            pltpu.VMEM((GROUP, rows, width), bf16),
            pltpu.VMEM((GROUP, rows, width), bf16),
            pltpu.VMEM((GROUP, rows, width), bf16),
            pltpu.VMEM((rows, width), bf16),
            DMA((len(inputs),)),
            DMA,
        ]
        + gather_scratch() + gather_scratch() + gather_scratch()
        + [
            DMA((planes,)), DMA((planes,)), DMA((GROUP,)), DMA((GROUP,)),
            DMA((GROUP,)), DMA((GROUP,)), DMA((3 * GROUP,)), DMA((3 * GROUP,)),
            DMA((8,)), DMA((8,)), DMA((16,)), DMA((16,)),
            DMA((9,)), DMA((8,)), DMA((3,)), DMA((5,)),
        ]
        + scatter_scratch(rows, width),
        cid,
        100,
        56,
    )(small, cosine, sine, *inputs)


class PlaceSums:
    SENDS, RECVS = 8, 6

    def __init__(self, piece, got, far, near, relay, send, recv):
        z, low, y = (lax.axis_index(a) for a in ("zh", "st", "y"))
        to_z, to_y = {"zh": 1 - z}, {"y": 1 - y}
        beside, middle = {"st": 1 - low}, {"zh": 1 - z, "st": 1 - low}
        self.outer, self.inner = z == low, z != low
        self.got, self.far, self.near = got, far, near
        self.y_far = remote(piece(1 - z, 1 - y), got.at[0], send.at[0], recv.at[0], to_y)
        self.y_near = remote(piece(z, 1 - y), got.at[1], send.at[1], recv.at[1], to_y)
        self.loads = [
            pltpu.make_async_copy(piece(1 - z, y), far, send.at[2]),
            pltpu.make_async_copy(piece(z, y), near, send.at[3]),
        ]

        def half(ref, h):
            if len(far.shape) == 3:
                return ref.at[h]
            count = far.shape[0] // 2
            return ref.at[pl.ds(h * count, count)]

        self.direct, self.toward, self.onward = [], [], []
        for h in range(2):
            dst = half(got.at[2], h)
            self.direct.append(
                remote(half(far, h), dst, send.at[4 + h], recv.at[2 + h], to_z)
            )
            self.toward.append(
                remote(half(far, h), half(relay, h), send.at[4 + h], recv.at[4 + h], beside)
            )
            self.onward.append(
                remote(half(relay, h), dst, send.at[6 + h], recv.at[2 + h], middle)
            )

    def load(self):
        for c in self.loads:
            c.start()

    def over_z(self, late=False):
        self.loads[0].wait()
        self.y_far.wait_recv()
        self.each(lambda at: self.put(at))
        Spread.start_z(self, 0, 1 if late else 2)

    def start_late(self):
        Spread.start_z(self, 1, 2)

    def relay(self, half):
        @pl.when(self.inner)
        def _():
            self.toward[half].wait_recv()
            self.onward[half].start()

    def put(self, at):
        self.far[at] = (self.far[at].astype(f32) + self.got[(0,) + at].astype(f32)).astype(bf16)

    def each(self, visit):
        lead, rows = self.far.shape[:-2], self.far.shape[-2]

        def inner(i, _):
            part = pl.ds(pl.multiple_of(i * 32, 32), 32)
            if lead:
                for k in range(lead[0]):
                    visit((k, part))
            else:
                visit((part,))
            return 0

        lax.fori_loop(0, rows // 32, inner, 0)

    def total(self, at):
        return (self.near[at].astype(f32) + self.got[(1,) + at].astype(f32)) + self.got[
            (2,) + at
        ].astype(f32)

    def arrive(self):
        self.loads[1].wait()
        self.y_near.wait_recv()
        for c in self.direct:
            c.wait_recv()

    def drain(self):
        for c in [self.y_far, self.y_near] + self.direct:
            c.wait_send()

        @pl.when(self.inner)
        def _():
            for c in self.onward:
                c.wait_send()


def backward_pass(x, act, down_w, middle, tokens, cotangent, gains, headgate, qkv_w, out_w, hidden_one,
                  qkv, low, gate, mixed, gated, starts, down_grad, ffn_grad, docs, shards, cid):
    _, rows, width = x.shape
    planes = 4
    streams = GROUP // shards
    length = rows * shards
    group_rows = rows * GROUP
    qcols = gate.shape[1]
    qkv_cols = qkv.shape[1]
    kcols = (qkv_cols - qcols) // 2
    heads = qcols // HEAD_SIZE
    brows = down_grad.shape[2]
    both = ffn_grad.shape[4]
    hidden = both // 2
    wrows = width // (planes * GROUP)
    gain_rows = width // 128
    score_scale = HEAD_SIZE ** (-0.5)
    cosine, sine = rope_constants(length)
    srows = 24
    inputs = [
        x, middle, tokens, cotangent, headgate, qkv_w, out_w, qkv, low, gate, mixed, gated,
    ]

    def body(
        gains_ref, starts_ref, cos_ref, sin_ref, act_in, dw_in, h1_ref, down_ref, ffn_ref,
        i0, i1, i2, i3, i4, i5, i6, i7, i8, i9, i10, i11,
        t0, t1, t2, t3, t4, t5, t6, t7, t8, s_out, final_ref,
        layer_ref, tgrad_ref, gate_out, up_out, query_out, key_out, value_out, o_out, down_out,
        fsem, dw_ref, product_ref, act_sem, dw_sem, product_sem, partial, mid_ref, tok_ref, cot_ref, hg_ref, wq_ref, wout_ref, qkv_ref, low_ref, gate_ref,
        mixed_ref, gated_ref,
        held, db_all, dmid, gq, dgl, dk_acc, dv_acc, dmix, small, stage, s_got, s_held, s_line,
        g_got, g_far, g_near, g_in, d_got, d_far, d_near, q_own, q_got, q_far, q_near, q_in,
        o_own, o_got, o_far, o_near, o_in, g_relay, d_relay, q_relay, o_relay,
        pair, out, near, far, rsend, rrecv, r2send, r2recv, r3send, r3recv, csend, crecv,
        isem, gsend, grecv, dsend, drecv, qsend, qrecv, osend, orecv, gxsend, gxrecv, qxsend,
        qxrecv, oxsend, oxrecv, asend, arecv, bsend, brecv, lsem, turn,
    ):
        sources = [i0, i1, i2, i3, i4, i5, i6, i7, i8, i9, i10, i11]
        targets = [
            partial, mid_ref, tok_ref, cot_ref, hg_ref, wq_ref, wout_ref, qkv_ref, low_ref,
            gate_ref, mixed_ref, gated_ref,
        ]
        finals = [
            pltpu.make_async_copy(ready, target, fsem.at[i])
            for i, (ready, target) in enumerate(
                (
                    (layer_ref, t0), (tgrad_ref, t1), (gate_out, t2), (up_out, t3),
                    (query_out, t4), (key_out, t5), (value_out, t6), (o_out, t7), (down_out, t8),
                )
            )
        ]
        place = Place(shards)
        tp, dp, flat = place.tp, place.dp(), place.flat()
        high, y, seq = lax.axis_index("zh"), lax.axis_index("y"), lax.axis_index("seq")
        loads = [
            pltpu.make_async_copy(s, t, isem.at[i])
            for i, (s, t) in enumerate(zip(sources, targets))
        ]
        for c in loads[:4]:
            c.start()
        load_act = [
            pltpu.make_async_copy(act_in.at[:, pl.ds(0, qkv_cols)], gq, act_sem.at[0]),
            pltpu.make_async_copy(act_in.at[:, pl.ds(qkv_cols, qcols)], dmix, act_sem.at[1]),
        ]
        for c in load_act:
            c.start()
        barrier = pltpu.get_barrier_semaphore()

        def signal(device, semaphore=barrier):
            pl.semaphore_signal(
                semaphore, inc=1, device_id=device, device_id_type=pl.DeviceIdType.MESH
            )

        for device in group_peers(place):
            signal(device)
        for k in range(1, planes):
            signal(place.dp_device((dp + k) % planes))
        owner = place.head(tp) * planes + dp
        source = {"st": lax.axis_index("st"), "seq": high * 2 + y}
        source.update(place.dp_device(seq))

        @pl.when(owner != flat)
        def _():
            signal(source)

        inner = high != lax.axis_index("st")

        @pl.when(inner)
        def _():
            signal({"zh": 1 - high, "st": 1 - lax.axis_index("st")})

        pl.semaphore_wait(
            barrier,
            GROUP + planes - 2 + (owner != flat).astype(jnp.int32) + inner.astype(jnp.int32),
        )

        ffn = PlaceSums(
            lambda zp, yp: ffn_ref.at[zp, :, yp], g_got, g_far, g_near, g_relay, gsend, grecv
        )
        down = PlaceSums(lambda zp, yp: down_ref.at[zp, yp], d_got, d_far, d_near, d_relay, dsend, drecv)
        down.y_far.start()
        ffn.y_far.start()
        ffn.y_near.start()
        down.load()
        ffn.load()
        for c in loads[4:]:
            c.start()

        small[...] = jnp.zeros_like(small)
        gain_all = gains_ref[...]
        gain_one = jnp.concatenate([gain_all[i : i + 1] for i in range(gain_rows)], axis=1)
        gain_two = jnp.concatenate(
            [gain_all[gain_rows + i : gain_rows + i + 1] for i in range(gain_rows)], axis=1
        )
        query_gain = gain_all[2 * gain_rows : 2 * gain_rows + 1]
        key_gain = gain_all[2 * gain_rows + 1 : 2 * gain_rows + 2]
        for c in loads[:4]:
            c.wait()

        def emit_dm(part, total):
            value = mid_ref[part]
            scale = rms_scale(value)
            normed = value * scale
            small[17:18] += jnp.sum(total * normed, axis=0, keepdims=True)
            dm = cot_ref[part].astype(f32) + norm_back(total * gain_two, normed, scale)
            dmid[part] = dm
            held[part] = dm.astype(bf16)

        ring_scatter(place, partial, pair, out, near, far, rsend, rrecv, emit_dm)
        grad = RingGather(place, held, db_all, csend, crecv)
        grad.start()
        h1_all = partial
        load_h1 = pltpu.make_async_copy(h1_ref, h1_all, lsem.at[0])
        load_h1.start()

        for c in load_act:
            c.wait()
        fine = dw_ref.shape[2]
        blocks = width // fine

        def columns(i):
            return pl.ds(pl.multiple_of(i * fine, fine), fine)

        def weight_load(i):
            return pltpu.make_async_copy(
                dw_in.at[:, columns(i)], dw_ref.at[i % 2], dw_sem.at[i % 2]
            )

        def product_store(i):
            return pltpu.make_async_copy(
                product_ref.at[i % 2], final_ref.at[:, :, columns(i)], product_sem.at[i % 2]
            )

        weight_load(0).start()

        def down_product(i, _):
            @pl.when(i + 1 < blocks)
            def _():
                weight_load(i + 1).start()

            weight_load(i).wait()

            @pl.when(i >= 2)
            def _():
                product_store(i - 2).wait()

            product = jnp.dot(
                gq[...], dw_ref[i % 2, 0:qkv_cols], preferred_element_type=f32
            ) + jnp.dot(dmix[...], dw_ref[i % 2, qkv_cols:], preferred_element_type=f32)
            product_ref[i % 2] = product.astype(bf16).reshape(GROUP, rows, fine)
            product_store(i).start()
            return 0

        lax.fori_loop(0, blocks, down_product, 0)
        for i in (blocks - 2, blocks - 1):
            product_store(i).wait()
        down.over_z()
        grad.pass_on()
        down.relay(0)
        grad.step_across()
        down.relay(1)
        grad.step_far()
        for c in loads[4:]:
            c.wait()
        grad.finish()

        lanes = lax.broadcasted_iota(jnp.int32, (1, 128), 1)
        head = place.head(tp)
        def open_out(s, _):
            part = pl.ds(pl.multiple_of(s * length, length), length)
            db = db_all[pl.ds(s * shards, shards)].reshape(length, width)
            da = lax.dot_general(
                db, wout_ref[...], (((1,), (1,)), ((), ())), preferred_element_type=f32
            )
            logits = jnp.zeros((length, 128), f32)
            for g in range(heads):
                at = g * HEAD_SIZE
                piece = da[:, at : at + HEAD_SIZE]
                opened = gate_ref[part, at : at + HEAD_SIZE]
                dmix[part, at : at + HEAD_SIZE] = (piece * opened).astype(bf16)
                own = jnp.sum(
                    piece * mixed_ref[part, at : at + HEAD_SIZE].astype(f32), axis=1,
                    keepdims=True,
                )
                logits = jnp.where(
                    lanes == head * heads + g, own * opened * (1.0 - opened), logits
                )
            dgl[part] = logits.astype(bf16)
            return 0

        lax.fori_loop(0, streams, open_out, 0)
        wide = 512
        def out_grad(i, _):
            cols = pl.ds(pl.multiple_of(i * wide, wide), wide)
            product = lax.dot_general(
                gated_ref[...], db_all[:, :, cols].reshape(group_rows, wide),
                (((0,), (0,)), ((), ())), preferred_element_type=f32,
            ).astype(bf16)
            for j in range(planes):
                o_own[j // 2, j % 2, :, cols] = product[j * wrows : (j + 1) * wrows]
            return 0

        lax.fori_loop(0, width // wide, out_grad, 0)
        outs = PlaceSums(lambda zp, yp: o_own.at[zp, yp], o_got, o_far, o_near, o_relay, osend, orecv)
        outs.y_far.start()
        outs.load()
        ffn.over_z(True)

        block = 128

        def attend_back(s, carried):
            query_part, key_part = carried
            base = pl.multiple_of(s * length, length)
            row = starts_ref[pl.ds(s, 1)]
            dk_acc[...] = jnp.zeros_like(dk_acc)
            dv_acc[...] = jnp.zeros_like(dv_acc)

            def back(grad_rotated, raw, gain):
                grad_gained = grad_rotated * cos_ref[...] - pltpu.roll(
                    grad_rotated, HEAD_SIZE // 2, 1
                ) * sin_ref[...]
                scale = rms_scale(raw)
                normed = raw * scale
                return (
                    jnp.sum(grad_gained * normed, axis=0, keepdims=True),
                    norm_back(grad_gained * gain, normed, scale).astype(bf16),
                )

            for r in range(0, length, block):
                keys = r + block
                allowed = document_mask(row, docs, r, block, keys)
                key = low_ref[pl.ds(base, keys), qcols : qcols + HEAD_SIZE]
                value = low_ref[pl.ds(base, keys), qcols + HEAD_SIZE :]
                part = pl.ds(base + r, block)
                for g in range(heads):
                    at = g * HEAD_SIZE
                    query = low_ref[part, at : at + HEAD_SIZE]
                    scores = (
                        lax.dot_general(
                            query, key, (((1,), (1,)), ((), ())), preferred_element_type=f32
                        )
                        * score_scale
                    )
                    scores = jnp.where(allowed, scores, MASK_FILL)
                    weights = jnp.exp(scores - jnp.max(scores, axis=1, keepdims=True))
                    probs = weights / jnp.sum(weights, axis=1, keepdims=True)
                    dout = dmix[part, at : at + HEAD_SIZE]
                    dprobs = lax.dot_general(
                        dout, value, (((1,), (1,)), ((), ())), preferred_element_type=f32
                    )
                    delta = jnp.sum(probs * dprobs, axis=1, keepdims=True)
                    dscores = (probs * (dprobs - delta)).astype(bf16)
                    dq = jnp.dot(dscores, key, preferred_element_type=f32) * score_scale
                    gq[part, at : at + HEAD_SIZE] = dq.astype(bf16)
                    dk_acc[0:keys] += lax.dot_general(
                        dscores, query, (((0,), (0,)), ((), ())), preferred_element_type=f32
                    )
                    dv_acc[0:keys] += lax.dot_general(
                        probs.astype(bf16), dout, (((0,), (0,)), ((), ())),
                        preferred_element_type=f32,
                    )
            part = pl.ds(base, length)
            for g in range(heads):
                at = g * HEAD_SIZE
                sums, grads = back(
                    gq[part, at : at + HEAD_SIZE].astype(f32), qkv_ref[part, at : at + HEAD_SIZE],
                    query_gain,
                )
                query_part = query_part + sums
                gq[part, at : at + HEAD_SIZE] = grads
            sums, grads = back(
                (dk_acc[...] * score_scale).astype(bf16).astype(f32),
                qkv_ref[part, qcols : qcols + HEAD_SIZE], key_gain,
            )
            key_part = key_part + sums
            gq[part, qcols : qcols + HEAD_SIZE] = grads
            gq[part, qcols + HEAD_SIZE :] = dv_acc[...].astype(bf16)
            return query_part, key_part

        query_part, key_part = lax.fori_loop(
            0, streams, attend_back,
            (jnp.zeros((1, HEAD_SIZE), f32), jnp.zeros((1, HEAD_SIZE), f32)),
        )

        load_h1.wait()
        def qkv_grad(n, _):
            cols = pl.ds(pl.multiple_of(n * 256, 256), 256)
            product = lax.dot_general(
                h1_all[:, :, cols].reshape(group_rows, 256), gq[...], (((0,), (0,)), ((), ())),
                preferred_element_type=f32,
            )
            q_own[n // 4, n // 2 % 2, n % 2] = product.astype(bf16)
            return 0

        lax.fori_loop(0, width // 256, qkv_grad, 0, unroll=4)
        qkvs = PlaceSums(lambda zp, yp: q_own.at[zp, :, yp], q_got, q_far, q_near, q_relay, qsend, qrecv)
        qkvs.y_far.start()
        outs.y_near.start()
        qkvs.y_near.start()
        down.y_near.start()
        qkvs.load()
        def headgate_grad(i, _):
            cols = pl.ds(pl.multiple_of(i * wide, wide), wide)
            small[0:16, cols] = lax.dot_general(
                dgl[...], h1_all[:, :, cols].reshape(group_rows, wide),
                (((0,), (0,)), ((), ())), preferred_element_type=f32,
            )[0:16]
            return 0

        lax.fori_loop(0, width // wide, headgate_grad, 0)

        def dh1(i, _):
            s = i // (width // wide)
            at = pl.multiple_of(i % (width // wide) * wide, wide)
            part, cols = pl.ds(pl.multiple_of(s * length, length), length), pl.ds(at, wide)
            product = lax.dot_general(
                gq[part], wq_ref[cols], (((1,), (1,)), ((), ())), preferred_element_type=f32
            ) + lax.dot_general(
                dgl[part], hg_ref[cols], (((1,), (1,)), ((), ())), preferred_element_type=f32
            )
            partial[pl.ds(s * shards, shards), :, cols] = product.astype(bf16).reshape(
                shards, rows, wide
            )
            return 0

        lax.fori_loop(0, streams * (width // wide), dh1, 0, unroll=2)

        def emit_tokens(part, total):
            tok = tok_ref[part].astype(f32)
            scale = rms_scale(tok)
            normed = tok * scale
            small[16:17] += jnp.sum(total * normed, axis=0, keepdims=True)
            tgrad_ref[part] = (
                dmid[part] + norm_back(total * gain_one, normed, scale)
            ).astype(bf16)

        load_final = pltpu.make_async_copy(final_ref, db_all, lsem.at[1])
        load_final.start()
        ring_scatter(
            place, partial, pair, out, near, far, r2send, r2recv, emit_tokens,
            (lambda: ffn.relay(0), ffn.start_late),
        )
        finals[1].start()
        ring_peers = [place.right(), place.left(), place.partner()]
        for device in ring_peers:
            signal(device, turn)
        outs.over_z()
        qkvs.over_z()
        ffn.relay(1)

        small[18:19] = jnp.concatenate([query_part] * gain_rows, axis=1)
        small[19:20] = jnp.concatenate([key_part] * gain_rows, axis=1)
        for t in range(GROUP):
            for d in range(planes):
                lane = columns_of(d, t, shards) // 2 * 128
                stage[t, d * srows : (d + 1) * srows] = small[:, lane : lane + 128]
        sums = Exchange(place, stage, s_got, asend, arecv)
        sums.start()

        load_final.wait()
        pl.semaphore_wait(turn, len(ring_peers))

        def emit_layer(part, total):
            layer_ref[part] = (mid_ref[part] + total).astype(bf16)

        def first():
            outs.relay(0)
            outs.relay(1)

        def scatter_rows(total, ready, send, recv, into):
            def keep(at):
                ready[at] = total(at).astype(bf16)

            copies = []
            for k in range(GROUP):
                peer = (tp + k) % GROUP
                src = ready.at[peer // shards, pl.ds(peer % shards * wrows, wrows)]
                if k == 0:
                    copies.append(pltpu.make_async_copy(src, into.at[tp], send.at[0]))
                else:
                    copies.append(
                        remote(src, into.at[tp], send.at[k], recv.at[k], place.device(peer))
                    )
            return keep, copies

        keep_ffn, ffn_rows = scatter_rows(ffn.total, g_near, gxsend, gxrecv, g_in)

        def second():
            qkvs.relay(0)
            qkvs.relay(1)
            ffn.arrive()
            ffn.each(keep_ffn)
            for c in ffn_rows:
                c.start()

        ring_scatter(
            place, db_all, pair, out, near, far, r3send, r3recv, emit_layer, (first, second)
        )
        finals[0].start()
        sums.finish()
        s_held[...] = jnp.sum(s_got[...], axis=0).reshape(s_held.shape)
        line_own = pltpu.make_async_copy(s_held.at[dp], s_line.at[dp], bsend.at[0])
        line_own.start()
        lines = []
        for k in range(1, planes):
            to = (dp + k) % planes
            lines.append(
                remote(
                    s_held.at[to], s_line.at[dp], bsend.at[k], brecv.at[k], place.dp_device(to)
                )
            )
            lines[-1].start()

        down.arrive()

        def put_down(at):
            down_out[at] = down.total(at)

        down.each(put_down)
        finals[8].start()

        def landed(copies):
            copies[0].wait()
            for c in copies[1:]:
                c.wait_recv()

        landed(ffn_rows)
        def unpack_rows(i, _):
            part = pl.ds(pl.multiple_of(i * 16, 16), 16)
            for t in range(GROUP):
                for d in range(planes):
                    column = columns_of(d, t, shards)
                    for m, ref in enumerate((gate_out, up_out)):
                        lane = m * hidden + d * brows
                        ref[part, column * brows : (column + 1) * brows] = g_in[
                            t, part, lane : lane + brows
                        ].astype(f32)
            return 0

        lax.fori_loop(0, wrows // 16, unpack_rows, 0)
        finals[2].start()
        finals[3].start()

        outs.arrive()

        def keep_out(at):
            o_near[at] = outs.total(at).astype(bf16)

        outs.each(keep_out)
        out_own = pltpu.make_async_copy(o_near, o_in, oxsend)
        out_far = remote(o_near, o_in, oxsend, oxrecv, place.any_device(owner))

        @pl.when(owner == flat)
        def _():
            out_own.start()

        @pl.when(owner != flat)
        def _():
            out_far.start()

        qkvs.arrive()
        keep, qkv_rows = scatter_rows(qkvs.total, q_near, qxsend, qxrecv, q_in)
        qkvs.each(keep)
        for c in qkv_rows:
            c.start()

        landed(qkv_rows)
        for t in range(GROUP):
            home = place.head(t)
            query_out[:, home * qcols : (home + 1) * qcols] = q_in[t, :, :qcols].astype(f32)
            key_out[:, home * kcols : (home + 1) * kcols] = q_in[
                t, :, qcols : qcols + kcols
            ].astype(f32)
            value_out[:, home * kcols : (home + 1) * kcols] = q_in[
                t, :, qcols + kcols :
            ].astype(f32)

        for c in finals[4:7]:
            c.start()

        @pl.when(owner == flat)
        def _():
            out_own.wait()

        @pl.when(owner != flat)
        def _():
            out_far.wait()

        o_out[...] = o_in[...].astype(f32)
        finals[7].start()
        for c in lines:
            c.wait_recv()
        line_own.wait()
        summed = jnp.sum(s_line[...], axis=0)
        per_row = 128 // wrows
        gcols = HEAD_SIZE // (planes * GROUP)
        s_out[...] = jnp.where(
            lax.broadcasted_iota(jnp.int32, (srows, 128), 0) < 18,
            pltpu.roll(summed, (128 - flat % per_row * wrows) % 128, 1),
            pltpu.roll(summed, (128 - flat * gcols) % 128, 1),
        )
        for c in lines + ffn_rows[1:] + qkv_rows[1:]:
            c.wait_send()
        for c in (ffn, down, qkvs, outs):
            c.drain()
        for c in finals:
            c.wait()

    shape = jax.ShapeDtypeStruct
    vmem = pltpu.VMEM
    wide_rows = shards * wrows
    return pallas(
        body,
        [
            shape((rows, width), bf16),
            shape((rows, width), bf16),
            shape((wrows, hidden * GROUP), f32),
            shape((wrows, hidden * GROUP), f32),
            shape((wrows, qcols * GROUP), f32),
            shape((wrows, kcols * GROUP), f32),
            shape((wrows, kcols * GROUP), f32),
            shape((wrows, width), f32),
            shape((brows, width), f32),
            shape((srows, 128), f32),
            shape((GROUP, rows, width), bf16),
        ],
        [VMEM] * 4 + [ANY] * (5 + len(inputs)),
        [ANY] * 9 + [VMEM, ANY],
        [
            vmem((rows, width), bf16),
            vmem((rows, width), bf16),
            vmem((wrows, hidden * GROUP), f32),
            vmem((wrows, hidden * GROUP), f32),
            vmem((wrows, qcols * GROUP), f32),
            vmem((wrows, kcols * GROUP), f32),
            vmem((wrows, kcols * GROUP), f32),
            vmem((wrows, width), f32),
            vmem((brows, width), f32),
            DMA((9,)),
            vmem((2, act.shape[1], 256), bf16),
            vmem((2, GROUP, rows, 256), bf16),
            DMA((2,)), DMA((2,)), DMA((2,)),
        ]
        + [vmem(i.shape, i.dtype) for i in inputs]
        + [
            vmem((rows, width), bf16),
            vmem((GROUP, rows, width), bf16),
            vmem((rows, width), f32),
            vmem((group_rows, qkv_cols), bf16),
            vmem((group_rows, 128), bf16),
            vmem((length, HEAD_SIZE), f32),
            vmem((length, HEAD_SIZE), f32),
            vmem((group_rows, qcols), bf16),
            vmem((srows, width), f32),
            vmem((GROUP, planes * srows, 128), f32),
            vmem((GROUP, planes * srows, 128), f32),
            vmem((planes, srows, 128), f32),
            vmem((planes, srows, 128), f32),
            vmem((3, streams, wide_rows, both), bf16),
            vmem((streams, wide_rows, both), bf16),
            vmem((streams, wide_rows, both), bf16),
            vmem((GROUP, wrows, both), bf16),
            vmem((3, brows, width), bf16),
            vmem((brows, width), bf16),
            vmem((brows, width), bf16),
            vmem((2, streams, 2, wide_rows, qkv_cols), bf16),
            vmem((3, streams, wide_rows, qkv_cols), bf16),
            vmem((streams, wide_rows, qkv_cols), bf16),
            vmem((streams, wide_rows, qkv_cols), bf16),
            vmem((GROUP, wrows, qkv_cols), bf16),
            vmem((2, 2, wrows, width), bf16),
            vmem((3, wrows, width), bf16),
            vmem((wrows, width), bf16),
            vmem((wrows, width), bf16),
            vmem((wrows, width), bf16),
            vmem((streams, wide_rows, both), bf16),
            vmem((brows, width), bf16),
            vmem((streams, wide_rows, qkv_cols), bf16),
            vmem((wrows, width), bf16),
        ]
        + scatter_scratch(rows, width)
        + [DMA((10,)), DMA((10,)), DMA((10,)), DMA((10,))]
        + gather_scratch()
        + [DMA((len(inputs),))]
        + [DMA((PlaceSums.SENDS,)), DMA((PlaceSums.RECVS,))] * 4
        + [DMA((GROUP,)), DMA((GROUP,)), DMA((GROUP,)), DMA((GROUP,)), DMA, DMA]
        + [DMA((GROUP,)), DMA((GROUP,)), DMA((planes,)), DMA((planes,)), DMA((2,))]
        + [pltpu.SemaphoreType.REGULAR],
        cid,
        180,
        63,
    )(gains, starts, cosine, sine, act, down_w, hidden_one, down_grad, ffn_grad, *inputs)


def store(*arrays):
    count = len(arrays)

    def body(*refs):
        load_sem, store_sem = refs[-2:]
        staged = refs[2 * count : 3 * count]
        loads = [
            pltpu.make_async_copy(refs[i], staged[i], load_sem.at[i]) for i in range(count)
        ]
        stores = [
            pltpu.make_async_copy(staged[i], refs[count + i], store_sem.at[i])
            for i in range(count)
        ]
        for c in loads:
            c.start()
        for load, c in zip(loads, stores):
            load.wait()
            c.start()
        for c in stores:
            c.wait()

    return pl.pallas_call(
        body,
        out_shape=[jax.ShapeDtypeStruct(a.shape, a.dtype) for a in arrays],
        in_specs=[ANY] * count,
        out_specs=[ANY] * count,
        scratch_shapes=[pltpu.VMEM(a.shape, a.dtype) for a in arrays]
        + [DMA((count,)), DMA((count,))],
        compiler_params=pltpu.CompilerParams(vmem_limit_bytes=62 * 1024 * 1024),
    )(*arrays)


def settle(qkv_grad, out_grad, small, qcols, kcols, planes, direct, shards, cid):
    srows = small.shape[1] // planes
    cols = small.shape[2]
    wrows, width = out_grad.shape

    def body(
        q_ref, o_ref, s_ref, query_out, key_out, value_out, o_out, s_out, q_got, o_got, got, held,
        line, qsend, qrecv, osend, orecv, asend, arecv, bsend, brecv,
    ):
        place = Place(shards)
        tp, dp, flat = place.tp, place.dp(), place.flat()
        barrier = pltpu.get_barrier_semaphore()

        def signal(device):
            pl.semaphore_signal(
                barrier, inc=1, device_id=device, device_id_type=pl.DeviceIdType.MESH
            )

        for device in group_peers(place):
            signal(device)
        for k in range(1, planes):
            signal(place.dp_device((dp + k) % planes))
        if direct:
            owner = place.head(tp) * planes + dp
            high, y = lax.axis_index("zh"), lax.axis_index("y")
            source = {"st": lax.axis_index("st"), "seq": high * 2 + y}
            source.update(place.dp_device(lax.axis_index("seq")))

            @pl.when(owner != flat)
            def _():
                signal(source)

            pl.semaphore_wait(barrier, GROUP + planes - 2 + (owner != flat).astype(jnp.int32))
        else:
            pl.semaphore_wait(barrier, GROUP + planes - 2)

        sums = Exchange(place, s_ref, got, asend, arecv)
        sums.start()
        qkv = Exchange(place, q_ref, q_got, qsend, qrecv)
        qkv.start()
        if direct:
            out_own = pltpu.make_async_copy(o_ref, o_got, osend)
            out_far = remote(o_ref, o_got, osend, orecv, place.any_device(owner))

            @pl.when(owner == flat)
            def _():
                out_own.start()

            @pl.when(owner != flat)
            def _():
                out_far.start()

        sums.finish()
        held[...] = jnp.sum(got[...], axis=0).reshape(held.shape)
        line_own = pltpu.make_async_copy(held.at[dp], line.at[dp], bsend.at[0])
        line_own.start()
        lines = []
        for k in range(1, planes):
            to = (dp + k) % planes
            lines.append(
                remote(held.at[to], line.at[dp], bsend.at[k], brecv.at[k], place.dp_device(to))
            )
            lines[-1].start()
        qkv.finish()
        for t in range(GROUP):
            head = place.head(t)
            query_out[:, head * qcols : (head + 1) * qcols] = q_got[t, :, :qcols].astype(f32)
            key_out[:, head * kcols : (head + 1) * kcols] = q_got[
                t, :, qcols : qcols + kcols
            ].astype(f32)
            value_out[:, head * kcols : (head + 1) * kcols] = q_got[t, :, qcols + kcols :].astype(
                f32
            )
        if direct:

            @pl.when(owner == flat)
            def _():
                out_own.wait()

            @pl.when(owner != flat)
            def _():
                out_far.wait()

            o_out[...] = o_got[...].astype(f32)
        else:
            o_out[...] = o_ref[...].astype(f32)
        for c in lines:
            c.wait_recv()
        line_own.wait()
        s_out[...] = jnp.sum(line[...], axis=0)
        for c in lines:
            c.wait_send()

    return pallas(
        body,
        [
            jax.ShapeDtypeStruct((wrows, GROUP * qcols), f32),
            jax.ShapeDtypeStruct((wrows, GROUP * kcols), f32),
            jax.ShapeDtypeStruct((wrows, GROUP * kcols), f32),
            jax.ShapeDtypeStruct((wrows, width), f32),
            jax.ShapeDtypeStruct((srows, cols), f32),
        ],
        [VMEM, VMEM, VMEM],
        [VMEM] * 5,
        [
            pltpu.VMEM(qkv_grad.shape, bf16),
            pltpu.VMEM(out_grad.shape, bf16),
            pltpu.VMEM(small.shape, f32),
            pltpu.VMEM((planes, srows, cols), f32),
            pltpu.VMEM((planes, srows, cols), f32),
            DMA((GROUP,)), DMA((GROUP,)), DMA, DMA,
            DMA((GROUP,)), DMA((GROUP,)), DMA((planes,)), DMA((planes,)),
        ],
        cid,
        20,
    )(qkv_grad, out_grad, small)


def local(
    tokens, doc_starts, attn_gain, query_gain, key_gain, w_query, key_weight, value_weight,
    w_headgate, w_out, ffn_gain, w_gate, w_up, w_down, cotangent,
):
    zs, ys = lax.axis_size("zh"), lax.axis_size("y")
    planes = zs * ys
    direct = zs == 2 and ys == 2
    streams = lax.axis_size("st")
    shards = lax.axis_size("seq")
    devices = planes * GROUP
    rows, width = tokens.shape
    length = rows * shards
    group_rows = rows * GROUP
    wrows = w_query.shape[0]
    brows = w_down.shape[0]
    hidden = brows * planes
    qcols = w_query.shape[1] // GROUP
    kcols = key_weight.shape[1] // GROUP
    group_heads = qcols // HEAD_SIZE
    all_heads = w_headgate.shape[1]
    score_scale = HEAD_SIZE ** (-0.5)
    dp = lax.axis_index(DP)
    tp = lax.axis_index(TP)

    hg = wrows * all_heads
    gcols = query_gain.shape[0]
    at = hg + 2 * wrows
    count = at + 2 * gcols
    sums = -(-count // 1024) * 8
    docs = doc_starts.shape[1]
    qkv_cols = qcols + 2 * kcols
    starts_row = jnp.concatenate(
        [(doc_starts[0] // 128).astype(bf16), (doc_starts[0] % 128).astype(bf16)]
    )
    headgate_rows = jnp.pad(w_headgate, ((0, 0), (0, 128 - all_heads)))
    if direct:
        gain_rows = width // 128
        others = [attn_gain, ffn_gain, query_gain, key_gain, starts_row]
        small = jnp.pad(w_headgate, ((0, 16), (0, 128 - all_heads)))
        for i, row in enumerate(others):
            small = small + jnp.pad(
                row[None], ((wrows + i, 15 - i), (0, 128 - row.shape[0]))
            )
        (
            cot_all, ffn_w, down_w, hidden_one, hidden_two, small, gains, qkv_w, out_w, qkv,
            low, gate_full, mixed, gated, middle, headgate, starts,
        ) = forward_pass(
            tokens, cotangent, small, w_out, w_query, key_weight, value_weight, w_gate, w_up,
            w_down, docs, shards, 0,
        )
        cot_all = cot_all.reshape(group_rows, width)
        hidden_two = hidden_two.reshape(group_rows, width)
        ffn_w = ffn_w.reshape(width, 2 * hidden)
        down_w = down_w.reshape(hidden, width)
        gate_up = mm(hidden_two, ffn_w)
        gate_pre, up_proj = gate_up[:, :hidden], gate_up[:, hidden:]
        gate_sig = jax.nn.sigmoid(gate_pre)
        inner_act = (gate_pre * gate_sig * up_proj).astype(bf16)
        down_grad = mm_t(inner_act, cot_all).astype(bf16)
        grad_inner = mm_b(cot_all, down_w)
        grad_gate = grad_inner * up_proj * gate_sig * (1.0 + gate_pre * (1.0 - gate_sig))
        grad_up = grad_inner * gate_pre * gate_sig
        grad_gu = jnp.concatenate([grad_gate.astype(bf16), grad_up.astype(bf16)], axis=1)
        ffn_grad = mm_t(hidden_two, grad_gu).astype(bf16)
        places = (GROUP, rows, width)
        (
            layer_out, tokens_grad, gate_grad, up_grad, query_grad, key_grad, value_grad,
            out_grad, down_grad, small_sum, _,
        ) = backward_pass(
            mm_b(grad_gu, ffn_w).astype(bf16).reshape(places),
            inner_act, down_w, middle, tokens, cotangent, gains, headgate,
            qkv_w.reshape(width, qkv_cols), out_w.reshape(qcols, width), hidden_one, qkv, low,
            gate_full, mixed, gated, starts, down_grad.reshape(zs, ys, brows, width),
            ffn_grad.reshape(zs, streams, ys, shards * wrows, 2 * hidden), docs, shards, 1,
        )
        (
            layer_out, tokens_grad, gate_grad, up_grad, query_grad, key_grad, value_grad,
            out_grad, down_grad,
        ) = store(
            layer_out, tokens_grad, gate_grad, up_grad, query_grad, key_grad, value_grad,
            out_grad, down_grad,
        )
        return (
            layer_out,
            tokens_grad,
            small_sum[all_heads, :wrows],
            small_sum[18, :gcols],
            small_sum[19, :gcols],
            query_grad,
            key_grad,
            value_grad,
            small_sum[:all_heads, :wrows].T,
            out_grad,
            small_sum[all_heads + 1, :wrows],
            gate_grad,
            up_grad,
            down_grad,
        )
    else:
        srows = -(-(wrows + 6) // 16) * 16
        others = [attn_gain, ffn_gain, query_gain, key_gain, starts_row[:docs], starts_row[docs:]]
        small = jnp.concatenate(
            [headgate_rows]
            + [jnp.pad(row, (0, 128 - row.shape[0]))[None] for row in others]
            + [jnp.zeros((srows - wrows - 6, 128), bf16)]
        )
        tokens_all, cot_all, small, qkv_w, ffn_own = front(
            tokens, cotangent, small, w_out, w_query, key_weight, value_weight, w_gate, w_up,
            w_down, planes, False, shards, 0,
        )
        tokens_all = tokens_all.reshape(group_rows, width)
        cot_all = cot_all.reshape(group_rows, width)
        qkv_w = over_dp(qkv_w[0])
        ffn_w = over_dp(ffn_own)
        down_w = lax.all_gather(w_down, DP, axis=0, tiled=True)
        out_w = lax.all_gather(w_out, ALL, axis=0, tiled=True)
        out_w = lax.dynamic_slice_in_dim(out_w, tp * qcols, qcols, 0)
        head = tp
        here = pick(small[::shards], 1, dp)
        starts = here[:, wrows + 4, :docs].astype(jnp.int32) * 128
        starts = starts + here[:, wrows + 5, :docs].astype(jnp.int32)
    small = small.reshape(streams, shards, zs, ys, srows, 128).transpose(2, 0, 3, 1, 4, 5)
    small = small.reshape(devices, srows, 128)
    headgate_all = small[:, :wrows, :all_heads].reshape(width, all_heads)
    if not direct:
        attn_gain_f = small[:, wrows, :wrows].reshape(1, -1).astype(f32)
        ffn_gain_f = small[:, wrows + 1, :wrows].reshape(1, -1).astype(f32)
        query_gain_f = small[:, wrows + 2, :gcols].reshape(-1).astype(f32)
        key_gain_f = small[:, wrows + 3, :gcols].reshape(-1).astype(f32)
    headgate_own = lax.dynamic_slice_in_dim(headgate_all, head * group_heads, group_heads, 1)

    if not direct:
        residual_all = tokens_all.astype(f32)
        hidden_all = (residual_all * rms_scale(residual_all) * attn_gain_f).astype(bf16)
        qkv = mm(hidden_all, qkv_w)
    query_raw = qkv[:, :qcols].reshape(group_rows, group_heads, HEAD_SIZE)
    key_raw = qkv[:, qcols : qcols + kcols].reshape(group_rows, 1, HEAD_SIZE)
    value = qkv[:, qcols + kcols :].astype(bf16).reshape(streams, length, HEAD_SIZE)
    positions = jnp.tile(jnp.arange(length, dtype=jnp.int32), streams)
    cosine, sine = rotary_tables(positions)
    query_scale = rms_scale(query_raw)
    query_normed = query_raw * query_scale
    query = rotate(query_normed * query_gain_f, cosine, sine).astype(bf16)
    query = query.reshape(streams, length, group_heads, HEAD_SIZE)
    key_scale = rms_scale(key_raw)
    key_normed = key_raw * key_scale
    key = rotate(key_normed * key_gain_f, cosine, sine).astype(bf16)
    key = key.reshape(streams, length, HEAD_SIZE)
    stream_pos = jnp.arange(length, dtype=jnp.int32)
    segment = jnp.sum((stream_pos[None, :, None] >= starts[:, None, :]).astype(jnp.int32), axis=2)
    allowed = (stream_pos[:, None] >= stream_pos[None, :])[None] & (
        segment[:, :, None] == segment[:, None, :]
    )
    scores = jnp.einsum("bqgd,bkd->bgqk", query, key, preferred_element_type=f32) * score_scale
    scores = jnp.where(allowed[:, None], scores, MASK_FILL)
    row_max = jnp.max(scores, axis=-1, keepdims=True)
    weights = jnp.exp(scores - row_max)
    probs = weights / jnp.sum(weights, axis=-1, keepdims=True)
    probs_low = probs.astype(bf16)
    if not direct:
        mixed = jnp.einsum(
            "bgqk,bkd->bqgd", probs_low, value, preferred_element_type=f32
        ).astype(bf16)
    mixed_f = mixed.astype(f32).reshape(group_rows, group_heads, HEAD_SIZE)
    if direct:
        head_gate = gate_full.reshape(group_rows, group_heads, HEAD_SIZE)[:, :, :1]
    else:
        head_gate = jax.nn.sigmoid(mm(hidden_all, headgate_own))[:, :, None]
        gated = (mixed_f * head_gate).astype(bf16).reshape(group_rows, qcols)

    def parts(x):
        return x.astype(bf16).reshape(GROUP, rows, width)

    if not direct:
        middle, hidden_two = middle_step(
            parts(mm(gated, out_w)), tokens, ffn_gain_f, None, shards, 2
        )
        hidden_two = hidden_two.reshape(group_rows, width)

    gate_up = mm(hidden_two, ffn_w)
    gate_pre, up_proj = gate_up[:, :hidden], gate_up[:, hidden:]
    gate_sig = jax.nn.sigmoid(gate_pre)
    inner_act = (gate_pre * gate_sig * up_proj).astype(bf16)
    down_grad = mm_t(inner_act, cot_all).astype(bf16).reshape(zs, ys, brows, width)
    if direct:
        down_sum = PlaceSum(down_grad)
        down_sum.over_y()
    else:
        down_grad = scatter_dp(down_grad)
    grad_inner = mm_b(cot_all, down_w)
    grad_gate = (grad_inner * up_proj * gate_sig * (1.0 + gate_pre * (1.0 - gate_sig))).astype(bf16)
    grad_up = (grad_inner * gate_pre * gate_sig).astype(bf16)
    grad_gu = jnp.concatenate([grad_gate, grad_up], axis=1)
    ffn_grad = mm_t(hidden_two, grad_gu).astype(bf16)
    grad_gu, ffn_grad = lax.optimization_barrier((grad_gu, ffn_grad))
    if not direct:
        ffn_grad = scatter_dp(by_place(ffn_grad))
    grad_middle, ffn_gain_part, grad_branch, *ffn_first = middle_back(
        parts(mm_b(grad_gu, ffn_w)), middle, cotangent, ffn_gain_f,
        ffn_grad.reshape(zs, streams, ys, -1, 2 * hidden) if direct else None, shards, 3,
    )
    if direct:
        grad_branch, down_sum.far, down_sum.near, ffn_first = lax.optimization_barrier(
            (grad_branch, down_sum.far, down_sum.near, ffn_first[0])
        )
        down_z = down_sum.over_z()
        ffn_sum = PlaceSum(by_place(ffn_grad))
        ffn_sum.take(ffn_first.reshape(-1, 2 * hidden), None)
        ffn_z = ffn_sum.over_z()
        ffn_sum.near = ffn_sum.over_y_near()
    grad_branch = grad_branch.reshape(group_rows, width)
    layer_out = scatter_sum(parts(mm(inner_act, down_w)), middle, shards, 4)

    out_grad = mm_t(gated, grad_branch).astype(bf16).reshape(zs, ys, wrows, width)
    grad_gated = mm_b(grad_branch, out_w).reshape(group_rows, group_heads, HEAD_SIZE)
    grad_mixed = (grad_gated * head_gate).astype(bf16).reshape(
        streams, length, group_heads, HEAD_SIZE
    )
    gate_flat = head_gate[:, :, 0]
    grad_logit = (
        jnp.sum(grad_gated * mixed_f, axis=-1) * gate_flat * (1.0 - gate_flat)
    ).astype(bf16)
    grad_probs = jnp.einsum("bqgd,bkd->bgqk", grad_mixed, value, preferred_element_type=f32)
    row_delta = jnp.sum(probs * grad_probs, axis=-1, keepdims=True)
    grad_scores = (probs * (grad_probs - row_delta)).astype(bf16)
    grad_query = (
        jnp.einsum("bgqk,bkd->bqgd", grad_scores, key, preferred_element_type=f32) * score_scale
    ).astype(bf16)
    grad_key = (
        jnp.einsum("bgqk,bqgd->bkd", grad_scores, query, preferred_element_type=f32) * score_scale
    ).astype(bf16)
    grad_value = jnp.einsum(
        "bgqk,bqgd->bkd", probs_low, grad_mixed, preferred_element_type=f32
    ).astype(bf16)
    gqn = rotate_back(
        grad_query.astype(f32).reshape(group_rows, group_heads, HEAD_SIZE), cosine, sine
    )
    query_gain_part = jnp.sum(gqn * query_normed, axis=(0, 1))
    grad_query_raw = norm_back(gqn * query_gain_f, query_normed, query_scale).astype(bf16)
    gkn = rotate_back(grad_key.astype(f32).reshape(group_rows, 1, HEAD_SIZE), cosine, sine)
    key_gain_part = jnp.sum(gkn * key_normed, axis=(0, 1))
    grad_key_raw = norm_back(gkn * key_gain_f, key_normed, key_scale).astype(bf16)
    grad_qkv = jnp.concatenate(
        [
            grad_query_raw.reshape(group_rows, qcols),
            grad_key_raw.reshape(group_rows, kcols),
            grad_value.reshape(group_rows, kcols),
        ],
        axis=1,
    )
    qkv_grad = mm_t(hidden_all, grad_qkv).astype(bf16)
    if direct:
        qkv_grad, out_grad, grad_qkv, down_z = lax.optimization_barrier(
            (qkv_grad, out_grad, grad_qkv, down_z)
        )
        down_grad = down_sum.total(down_z)
        qkv_sum, out_sum = PlaceSum(by_place(qkv_grad)), PlaceSum(out_grad)
        qkv_sum.over_y()
        out_sum.over_y()
        qkv_z, out_z = qkv_sum.over_z(), out_sum.over_z()
        ffn_grad = ffn_sum.total(ffn_z)
        qkv_grad, out_grad = qkv_sum.total(qkv_z), out_sum.total(out_z)
    else:
        qkv_grad = scatter_dp(by_place(qkv_grad))
        out_grad = lax.dynamic_update_slice(
            jnp.zeros((width, width), bf16), out_grad.reshape(qcols, width), (tp * qcols, 0)
        )
        out_grad = lax.psum_scatter(out_grad, ALL, scatter_dimension=0, tiled=True)
    tokens_grad, attn_gain_part = tokens_back(
        parts(mm_b(grad_qkv, qkv_w) + mm_b(grad_logit, headgate_own)),
        tokens, grad_middle, attn_gain_f, shards, 5,
    )
    headgate_part = mm_t(hidden_all, grad_logit)
    headgate_part = lax.dynamic_update_slice(
        jnp.zeros((width, all_heads), f32), headgate_part, (0, head * group_heads)
    )

    small_sum = jnp.concatenate(
        [
            headgate_part.reshape(devices, hg),
            attn_gain_part.reshape(devices, wrows),
            ffn_gain_part.reshape(devices, wrows),
            query_gain_part.reshape(devices, gcols),
            key_gain_part.reshape(devices, gcols),
        ],
        axis=1,
    )
    small_sum = jnp.pad(small_sum, ((0, 0), (0, sums * 128 - count)))
    small_sum = small_sum.reshape(zs, streams, ys, shards, sums, 128)
    small_sum = small_sum.transpose(1, 3, 0, 2, 4, 5)
    small_sum = small_sum.reshape(GROUP, planes * sums, 128)

    gate_grad, up_grad = exchange_back(
        ffn_grad.reshape(GROUP, wrows, 2 * hidden), planes, shards, 6
    )
    query_grad, key_grad, value_grad, out_grad, small_sum = settle(
        qkv_grad.reshape(GROUP, wrows, qkv_cols), out_grad, small_sum, qcols, kcols, planes,
        direct, shards, 7,
    )
    small_sum = small_sum.reshape(-1)
    return (
        layer_out,
        tokens_grad,
        small_sum[hg : hg + wrows],
        small_sum[at : at + gcols],
        small_sum[at + gcols : at + 2 * gcols],
        query_grad,
        key_grad,
        value_grad,
        small_sum[:hg].reshape(wrows, all_heads),
        out_grad,
        small_sum[hg + wrows : hg + 2 * wrows],
        gate_grad,
        up_grad,
        down_grad.astype(f32),
    )


def solution(mesh):
    shards = mesh.shape["seq"]
    planes = (2, 2, 2) if shards == 4 and mesh.size == 32 else (1, GROUP // shards, -1)
    grouped = Mesh(mesh.devices.reshape(planes + (shards,)), ALL)
    two = P(ALL, None)
    one = P(ALL)
    return jax.shard_map(
        local,
        mesh=grouped,
        in_specs=(
            two, P(("zh", "st", "y"), None), one, one, one, two, two, two, two, two, one, two, two,
            two, two,
        ),
        out_specs=(two, two, one, one, one, two, two, two, two, two, one, two, two, two),
        check_vma=False,
    )
```

```python
import jax
import jax.numpy as jnp
import numpy as np
from jax import lax
from jax.experimental import pallas as pl
from jax.experimental.pallas import tpu as pltpu
from jax.sharding import Mesh, PartitionSpec as P

QUERY_HEADS = 16
KEY_VALUE_HEADS = 8
HEAD_SIZE = 128
GROUP = 8
NORM_EPS = 1e-06
ROPE_BASE = 1000000.0
MASK_FILL = -1e30

DP = ("zh", "y")
TP = ("st", "seq")
ALL = ("zh", "st", "y", "seq")
f32 = jnp.float32
bf16 = jnp.bfloat16


def rms_scale(vector):
    return lax.rsqrt(jnp.mean(vector * vector, axis=-1, keepdims=True) + NORM_EPS)


def rotary_tables(positions):
    half_width = HEAD_SIZE // 2
    exponent = jnp.arange(half_width, dtype=jnp.int32).astype(f32) * (2.0 / HEAD_SIZE)
    inverse = jnp.power(ROPE_BASE, -exponent)
    angles = positions.astype(f32)[:, None] * inverse[None, :]
    return (jnp.cos(angles)[:, None, :], jnp.sin(angles)[:, None, :])


def rotate(vector, cosine, sine):
    a, b = jnp.split(vector, 2, axis=-1)
    return jnp.concatenate([a * cosine - b * sine, b * cosine + a * sine], axis=-1)


def rotate_back(vector, cosine, sine):
    a, b = jnp.split(vector, 2, axis=-1)
    return jnp.concatenate([a * cosine + b * sine, b * cosine - a * sine], axis=-1)


def norm_back(grad, normed, scale):
    return scale * (grad - normed * jnp.mean(grad * normed, axis=-1, keepdims=True))


def mm(left, right):
    return jnp.dot(left, right, preferred_element_type=f32)


def mm_t(left, right):
    return lax.dot_general(left, right, (((0,), (0,)), ((), ())), preferred_element_type=f32)


def mm_b(left, right):
    return lax.dot_general(left, right, (((1,), (1,)), ((), ())), preferred_element_type=f32)


SWAP = [(0, 1), (1, 0)]


def over_dp(x):
    streams, shards = lax.axis_size("st"), lax.axis_size("seq")
    zs, ys = lax.axis_size("zh"), lax.axis_size("y")
    rows, columns = x.shape[1] * shards, x.shape[2]
    whole = lax.all_gather(x, DP, axis=0, tiled=False)
    whole = whole.reshape(zs, ys, streams, rows, columns).transpose(0, 2, 1, 3, 4)
    return whole.reshape(-1, columns)


def pick(x, axis, index):
    return lax.dynamic_index_in_dim(x, index, axis, keepdims=False)


def plus(left, right):
    return left.astype(f32) + right.astype(f32)


class PlaceSum:
    def __init__(self, x):
        self.x = x
        self.z, self.y = lax.axis_index("zh"), lax.axis_index("y")

    def piece(self, zp, yp):
        return pick(pick(self.x, 0, zp), 0, yp)

    def over_y(self):
        got = lax.ppermute(pick(self.x, 1, 1 - self.y), "y", SWAP)
        self.take(pick(got, 0, 1 - self.z), pick(got, 0, self.z))

    def over_y_near(self):
        return lax.ppermute(self.piece(self.z, 1 - self.y), "y", SWAP)

    def take(self, far, near):
        self.far, self.near = far, near

    def over_z(self):
        far = plus(self.piece(1 - self.z, self.y), self.far).astype(bf16)
        return lax.ppermute(far, "zh", SWAP)

    def total(self, got):
        return (plus(self.piece(self.z, self.y), self.near) + got.astype(f32)).astype(bf16)


def scatter_dp(x):
    zs, ys = x.shape[:2]
    return lax.psum_scatter(
        x.reshape((zs * ys,) + x.shape[2:]), DP, scatter_dimension=0, tiled=False
    )


def by_place(x):
    streams = lax.axis_size("st")
    zs, ys = lax.axis_size("zh"), lax.axis_size("y")
    columns = x.shape[1]
    x = x.reshape(zs, streams, ys, -1, columns).transpose(0, 2, 1, 3, 4)
    return x.reshape(zs, ys, -1, columns)


def pallas(body, out_shape, in_specs, out_specs, scratch, cid, micros, mib=40):
    return pl.pallas_call(
        body,
        out_shape=out_shape,
        in_specs=in_specs,
        out_specs=out_specs,
        scratch_shapes=scratch,
        compiler_params=pltpu.CompilerParams(
            collective_id=cid, has_side_effects=True, vmem_limit_bytes=mib * 1024 * 1024
        ),
        cost_estimate=pl.CostEstimate(
            flops=0, bytes_accessed=int(micros * 3.6e5), transcendentals=0
        ),
    )


ANY = pl.BlockSpec(memory_space=pl.ANY)
VMEM = pl.BlockSpec(memory_space=pltpu.VMEM)
DMA = pltpu.SemaphoreType.DMA


def remote(src, dst, send, recv, device):
    return pltpu.make_async_remote_copy(
        src_ref=src,
        dst_ref=dst,
        send_sem=send,
        recv_sem=recv,
        device_id=device,
        device_id_type=pl.DeviceIdType.MESH,
    )


class Place:
    def __init__(self, shards):
        self.shards = shards
        self.tp = lax.axis_index("st") * shards + lax.axis_index("seq")
        self.core = self.tp % 2
        self.ring = self.turn(self.tp // 2)

    def turn(self, place):
        if self.shards == GROUP:
            return place
        return place + (place // 2) * (1 - 2 * (place % 2))

    def head(self, index):
        if self.shards == GROUP:
            return index
        return index // 4 * 2 + index % 4 // 2 * 4 + index % 2

    def block(self, ahead, other=False):
        ring = self.ring
        if ahead == 1:
            ring = ring + 1 - 2 * (ring % 2)
        elif ahead == 3:
            ring = 3 - ring
        elif ahead == 2:
            ring = (ring + 2) % 4
        core = 1 - self.core if other else self.core
        return self.turn(ring) * 2 + core

    def device(self, index):
        return {"st": index // self.shards, "seq": index % self.shards}

    def dp_device(self, dp):
        ys = lax.axis_size("y")
        return {"zh": dp // ys, "y": dp % ys}

    def any_device(self, flat):
        ys, streams = lax.axis_size("y"), lax.axis_size("st")
        return {
            "zh": flat // (streams * ys * self.shards),
            "st": flat // (ys * self.shards) % streams,
            "y": flat // self.shards % ys,
            "seq": flat % self.shards,
        }

    def flat(self):
        ys, streams = lax.axis_size("y"), lax.axis_size("st")
        z, y = lax.axis_index("zh"), lax.axis_index("y")
        st, seq = lax.axis_index("st"), lax.axis_index("seq")
        return ((z * streams + st) * ys + y) * self.shards + seq

    def dp(self):
        return lax.axis_index("zh") * lax.axis_size("y") + lax.axis_index("y")

    def right(self):
        return self.device(self.block(1))

    def left(self):
        return self.device(self.block(3))

    def across(self):
        return {"y": 1 - lax.axis_index("y")}

    def partner(self):
        return self.device(self.block(0, True))


def greet(devices):
    barrier = pltpu.get_barrier_semaphore()
    for device in devices:
        pl.semaphore_signal(
            barrier, inc=1, device_id=device, device_id_type=pl.DeviceIdType.MESH
        )
    pl.semaphore_wait(barrier, len(devices))


class RingGather:
    SEMS = 11

    def __init__(self, place, own, out, send, recv, one_way=False):
        rows = out.shape[1]
        half = rows // 2
        first, second = pl.ds(0, half), pl.ds(half, half)
        me, near, next_, opposite = (place.block(i) for i in (0, 1, 3, 2))
        to_near, to_next, to_partner = place.device(near), place.device(next_), place.partner()

        def copy(index, src, block, part, device):
            return remote(src, out.at[block, part], send.at[index], recv.at[index], device)

        self.local = pltpu.make_async_copy(own, out.at[me], send.at[self.SEMS])
        self.next = [
            copy(0, own.at[first], me, first, to_next),
            copy(1, own.at[second], me, second, to_next),
        ]
        self.near = [
            copy(2, own.at[first], me, first, to_near),
            copy(3, own.at[second], me, second, to_near),
        ]
        self.mate = remote(own, out.at[me], send.at[4], recv.at[4], to_partner)
        self.on = [copy(5, out.at[next_, first], next_, first, to_near)]
        if one_way:
            self.on.append(copy(6, out.at[next_, second], next_, second, to_near))
        else:
            self.on.append(copy(6, out.at[near, second], near, second, to_next))
        self.one_way = one_way
        self.across = [
            remote(out.at[next_], out.at[next_], send.at[7], recv.at[7], to_partner),
            remote(out.at[near], out.at[near], send.at[8], recv.at[8], to_partner),
            copy(9, out.at[opposite, first], opposite, first, to_partner),
            copy(10, out.at[opposite, second], opposite, second, to_partner),
        ]

    def start(self):
        self.next[0].start()
        self.near[0 if self.one_way else 1].start()
        self.next[1].start()
        self.near[1 if self.one_way else 0].start()
        self.mate.start()
        self.local.start()

    def pass_on(self):
        self.next[0].wait_recv()
        self.on[0].start()
        if self.one_way:
            self.next[1].wait_recv()
        else:
            self.near[1].wait_recv()
        self.on[1].start()

    def step_across(self):
        if not self.one_way:
            self.next[1].wait_recv()
        self.across[0].start()
        self.near[0].wait_recv()
        if self.one_way:
            self.near[1].wait_recv()
        self.across[1].start()

    def step_far(self):
        self.on[0].wait_recv()
        self.across[2].start()
        self.on[1].wait_recv()
        self.across[3].start()

    def finish(self):
        self.mate.wait_recv()
        for c in self.across:
            c.wait_recv()
        for c in self.next + self.near + [self.mate] + self.on + self.across:
            c.wait_send()
        self.local.wait()

    def run(self):
        self.start()
        self.pass_on()
        self.step_across()
        self.step_far()
        self.finish()


def ring_scatter(place, x, pair, out, near, far, send, recv, emit, between=()):
    between = list(between) + [lambda: None] * 3
    rows = x.shape[1]
    half = rows // 2
    step = 32
    to_left, to_right, to_partner = place.left(), place.right(), place.partner()
    swaps = {}
    for q in (2, 1, 3, 0):
        swaps[q] = remote(
            x.at[place.block(q, True)], pair.at[q], send.at[q], recv.at[q], to_partner
        )
        swaps[q].start()

    def add(q, low, high, extra=None):
        block = place.block(q)

        def one(i, _):
            part = pl.ds(pl.multiple_of(low + i * step, step), step)
            total = x[block, part].astype(f32) + pair[q, part].astype(f32)
            if extra is not None:
                inner = pl.ds(pl.multiple_of(i * step, step), step)
                total = total + far[extra, inner].astype(f32)
            out[q - 1, part] = total.astype(bf16)
            return 0

        lax.fori_loop(0, (high - low) // step, one, 0)

    first, second = pl.ds(0, half), pl.ds(half, half)

    def send_to(index, q, part, dst, device):
        c = remote(out.at[q - 1, part], dst, send.at[index], recv.at[index], device)
        c.start()
        return c

    swaps[2].wait_recv()
    add(2, 0, half)
    a = send_to(4, 2, first, far.at[0], to_right)
    add(2, half, rows)
    b = send_to(5, 2, second, far.at[1], to_left)
    swaps[1].wait_recv()
    add(1, 0, half)
    c = send_to(6, 1, first, near.at[0, first], to_right)
    swaps[3].wait_recv()
    add(3, half, rows)
    d = send_to(7, 3, second, near.at[1, second], to_left)
    between[0]()
    a.wait_recv()
    add(3, 0, half, 0)
    e = send_to(8, 3, first, near.at[1, first], to_left)
    b.wait_recv()
    add(1, half, rows, 1)
    g = send_to(9, 1, second, near.at[0, second], to_right)
    between[1]()
    swaps[0].wait_recv()
    own = place.block(0)
    c.wait_recv()
    d.wait_recv()
    e.wait_recv()
    g.wait_recv()

    def last(i, _):
        part = pl.ds(pl.multiple_of(i * step, step), step)
        emit(
            part,
            (x[own, part].astype(f32) + pair[0, part].astype(f32))
            + (near[0, part].astype(f32) + near[1, part].astype(f32)),
        )
        return 0

    lax.fori_loop(0, rows // step, last, 0)
    for copy in list(swaps.values()) + [a, b, c, d, e, g]:
        copy.wait_send()


def scatter_scratch(rows, width):
    return [
        pltpu.VMEM((4, rows, width), bf16),
        pltpu.VMEM((3, rows, width), bf16),
        pltpu.VMEM((2, rows, width), bf16),
        pltpu.VMEM((2, rows // 2, width), bf16),
        DMA((10,)),
        DMA((10,)),
    ]


def gather_scratch():
    return [DMA((RingGather.SEMS + 1,)), DMA((RingGather.SEMS,))]


def scatter_sum(x, base, shards, cid):
    _, rows, width = x.shape

    def body(x_ref, base_ref, out_ref, pair, out, near, far, send, recv):
        place = Place(shards)
        greet([place.right(), place.left(), place.partner()])

        def emit(part, total):
            out_ref[part] = (base_ref[part] + total).astype(bf16)

        ring_scatter(place, x_ref, pair, out, near, far, send, recv, emit)

    return pallas(
        body, jax.ShapeDtypeStruct((rows, width), bf16), [VMEM, VMEM], VMEM,
        scatter_scratch(rows, width), cid, 25,
    )(x, base)


def middle_step(x, tokens, gain, carry, shards, cid):
    _, rows, width = x.shape
    carries = [] if carry is None else [carry]

    def body(x_ref, tok_ref, gain_ref, *refs):
        refs = list(refs)
        carry_ref = refs.pop(0) if carries else None
        mid_ref, all_ref = refs.pop(0), refs.pop(0)
        carry_out = refs.pop(0) if carries else None
        held, pair, out, near, far, send, recv, gsend, grecv, ysend, yrecv = refs
        place = Place(shards)
        greet(
            [place.right(), place.left(), place.partner()]
            + ([place.across()] if carries else [])
        )
        if carries:
            over = remote(carry_ref, carry_out, ysend, yrecv, place.across())
            over.start()

        def emit(part, total):
            middle = tok_ref[part].astype(f32) + total
            mid_ref[part] = middle
            held[part] = (middle * rms_scale(middle) * gain_ref[...]).astype(bf16)

        ring_scatter(place, x_ref, pair, out, near, far, send, recv, emit)
        RingGather(place, held, all_ref, gsend, grecv).run()
        if carries:
            over.wait()

    return pallas(
        body,
        [
            jax.ShapeDtypeStruct((rows, width), f32),
            jax.ShapeDtypeStruct((GROUP, rows, width), bf16),
        ]
        + [jax.ShapeDtypeStruct(c.shape, c.dtype) for c in carries],
        [VMEM, VMEM, VMEM] + [ANY] * len(carries),
        [VMEM, ANY] + [ANY] * len(carries),
        [pltpu.VMEM((rows, width), bf16)] + scatter_scratch(rows, width) + gather_scratch()
        + [DMA, DMA],
        cid,
        50,
    )(x, tokens, gain, *carries)


def middle_back(x, middle, cotangent, gain, grads, shards, cid):
    _, rows, width = x.shape
    carries = [] if grads is None else [grads]

    def body(x_ref, mid_ref, cot_ref, gain_ref, *refs):
        refs = list(refs)
        grads_ref = refs.pop(0) if carries else None
        dm_ref, part_ref, all_ref = refs.pop(0), refs.pop(0), refs.pop(0)
        grads_out = refs.pop(0) if carries else None
        held, pair, out, near, far, send, recv, gsend, grecv, ysend, yrecv = refs
        place = Place(shards)
        greet(
            [place.right(), place.left(), place.partner()]
            + ([place.across()] if carries else [])
        )
        if carries:
            z, y = lax.axis_index("zh"), lax.axis_index("y")
            over = [
                remote(
                    grads_ref.at[1 - z, st, 1 - y], grads_out.at[st], ysend.at[st],
                    yrecv.at[st], place.across(),
                )
                for st in range(grads.shape[1])
            ]
            for c in over:
                c.start()
        part_ref[...] = jnp.zeros_like(part_ref)

        def emit(part, total):
            middle = mid_ref[part]
            scale = rms_scale(middle)
            normed = middle * scale
            part_ref[...] += jnp.sum(total * normed, axis=0, keepdims=True)
            dm = cot_ref[part].astype(f32) + norm_back(total * gain_ref[...], normed, scale)
            dm_ref[part] = dm
            held[part] = dm.astype(bf16)

        ring_scatter(place, x_ref, pair, out, near, far, send, recv, emit)
        RingGather(place, held, all_ref, gsend, grecv).run()
        if carries:
            for c in over:
                c.wait()

    return pallas(
        body,
        [
            jax.ShapeDtypeStruct((rows, width), f32),
            jax.ShapeDtypeStruct((1, width), f32),
            jax.ShapeDtypeStruct((GROUP, rows, width), bf16),
        ]
        + [jax.ShapeDtypeStruct((c.shape[1],) + c.shape[3:], c.dtype) for c in carries],
        [VMEM, VMEM, VMEM, VMEM] + [ANY] * len(carries),
        [VMEM, VMEM, ANY] + [ANY] * len(carries),
        [pltpu.VMEM((rows, width), bf16)] + scatter_scratch(rows, width) + gather_scratch()
        + [DMA((2,)), DMA((2,))],
        cid,
        50,
    )(x, middle, cotangent, gain, *carries)


def tokens_back(x, tokens, dm, gain, shards, cid):
    _, rows, width = x.shape

    def body(
        x_ref, tok_ref, dm_ref, gain_ref, grad_ref, part_ref, pair, out, near, far, send, recv
    ):
        place = Place(shards)
        greet([place.right(), place.left(), place.partner()])
        part_ref[...] = jnp.zeros_like(part_ref)

        def emit(part, total):
            tok = tok_ref[part].astype(f32)
            scale = rms_scale(tok)
            normed = tok * scale
            part_ref[...] += jnp.sum(total * normed, axis=0, keepdims=True)
            grad_ref[part] = (
                dm_ref[part] + norm_back(total * gain_ref[...], normed, scale)
            ).astype(bf16)

        ring_scatter(place, x_ref, pair, out, near, far, send, recv, emit)

    return pallas(
        body,
        (
            jax.ShapeDtypeStruct((rows, width), bf16),
            jax.ShapeDtypeStruct((1, width), f32),
        ),
        [VMEM, VMEM, VMEM, VMEM],
        (VMEM, VMEM),
        scatter_scratch(rows, width),
        cid,
        25,
    )(x, tokens, dm, gain)


class Exchange:
    SEMS = GROUP

    def __init__(self, place, x, out, send, recv):
        self.local = pltpu.make_async_copy(x.at[place.tp], out.at[place.tp], send.at[0])
        self.copies = []
        for k in range(1, GROUP):
            peer = (place.tp + k) % GROUP
            self.copies.append(
                remote(x.at[peer], out.at[place.tp], send.at[k], recv.at[k], place.device(peer))
            )

    def start(self):
        for c in self.copies:
            c.start()
        self.local.start()

    def finish(self):
        for c in self.copies:
            c.wait_recv()
        for c in self.copies:
            c.wait_send()
        self.local.wait()


def group_peers(place):
    return [place.device((place.tp + k) % GROUP) for k in range(1, GROUP)]


def columns_of(dp, t, shards):
    ys, streams = lax.axis_size("y"), lax.axis_size("st")
    z, y = dp // ys, dp % ys
    return ((z * streams + t // shards) * ys + y) * shards + t % shards


def exchange_back(x, planes, shards, cid):
    _, wrows, both = x.shape
    hidden = both // 2
    brows = hidden // planes
    step = min(wrows, 32)

    def body(x_ref, gate_ref, up_ref, got, send, recv):
        place = Place(shards)
        greet(group_peers(place))
        run = Exchange(place, x_ref, got, send, recv)
        run.start()
        run.finish()
        for t in range(GROUP):
            for dp in range(planes):
                flat = columns_of(dp, t, shards)
                for m, out in enumerate((gate_ref, up_ref)):
                    for at in range(0, wrows, step):
                        part = pl.ds(at, step)
                        out[part, flat * brows : (flat + 1) * brows] = got[
                            t, part, m * hidden + dp * brows : m * hidden + (dp + 1) * brows
                        ].astype(f32)

    shape = jax.ShapeDtypeStruct((wrows, hidden * GROUP), f32)
    return pallas(
        body, (shape, shape), [VMEM], (VMEM, VMEM),
        [pltpu.VMEM(x.shape, bf16), DMA((GROUP,)), DMA((GROUP,))], cid, 25,
    )(x)


class PlaceGather:
    SEMS = 5

    def __init__(self, own, out, send, recv, halves):
        z, y = lax.axis_index("zh"), lax.axis_index("y")
        dp, across = z * 2 + y, (1 - z) * 2 + y
        to_z, to_y = {"zh": 1 - z}, {"y": 1 - y}

        def copy(index, src, slot, part, device):
            return remote(
                src.at[part], out.at[slot, part], send.at[index], recv.at[index], device
            )

        first, second = halves
        self.local = pltpu.make_async_copy(own, out.at[dp], send.at[send.shape[0] - 1])
        self.z = [copy(0, own, dp, first, to_z), copy(1, own, dp, second, to_z)]
        self.y = [
            remote(own, out.at[dp], send.at[2], recv.at[2], to_y),
            copy(3, out.at[across], across, first, to_y),
            copy(4, out.at[across], across, second, to_y),
        ]

    def forward(self, half):
        self.z[half].wait_recv()
        self.y[1 + half].start()

    def finish(self):
        for c in self.y:
            c.wait_recv()
        for c in self.z + self.y:
            c.wait_send()


def front(tokens, cotangent, small, w_out, w_query, key_weight, value_weight, w_gate, w_up,
          w_down, planes, direct, shards, cid):
    rows, width = tokens.shape
    wrows = w_out.shape[0]
    srows, scols = small.shape
    brows = w_down.shape[0]
    hidden = brows * planes
    parts = [w_query.shape[1] // GROUP, key_weight.shape[1] // GROUP, value_weight.shape[1] // GROUP]
    qkv = sum(parts)
    slots = planes if direct else 1
    inputs = [tokens, cotangent, w_query, key_weight, value_weight, w_gate, w_up]
    if direct:
        inputs += [w_down, w_out]

    def body(*refs):
        refs = list(refs)

        def take(count):
            taken = refs[:count]
            del refs[:count]
            return taken

        small_ref, = take(1)
        sources = take(len(inputs))
        tok_all, cot_all, small_all, attn_all, ffn_all = take(5)
        down_all, wout_all = take(2) if direct else (None, None)
        held = take(len(inputs))
        (pack, isem, tsend, trecv, csend, crecv, ssend, srecv, psend, precv, fsend, frecv, asend,
         arecv, aasend, aarecv, dsend, drecv, wsend, wrecv) = refs
        place = Place(shards)
        tp, dp, flat = place.tp, place.dp(), place.flat()

        loads = [
            pltpu.make_async_copy(s, h, isem.at[i]) for i, (s, h) in enumerate(zip(sources, held))
        ]
        for i in (2, 3, 4, 0, 5, 6) + ((7, 8) if direct else ()) + (1,):
            loads[i].start()
        tok_ref, cot_ref, wq_ref, wk_ref, wv_ref, wg_ref, wu_ref = held[:7]

        barrier = pltpu.get_barrier_semaphore()

        def signal(device):
            pl.semaphore_signal(
                barrier, inc=1, device_id=device, device_id_type=pl.DeviceIdType.MESH
            )

        for device in group_peers(place):
            signal(device)
        for k in range(1, planes):
            signal(place.dp_device((dp + k) % planes))
        if direct:
            high, low = lax.axis_index("zh"), lax.axis_index("st")
            y, seq = lax.axis_index("y"), lax.axis_index("seq")
            to_seq = high * 2 + y
            from_high, from_y = seq // 2, seq % 2
            selfish = seq == to_seq
            mine = y == from_y
            for j in range(4):

                @pl.when(jnp.logical_and(mine, (from_high * 4 + j) != (high * 4 + seq)))
                def _():
                    signal({"zh": from_high, "seq": jnp.int32(j)})

            pl.semaphore_wait(
                barrier, GROUP - 1 + planes - 1 + 2 - selfish.astype(jnp.int32)
            )
        else:
            pl.semaphore_wait(barrier, GROUP - 1 + planes - 1)

        here = dp if direct else 0
        attn = []
        at = 0
        for i, (ref, cols) in enumerate(zip((wq_ref, wk_ref, wv_ref), parts)):
            loads[2 + i].wait()
            for k in range(GROUP):
                peer = (tp + k) % GROUP
                column = place.head(peer) * cols
                src = ref.at[:, pl.ds(pl.multiple_of(column, cols), cols)]
                dst = attn_all.at[here, tp, :, pl.ds(at, cols)]
                sem = i * GROUP + k
                if k == 0:
                    attn.append(pltpu.make_async_copy(src, dst, asend.at[sem]))
                else:
                    attn.append(
                        remote(src, dst, asend.at[sem], arecv.at[sem], place.device(peer))
                    )
                attn[-1].start()
            at += cols

        small_own = pltpu.make_async_copy(small_ref, small_all.at[tp, dp], ssend.at[0])
        small_own.start()
        small_dp = []
        for k in range(1, planes):
            small_dp.append(
                remote(
                    small_ref, small_all.at[tp, dp], ssend.at[k], srecv.at[k],
                    place.dp_device((dp + k) % planes),
                )
            )
            small_dp[-1].start()

        if direct:
            down_ref, wout_ref = held[7:]
            loads[7].wait()
            half = brows // 2
            down_dp = PlaceGather(
                down_ref, down_all, dsend, drecv, (pl.ds(0, half), pl.ds(half, half))
            )
            down_dp.z[0].start()
        loads[0].wait()
        tok = RingGather(place, tok_ref, tok_all, tsend, trecv, direct)
        tok.start()

        loads[5].wait()
        loads[6].wait()
        for t in range(GROUP):
            for d in range(planes):
                column = columns_of(d, t, shards)
                for m, ref in enumerate((wg_ref, wu_ref)):
                    lane = m * hidden + d * brows
                    pack[t, :, lane : lane + brows] = ref[:, column * brows : (column + 1) * brows]
        ffn = Exchange(place, pack, ffn_all, fsend, frecv)
        ffn.start()

        if direct:
            down_dp.y[0].start()
            down_dp.local.start()
            loads[8].wait()
            wout_copies = [
                remote(
                    wout_ref, wout_all.at[seq], wsend.at[k], wrecv.at[seq],
                    {"zh": z, "seq": to_seq},
                )
                for k, z in enumerate((high, 1 - high))
            ]
            wout_own = pltpu.make_async_copy(wout_ref, wout_all.at[seq], wsend.at[0])
            wout_over = remote(
                wout_all, wout_all, wsend.at[2], wrecv.at[4], place.across()
            )

            @pl.when(selfish)
            def _():
                wout_own.start()

            @pl.when(jnp.logical_not(selfish))
            def _():
                wout_copies[0].start()

            wout_copies[1].start()

        for i in range(3 * GROUP):
            if i % GROUP == 0:
                attn[i].wait()
            else:
                attn[i].wait_recv()
        if direct:
            half = GROUP // 2
            attn_dp = PlaceGather(
                attn_all.at[dp], attn_all, aasend, aarecv, (pl.ds(0, half), pl.ds(half, half))
            )
            attn_dp.z[0].start()
            attn_dp.y[0].start()
            attn_dp.z[1].start()
            down_dp.z[1].start()

        small_own.wait()
        for c in small_dp:
            c.wait_recv()
        small_tp = []
        for k in range(1, GROUP):
            small_tp.append(
                remote(
                    small_all.at[tp], small_all.at[tp], psend.at[k], precv.at[k],
                    place.device((tp + k) % GROUP),
                )
            )
            small_tp[-1].start()

        loads[1].wait()
        cot = RingGather(place, cot_ref, cot_all, csend, crecv, direct)
        tok.pass_on()
        cot.start()
        tok.step_across()
        if direct:
            down_dp.forward(0)

            @pl.when(mine)
            def _():
                for j in range(4):

                    @pl.when((from_high * 4 + j) != (high * 4 + seq))
                    def _():
                        remote(
                            wout_ref, wout_all.at[j], wsend.at[0], wrecv.at[j], place.across()
                        ).wait_recv()

                @pl.when(selfish)
                def _():
                    wout_own.wait()

                wout_over.start()

            attn_dp.forward(0)
        tok.step_far()
        cot.pass_on()
        if direct:
            attn_dp.forward(1)
        cot.step_across()
        if direct:
            down_dp.forward(1)
        cot.step_far()
        tok.finish()
        cot.finish()
        ffn.finish()
        for i in range(3 * GROUP):
            if i % GROUP:
                attn[i].wait_send()
        for c in small_tp:
            c.wait_recv()
        for c in small_dp + small_tp:
            c.wait_send()
        if direct:
            attn_dp.finish()
            down_dp.finish()
            down_dp.local.wait()

            @pl.when(jnp.logical_not(selfish))
            def _():
                wout_copies[0].wait_send()

            wout_copies[1].wait_send()

            @pl.when(mine)
            def _():
                wout_over.wait_send()

            @pl.when(jnp.logical_not(mine))
            def _():
                wout_over.wait_recv()

    shapes = [
        jax.ShapeDtypeStruct((GROUP, rows, width), bf16),
        jax.ShapeDtypeStruct((GROUP, rows, width), bf16),
        jax.ShapeDtypeStruct((GROUP, planes, srows, scols), bf16),
        jax.ShapeDtypeStruct((slots, GROUP, wrows, qkv), bf16),
        jax.ShapeDtypeStruct((GROUP, wrows, 2 * hidden), bf16),
    ]
    if direct:
        shapes += [
            jax.ShapeDtypeStruct((planes, brows, width), bf16),
            jax.ShapeDtypeStruct((planes, wrows, width), bf16),
        ]
    return pallas(
        body,
        shapes,
        [VMEM] + [ANY] * len(inputs),
        [ANY, ANY, VMEM] + [ANY] * (len(shapes) - 3),
        [pltpu.VMEM(x.shape, x.dtype) for x in inputs]
        + [pltpu.VMEM((GROUP, wrows, 2 * hidden), bf16), DMA((len(inputs),))]
        + gather_scratch() + gather_scratch()
        + [
            DMA((planes,)), DMA((planes,)), DMA((GROUP,)), DMA((GROUP,)),
            DMA((GROUP,)), DMA((GROUP,)), DMA((3 * GROUP,)), DMA((3 * GROUP,)),
            DMA((PlaceGather.SEMS,)), DMA((PlaceGather.SEMS,)),
            DMA((PlaceGather.SEMS + 1,)), DMA((PlaceGather.SEMS,)), DMA((3,)), DMA((5,)),
        ],
        cid,
        60,
    )(small, *inputs)


class Spread:
    def __init__(self, own, piece, relay, send, recv):
        z, low, y = (lax.axis_index(a) for a in ("zh", "st", "y"))
        to_z, to_y = {"zh": 1 - z}, {"y": 1 - y}
        beside, middle = {"st": 1 - low}, {"zh": 1 - z, "st": 1 - low}
        self.outer = z == low
        self.inner = z != low
        count = relay.shape[0]
        self.direct, self.toward, self.onward, self.y, self.on = [], [], [], [], []
        for h in range(count):
            at_y, at_on, at_more = count + h, 2 * count + h, 3 * count + h
            here, there = piece(z, h, y), piece(1 - z, h, y)
            self.direct.append(remote(own(h), here, send.at[h], recv.at[h], to_z))
            self.toward.append(
                remote(own(h), relay.at[h], send.at[h], recv.at[at_more], beside)
            )
            self.onward.append(
                remote(relay.at[h], here, send.at[at_more], recv.at[h], middle)
            )
            self.y.append(remote(own(h), here, send.at[at_y], recv.at[at_y], to_y))
            self.on.append(remote(there, there, send.at[at_on], recv.at[at_on], to_y))

    def start_z(self, first=0, last=None):
        @pl.when(self.outer)
        def _():
            for c in self.toward[first:last]:
                c.start()

        @pl.when(self.inner)
        def _():
            for c in self.direct[first:last]:
                c.start()

    def start_y(self):
        for c in self.y:
            c.start()

    def relay(self, half):
        @pl.when(self.inner)
        def _():
            self.toward[half].wait_recv()
            self.onward[half].start()

    def forward(self, half):
        self.direct[half].wait_recv()
        self.on[half].start()

    def finish(self):
        for c in self.y + self.on:
            c.wait_recv()
        for c in self.direct + self.y + self.on:
            c.wait_send()

        @pl.when(self.inner)
        def _():
            for c in self.onward:
                c.wait_send()


def rope_constants(length):
    exponent = np.arange(HEAD_SIZE // 2, dtype=np.float32) * np.float32(2.0 / HEAD_SIZE)
    inverse = np.power(np.float32(ROPE_BASE), -exponent).astype(np.float32)
    angles = np.arange(length, dtype=np.float32)[:, None] * inverse[None, :]
    cosine, sine = np.cos(angles.astype(np.float64)), np.sin(angles.astype(np.float64))
    return (
        jnp.asarray(np.concatenate([cosine, cosine], axis=1).astype(np.float32)),
        jnp.asarray(np.concatenate([-sine, sine], axis=1).astype(np.float32)),
    )


def document_mask(row, docs, low, count, keys):
    at_row = low + lax.broadcasted_iota(jnp.int32, (count, 1), 0)
    at_col = lax.broadcasted_iota(jnp.int32, (1, keys), 1)
    seg_row = jnp.zeros((count, 1), jnp.int32)
    seg_col = jnp.zeros((1, keys), jnp.int32)
    for d in range(docs):
        start = (row[:, d : d + 1] * 128.0 + row[:, docs + d : docs + d + 1]).astype(jnp.int32)
        seg_row = seg_row + jnp.where(at_row >= start, 1, 0)
        seg_col = seg_col + jnp.where(at_col >= start, 1, 0)
    return jnp.logical_and(at_row >= at_col, seg_row == seg_col)


def forward_pass(tokens, cotangent, small, w_out, w_query, key_weight, value_weight, w_gate,
                 w_up, w_down, docs, shards, cid):
    rows, width = tokens.shape
    wrows = w_out.shape[0]
    brows = w_down.shape[0]
    planes = 4
    hidden = brows * planes
    parts = [w_query.shape[1] // GROUP, key_weight.shape[1] // GROUP, value_weight.shape[1] // GROUP]
    qkv = sum(parts)
    qcols = parts[0]
    heads = qcols // HEAD_SIZE
    group_rows = rows * GROUP
    length = rows * shards
    streams = GROUP // shards
    gain_rows = width // 128
    grows = -(-(2 * gain_rows + 3) // 16) * 16
    srows = wrows + grows
    gcols = HEAD_SIZE // (planes * GROUP)
    cosine, sine = rope_constants(length)
    inputs = [tokens, cotangent, w_query, key_weight, value_weight, w_gate, w_up, w_down, w_out]
    score_scale = HEAD_SIZE ** (-0.5)

    def body(
        raw_ref, cos_ref, sin_ref, s0, s1, s2, s3, s4, s5, s6, s7, s8,
        cot_all, ffn_all, down_all, h1_out, h2_all, small_all, gains_ref, attn_all, wout_all,
        qkv_ref, low_ref, gate_ref, mixed_ref, gated_ref, mid_ref, hg, starts_ref,
        h0, h1, h2, h3, h4, h5, h6, h7, h8, small_ref, pack, attn_relay, ffn_relay, down_relay, tok_all, hid, partial, held_two, isem, osem,
        tsend, trecv, csend, crecv, gsend, grecv, ssend, srecv, psend, precv, fsend, frecv, asend,
        arecv, aasend, aarecv, ffsend, ffrecv, dsend, drecv, wsend, wrecv, pair, out, near, far,
        rsend, rrecv,
    ):
        sources = [s0, s1, s2, s3, s4, s5, s6, s7, s8]
        held = [h0, h1, h2, h3, h4, h5, h6, h7, h8]
        place = Place(shards)
        tp, dp = place.tp, place.dp()
        high, low = lax.axis_index("zh"), lax.axis_index("st")
        y, seq = lax.axis_index("y"), lax.axis_index("seq")
        loads = [
            pltpu.make_async_copy(s, h, isem.at[i]) for i, (s, h) in enumerate(zip(sources, held))
        ]
        for i in (2, 3, 4, 8, 0, 5, 6, 7, 1):
            loads[i].start()
        tok_ref, cot_ref, wq_ref, wk_ref, wv_ref, wg_ref, wu_ref, down_ref, wout_ref = held

        barrier = pltpu.get_barrier_semaphore()

        def signal(device):
            pl.semaphore_signal(
                barrier, inc=1, device_id=device, device_id_type=pl.DeviceIdType.MESH
            )

        for device in group_peers(place):
            signal(device)
        for k in range(1, planes):
            signal(place.dp_device((dp + k) % planes))
        to_seq = high * 2 + y
        from_high, from_y = seq // 2, seq % 2
        selfish = seq == to_seq
        mine = y == from_y
        for j in range(4):

            @pl.when(jnp.logical_and(mine, (from_high * 4 + j) != (high * 4 + seq)))
            def _():
                signal({"zh": from_high, "seq": jnp.int32(j)})

        inner = high != low

        @pl.when(inner)
        def _():
            signal({"zh": 1 - high, "st": 1 - low})

        pl.semaphore_wait(
            barrier,
            GROUP - 1 + planes - 1 + 2 - selfish.astype(jnp.int32) + inner.astype(jnp.int32),
        )

        attn = []
        at = 0
        for i, (ref, cols) in enumerate(zip((wq_ref, wk_ref, wv_ref), parts)):
            loads[2 + i].wait()
            for k in range(GROUP):
                peer = (tp + k) % GROUP
                column = place.head(peer) * cols
                src = ref.at[:, pl.ds(pl.multiple_of(column, cols), cols)]
                dst = attn_all.at[high, low, y, pl.ds(seq * wrows, wrows), pl.ds(at, cols)]
                sem = i * GROUP + k
                if k == 0:
                    attn.append(pltpu.make_async_copy(src, dst, asend.at[sem]))
                else:
                    attn.append(
                        remote(src, dst, asend.at[sem], arecv.at[sem], place.device(peer))
                    )
                attn[-1].start()
            at += cols

        small_ref[0:wrows] = raw_ref[0:wrows]
        flat = place.flat()
        block = raw_ref[wrows : wrows + 16].astype(f32)
        row_of = lax.broadcasted_iota(jnp.int32, (grows, 128), 0)
        placed = jnp.zeros((grows, 128), f32)
        per_row = 128 // wrows
        for i, (at, shift) in enumerate(
            (
                (flat // per_row, flat % per_row * wrows),
                (gain_rows + flat // per_row, flat % per_row * wrows),
                (2 * gain_rows, flat * gcols),
                (2 * gain_rows + 1, flat * gcols),
                (2 * gain_rows + 2, 0),
            )
        ):
            row = jnp.broadcast_to(block[i : i + 1], (grows, 128))
            placed = jnp.where(row_of == at, pltpu.roll(row, shift, 1), placed)
        small_ref[wrows:] = placed.astype(bf16)
        small_own = pltpu.make_async_copy(small_ref, small_all.at[tp, dp], ssend.at[0])
        small_own.start()
        small_dp = []
        for k in range(1, planes):
            small_dp.append(
                remote(
                    small_ref, small_all.at[tp, dp], ssend.at[k], srecv.at[k],
                    place.dp_device((dp + k) % planes),
                )
            )
            small_dp[-1].start()

        loads[5].wait()
        loads[6].wait()
        def pack_rows(i, _):
            part = pl.ds(pl.multiple_of(i * 16, 16), 16)
            for t in range(GROUP):
                for d in range(planes):
                    column = columns_of(d, t, shards)
                    for m, ref in enumerate((wg_ref, wu_ref)):
                        lane = m * hidden + d * brows
                        pack[t, part, lane : lane + brows] = ref[
                            part, column * brows : (column + 1) * brows
                        ]
            return 0

        lax.fori_loop(0, wrows // 16, pack_rows, 0)

        def arrived(copies):
            for i, c in enumerate(copies):
                if i % GROUP == 0:
                    c.wait()
                else:
                    c.wait_recv()

        arrived(attn)

        def attn_piece(zp, half, yp):
            return attn_all.at[zp, half, yp]

        attn_dp = Spread(
            lambda half: attn_piece(high, half, y), attn_piece, attn_relay, aasend, aarecv
        )
        attn_dp.start_z()
        attn_dp.start_y()
        loads[0].wait()
        tok = RingGather(place, tok_ref, tok_all, tsend, trecv, True)
        tok.start()
        small_own.wait()
        for c in small_dp:
            c.wait_recv()
        small_tp = []
        for k in range(1, GROUP):
            small_tp.append(
                remote(
                    small_all.at[tp], small_all.at[tp], psend.at[k], precv.at[k],
                    place.device((tp + k) % GROUP),
                )
            )
            small_tp[-1].start()
        attn_dp.relay(0)
        attn_dp.relay(1)

        loads[7].wait()
        half_rows = brows // 2

        def down_piece(zp, half, yp):
            return down_all.at[zp * 2 + yp, pl.ds(half * half_rows, half_rows)]

        down_dp = Spread(
            lambda half: down_ref.at[pl.ds(half * half_rows, half_rows)], down_piece, down_relay,
            dsend, drecv,
        )
        down_own = pltpu.make_async_copy(down_ref, down_all.at[dp], dsend.at[8])
        down_own.start()
        down_dp.start_z()
        tok.pass_on()
        ffn_dst = ffn_all.at[high, low, y, pl.ds(seq * wrows, wrows)]
        ffn = [pltpu.make_async_copy(pack.at[tp], ffn_dst, fsend.at[0])]
        for k, (ahead, other) in enumerate(
            ((3, False), (3, True), (0, True), (1, False), (1, True), (2, False), (2, True))
        ):
            peer = place.block(ahead, other)
            ffn.append(
                remote(
                    pack.at[peer], ffn_dst, fsend.at[k + 1], frecv.at[k + 1], place.device(peer)
                )
            )
        for c in ffn[:4]:
            c.start()
        loads[8].wait()
        wout_copies = [
            remote(
                wout_ref, wout_all.at[seq], wsend.at[k], wrecv.at[seq], {"zh": z, "seq": to_seq}
            )
            for k, z in enumerate((high, 1 - high))
        ]
        wout_own = pltpu.make_async_copy(wout_ref, wout_all.at[seq], wsend.at[0])
        wout_over = remote(wout_all, wout_all, wsend.at[2], wrecv.at[4], place.across())
        wout_copies[1].start()

        @pl.when(selfish)
        def _():
            wout_own.start()

        @pl.when(jnp.logical_not(selfish))
        def _():
            wout_copies[0].start()

        attn_dp.forward(0)
        attn_dp.forward(1)
        down_dp.start_y()
        tok.step_across()
        down_dp.relay(0)
        tok.step_far()
        for c in ffn[4:]:
            c.start()

        @pl.when(mine)
        def _():
            for j in range(4):

                @pl.when((from_high * 4 + j) != (high * 4 + seq))
                def _():
                    remote(
                        wout_ref, wout_all.at[j], wsend.at[0], wrecv.at[j], place.across()
                    ).wait_recv()

            @pl.when(selfish)
            def _():
                wout_own.wait()

            wout_over.start()

        for c in small_tp:
            c.wait_recv()
        gains = jnp.zeros((grows, 128), f32)
        for t in range(GROUP):
            for d in range(planes):
                gains = gains + small_all[t, d, pl.ds(wrows, grows)].astype(f32)
                flat = columns_of(d, t, shards)
                hg[flat * wrows : (flat + 1) * wrows] = small_all[t, d, pl.ds(0, wrows)]
        gains_ref[...] = gains
        gain_one = jnp.concatenate([gains[i : i + 1] for i in range(gain_rows)], axis=1)
        gain_two = jnp.concatenate(
            [gains[gain_rows + i : gain_rows + i + 1] for i in range(gain_rows)], axis=1
        )
        query_gain = gains[2 * gain_rows : 2 * gain_rows + 1]
        key_gain = gains[2 * gain_rows + 1 : 2 * gain_rows + 2]
        starts = []
        for st in range(streams):
            block = small_all[st * shards, dp, pl.ds(wrows, grows)].astype(f32)
            starts.append(block[2 * gain_rows + 2 : 2 * gain_rows + 3])
            starts_ref[st : st + 1] = starts[st]

        tok.finish()
        step = 32

        def norm(i, _):
            block = i // (rows // step)
            inner = pl.ds(pl.multiple_of(i % (rows // step) * step, step), step)
            value = tok_all[block, inner].astype(f32)
            hid[block, inner] = (value * rms_scale(value) * gain_one).astype(bf16)
            return 0

        lax.fori_loop(0, group_rows // step, norm, 0)
        save = pltpu.make_async_copy(hid, h1_out, osem)
        save.start()
        down_dp.relay(1)
        attn_dp.finish()
        weight = attn_all[...].reshape(width, qkv)
        head = place.head(tp)
        lanes = lax.broadcasted_iota(jnp.int32, (1, 128), 1)

        def rotary(x, gain, s):
            scaled = x * rms_scale(x) * gain
            return (
                scaled * cos_ref[...] + pltpu.roll(scaled, HEAD_SIZE // 2, 1) * sin_ref[...]
            ).astype(bf16)

        def project(s, _):
            part = pl.ds(pl.multiple_of(s * length, length), length)
            normed = hid[pl.ds(s * shards, shards)].reshape(length, width)
            raw = jnp.dot(normed, weight, preferred_element_type=f32)
            qkv_ref[part] = raw
            logit = jnp.dot(normed, hg[...], preferred_element_type=f32)
            for g in range(heads):
                at = g * HEAD_SIZE
                low_ref[part, at : at + HEAD_SIZE] = rotary(
                    raw[:, at : at + HEAD_SIZE], query_gain, s
                )
                own = jnp.sum(
                    jnp.where(lanes == head * heads + g, logit, 0.0), axis=1, keepdims=True
                )
                gate_ref[part, at : at + HEAD_SIZE] = jnp.broadcast_to(
                    jax.nn.sigmoid(own), (length, HEAD_SIZE)
                )
            low_ref[part, qcols : qcols + HEAD_SIZE] = rotary(
                raw[:, qcols : qcols + HEAD_SIZE], key_gain, s
            )
            low_ref[part, qcols + HEAD_SIZE :] = raw[:, qcols + HEAD_SIZE :].astype(bf16)
            return 0

        lax.fori_loop(0, streams, project, 0)
        arrived(ffn)

        quarter = shards * wrows // 2

        def ffn_piece(zp, half, yp):
            return ffn_all.at[zp, half // 2, yp, pl.ds(half % 2 * quarter, quarter)]

        ffn_dp = Spread(
            lambda half: ffn_piece(high, half, y), ffn_piece, ffn_relay, ffsend, ffrecv
        )
        ffn_dp.start_z(0, 2)
        ffn_dp.start_y()
        block = 128
        def attend(s, _):
            base = pl.multiple_of(s * length, length)
            row = starts_ref[pl.ds(s, 1)]
            for r in range(0, length, block):
                keys = r + block
                allowed = document_mask(row, docs, r, block, keys)
                key = low_ref[pl.ds(base, keys), qcols : qcols + HEAD_SIZE]
                value = low_ref[pl.ds(base, keys), qcols + HEAD_SIZE :]
                part = pl.ds(base + r, block)
                for g in range(heads):
                    at = g * HEAD_SIZE
                    scores = (
                        lax.dot_general(
                            low_ref[part, at : at + HEAD_SIZE], key, (((1,), (1,)), ((), ())),
                            preferred_element_type=f32,
                        )
                        * score_scale
                    )
                    scores = jnp.where(allowed, scores, MASK_FILL)
                    weights = jnp.exp(scores - jnp.max(scores, axis=1, keepdims=True))
                    probs = weights / jnp.sum(weights, axis=1, keepdims=True)
                    mixed = jnp.dot(
                        probs.astype(bf16), value, preferred_element_type=f32
                    ).astype(bf16)
                    mixed_ref[part, at : at + HEAD_SIZE] = mixed
                    gated_ref[part, at : at + HEAD_SIZE] = (
                        mixed.astype(f32) * gate_ref[part, at : at + HEAD_SIZE]
                    ).astype(bf16)
            return 0

        lax.fori_loop(0, streams, attend, 0)

        @pl.when(jnp.logical_not(mine))
        def _():
            wout_over.wait_recv()

        wide = 512
        def give(i, _):
            s = i // (width // wide)
            cols = pl.ds(pl.multiple_of(i % (width // wide) * wide, wide), wide)
            product = jnp.dot(
                gated_ref[pl.ds(pl.multiple_of(s * length, length), length)],
                wout_all[:, :, cols].reshape(qcols, wide),
                preferred_element_type=f32,
            )
            partial[pl.ds(s * shards, shards), :, cols] = product.astype(bf16).reshape(
                shards, rows, wide
            )
            return 0

        lax.fori_loop(0, streams * (width // wide), give, 0)

        def emit(part, total):
            middle = tok_ref[part].astype(f32) + total
            mid_ref[part] = middle
            held_two[part] = (middle * rms_scale(middle) * gain_two).astype(bf16)

        def first():
            ffn_dp.relay(0)
            down_dp.forward(0)

        def second():
            ffn_dp.relay(1)
            ffn_dp.start_z(2, 3)
            down_dp.forward(1)
            ffn_dp.forward(0)

        ring_scatter(
            place, partial, pair, out, near, far, rsend, rrecv, emit, (first, second)
        )
        two = RingGather(place, held_two, h2_all, gsend, grecv, True)
        two.start()
        ffn_dp.forward(1)
        ffn_dp.relay(2)
        two.pass_on()
        ffn_dp.start_z(3, 4)
        loads[1].wait()
        cot = RingGather(place, cot_ref, cot_all, csend, crecv, True)
        cot.start()
        ffn_dp.relay(3)
        two.step_across()
        ffn_dp.forward(2)
        two.step_far()
        cot.pass_on()
        ffn_dp.forward(3)
        cot.step_across()
        cot.step_far()
        two.finish()
        cot.finish()
        ffn_dp.finish()
        down_dp.finish()
        down_own.wait()
        save.wait()
        for i, c in enumerate(attn):
            if i % GROUP:
                c.wait_send()
        for c in ffn[1:] + small_dp + small_tp:
            c.wait_send()

        @pl.when(jnp.logical_not(selfish))
        def _():
            wout_copies[0].wait_send()

        wout_copies[1].wait_send()

        @pl.when(mine)
        def _():
            wout_over.wait_send()

    pieces = (2, streams, 2, shards * wrows)
    shape = jax.ShapeDtypeStruct
    return pallas(
        body,
        [
            shape((GROUP, rows, width), bf16),
            shape(pieces + (2 * hidden,), bf16),
            shape((planes, brows, width), bf16),
            shape((GROUP, rows, width), bf16),
            shape((GROUP, rows, width), bf16),
            shape((GROUP, planes, srows, 128), bf16),
            shape((grows, 128), f32),
            shape(pieces + (qkv,), bf16),
            shape((planes, wrows, width), bf16),
            shape((group_rows, qkv), f32),
            shape((group_rows, qkv), bf16),
            shape((group_rows, qcols), f32),
            shape((group_rows, qcols), bf16),
            shape((group_rows, qcols), bf16),
            shape((rows, width), f32),
            shape((width, 128), bf16),
            shape((streams, 128), f32),
        ],
        [VMEM] * 3 + [ANY] * len(inputs),
        [ANY] * 5 + [VMEM] * 12,
        [pltpu.VMEM(x.shape, x.dtype) for x in inputs]
        + [
            pltpu.VMEM((srows, 128), bf16),
            pltpu.VMEM((GROUP, wrows, 2 * hidden), bf16),
            pltpu.VMEM((2, shards * wrows, qkv), bf16),
            pltpu.VMEM((4, shards * wrows // 2, 2 * hidden), bf16),
            pltpu.VMEM((2, brows // 2, width), bf16),
            pltpu.VMEM((GROUP, rows, width), bf16),
            pltpu.VMEM((GROUP, rows, width), bf16),
            pltpu.VMEM((GROUP, rows, width), bf16),
            pltpu.VMEM((rows, width), bf16),
            DMA((len(inputs),)),
            DMA,
        ]
        + gather_scratch() + gather_scratch() + gather_scratch()
        + [
            DMA((planes,)), DMA((planes,)), DMA((GROUP,)), DMA((GROUP,)),
            DMA((GROUP,)), DMA((GROUP,)), DMA((3 * GROUP,)), DMA((3 * GROUP,)),
            DMA((8,)), DMA((8,)), DMA((16,)), DMA((16,)),
            DMA((9,)), DMA((8,)), DMA((3,)), DMA((5,)),
        ]
        + scatter_scratch(rows, width),
        cid,
        100,
        56,
    )(small, cosine, sine, *inputs)


class PlaceSums:
    SENDS, RECVS = 8, 6

    def __init__(self, piece, got, far, near, relay, send, recv):
        z, low, y = (lax.axis_index(a) for a in ("zh", "st", "y"))
        to_z, to_y = {"zh": 1 - z}, {"y": 1 - y}
        beside, middle = {"st": 1 - low}, {"zh": 1 - z, "st": 1 - low}
        self.outer, self.inner = z == low, z != low
        self.got, self.far, self.near = got, far, near
        self.y_far = remote(piece(1 - z, 1 - y), got.at[0], send.at[0], recv.at[0], to_y)
        self.y_near = remote(piece(z, 1 - y), got.at[1], send.at[1], recv.at[1], to_y)
        self.loads = [
            pltpu.make_async_copy(piece(1 - z, y), far, send.at[2]),
            pltpu.make_async_copy(piece(z, y), near, send.at[3]),
        ]

        def half(ref, h):
            if len(far.shape) == 3:
                return ref.at[h]
            count = far.shape[0] // 2
            return ref.at[pl.ds(h * count, count)]

        self.direct, self.toward, self.onward = [], [], []
        for h in range(2):
            dst = half(got.at[2], h)
            self.direct.append(
                remote(half(far, h), dst, send.at[4 + h], recv.at[2 + h], to_z)
            )
            self.toward.append(
                remote(half(far, h), half(relay, h), send.at[4 + h], recv.at[4 + h], beside)
            )
            self.onward.append(
                remote(half(relay, h), dst, send.at[6 + h], recv.at[2 + h], middle)
            )

    def load(self):
        for c in self.loads:
            c.start()

    def over_z(self, late=False):
        self.loads[0].wait()
        self.y_far.wait_recv()
        self.each(lambda at: self.put(at))
        Spread.start_z(self, 0, 1 if late else 2)

    def start_late(self):
        Spread.start_z(self, 1, 2)

    def relay(self, half):
        @pl.when(self.inner)
        def _():
            self.toward[half].wait_recv()
            self.onward[half].start()

    def put(self, at):
        self.far[at] = (self.far[at].astype(f32) + self.got[(0,) + at].astype(f32)).astype(bf16)

    def each(self, visit):
        lead, rows = self.far.shape[:-2], self.far.shape[-2]

        def inner(i, _):
            part = pl.ds(pl.multiple_of(i * 32, 32), 32)
            if lead:
                for k in range(lead[0]):
                    visit((k, part))
            else:
                visit((part,))
            return 0

        lax.fori_loop(0, rows // 32, inner, 0)

    def total(self, at):
        return (self.near[at].astype(f32) + self.got[(1,) + at].astype(f32)) + self.got[
            (2,) + at
        ].astype(f32)

    def arrive(self):
        self.loads[1].wait()
        self.y_near.wait_recv()
        for c in self.direct:
            c.wait_recv()

    def drain(self):
        for c in [self.y_far, self.y_near] + self.direct:
            c.wait_send()

        @pl.when(self.inner)
        def _():
            for c in self.onward:
                c.wait_send()


def backward_pass(x, act, down_w, middle, tokens, cotangent, gains, headgate, qkv_w, out_w, hidden_one,
                  qkv, low, gate, mixed, gated, starts, down_grad, ffn_grad, docs, shards, cid):
    _, rows, width = x.shape
    planes = 4
    streams = GROUP // shards
    length = rows * shards
    group_rows = rows * GROUP
    qcols = gate.shape[1]
    qkv_cols = qkv.shape[1]
    kcols = (qkv_cols - qcols) // 2
    heads = qcols // HEAD_SIZE
    brows = down_grad.shape[2]
    both = ffn_grad.shape[4]
    hidden = both // 2
    wrows = width // (planes * GROUP)
    gain_rows = width // 128
    score_scale = HEAD_SIZE ** (-0.5)
    cosine, sine = rope_constants(length)
    srows = 24
    inputs = [
        x, middle, tokens, cotangent, headgate, qkv_w, out_w, qkv, low, gate, mixed, gated,
    ]

    def body(
        gains_ref, starts_ref, cos_ref, sin_ref, act_in, dw_in, h1_ref, down_ref, ffn_ref,
        i0, i1, i2, i3, i4, i5, i6, i7, i8, i9, i10, i11,
        t0, t1, t2, t3, t4, t5, t6, t7, t8, s_out, final_ref,
        layer_ref, tgrad_ref, gate_out, up_out, query_out, key_out, value_out, o_out, down_out,
        fsem, dw_ref, product_ref, act_sem, dw_sem, product_sem, partial, mid_ref, tok_ref, cot_ref, hg_ref, wq_ref, wout_ref, qkv_ref, low_ref, gate_ref,
        mixed_ref, gated_ref,
        held, db_all, dmid, gq, dgl, dk_acc, dv_acc, dmix, small, stage, s_got, s_held, s_line,
        g_got, g_far, g_near, g_in, d_got, d_far, d_near, q_own, q_got, q_far, q_near, q_in,
        o_own, o_got, o_far, o_near, o_in, g_relay, d_relay, q_relay, o_relay,
        pair, out, near, far, rsend, rrecv, r2send, r2recv, r3send, r3recv, csend, crecv,
        isem, gsend, grecv, dsend, drecv, qsend, qrecv, osend, orecv, gxsend, gxrecv, qxsend,
        qxrecv, oxsend, oxrecv, asend, arecv, bsend, brecv, lsem, turn,
    ):
        sources = [i0, i1, i2, i3, i4, i5, i6, i7, i8, i9, i10, i11]
        targets = [
            partial, mid_ref, tok_ref, cot_ref, hg_ref, wq_ref, wout_ref, qkv_ref, low_ref,
            gate_ref, mixed_ref, gated_ref,
        ]
        finals = [
            pltpu.make_async_copy(ready, target, fsem.at[i])
            for i, (ready, target) in enumerate(
                (
                    (layer_ref, t0), (tgrad_ref, t1), (gate_out, t2), (up_out, t3),
                    (query_out, t4), (key_out, t5), (value_out, t6), (o_out, t7), (down_out, t8),
                )
            )
        ]
        place = Place(shards)
        tp, dp, flat = place.tp, place.dp(), place.flat()
        high, y, seq = lax.axis_index("zh"), lax.axis_index("y"), lax.axis_index("seq")
        loads = [
            pltpu.make_async_copy(s, t, isem.at[i])
            for i, (s, t) in enumerate(zip(sources, targets))
        ]
        for c in loads[:4]:
            c.start()
        load_act = [
            pltpu.make_async_copy(act_in.at[:, pl.ds(0, qkv_cols)], gq, act_sem.at[0]),
            pltpu.make_async_copy(act_in.at[:, pl.ds(qkv_cols, qcols)], dmix, act_sem.at[1]),
        ]
        for c in load_act:
            c.start()
        barrier = pltpu.get_barrier_semaphore()

        def signal(device, semaphore=barrier):
            pl.semaphore_signal(
                semaphore, inc=1, device_id=device, device_id_type=pl.DeviceIdType.MESH
            )

        for device in group_peers(place):
            signal(device)
        for k in range(1, planes):
            signal(place.dp_device((dp + k) % planes))
        owner = place.head(tp) * planes + dp
        source = {"st": lax.axis_index("st"), "seq": high * 2 + y}
        source.update(place.dp_device(seq))

        @pl.when(owner != flat)
        def _():
            signal(source)

        inner = high != lax.axis_index("st")

        @pl.when(inner)
        def _():
            signal({"zh": 1 - high, "st": 1 - lax.axis_index("st")})

        pl.semaphore_wait(
            barrier,
            GROUP + planes - 2 + (owner != flat).astype(jnp.int32) + inner.astype(jnp.int32),
        )

        ffn = PlaceSums(
            lambda zp, yp: ffn_ref.at[zp, :, yp], g_got, g_far, g_near, g_relay, gsend, grecv
        )
        down = PlaceSums(lambda zp, yp: down_ref.at[zp, yp], d_got, d_far, d_near, d_relay, dsend, drecv)
        down.y_far.start()
        ffn.y_far.start()
        ffn.y_near.start()
        down.load()
        ffn.load()
        for c in loads[4:]:
            c.start()

        small[...] = jnp.zeros_like(small)
        gain_all = gains_ref[...]
        gain_one = jnp.concatenate([gain_all[i : i + 1] for i in range(gain_rows)], axis=1)
        gain_two = jnp.concatenate(
            [gain_all[gain_rows + i : gain_rows + i + 1] for i in range(gain_rows)], axis=1
        )
        query_gain = gain_all[2 * gain_rows : 2 * gain_rows + 1]
        key_gain = gain_all[2 * gain_rows + 1 : 2 * gain_rows + 2]
        for c in loads[:4]:
            c.wait()

        def emit_dm(part, total):
            value = mid_ref[part]
            scale = rms_scale(value)
            normed = value * scale
            small[17:18] += jnp.sum(total * normed, axis=0, keepdims=True)
            dm = cot_ref[part].astype(f32) + norm_back(total * gain_two, normed, scale)
            dmid[part] = dm
            held[part] = dm.astype(bf16)

        ring_scatter(place, partial, pair, out, near, far, rsend, rrecv, emit_dm)
        grad = RingGather(place, held, db_all, csend, crecv)
        grad.start()
        h1_all = partial
        load_h1 = pltpu.make_async_copy(h1_ref, h1_all, lsem.at[0])
        load_h1.start()

        for c in load_act:
            c.wait()
        fine = dw_ref.shape[2]
        blocks = width // fine

        def columns(i):
            return pl.ds(pl.multiple_of(i * fine, fine), fine)

        def weight_load(i):
            return pltpu.make_async_copy(
                dw_in.at[:, columns(i)], dw_ref.at[i % 2], dw_sem.at[i % 2]
            )

        def product_store(i):
            return pltpu.make_async_copy(
                product_ref.at[i % 2], final_ref.at[:, :, columns(i)], product_sem.at[i % 2]
            )

        weight_load(0).start()

        def down_product(i, _):
            @pl.when(i + 1 < blocks)
            def _():
                weight_load(i + 1).start()

            weight_load(i).wait()

            @pl.when(i >= 2)
            def _():
                product_store(i - 2).wait()

            product = jnp.dot(
                gq[...], dw_ref[i % 2, 0:qkv_cols], preferred_element_type=f32
            ) + jnp.dot(dmix[...], dw_ref[i % 2, qkv_cols:], preferred_element_type=f32)
            product_ref[i % 2] = product.astype(bf16).reshape(GROUP, rows, fine)
            product_store(i).start()
            return 0

        lax.fori_loop(0, blocks, down_product, 0)
        for i in (blocks - 2, blocks - 1):
            product_store(i).wait()
        down.over_z()
        grad.pass_on()
        down.relay(0)
        grad.step_across()
        down.relay(1)
        grad.step_far()
        for c in loads[4:]:
            c.wait()
        grad.finish()

        lanes = lax.broadcasted_iota(jnp.int32, (1, 128), 1)
        head = place.head(tp)
        def open_out(s, _):
            part = pl.ds(pl.multiple_of(s * length, length), length)
            db = db_all[pl.ds(s * shards, shards)].reshape(length, width)
            da = lax.dot_general(
                db, wout_ref[...], (((1,), (1,)), ((), ())), preferred_element_type=f32
            )
            logits = jnp.zeros((length, 128), f32)
            for g in range(heads):
                at = g * HEAD_SIZE
                piece = da[:, at : at + HEAD_SIZE]
                opened = gate_ref[part, at : at + HEAD_SIZE]
                dmix[part, at : at + HEAD_SIZE] = (piece * opened).astype(bf16)
                own = jnp.sum(
                    piece * mixed_ref[part, at : at + HEAD_SIZE].astype(f32), axis=1,
                    keepdims=True,
                )
                logits = jnp.where(
                    lanes == head * heads + g, own * opened * (1.0 - opened), logits
                )
            dgl[part] = logits.astype(bf16)
            return 0

        lax.fori_loop(0, streams, open_out, 0)
        wide = 512
        def out_grad(i, _):
            cols = pl.ds(pl.multiple_of(i * wide, wide), wide)
            product = lax.dot_general(
                gated_ref[...], db_all[:, :, cols].reshape(group_rows, wide),
                (((0,), (0,)), ((), ())), preferred_element_type=f32,
            ).astype(bf16)
            for j in range(planes):
                o_own[j // 2, j % 2, :, cols] = product[j * wrows : (j + 1) * wrows]
            return 0

        lax.fori_loop(0, width // wide, out_grad, 0)
        outs = PlaceSums(lambda zp, yp: o_own.at[zp, yp], o_got, o_far, o_near, o_relay, osend, orecv)
        outs.y_far.start()
        outs.load()
        ffn.over_z(True)

        block = 128

        def attend_back(s, carried):
            query_part, key_part = carried
            base = pl.multiple_of(s * length, length)
            row = starts_ref[pl.ds(s, 1)]
            dk_acc[...] = jnp.zeros_like(dk_acc)
            dv_acc[...] = jnp.zeros_like(dv_acc)

            def back(grad_rotated, raw, gain):
                grad_gained = grad_rotated * cos_ref[...] - pltpu.roll(
                    grad_rotated, HEAD_SIZE // 2, 1
                ) * sin_ref[...]
                scale = rms_scale(raw)
                normed = raw * scale
                return (
                    jnp.sum(grad_gained * normed, axis=0, keepdims=True),
                    norm_back(grad_gained * gain, normed, scale).astype(bf16),
                )

            for r in range(0, length, block):
                keys = r + block
                allowed = document_mask(row, docs, r, block, keys)
                key = low_ref[pl.ds(base, keys), qcols : qcols + HEAD_SIZE]
                value = low_ref[pl.ds(base, keys), qcols + HEAD_SIZE :]
                part = pl.ds(base + r, block)
                for g in range(heads):
                    at = g * HEAD_SIZE
                    query = low_ref[part, at : at + HEAD_SIZE]
                    scores = (
                        lax.dot_general(
                            query, key, (((1,), (1,)), ((), ())), preferred_element_type=f32
                        )
                        * score_scale
                    )
                    scores = jnp.where(allowed, scores, MASK_FILL)
                    weights = jnp.exp(scores - jnp.max(scores, axis=1, keepdims=True))
                    probs = weights / jnp.sum(weights, axis=1, keepdims=True)
                    dout = dmix[part, at : at + HEAD_SIZE]
                    dprobs = lax.dot_general(
                        dout, value, (((1,), (1,)), ((), ())), preferred_element_type=f32
                    )
                    delta = jnp.sum(probs * dprobs, axis=1, keepdims=True)
                    dscores = (probs * (dprobs - delta)).astype(bf16)
                    dq = jnp.dot(dscores, key, preferred_element_type=f32) * score_scale
                    gq[part, at : at + HEAD_SIZE] = dq.astype(bf16)
                    dk_acc[0:keys] += lax.dot_general(
                        dscores, query, (((0,), (0,)), ((), ())), preferred_element_type=f32
                    )
                    dv_acc[0:keys] += lax.dot_general(
                        probs.astype(bf16), dout, (((0,), (0,)), ((), ())),
                        preferred_element_type=f32,
                    )
            part = pl.ds(base, length)
            for g in range(heads):
                at = g * HEAD_SIZE
                sums, grads = back(
                    gq[part, at : at + HEAD_SIZE].astype(f32), qkv_ref[part, at : at + HEAD_SIZE],
                    query_gain,
                )
                query_part = query_part + sums
                gq[part, at : at + HEAD_SIZE] = grads
            sums, grads = back(
                (dk_acc[...] * score_scale).astype(bf16).astype(f32),
                qkv_ref[part, qcols : qcols + HEAD_SIZE], key_gain,
            )
            key_part = key_part + sums
            gq[part, qcols : qcols + HEAD_SIZE] = grads
            gq[part, qcols + HEAD_SIZE :] = dv_acc[...].astype(bf16)
            return query_part, key_part

        query_part, key_part = lax.fori_loop(
            0, streams, attend_back,
            (jnp.zeros((1, HEAD_SIZE), f32), jnp.zeros((1, HEAD_SIZE), f32)),
        )

        load_h1.wait()
        def qkv_grad(n, _):
            cols = pl.ds(pl.multiple_of(n * 256, 256), 256)
            product = lax.dot_general(
                h1_all[:, :, cols].reshape(group_rows, 256), gq[...], (((0,), (0,)), ((), ())),
                preferred_element_type=f32,
            )
            q_own[n // 4, n // 2 % 2, n % 2] = product.astype(bf16)
            return 0

        lax.fori_loop(0, width // 256, qkv_grad, 0, unroll=4)
        qkvs = PlaceSums(lambda zp, yp: q_own.at[zp, :, yp], q_got, q_far, q_near, q_relay, qsend, qrecv)
        qkvs.y_far.start()
        outs.y_near.start()
        qkvs.y_near.start()
        down.y_near.start()
        qkvs.load()
        def headgate_grad(i, _):
            cols = pl.ds(pl.multiple_of(i * wide, wide), wide)
            small[0:16, cols] = lax.dot_general(
                dgl[...], h1_all[:, :, cols].reshape(group_rows, wide),
                (((0,), (0,)), ((), ())), preferred_element_type=f32,
            )[0:16]
            return 0

        lax.fori_loop(0, width // wide, headgate_grad, 0)

        def dh1(i, _):
            s = i // (width // wide)
            at = pl.multiple_of(i % (width // wide) * wide, wide)
            part, cols = pl.ds(pl.multiple_of(s * length, length), length), pl.ds(at, wide)
            product = lax.dot_general(
                gq[part], wq_ref[cols], (((1,), (1,)), ((), ())), preferred_element_type=f32
            ) + lax.dot_general(
                dgl[part], hg_ref[cols], (((1,), (1,)), ((), ())), preferred_element_type=f32
            )
            partial[pl.ds(s * shards, shards), :, cols] = product.astype(bf16).reshape(
                shards, rows, wide
            )
            return 0

        lax.fori_loop(0, streams * (width // wide), dh1, 0, unroll=2)

        def emit_tokens(part, total):
            tok = tok_ref[part].astype(f32)
            scale = rms_scale(tok)
            normed = tok * scale
            small[16:17] += jnp.sum(total * normed, axis=0, keepdims=True)
            tgrad_ref[part] = (
                dmid[part] + norm_back(total * gain_one, normed, scale)
            ).astype(bf16)

        load_final = pltpu.make_async_copy(final_ref, db_all, lsem.at[1])
        load_final.start()
        ring_scatter(
            place, partial, pair, out, near, far, r2send, r2recv, emit_tokens,
            (lambda: ffn.relay(0), ffn.start_late),
        )
        finals[1].start()
        ring_peers = [place.right(), place.left(), place.partner()]
        for device in ring_peers:
            signal(device, turn)
        outs.over_z()
        qkvs.over_z()
        ffn.relay(1)

        small[18:19] = jnp.concatenate([query_part] * gain_rows, axis=1)
        small[19:20] = jnp.concatenate([key_part] * gain_rows, axis=1)
        for t in range(GROUP):
            for d in range(planes):
                lane = columns_of(d, t, shards) // 2 * 128
                stage[t, d * srows : (d + 1) * srows] = small[:, lane : lane + 128]
        sums = Exchange(place, stage, s_got, asend, arecv)
        sums.start()

        load_final.wait()
        pl.semaphore_wait(turn, len(ring_peers))

        def emit_layer(part, total):
            layer_ref[part] = (mid_ref[part] + total).astype(bf16)

        def first():
            outs.relay(0)
            outs.relay(1)

        def scatter_rows(total, ready, send, recv, into):
            def keep(at):
                ready[at] = total(at).astype(bf16)

            copies = []
            for k in range(GROUP):
                peer = (tp + k) % GROUP
                src = ready.at[peer // shards, pl.ds(peer % shards * wrows, wrows)]
                if k == 0:
                    copies.append(pltpu.make_async_copy(src, into.at[tp], send.at[0]))
                else:
                    copies.append(
                        remote(src, into.at[tp], send.at[k], recv.at[k], place.device(peer))
                    )
            return keep, copies

        keep_ffn, ffn_rows = scatter_rows(ffn.total, g_near, gxsend, gxrecv, g_in)

        def second():
            qkvs.relay(0)
            qkvs.relay(1)
            ffn.arrive()
            ffn.each(keep_ffn)
            for c in ffn_rows:
                c.start()

        ring_scatter(
            place, db_all, pair, out, near, far, r3send, r3recv, emit_layer, (first, second)
        )
        finals[0].start()
        sums.finish()
        s_held[...] = jnp.sum(s_got[...], axis=0).reshape(s_held.shape)
        line_own = pltpu.make_async_copy(s_held.at[dp], s_line.at[dp], bsend.at[0])
        line_own.start()
        lines = []
        for k in range(1, planes):
            to = (dp + k) % planes
            lines.append(
                remote(
                    s_held.at[to], s_line.at[dp], bsend.at[k], brecv.at[k], place.dp_device(to)
                )
            )
            lines[-1].start()

        down.arrive()

        def put_down(at):
            down_out[at] = down.total(at)

        down.each(put_down)
        finals[8].start()

        def landed(copies):
            copies[0].wait()
            for c in copies[1:]:
                c.wait_recv()

        landed(ffn_rows)
        def unpack_rows(i, _):
            part = pl.ds(pl.multiple_of(i * 16, 16), 16)
            for t in range(GROUP):
                for d in range(planes):
                    column = columns_of(d, t, shards)
                    for m, ref in enumerate((gate_out, up_out)):
                        lane = m * hidden + d * brows
                        ref[part, column * brows : (column + 1) * brows] = g_in[
                            t, part, lane : lane + brows
                        ].astype(f32)
            return 0

        lax.fori_loop(0, wrows // 16, unpack_rows, 0)
        finals[2].start()
        finals[3].start()

        outs.arrive()

        def keep_out(at):
            o_near[at] = outs.total(at).astype(bf16)

        outs.each(keep_out)
        out_own = pltpu.make_async_copy(o_near, o_in, oxsend)
        out_far = remote(o_near, o_in, oxsend, oxrecv, place.any_device(owner))

        @pl.when(owner == flat)
        def _():
            out_own.start()

        @pl.when(owner != flat)
        def _():
            out_far.start()

        qkvs.arrive()
        keep, qkv_rows = scatter_rows(qkvs.total, q_near, qxsend, qxrecv, q_in)
        qkvs.each(keep)
        for c in qkv_rows:
            c.start()

        landed(qkv_rows)
        for t in range(GROUP):
            home = place.head(t)
            query_out[:, home * qcols : (home + 1) * qcols] = q_in[t, :, :qcols].astype(f32)
            key_out[:, home * kcols : (home + 1) * kcols] = q_in[
                t, :, qcols : qcols + kcols
            ].astype(f32)
            value_out[:, home * kcols : (home + 1) * kcols] = q_in[
                t, :, qcols + kcols :
            ].astype(f32)

        for c in finals[4:7]:
            c.start()

        @pl.when(owner == flat)
        def _():
            out_own.wait()

        @pl.when(owner != flat)
        def _():
            out_far.wait()

        o_out[...] = o_in[...].astype(f32)
        finals[7].start()
        for c in lines:
            c.wait_recv()
        line_own.wait()
        summed = jnp.sum(s_line[...], axis=0)
        per_row = 128 // wrows
        gcols = HEAD_SIZE // (planes * GROUP)
        s_out[...] = jnp.where(
            lax.broadcasted_iota(jnp.int32, (srows, 128), 0) < 18,
            pltpu.roll(summed, (128 - flat % per_row * wrows) % 128, 1),
            pltpu.roll(summed, (128 - flat * gcols) % 128, 1),
        )
        for c in lines + ffn_rows[1:] + qkv_rows[1:]:
            c.wait_send()
        for c in (ffn, down, qkvs, outs):
            c.drain()
        for c in finals:
            c.wait()

    shape = jax.ShapeDtypeStruct
    vmem = pltpu.VMEM
    wide_rows = shards * wrows
    return pallas(
        body,
        [
            shape((rows, width), bf16),
            shape((rows, width), bf16),
            shape((wrows, hidden * GROUP), f32),
            shape((wrows, hidden * GROUP), f32),
            shape((wrows, qcols * GROUP), f32),
            shape((wrows, kcols * GROUP), f32),
            shape((wrows, kcols * GROUP), f32),
            shape((wrows, width), f32),
            shape((brows, width), f32),
            shape((srows, 128), f32),
            shape((GROUP, rows, width), bf16),
        ],
        [VMEM] * 4 + [ANY] * (5 + len(inputs)),
        [ANY] * 9 + [VMEM, ANY],
        [
            vmem((rows, width), bf16),
            vmem((rows, width), bf16),
            vmem((wrows, hidden * GROUP), f32),
            vmem((wrows, hidden * GROUP), f32),
            vmem((wrows, qcols * GROUP), f32),
            vmem((wrows, kcols * GROUP), f32),
            vmem((wrows, kcols * GROUP), f32),
            vmem((wrows, width), f32),
            vmem((brows, width), f32),
            DMA((9,)),
            vmem((2, act.shape[1], 256), bf16),
            vmem((2, GROUP, rows, 256), bf16),
            DMA((2,)), DMA((2,)), DMA((2,)),
        ]
        + [vmem(i.shape, i.dtype) for i in inputs]
        + [
            vmem((rows, width), bf16),
            vmem((GROUP, rows, width), bf16),
            vmem((rows, width), f32),
            vmem((group_rows, qkv_cols), bf16),
            vmem((group_rows, 128), bf16),
            vmem((length, HEAD_SIZE), f32),
            vmem((length, HEAD_SIZE), f32),
            vmem((group_rows, qcols), bf16),
            vmem((srows, width), f32),
            vmem((GROUP, planes * srows, 128), f32),
            vmem((GROUP, planes * srows, 128), f32),
            vmem((planes, srows, 128), f32),
            vmem((planes, srows, 128), f32),
            vmem((3, streams, wide_rows, both), bf16),
            vmem((streams, wide_rows, both), bf16),
            vmem((streams, wide_rows, both), bf16),
            vmem((GROUP, wrows, both), bf16),
            vmem((3, brows, width), bf16),
            vmem((brows, width), bf16),
            vmem((brows, width), bf16),
            vmem((2, streams, 2, wide_rows, qkv_cols), bf16),
            vmem((3, streams, wide_rows, qkv_cols), bf16),
            vmem((streams, wide_rows, qkv_cols), bf16),
            vmem((streams, wide_rows, qkv_cols), bf16),
            vmem((GROUP, wrows, qkv_cols), bf16),
            vmem((2, 2, wrows, width), bf16),
            vmem((3, wrows, width), bf16),
            vmem((wrows, width), bf16),
            vmem((wrows, width), bf16),
            vmem((wrows, width), bf16),
            vmem((streams, wide_rows, both), bf16),
            vmem((brows, width), bf16),
            vmem((streams, wide_rows, qkv_cols), bf16),
            vmem((wrows, width), bf16),
        ]
        + scatter_scratch(rows, width)
        + [DMA((10,)), DMA((10,)), DMA((10,)), DMA((10,))]
        + gather_scratch()
        + [DMA((len(inputs),))]
        + [DMA((PlaceSums.SENDS,)), DMA((PlaceSums.RECVS,))] * 4
        + [DMA((GROUP,)), DMA((GROUP,)), DMA((GROUP,)), DMA((GROUP,)), DMA, DMA]
        + [DMA((GROUP,)), DMA((GROUP,)), DMA((planes,)), DMA((planes,)), DMA((2,))]
        + [pltpu.SemaphoreType.REGULAR],
        cid,
        180,
        63,
    )(gains, starts, cosine, sine, act, down_w, hidden_one, down_grad, ffn_grad, *inputs)


def store(*arrays):
    count = len(arrays)
    pieces = []
    for i, a in enumerate(arrays):
        step = a.shape[0] // 4 if a.shape[0] * a.shape[1] > 300000 else a.shape[0] // 2
        pieces += [(i, pl.ds(at, step)) for at in range(0, a.shape[0], step)]

    def body(*refs):
        load_sem, store_sem = refs[-2:]
        staged = refs[2 * count : 3 * count]
        loads, stores = [], []
        for n, (i, part) in enumerate(pieces):
            loads.append(
                pltpu.make_async_copy(refs[i].at[part], staged[i].at[part], load_sem.at[n])
            )
            stores.append(
                pltpu.make_async_copy(
                    staged[i].at[part], refs[count + i].at[part], store_sem.at[n]
                )
            )
        for c in loads:
            c.start()
        for load, c in zip(loads, stores):
            load.wait()
            c.start()
        for c in stores:
            c.wait()

    return pl.pallas_call(
        body,
        out_shape=[jax.ShapeDtypeStruct(a.shape, a.dtype) for a in arrays],
        in_specs=[ANY] * count,
        out_specs=[ANY] * count,
        scratch_shapes=[pltpu.VMEM(a.shape, a.dtype) for a in arrays]
        + [DMA((len(pieces),)), DMA((len(pieces),))],
        compiler_params=pltpu.CompilerParams(vmem_limit_bytes=62 * 1024 * 1024),
    )(*arrays)


def settle(qkv_grad, out_grad, small, qcols, kcols, planes, direct, shards, cid):
    srows = small.shape[1] // planes
    cols = small.shape[2]
    wrows, width = out_grad.shape

    def body(
        q_ref, o_ref, s_ref, query_out, key_out, value_out, o_out, s_out, q_got, o_got, got, held,
        line, qsend, qrecv, osend, orecv, asend, arecv, bsend, brecv,
    ):
        place = Place(shards)
        tp, dp, flat = place.tp, place.dp(), place.flat()
        barrier = pltpu.get_barrier_semaphore()

        def signal(device):
            pl.semaphore_signal(
                barrier, inc=1, device_id=device, device_id_type=pl.DeviceIdType.MESH
            )

        for device in group_peers(place):
            signal(device)
        for k in range(1, planes):
            signal(place.dp_device((dp + k) % planes))
        if direct:
            owner = place.head(tp) * planes + dp
            high, y = lax.axis_index("zh"), lax.axis_index("y")
            source = {"st": lax.axis_index("st"), "seq": high * 2 + y}
            source.update(place.dp_device(lax.axis_index("seq")))

            @pl.when(owner != flat)
            def _():
                signal(source)

            pl.semaphore_wait(barrier, GROUP + planes - 2 + (owner != flat).astype(jnp.int32))
        else:
            pl.semaphore_wait(barrier, GROUP + planes - 2)

        sums = Exchange(place, s_ref, got, asend, arecv)
        sums.start()
        qkv = Exchange(place, q_ref, q_got, qsend, qrecv)
        qkv.start()
        if direct:
            out_own = pltpu.make_async_copy(o_ref, o_got, osend)
            out_far = remote(o_ref, o_got, osend, orecv, place.any_device(owner))

            @pl.when(owner == flat)
            def _():
                out_own.start()

            @pl.when(owner != flat)
            def _():
                out_far.start()

        sums.finish()
        held[...] = jnp.sum(got[...], axis=0).reshape(held.shape)
        line_own = pltpu.make_async_copy(held.at[dp], line.at[dp], bsend.at[0])
        line_own.start()
        lines = []
        for k in range(1, planes):
            to = (dp + k) % planes
            lines.append(
                remote(held.at[to], line.at[dp], bsend.at[k], brecv.at[k], place.dp_device(to))
            )
            lines[-1].start()
        qkv.finish()
        for t in range(GROUP):
            head = place.head(t)
            query_out[:, head * qcols : (head + 1) * qcols] = q_got[t, :, :qcols].astype(f32)
            key_out[:, head * kcols : (head + 1) * kcols] = q_got[
                t, :, qcols : qcols + kcols
            ].astype(f32)
            value_out[:, head * kcols : (head + 1) * kcols] = q_got[t, :, qcols + kcols :].astype(
                f32
            )
        if direct:

            @pl.when(owner == flat)
            def _():
                out_own.wait()

            @pl.when(owner != flat)
            def _():
                out_far.wait()

            o_out[...] = o_got[...].astype(f32)
        else:
            o_out[...] = o_ref[...].astype(f32)
        for c in lines:
            c.wait_recv()
        line_own.wait()
        s_out[...] = jnp.sum(line[...], axis=0)
        for c in lines:
            c.wait_send()

    return pallas(
        body,
        [
            jax.ShapeDtypeStruct((wrows, GROUP * qcols), f32),
            jax.ShapeDtypeStruct((wrows, GROUP * kcols), f32),
            jax.ShapeDtypeStruct((wrows, GROUP * kcols), f32),
            jax.ShapeDtypeStruct((wrows, width), f32),
            jax.ShapeDtypeStruct((srows, cols), f32),
        ],
        [VMEM, VMEM, VMEM],
        [VMEM] * 5,
        [
            pltpu.VMEM(qkv_grad.shape, bf16),
            pltpu.VMEM(out_grad.shape, bf16),
            pltpu.VMEM(small.shape, f32),
            pltpu.VMEM((planes, srows, cols), f32),
            pltpu.VMEM((planes, srows, cols), f32),
            DMA((GROUP,)), DMA((GROUP,)), DMA, DMA,
            DMA((GROUP,)), DMA((GROUP,)), DMA((planes,)), DMA((planes,)),
        ],
        cid,
        20,
    )(qkv_grad, out_grad, small)


def local(
    tokens, doc_starts, attn_gain, query_gain, key_gain, w_query, key_weight, value_weight,
    w_headgate, w_out, ffn_gain, w_gate, w_up, w_down, cotangent,
):
    zs, ys = lax.axis_size("zh"), lax.axis_size("y")
    planes = zs * ys
    direct = zs == 2 and ys == 2
    streams = lax.axis_size("st")
    shards = lax.axis_size("seq")
    devices = planes * GROUP
    rows, width = tokens.shape
    length = rows * shards
    group_rows = rows * GROUP
    wrows = w_query.shape[0]
    brows = w_down.shape[0]
    hidden = brows * planes
    qcols = w_query.shape[1] // GROUP
    kcols = key_weight.shape[1] // GROUP
    group_heads = qcols // HEAD_SIZE
    all_heads = w_headgate.shape[1]
    score_scale = HEAD_SIZE ** (-0.5)
    dp = lax.axis_index(DP)
    tp = lax.axis_index(TP)

    hg = wrows * all_heads
    gcols = query_gain.shape[0]
    at = hg + 2 * wrows
    count = at + 2 * gcols
    sums = -(-count // 1024) * 8
    docs = doc_starts.shape[1]
    qkv_cols = qcols + 2 * kcols
    starts_row = jnp.concatenate(
        [(doc_starts[0] // 128).astype(bf16), (doc_starts[0] % 128).astype(bf16)]
    )
    headgate_rows = jnp.pad(w_headgate, ((0, 0), (0, 128 - all_heads)))
    if direct:
        gain_rows = width // 128
        others = [attn_gain, ffn_gain, query_gain, key_gain, starts_row]
        small = jnp.pad(w_headgate, ((0, 16), (0, 128 - all_heads)))
        for i, row in enumerate(others):
            small = small + jnp.pad(
                row[None], ((wrows + i, 15 - i), (0, 128 - row.shape[0]))
            )
        (
            cot_all, ffn_w, down_w, hidden_one, hidden_two, small, gains, qkv_w, out_w, qkv,
            low, gate_full, mixed, gated, middle, headgate, starts,
        ) = forward_pass(
            tokens, cotangent, small, w_out, w_query, key_weight, value_weight, w_gate, w_up,
            w_down, docs, shards, 0,
        )
        cot_all = cot_all.reshape(group_rows, width)
        hidden_two = hidden_two.reshape(group_rows, width)
        ffn_w = ffn_w.reshape(width, 2 * hidden)
        down_w = down_w.reshape(hidden, width)
        gate_up = mm(hidden_two, ffn_w)
        gate_pre, up_proj = gate_up[:, :hidden], gate_up[:, hidden:]
        gate_sig = jax.nn.sigmoid(gate_pre)
        inner_act = (gate_pre * gate_sig * up_proj).astype(bf16)
        down_grad = mm_t(inner_act, cot_all).astype(bf16)
        grad_inner = mm_b(cot_all, down_w)
        grad_gate = grad_inner * up_proj * gate_sig * (1.0 + gate_pre * (1.0 - gate_sig))
        grad_up = grad_inner * gate_pre * gate_sig
        grad_gu = jnp.concatenate([grad_gate.astype(bf16), grad_up.astype(bf16)], axis=1)
        ffn_grad = mm_t(hidden_two, grad_gu).astype(bf16)
        places = (GROUP, rows, width)
        (
            layer_out, tokens_grad, gate_grad, up_grad, query_grad, key_grad, value_grad,
            out_grad, down_grad, small_sum, _,
        ) = backward_pass(
            mm_b(grad_gu, ffn_w).astype(bf16).reshape(places),
            inner_act, down_w, middle, tokens, cotangent, gains, headgate,
            qkv_w.reshape(width, qkv_cols), out_w.reshape(qcols, width), hidden_one, qkv, low,
            gate_full, mixed, gated, starts, down_grad.reshape(zs, ys, brows, width),
            ffn_grad.reshape(zs, streams, ys, shards * wrows, 2 * hidden), docs, shards, 1,
        )
        (
            layer_out, tokens_grad, gate_grad, up_grad, query_grad, key_grad, value_grad,
            out_grad, down_grad,
        ) = store(
            layer_out, tokens_grad, gate_grad, up_grad, query_grad, key_grad, value_grad,
            out_grad, down_grad,
        )
        return (
            layer_out,
            tokens_grad,
            small_sum[all_heads, :wrows],
            small_sum[18, :gcols],
            small_sum[19, :gcols],
            query_grad,
            key_grad,
            value_grad,
            small_sum[:all_heads, :wrows].T,
            out_grad,
            small_sum[all_heads + 1, :wrows],
            gate_grad,
            up_grad,
            down_grad,
        )
    else:
        srows = -(-(wrows + 6) // 16) * 16
        others = [attn_gain, ffn_gain, query_gain, key_gain, starts_row[:docs], starts_row[docs:]]
        small = jnp.concatenate(
            [headgate_rows]
            + [jnp.pad(row, (0, 128 - row.shape[0]))[None] for row in others]
            + [jnp.zeros((srows - wrows - 6, 128), bf16)]
        )
        tokens_all, cot_all, small, qkv_w, ffn_own = front(
            tokens, cotangent, small, w_out, w_query, key_weight, value_weight, w_gate, w_up,
            w_down, planes, False, shards, 0,
        )
        tokens_all = tokens_all.reshape(group_rows, width)
        cot_all = cot_all.reshape(group_rows, width)
        qkv_w = over_dp(qkv_w[0])
        ffn_w = over_dp(ffn_own)
        down_w = lax.all_gather(w_down, DP, axis=0, tiled=True)
        out_w = lax.all_gather(w_out, ALL, axis=0, tiled=True)
        out_w = lax.dynamic_slice_in_dim(out_w, tp * qcols, qcols, 0)
        head = tp
        here = pick(small[::shards], 1, dp)
        starts = here[:, wrows + 4, :docs].astype(jnp.int32) * 128
        starts = starts + here[:, wrows + 5, :docs].astype(jnp.int32)
    small = small.reshape(streams, shards, zs, ys, srows, 128).transpose(2, 0, 3, 1, 4, 5)
    small = small.reshape(devices, srows, 128)
    headgate_all = small[:, :wrows, :all_heads].reshape(width, all_heads)
    if not direct:
        attn_gain_f = small[:, wrows, :wrows].reshape(1, -1).astype(f32)
        ffn_gain_f = small[:, wrows + 1, :wrows].reshape(1, -1).astype(f32)
        query_gain_f = small[:, wrows + 2, :gcols].reshape(-1).astype(f32)
        key_gain_f = small[:, wrows + 3, :gcols].reshape(-1).astype(f32)
    headgate_own = lax.dynamic_slice_in_dim(headgate_all, head * group_heads, group_heads, 1)

    if not direct:
        residual_all = tokens_all.astype(f32)
        hidden_all = (residual_all * rms_scale(residual_all) * attn_gain_f).astype(bf16)
        qkv = mm(hidden_all, qkv_w)
    query_raw = qkv[:, :qcols].reshape(group_rows, group_heads, HEAD_SIZE)
    key_raw = qkv[:, qcols : qcols + kcols].reshape(group_rows, 1, HEAD_SIZE)
    value = qkv[:, qcols + kcols :].astype(bf16).reshape(streams, length, HEAD_SIZE)
    positions = jnp.tile(jnp.arange(length, dtype=jnp.int32), streams)
    cosine, sine = rotary_tables(positions)
    query_scale = rms_scale(query_raw)
    query_normed = query_raw * query_scale
    query = rotate(query_normed * query_gain_f, cosine, sine).astype(bf16)
    query = query.reshape(streams, length, group_heads, HEAD_SIZE)
    key_scale = rms_scale(key_raw)
    key_normed = key_raw * key_scale
    key = rotate(key_normed * key_gain_f, cosine, sine).astype(bf16)
    key = key.reshape(streams, length, HEAD_SIZE)
    stream_pos = jnp.arange(length, dtype=jnp.int32)
    segment = jnp.sum((stream_pos[None, :, None] >= starts[:, None, :]).astype(jnp.int32), axis=2)
    allowed = (stream_pos[:, None] >= stream_pos[None, :])[None] & (
        segment[:, :, None] == segment[:, None, :]
    )
    scores = jnp.einsum("bqgd,bkd->bgqk", query, key, preferred_element_type=f32) * score_scale
    scores = jnp.where(allowed[:, None], scores, MASK_FILL)
    row_max = jnp.max(scores, axis=-1, keepdims=True)
    weights = jnp.exp(scores - row_max)
    probs = weights / jnp.sum(weights, axis=-1, keepdims=True)
    probs_low = probs.astype(bf16)
    if not direct:
        mixed = jnp.einsum(
            "bgqk,bkd->bqgd", probs_low, value, preferred_element_type=f32
        ).astype(bf16)
    mixed_f = mixed.astype(f32).reshape(group_rows, group_heads, HEAD_SIZE)
    if direct:
        head_gate = gate_full.reshape(group_rows, group_heads, HEAD_SIZE)[:, :, :1]
    else:
        head_gate = jax.nn.sigmoid(mm(hidden_all, headgate_own))[:, :, None]
        gated = (mixed_f * head_gate).astype(bf16).reshape(group_rows, qcols)

    def parts(x):
        return x.astype(bf16).reshape(GROUP, rows, width)

    if not direct:
        middle, hidden_two = middle_step(
            parts(mm(gated, out_w)), tokens, ffn_gain_f, None, shards, 2
        )
        hidden_two = hidden_two.reshape(group_rows, width)

    gate_up = mm(hidden_two, ffn_w)
    gate_pre, up_proj = gate_up[:, :hidden], gate_up[:, hidden:]
    gate_sig = jax.nn.sigmoid(gate_pre)
    inner_act = (gate_pre * gate_sig * up_proj).astype(bf16)
    down_grad = mm_t(inner_act, cot_all).astype(bf16).reshape(zs, ys, brows, width)
    if direct:
        down_sum = PlaceSum(down_grad)
        down_sum.over_y()
    else:
        down_grad = scatter_dp(down_grad)
    grad_inner = mm_b(cot_all, down_w)
    grad_gate = (grad_inner * up_proj * gate_sig * (1.0 + gate_pre * (1.0 - gate_sig))).astype(bf16)
    grad_up = (grad_inner * gate_pre * gate_sig).astype(bf16)
    grad_gu = jnp.concatenate([grad_gate, grad_up], axis=1)
    ffn_grad = mm_t(hidden_two, grad_gu).astype(bf16)
    grad_gu, ffn_grad = lax.optimization_barrier((grad_gu, ffn_grad))
    if not direct:
        ffn_grad = scatter_dp(by_place(ffn_grad))
    grad_middle, ffn_gain_part, grad_branch, *ffn_first = middle_back(
        parts(mm_b(grad_gu, ffn_w)), middle, cotangent, ffn_gain_f,
        ffn_grad.reshape(zs, streams, ys, -1, 2 * hidden) if direct else None, shards, 3,
    )
    if direct:
        grad_branch, down_sum.far, down_sum.near, ffn_first = lax.optimization_barrier(
            (grad_branch, down_sum.far, down_sum.near, ffn_first[0])
        )
        down_z = down_sum.over_z()
        ffn_sum = PlaceSum(by_place(ffn_grad))
        ffn_sum.take(ffn_first.reshape(-1, 2 * hidden), None)
        ffn_z = ffn_sum.over_z()
        ffn_sum.near = ffn_sum.over_y_near()
    grad_branch = grad_branch.reshape(group_rows, width)
    layer_out = scatter_sum(parts(mm(inner_act, down_w)), middle, shards, 4)

    out_grad = mm_t(gated, grad_branch).astype(bf16).reshape(zs, ys, wrows, width)
    grad_gated = mm_b(grad_branch, out_w).reshape(group_rows, group_heads, HEAD_SIZE)
    grad_mixed = (grad_gated * head_gate).astype(bf16).reshape(
        streams, length, group_heads, HEAD_SIZE
    )
    gate_flat = head_gate[:, :, 0]
    grad_logit = (
        jnp.sum(grad_gated * mixed_f, axis=-1) * gate_flat * (1.0 - gate_flat)
    ).astype(bf16)
    grad_probs = jnp.einsum("bqgd,bkd->bgqk", grad_mixed, value, preferred_element_type=f32)
    row_delta = jnp.sum(probs * grad_probs, axis=-1, keepdims=True)
    grad_scores = (probs * (grad_probs - row_delta)).astype(bf16)
    grad_query = (
        jnp.einsum("bgqk,bkd->bqgd", grad_scores, key, preferred_element_type=f32) * score_scale
    ).astype(bf16)
    grad_key = (
        jnp.einsum("bgqk,bqgd->bkd", grad_scores, query, preferred_element_type=f32) * score_scale
    ).astype(bf16)
    grad_value = jnp.einsum(
        "bgqk,bqgd->bkd", probs_low, grad_mixed, preferred_element_type=f32
    ).astype(bf16)
    gqn = rotate_back(
        grad_query.astype(f32).reshape(group_rows, group_heads, HEAD_SIZE), cosine, sine
    )
    query_gain_part = jnp.sum(gqn * query_normed, axis=(0, 1))
    grad_query_raw = norm_back(gqn * query_gain_f, query_normed, query_scale).astype(bf16)
    gkn = rotate_back(grad_key.astype(f32).reshape(group_rows, 1, HEAD_SIZE), cosine, sine)
    key_gain_part = jnp.sum(gkn * key_normed, axis=(0, 1))
    grad_key_raw = norm_back(gkn * key_gain_f, key_normed, key_scale).astype(bf16)
    grad_qkv = jnp.concatenate(
        [
            grad_query_raw.reshape(group_rows, qcols),
            grad_key_raw.reshape(group_rows, kcols),
            grad_value.reshape(group_rows, kcols),
        ],
        axis=1,
    )
    qkv_grad = mm_t(hidden_all, grad_qkv).astype(bf16)
    if direct:
        qkv_grad, out_grad, grad_qkv, down_z = lax.optimization_barrier(
            (qkv_grad, out_grad, grad_qkv, down_z)
        )
        down_grad = down_sum.total(down_z)
        qkv_sum, out_sum = PlaceSum(by_place(qkv_grad)), PlaceSum(out_grad)
        qkv_sum.over_y()
        out_sum.over_y()
        qkv_z, out_z = qkv_sum.over_z(), out_sum.over_z()
        ffn_grad = ffn_sum.total(ffn_z)
        qkv_grad, out_grad = qkv_sum.total(qkv_z), out_sum.total(out_z)
    else:
        qkv_grad = scatter_dp(by_place(qkv_grad))
        out_grad = lax.dynamic_update_slice(
            jnp.zeros((width, width), bf16), out_grad.reshape(qcols, width), (tp * qcols, 0)
        )
        out_grad = lax.psum_scatter(out_grad, ALL, scatter_dimension=0, tiled=True)
    tokens_grad, attn_gain_part = tokens_back(
        parts(mm_b(grad_qkv, qkv_w) + mm_b(grad_logit, headgate_own)),
        tokens, grad_middle, attn_gain_f, shards, 5,
    )
    headgate_part = mm_t(hidden_all, grad_logit)
    headgate_part = lax.dynamic_update_slice(
        jnp.zeros((width, all_heads), f32), headgate_part, (0, head * group_heads)
    )

    small_sum = jnp.concatenate(
        [
            headgate_part.reshape(devices, hg),
            attn_gain_part.reshape(devices, wrows),
            ffn_gain_part.reshape(devices, wrows),
            query_gain_part.reshape(devices, gcols),
            key_gain_part.reshape(devices, gcols),
        ],
        axis=1,
    )
    small_sum = jnp.pad(small_sum, ((0, 0), (0, sums * 128 - count)))
    small_sum = small_sum.reshape(zs, streams, ys, shards, sums, 128)
    small_sum = small_sum.transpose(1, 3, 0, 2, 4, 5)
    small_sum = small_sum.reshape(GROUP, planes * sums, 128)

    gate_grad, up_grad = exchange_back(
        ffn_grad.reshape(GROUP, wrows, 2 * hidden), planes, shards, 6
    )
    query_grad, key_grad, value_grad, out_grad, small_sum = settle(
        qkv_grad.reshape(GROUP, wrows, qkv_cols), out_grad, small_sum, qcols, kcols, planes,
        direct, shards, 7,
    )
    small_sum = small_sum.reshape(-1)
    return (
        layer_out,
        tokens_grad,
        small_sum[hg : hg + wrows],
        small_sum[at : at + gcols],
        small_sum[at + gcols : at + 2 * gcols],
        query_grad,
        key_grad,
        value_grad,
        small_sum[:hg].reshape(wrows, all_heads),
        out_grad,
        small_sum[hg + wrows : hg + 2 * wrows],
        gate_grad,
        up_grad,
        down_grad.astype(f32),
    )


def solution(mesh):
    shards = mesh.shape["seq"]
    planes = (2, 2, 2) if shards == 4 and mesh.size == 32 else (1, GROUP // shards, -1)
    grouped = Mesh(mesh.devices.reshape(planes + (shards,)), ALL)
    two = P(ALL, None)
    one = P(ALL)
    return jax.shard_map(
        local,
        mesh=grouped,
        in_specs=(
            two, P(("zh", "st", "y"), None), one, one, one, two, two, two, two, two, one, two, two,
            two, two,
        ),
        out_specs=(two, two, one, one, one, two, two, two, two, two, one, two, two, two),
        check_vma=False,
    )
```
